32 devices in a mesh: dp: 8 (over y, x, core), tensor: 4 (over z).
Axes of the slice: x: 2, y: 2, z: 4, core: 2. Of those that a mesh axis runs over, the one named last changes fastest.
Arguments:
- hidden_in: bfloat16 [3, 4096, 768], P(None, ('dp', 'tensor')), may hold values from -6 to 6
- segment_ids: int32 [3, 32, 128], P(None, ('dp', 'tensor')), may hold values from 0 to 7, never falling along the last dimension, each value on 1 to 32 neighbouring positions
- pooled_grad: float32 [3, 32, 8, 768], P(None, ('dp', 'tensor')), may hold values from -96 to 96
- qkv_weight: bfloat16 [3, 768, 768], P(None, 'dp', 'tensor'), may hold values from -0.21875 to 0.21875
- qv_bias: bfloat16 [2, 768], P(None, ('dp', 'tensor')), may hold values from -1.1953125 to 1.1953125
- out_weight: bfloat16 [768, 768], P('tensor', 'dp'), may hold values from -0.875 to 0.875
- out_bias: bfloat16 [768], P(('dp', 'tensor')), may hold values from -1.1953125 to 1.1953125
- norm1_gain: bfloat16 [768], P(('dp', 'tensor')), may hold values from 0.099609375 to 1.8984375
- norm1_shift: bfloat16 [768], P(('dp', 'tensor')), may hold values from -1.1953125 to 1.1953125
- up_weight: bfloat16 [768, 3072], P('dp', 'tensor'), may hold values from -0.21875 to 0.21875
- up_bias: bfloat16 [3072], P(('dp', 'tensor')), may hold values from -1.1953125 to 1.1953125
- down_weight: bfloat16 [3072, 768], P('tensor', 'dp'), may hold values from -0.109375 to 0.109375
- down_bias: bfloat16 [768], P(('dp', 'tensor')), may hold values from -1.1953125 to 1.1953125
- norm2_gain: bfloat16 [768], P(('dp', 'tensor')), may hold values from 0.099609375 to 1.8984375
- norm2_shift: bfloat16 [768], P(('dp', 'tensor')), may hold values from -1.1953125 to 1.1953125
Outputs:
- pooled_out: float32 [3, 32, 8, 768], P(None, ('dp', 'tensor'))
- input_grad: float32 [3, 4096, 768], P(None, ('dp', 'tensor'))
- qkv_weight_grad: float32 [3, 768, 768], P(None, 'dp', 'tensor')
- qv_bias_grad: float32 [2, 768], P(None, ('dp', 'tensor'))
- out_weight_grad: float32 [768, 768], P('tensor', 'dp')
- out_bias_grad: float32 [768], P(('dp', 'tensor'))
- norm1_gain_grad: float32 [768], P(('dp', 'tensor'))
- norm1_shift_grad: float32 [768], P(('dp', 'tensor'))
- up_weight_grad: float32 [768, 3072], P('dp', 'tensor')
- up_bias_grad: float32 [3072], P(('dp', 'tensor'))
- down_weight_grad: float32 [3072, 768], P('tensor', 'dp')
- down_bias_grad: float32 [768], P(('dp', 'tensor'))
- norm2_gain_grad: float32 [768], P(('dp', 'tensor'))
- norm2_shift_grad: float32 [768], P(('dp', 'tensor'))
The draws below stay inside these ranges and needn't reach their ends.
Inputs may be any that keep to these rules, and one draw needn't show every extreme that they name: `segment_ids`: in every row of 128 tokens the segment numbers never fall, each number from 0 to 7 occurs on 1 to 32 consecutive tokens, and some sentence has exactly 32 tokens.
All inputs are finite; a program needn't handle non-finite values.
Results may differ from the reference program's by a relative error of at most 0.013.
Values may be sent and summed in bfloat16 or wider, within the bound.
No kernel may reach another device: no remote copies, remote signals or barrier semaphores. Data moves between devices by JAX's collectives and lax.ppermute only.
A program may use at most 128 MiB of HBM per device.

```python
import math
import jax
import jax.numpy as jnp
import numpy as np
from jax import lax

D = 768
H = 12
HD = 64
FF = 3072
LEN = 128
SEGS = 8
SEG_MOST = 32
MB = 3
TOKENS = 4096
NROWS = 32


def with_spikes(values, stream_key, source, target, blocks, factor):
    def block_of(axis_at):
        return (jnp.arange(values.shape[axis_at]) // (values.shape[axis_at] // blocks)).reshape((-1,) + (1,) * (values.ndim - 1 - axis_at))

    near = jax.random.permutation(stream_key, blocks)[block_of(target)]
    other_side = (block_of(target) + blocks // 2) % blocks
    return jnp.where((block_of(source) == near) | (block_of(source) == other_side), factor * values, values)


def block_scale(own_key, shape, shards, low, largest):
    loudness = 1.0
    for axis_at, shards_of in shards:
        steps = jax.random.uniform(jax.random.fold_in(jax.random.fold_in(own_key, 6), axis_at), (shards_of,), jnp.float32, low / len(shards), largest / len(shards))
        loudness = loudness * jnp.repeat(jnp.exp(steps), shape[axis_at] // shards_of).reshape((-1,) + (1,) * (len(shape) - 1 - axis_at))
    return loudness


def length_profile(count, total, limit, slope):
    loads = [(1 << 20) // math.isqrt(grade ** slope) + 1 for grade in range(2, count + 1)]
    spare, holding = total - limit - (count - 1), [1] * (count - 1)
    while spare > 0:
        free = [i for i in range(count - 1) if holding[i] < limit]
        pool, left = sum([loads[i] for i in free]), spare
        for i in free:
            more = min(limit - holding[i], max(1, left * loads[i] // pool), spare)
            holding[i] = holding[i] + more
            spare = spare - more
    return np.array([limit] + holding)


def ragged_sizes(stream_key, number_of, total, limit, skew):
    if number_of == 2:
        one = jax.random.randint(stream_key, (), max(1, total - limit), min(limit, total - 1) + 1)
        return jnp.stack([one, total - one])
    tallies = jnp.asarray(length_profile(number_of, total, limit, skew), jnp.int32)
    pairs = (number_of - 1) // 2
    source_of, taker = tallies[1:1 + 2 * pairs:2], tallies[2:2 + 2 * pairs:2]
    slack = jnp.minimum(source_of - 1, limit - taker)
    shifted = jax.random.randint(jax.random.fold_in(stream_key, 1), (pairs,), 0, 1 << 20) % (slack + 1)
    tallies = tallies.at[1:1 + 2 * pairs:2].set(source_of - shifted).at[2:2 + 2 * pairs:2].set(taker + shifted)
    return tallies[jax.random.permutation(jax.random.fold_in(stream_key, 2), number_of)]


def centred(own_key, dims, width, limit, split=(), kind=jnp.bfloat16):
    factor_of = block_scale(own_key, dims, split, -0.22, 0.18) if split else 1.0
    values = jax.random.normal(own_key, dims, jnp.float32) * width * factor_of
    return jnp.minimum(jnp.maximum(values, -limit), limit).astype(kind)


def gaussian_with(stream_key, extent, spread, bound, pieces, heavy, kind=jnp.bfloat16):
    values = spread * jax.random.normal(stream_key, extent, jnp.float32)
    if pieces:
        values = values * block_scale(stream_key, extent, pieces, -0.22, 0.18)
    return jnp.clip(with_spikes(values, jax.random.fold_in(stream_key, 3), *heavy), -bound, bound).astype(kind)


def setup_inputs(seed: int = 0) -> dict:
    streams_of = jax.random.split(jax.random.key(seed), 16)
    return {
        "hidden_in": gaussian_with(streams_of[0], (MB, TOKENS, D), 1.0, 6.0, ((1, 32),), (1, 2, 32, 2.75)),
        "segment_ids": jax.vmap(lambda own: jnp.searchsorted(jnp.cumsum(ragged_sizes(own, SEGS, LEN, SEG_MOST, 0)), jnp.arange(LEN), side="right"))(jax.random.split(streams_of[1], MB * NROWS)).reshape((MB, NROWS, LEN)).astype(jnp.int32),
        "pooled_grad": gaussian_with(streams_of[2], (MB, NROWS, SEGS, D), 16.0, 96.0, ((1, 32),), (1, 3, 32, 2.75), jnp.float32),
        "qkv_weight": centred(streams_of[3], (3, D, D), D ** -0.5, 0.21875, ((1, 8), (2, 4))),
        "qv_bias": centred(streams_of[4], (2, D), 0.2, 1.1953125, ((1, 32),)),
        "out_weight": centred(streams_of[5], (D, D), (D // 16) ** -0.5, 0.875, ((0, 4), (1, 8))),
        "out_bias": centred(streams_of[6], (D,), 0.2, 1.1953125, ((0, 32),)),
        "norm1_gain": jnp.clip(1.0 + 0.18 * jax.random.normal(streams_of[7], (D,), jnp.float32), 0.099609375, 1.8984375).astype(jnp.bfloat16),
        "norm1_shift": centred(streams_of[8], (D,), 0.2, 1.1953125, ((0, 32),)),
        "up_weight": centred(streams_of[9], (D, FF), D ** -0.5, 0.21875, ((0, 8), (1, 4))),
        "up_bias": centred(streams_of[10], (FF,), 0.2, 1.1953125, ((0, 32),)),
        "down_weight": centred(streams_of[11], (FF, D), FF ** -0.5, 0.109375, ((0, 4), (1, 8))),
        "down_bias": centred(streams_of[12], (D,), 0.2, 1.1953125, ((0, 32),)),
        "norm2_gain": jnp.clip(1.0 + 0.18 * jax.random.normal(streams_of[13], (D,), jnp.float32), 0.099609375, 1.8984375).astype(jnp.bfloat16),
        "norm2_shift": centred(streams_of[14], (D,), 0.2, 1.1953125, ((0, 32),)),
    }


EPS = 1e-12
NEG = -1000000000.0
highest = lax.Precision.HIGHEST

@jax.custom_vjp
def low(v):
    return lax.optimization_barrier(v.astype(jnp.bfloat16)).astype(jnp.float32)

@jax.custom_vjp
def low_back(v):
    return v

def low_keep(v):
    return (low(v), None)

def low_pass(kept, grad):
    return (grad,)

def back_keep(v):
    return (v, None)

def back_low(kept, grad):
    return (low(grad),)
low.defvjp(low_keep, low_pass)
low_back.defvjp(back_keep, back_low)

def product(left_side, right_side):
    return jnp.dot(left_side, right_side, precision=highest, preferred_element_type=jnp.float32)

def normalize(values, gain, shift):
    center = values - lax.optimization_barrier(jnp.mean(values, axis=-1, keepdims=True))
    inverse = lax.rsqrt(lax.optimization_barrier(jnp.mean(center * center, axis=-1, keepdims=True)) + EPS)
    return center * inverse * gain + shift

def layer_block(rows_in, seg_block, qkv_weight, qv_bias, out_weight, out_bias, norm1_gain, norm1_shift, up_weight, up_bias, down_weight, down_bias, norm2_gain, norm2_shift):
    seq_count = seg_block.shape[0]
    token_count = rows_in.shape[0]
    query_rows = low_back(low(product(rows_in, qkv_weight[0]) + qv_bias[0]))
    key_rows = low_back(low(product(rows_in, qkv_weight[1])))
    value_rows = low_back(low(product(rows_in, qkv_weight[2]) + qv_bias[1]))
    shape_heads = (seq_count, LEN, H, HD)
    raw_scores = jnp.einsum('gqhd,gkhd->ghqk', query_rows.reshape(shape_heads), key_rows.reshape(shape_heads), precision=highest) * float(HD) ** (-0.5)
    raw_scores = low_back(raw_scores)
    same_segment = seg_block[:, None, :, None] == seg_block[:, None, None, :]
    prob_rows = low(jax.nn.softmax(jnp.where(same_segment, raw_scores, NEG), axis=-1))
    attended = jnp.einsum('ghqk,gkhd->gqhd', prob_rows, value_rows.reshape(shape_heads), precision=highest)
    attended = low_back(low(attended.reshape(token_count, D)))
    pre_one = low_back(product(attended, out_weight)) + out_bias + rows_in
    out_one = normalize(pre_one, norm1_gain, norm1_shift)
    normed_low = low_back(low(out_one))
    up_act = low_back(product(normed_low, up_weight) + up_bias)
    hidden_act = low(jax.nn.gelu(up_act, approximate=False))
    pre_two = low_back(product(hidden_act, down_weight)) + down_bias + out_one
    out_two = normalize(pre_two, norm2_gain, norm2_shift)
    onehot = (seg_block[:, :, None] == jnp.arange(SEGS, dtype=jnp.int32)[None, None, :]).astype(jnp.float32)
    counts = lax.optimization_barrier(jnp.sum(onehot, axis=1))
    sums = jnp.einsum('gls,gld->gsd', onehot, out_two.reshape(seq_count, LEN, D), precision=highest)
    return sums / counts[:, :, None]

def reference(hidden_in, segment_ids, pooled_grad, qkv_weight, qv_bias, out_weight, out_bias, norm1_gain, norm1_shift, up_weight, up_bias, down_weight, down_bias, norm2_gain, norm2_shift):
    params = tuple((item.astype(jnp.float32) for item in (qkv_weight, qv_bias, out_weight, out_bias, norm1_gain, norm1_shift, up_weight, up_bias, down_weight, down_bias, norm2_gain, norm2_shift)))
    seq_all = MB * NROWS
    per_block = 1
    for trial in range(1, seq_all + 1):
        if seq_all % trial == 0 and trial * LEN <= 4096:
            per_block = trial
    block_total = seq_all // per_block
    row_blocks = hidden_in.reshape(block_total, per_block * LEN, D)
    seg_blocks = segment_ids.reshape(block_total, per_block, LEN)
    grad_blocks = pooled_grad.reshape(block_total, per_block, SEGS, D)

    def scan_step(running, blocks):
        rows_now, seg_now, grad_now = blocks

        def forward(rows_in, *weights):
            return layer_block(rows_in, seg_now, *weights)
        pooled, pull = jax.vjp(forward, rows_now.astype(jnp.float32), *params)
        pulled = pull(grad_now)
        running = tuple((kept_sum + update for kept_sum, update in zip(running, pulled[1:])))
        return (running, (pooled, pulled[0]))
    initial = tuple((jnp.zeros(item.shape, jnp.float32) for item in params))
    totals, outputs = lax.scan(scan_step, initial, (row_blocks, seg_blocks, grad_blocks))
    pooled_all, input_grads = outputs
    return (pooled_all.reshape(MB, NROWS, SEGS, D), input_grads.reshape(MB, TOKENS, D), totals[0], totals[1], totals[2], totals[3], totals[4], totals[5], totals[6], totals[7], totals[8], totals[9], totals[10], totals[11])
```

```python
from functools import partial

import jax
import jax.numpy as jnp
from jax import lax
from jax.sharding import PartitionSpec as P

HD = 64
EPS = 1e-12
NEG = -1000000000.0
AXES = ("dp", "tensor")
f32 = jnp.float32
bf16 = jnp.bfloat16


def mm(spec, a, b):
    return jnp.einsum(spec, a, b, preferred_element_type=f32)


def normalize(values, gain, shift):
    center = values - jnp.mean(values, axis=-1, keepdims=True)
    inverse = lax.rsqrt(jnp.mean(center * center, axis=-1, keepdims=True) + EPS)
    normed = center * inverse
    return normed * gain + shift, normed, inverse


def normalize_back(grad_out, normed, inverse, gain):
    scaled = grad_out * gain
    return inverse * (
        scaled
        - jnp.mean(scaled, axis=-1, keepdims=True)
        - normed * jnp.mean(scaled * normed, axis=-1, keepdims=True)
    )


def per_device(
    hidden_in, segment_ids, pooled_grad, qkv_weight, qv_bias, out_weight, out_bias,
    norm1_gain, norm1_shift, up_weight, up_bias, down_weight, down_bias, norm2_gain, norm2_shift,
):
    n_dp, n_t = lax.axis_size("dp"), lax.axis_size("tensor")
    rows = qkv_weight.shape[1]
    hc = qkv_weight.shape[2]
    fc = up_weight.shape[1]
    D = rows * n_dp
    micro, tokens = hidden_in.shape[0], hidden_in.shape[1]
    seqs, L = segment_ids.shape[1], segment_ids.shape[2]
    G = micro * seqs
    T = micro * tokens
    segs = pooled_grad.shape[2]
    H = D // HD
    cols = 4 * hc + 2 * fc

    vecs = [qv_bias[0], qv_bias[1], out_bias, norm1_gain, norm1_shift, up_bias, down_bias, norm2_gain, norm2_shift]
    vlen = [v.shape[0] for v in vecs]
    vec = jnp.concatenate(vecs)
    main = jnp.concatenate(
        [qkv_weight[0], qkv_weight[1], qkv_weight[2], out_weight.T, up_weight, down_weight.T], axis=1
    )
    full = lax.all_gather(main, "dp", axis=0, tiled=True)
    full = lax.all_gather(full, "tensor", axis=0)
    vfull = lax.all_gather(lax.all_gather(vec, "tensor"), "dp").reshape(n_dp * n_t, -1).astype(f32)

    def take(lo, width):
        return full[:, :, lo : lo + width].transpose(1, 0, 2).reshape(D, n_t * width)

    wq, wk, wv, wot = (take(c * hc, hc) for c in range(4))
    wu, wdt = take(4 * hc, fc), take(4 * hc + fc, fc)
    offs = [0]
    for n in vlen:
        offs.append(offs[-1] + n)
    bq, bv, bo, g1, s1, bu, bd, g2, s2 = (vfull[:, offs[j] : offs[j + 1]].reshape(-1) for j in range(9))

    x = hidden_in.reshape(T, D)
    seg = segment_ids.reshape(G, L)
    heads = (G, L, H, HD)
    q = (mm("rd,de->re", x, wq) + bq).astype(bf16).reshape(heads)
    k = mm("rd,de->re", x, wk).astype(bf16).reshape(heads)
    v = (mm("rd,de->re", x, wv) + bv).astype(bf16).reshape(heads)
    scale = float(HD) ** -0.5
    same = seg[:, None, :, None] == seg[:, None, None, :]
    s = jnp.where(same, mm("gqhd,gkhd->ghqk", q, k) * scale, NEG)
    e = jnp.exp(s - jnp.max(s, axis=-1, keepdims=True))
    pf = e / jnp.sum(e, axis=-1, keepdims=True)
    pb = pf.astype(bf16)
    o = mm("ghqk,gkhd->gqhd", pb, v).astype(bf16).reshape(T, D)
    a = mm("re,de->rd", o, wot) + bo + x.astype(f32)
    n1, x1, r1 = normalize(a, g1, s1)
    n1b = n1.astype(bf16)
    u = mm("rd,df->rf", n1b, wu) + bu
    z, pull = jax.vjp(partial(jax.nn.gelu, approximate=False), u)
    z = z.astype(bf16)
    b = mm("rf,df->rd", z, wdt) + bd + n1
    y, x2, r2 = normalize(b, g2, s2)
    onehot = (seg[:, :, None] == jnp.arange(segs, dtype=jnp.int32)).astype(f32)
    counts = jnp.sum(onehot, axis=1)
    hi = lax.Precision.HIGHEST
    pooled = jnp.einsum("gls,gld->gsd", onehot, y.reshape(G, L, D), precision=hi) / counts[:, :, None]
    dy = jnp.einsum("gls,gsd->gld", onehot, pooled_grad.reshape(G, segs, D) / counts[:, :, None], precision=hi).reshape(T, D)
    db = normalize_back(dy, x2, r2, g2)
    g_g2, g_s2, g_bd = jnp.sum(dy * x2, 0), jnp.sum(dy, 0), jnp.sum(db, 0)
    dbb = db.astype(bf16)
    g_wdt = mm("rd,rf->df", dbb, z)
    du = pull(mm("rd,df->rf", dbb, wdt))[0].astype(bf16)
    g_wu = mm("rd,rf->df", n1b, du)
    g_bu = jnp.sum(du.astype(f32), 0)
    dn1 = mm("rf,df->rd", du, wu).astype(bf16).astype(f32) + db
    da = normalize_back(dn1, x1, r1, g1)
    g_g1, g_s1, g_bo = jnp.sum(dn1 * x1, 0), jnp.sum(dn1, 0), jnp.sum(da, 0)
    dab = da.astype(bf16)
    g_wot = mm("rd,re->de", dab, o)
    do = mm("rd,de->re", dab, wot).astype(bf16).reshape(heads)
    dp = mm("gqhd,gkhd->ghqk", do, v)
    ds = (pf * (dp - jnp.sum(pf * dp, axis=-1, keepdims=True))).astype(bf16)
    dv = mm("ghqk,gqhd->gkhd", pb, do).astype(bf16).reshape(T, D)
    dq = (mm("ghqk,gkhd->gqhd", ds, k) * scale).astype(bf16).reshape(T, D)
    dk = (mm("ghqk,gqhd->gkhd", ds, q) * scale).astype(bf16).reshape(T, D)
    g_q, g_k, g_v = (mm("rd,re->de", x, dd) for dd in (dq, dk, dv))
    g_bq, g_bv = jnp.sum(dq.astype(f32), 0), jnp.sum(dv.astype(f32), 0)
    dx = mm("re,de->rd", dq, wq) + mm("re,de->rd", dk, wk) + mm("re,de->rd", dv, wv) + da

    def blocks(g):
        return g.astype(bf16).reshape(D, n_t, -1).transpose(1, 0, 2)

    gfull = jnp.concatenate([blocks(g) for g in (g_q, g_k, g_v, g_wot, g_wu, g_wdt)], axis=2)
    gvec = jnp.concatenate(
        [g.reshape(n_dp * n_t, -1) for g in (g_bq, g_bv, g_bo, g_g1, g_s1, g_bu, g_bd, g_g2, g_s2)], axis=1
    )
    gmine = lax.psum_scatter(gfull, "tensor", scatter_dimension=0)
    gmine = lax.psum_scatter(gmine, "dp", scatter_dimension=0, tiled=True).astype(f32)
    gv = lax.psum_scatter(gvec, AXES, scatter_dimension=0)
    vo = [gv[offs[j] : offs[j + 1]] for j in range(9)]
    return (
        pooled.reshape(micro, seqs, segs, D),
        dx.reshape(micro, tokens, D),
        jnp.stack([gmine[:, c * hc : (c + 1) * hc] for c in range(3)]),
        jnp.stack([vo[0], vo[1]]),
        gmine[:, 3 * hc : 4 * hc].T,
        vo[2], vo[3], vo[4],
        gmine[:, 4 * hc : 4 * hc + fc],
        vo[5],
        gmine[:, 4 * hc + fc :].T,
        vo[6], vo[7], vo[8],
    )


def solution(mesh):
    both = P(AXES)
    row3 = P(None, AXES)
    return jax.shard_map(
        per_device,
        mesh=mesh,
        in_specs=(
            row3, row3, row3, P(None, "dp", "tensor"), row3, P("tensor", "dp"), both, both, both,
            P("dp", "tensor"), both, P("tensor", "dp"), both, both, both,
        ),
        out_specs=(
            row3, row3, P(None, "dp", "tensor"), row3, P("tensor", "dp"), both, both, both,
            P("dp", "tensor"), both, P("tensor", "dp"), both, both, both,
        ),
        check_vma=False,
    )
```

```python
from functools import partial

import jax
import jax.numpy as jnp
from jax import lax
from jax.experimental import pallas as pl
from jax.experimental.pallas import tpu as pltpu
from jax.sharding import PartitionSpec as P

HD = 64
EPS = 1e-12
NEG = -1000000000.0
SCALE = float(HD) ** -0.5
AXES = ("dp", "tensor")
f32 = jnp.float32
bf16 = jnp.bfloat16
HI = lax.Precision.HIGHEST
BLK = 96
VMEM_LIMIT = 40 * 1024 * 1024


def nn(a, b):
    return lax.dot_general(a, b, (((1,), (0,)), ((), ())), preferred_element_type=f32)


def nt(a, b):
    return lax.dot_general(a, b, (((1,), (1,)), ((), ())), preferred_element_type=f32)


def tn(a, b):
    return lax.dot_general(a, b, (((0,), (0,)), ((), ())), preferred_element_type=f32)


def mean_last(v):
    return jnp.sum(v, axis=-1, keepdims=True) * (1.0 / v.shape[-1])


def normalize(values):
    center = values - mean_last(values)
    inverse = lax.rsqrt(mean_last(center * center) + EPS)
    return center * inverse, inverse


def normalize_back(scaled, normed, inverse):
    return inverse * (scaled - mean_last(scaled) - normed * mean_last(scaled * normed))


def col_sum(v):
    return jnp.sum(v, axis=0, keepdims=True)


def attention_forward(x_ref, w_ref, bq_ref, bv_ref, segc_ref, segr_ref, vec_ref,
                      qkv_ref, p_ref, o_ref, n1_ref, x1_ref, r1_ref, n1b_ref, acc_ref):
    step = pl.program_id(0)
    hc = bq_ref.shape[-1]
    rows, length = segr_ref.shape
    x = x_ref[...]
    w = w_ref[...].reshape(x.shape[1], w_ref.shape[-1])
    qkv = nn(x, w[:, : 3 * hc])
    q = (qkv[:, :hc] + bq_ref[0]).astype(bf16)
    k = qkv[:, hc : 2 * hc].astype(bf16)
    v = (qkv[:, 2 * hc :] + bv_ref[0]).astype(bf16)
    qkv_ref[0, :, :hc] = q
    qkv_ref[0, :, hc : 2 * hc] = k
    qkv_ref[0, :, 2 * hc :] = v
    parts = []
    for g in range(rows):
        span = slice(g * length, (g + 1) * length)
        same = segc_ref[span, :] == segr_ref[g : g + 1, :]
        heads = []
        for h in range(hc // HD):
            cut = slice(h * HD, (h + 1) * HD)
            s = jnp.where(same, nt(q[span, cut], k[span, cut]) * SCALE, NEG)
            e = jnp.exp(s - jnp.max(s, axis=-1, keepdims=True))
            p = e / jnp.sum(e, axis=-1, keepdims=True)
            p_ref[0, g * (hc // HD) + h] = p
            heads.append(nn(p.astype(bf16), v[span, cut]).astype(bf16))
        parts.append(jnp.concatenate(heads, axis=1))
    o = jnp.concatenate(parts, axis=0)
    o_ref[0] = o
    add = nt(o, w[:, 3 * hc :])

    @pl.when(step == 0)
    def _():
        acc_ref[...] = add

    @pl.when(step > 0)
    def _():
        acc_ref[...] += add

    @pl.when(step == pl.num_programs(0) - 1)
    def _():
        a = acc_ref[...] + vec_ref[0:1, :] + x_ref[...].astype(f32)
        normed, inverse = normalize(a)
        n1 = normed * vec_ref[1:2, :] + vec_ref[2:3, :]
        n1_ref[...] = n1
        x1_ref[...] = normed
        r1_ref[...] = inverse
        n1b_ref[...] = n1.astype(bf16)


def erf(v):
    return lax.erf(v)


def up_forward(n_ref, w_ref, b_ref, z_ref, d_ref):
    w = w_ref[...].reshape(n_ref.shape[1], w_ref.shape[-1])
    u = nn(n_ref[...], w) + b_ref[0]
    phi = 0.5 + 0.5 * erf(u * (0.5**0.5))
    z_ref[0] = (u * phi).astype(bf16)
    d_ref[0] = phi + u * (jnp.exp(-0.5 * u * u) * 0.3989422804014327)


def down_forward(z_ref, w_ref, n1_ref, vec_ref, segc_ref, segr_ref, pg_ref,
                 pooled_ref, db_ref, dbb_ref, sums_ref, acc_ref):
    step = pl.program_id(0)
    width = n1_ref.shape[1]
    w = w_ref[...].reshape(width, w_ref.shape[-1])
    add = nt(z_ref[0], w)

    @pl.when(step == 0)
    def _():
        acc_ref[...] = add

    @pl.when(step > 0)
    def _():
        acc_ref[...] += add

    @pl.when(step == pl.num_programs(0) - 1)
    def _():
        rows, length = segr_ref.shape
        segs = pg_ref.shape[1]
        b = acc_ref[...] + vec_ref[3:4, :] + n1_ref[...]
        x2, r2 = normalize(b)
        y = x2 * vec_ref[4:5, :] + vec_ref[5:6, :]
        grads = []
        for g in range(rows):
            span = slice(g * length, (g + 1) * length)
            ids = lax.broadcasted_iota(jnp.int32, (segs, length), 0)
            hot_t = (ids == segr_ref[g : g + 1, :]).astype(f32)
            idc = lax.broadcasted_iota(jnp.int32, (length, segs), 1)
            hot = (idc == segc_ref[span, :]).astype(f32)
            count = jnp.sum(hot_t, axis=1, keepdims=True)
            sums = lax.dot_general(hot_t, y[span, :], (((1,), (0,)), ((), ())),
                                   precision=HI, preferred_element_type=f32)
            pooled_ref[g] = sums / count
            grads.append(lax.dot_general(hot, pg_ref[g] / count, (((1,), (0,)), ((), ())),
                                         precision=HI, preferred_element_type=f32))
        dy = jnp.concatenate(grads, axis=0)
        db = normalize_back(dy * vec_ref[4:5, :], x2, r2)
        db_ref[...] = db
        dbb_ref[...] = db.astype(bf16)
        sums_ref[0:1, :] = col_sum(db)
        sums_ref[1:2, :] = col_sum(dy * x2)
        sums_ref[2:3, :] = col_sum(dy)


def put_halves(grad, keep_ref, send_ref):
    half = grad.shape[0] // 2
    low = grad.astype(bf16)
    keep_ref[:, :, :BLK, :] = low[:half].reshape(half // BLK, 1, BLK, grad.shape[1])
    send_ref[:, :, :BLK, :] = low[half:].reshape(half // BLK, 1, BLK, grad.shape[1])


def down_weight(dbb_ref, z_ref, keep_ref, send_ref):
    put_halves(tn(dbb_ref[...], z_ref[0]), keep_ref, send_ref)


def up_backward(dbb_ref, wd_ref, wu_ref, d_ref, n1b_ref, db_ref, x1_ref, r1_ref, vec_ref,
                keep_ref, send_ref, bu_ref, da_ref, dab_ref, sums_ref, acc_ref):
    step = pl.program_id(0)
    width = dbb_ref.shape[1]
    wd = wd_ref[...].reshape(width, wd_ref.shape[-1])
    wu = wu_ref[...].reshape(width, wu_ref.shape[-1])
    du = (nn(dbb_ref[...], wd) * d_ref[0]).astype(bf16)
    bu_ref[0] = col_sum(du.astype(f32))
    put_halves(tn(n1b_ref[...], du), keep_ref, send_ref)
    add = nt(du, wu)

    @pl.when(step == 0)
    def _():
        acc_ref[...] = add

    @pl.when(step > 0)
    def _():
        acc_ref[...] += add

    @pl.when(step == pl.num_programs(0) - 1)
    def _():
        dn1 = acc_ref[...].astype(bf16).astype(f32) + db_ref[...]
        da = normalize_back(dn1 * vec_ref[1:2, :], x1_ref[...], r1_ref[...])
        da_ref[...] = da
        dab_ref[...] = da.astype(bf16)
        sums_ref[0:1, :] = col_sum(da)
        sums_ref[1:2, :] = col_sum(dn1 * x1_ref[...])
        sums_ref[2:3, :] = col_sum(dn1)


def attention_backward(dab_ref, x_ref, w_ref, qkv_ref, p_ref, o_ref, da_ref, perm_ref,
                       keep_ref, send_ref, bqv_ref, dx_ref, acc_ref):
    step = pl.program_id(0)
    width = x_ref.shape[1]
    hc = o_ref.shape[-1]
    w = w_ref[...].reshape(width, w_ref.shape[-1])
    dab = dab_ref[...]
    do = nn(dab, w[:, 3 * hc :]).astype(bf16)
    qkv = qkv_ref[0]
    n_heads = hc // HD
    rows = p_ref.shape[1] // n_heads
    length = p_ref.shape[2]
    pieces = [[], [], []]
    for g in range(rows):
        span = slice(g * length, (g + 1) * length)
        here = [[], [], []]
        for h in range(n_heads):
            lo = h * HD
            q = qkv[span, lo : lo + HD]
            k = qkv[span, hc + lo : hc + lo + HD]
            v = qkv[span, 2 * hc + lo : 2 * hc + lo + HD]
            g_o = do[span, lo : lo + HD]
            p = p_ref[0, g * n_heads + h]
            dp = nt(g_o, v)
            ds = (p * (dp - jnp.sum(p * dp, axis=-1, keepdims=True))).astype(bf16)
            here[0].append((nn(ds, k) * SCALE).astype(bf16))
            here[1].append((tn(ds, q) * SCALE).astype(bf16))
            here[2].append(tn(p.astype(bf16), g_o).astype(bf16))
        for c in range(3):
            pieces[c].append(jnp.concatenate(here[c], axis=1))
    grads = [jnp.concatenate(piece, axis=0) for piece in pieces]
    bqv_ref[0, 0:1, :] = col_sum(grads[0].astype(f32))
    bqv_ref[0, 1:2, :] = col_sum(grads[2].astype(f32))
    dqkv = jnp.concatenate(grads, axis=1)
    keep_ref[:, :, BLK:, :] = jnp.zeros((*keep_ref.shape[:2], keep_ref.shape[2] - BLK, keep_ref.shape[3]), bf16)
    send_ref[:, :, BLK:, :] = jnp.zeros((*send_ref.shape[:2], send_ref.shape[2] - BLK, send_ref.shape[3]), bf16)
    put_halves(jnp.concatenate([tn(x_ref[...], dqkv), tn(dab, o_ref[0])], axis=1), keep_ref, send_ref)
    add = nt(dqkv, w[:, : 3 * hc])

    @pl.when(step == 0)
    def _():
        acc_ref[...] = add

    @pl.when(step > 0)
    def _():
        acc_ref[...] += add

    @pl.when(step == pl.num_programs(0) - 1)
    def _():
        dx = acc_ref[...] + da_ref[...]
        high = dx.astype(bf16)
        rest = dx - high.astype(f32)
        mid = rest.astype(bf16)
        low = (rest - mid.astype(f32)).astype(bf16)
        perm = perm_ref[...]
        dx_ref[...] = nt(high, perm) + nt(mid, perm) + nt(low, perm)


def whole(a):
    nd = a.ndim
    return pl.BlockSpec(a.shape, lambda s: (0,) * nd, pipeline_mode=pl.Buffered(1))


def lead(a):
    nd = a.ndim
    return pl.BlockSpec((1,) + a.shape[1:], lambda s: (s,) + (0,) * (nd - 1))


def weight(a):
    if a.ndim == 5:
        return pl.BlockSpec((a.shape[0], 1, a.shape[2], BLK, a.shape[4]), lambda s: (0, s, 0, 0, 0))
    return pl.BlockSpec((a.shape[0], 1, BLK, a.shape[3]), lambda s: (0, s, 0, 0))


def half_spec(h):
    return pl.BlockSpec((h.shape[0], 1) + h.shape[2:], lambda s: (0, s, 0, 0))


def sds(shape, dtype):
    return jax.ShapeDtypeStruct(shape, dtype)


def call(body, name, n_t, ins, outs, scratch, flops):
    moved = sum(a.size * a.dtype.itemsize for a, _ in ins) + sum(a.size * a.dtype.itemsize for a, _ in outs)
    return pl.pallas_call(
        body,
        name=name,
        grid=(n_t,),
        in_specs=[s for _, s in ins],
        out_specs=[s for _, s in outs],
        out_shape=[a for a, _ in outs],
        scratch_shapes=scratch,
        compiler_params=pltpu.CompilerParams(
            dimension_semantics=("arbitrary",), vmem_limit_bytes=VMEM_LIMIT
        ),
        cost_estimate=pl.CostEstimate(flops=flops, transcendentals=0, bytes_accessed=moved),
    )(*[a for a, _ in ins])


def flips(shape):
    n_dp, n_t = shape
    size = n_dp * n_t
    core = n_t
    x_bit, y_bit = 2 * core, 4 * core

    def table(bit_of):
        return [(i, i ^ bit_of(i)) for i in range(size)]

    return {
        "a": table(lambda i: 1),
        "b": table(lambda i: 2),
        "C": table(lambda i: core),
        "2": table(lambda i: x_bit if i & core else y_bit),
        "3": table(lambda i: y_bit if i & core else x_bit),
    }


def gather_all(v, order, tables):
    held = v[None]
    for stage in order:
        held = jnp.concatenate([held, lax.ppermute(held, AXES, tables[stage])])
    return held


def scatter_all(keep, send, order, tables):
    for n, stage in enumerate(order):
        got = lax.ppermute(send, AXES, tables[stage])
        total = keep.astype(f32) + got.astype(f32)
        half = total.shape[0] // 2
        if n + 1 < len(order):
            keep, send = total[:half], total[half:].astype(bf16)
    return total[0]


def per_device(
    hidden_in, segment_ids, pooled_grad, qkv_weight, qv_bias, out_weight, out_bias,
    norm1_gain, norm1_shift, up_weight, up_bias, down_weight_in, down_bias, norm2_gain, norm2_shift,
):
    n_dp, n_t = lax.axis_size("dp"), lax.axis_size("tensor")
    at_dp, at_t = lax.axis_index("dp"), lax.axis_index("tensor")
    hc, fc = qkv_weight.shape[2], up_weight.shape[1]
    rows = qkv_weight.shape[1]
    D = rows * n_dp
    micro, tokens = hidden_in.shape[0], hidden_in.shape[1]
    seqs, L = segment_ids.shape[1], segment_ids.shape[2]
    G, T = micro * seqs, micro * tokens
    segs = pooled_grad.shape[2]
    n_i = D // BLK
    pairwise = (n_dp, n_t) == (8, 4) and 4 * hc == fc

    d_parts = [out_bias, norm1_gain, norm1_shift, down_bias, norm2_gain, norm2_shift]
    e_parts = [qv_bias[0], qv_bias[1], up_bias]
    dv, ev = out_bias.shape[0], sum(p.shape[0] for p in e_parts)
    vec = jnp.concatenate(d_parts + e_parts)
    nd = len(d_parts) * dv
    heads_in = jnp.concatenate([qkv_weight[0], qkv_weight[1], qkv_weight[2], out_weight.T], axis=1)
    down_t = down_weight_in.T

    if pairwise:
        tables = flips((n_dp, n_t))
        pad = jnp.zeros((8, 4 * hc), bf16)
        pad = lax.dynamic_update_slice(pad, vec[None], (0, 0))
        first = jnp.concatenate([heads_in, pad], axis=0)
        w_qo = gather_all(first, "2ab3C", tables).reshape(4, n_t, 2, BLK + 8, 4 * hc)
        w_up = gather_all(up_weight, "ab23C", tables).reshape(n_i, n_t, BLK, fc)
        w_down = gather_all(down_t, "ab23C", tables).reshape(n_i, n_t, BLK, fc)
        vecs = w_qo[:, :, :, BLK, : vec.shape[0]].transpose(0, 2, 1, 3).reshape(n_i * n_t, -1)
        rel = jnp.arange(n_i)
        core = (at_dp & 1) ^ (rel >> 2)
        s3, s2 = (rel >> 1) & 1, rel & 1
        dy, dx = jnp.where(core == 0, s2, s3), jnp.where(core == 0, s3, s2)
        absolute = ((((at_dp >> 2) & 1) ^ dy) << 2) | ((((at_dp >> 1) & 1) ^ dx) << 1) | core
        t_of = at_t ^ jnp.arange(n_t)
        i_p = jnp.repeat(absolute, n_t)
        t_p = jnp.tile(t_of, n_i)
        to_d = jnp.repeat(rel, n_t) * n_t + t_p
        to_e = (((i_p * n_t) // n_i) ^ at_t) * n_i + (i_p * n_t + t_p) % n_i
        slot = jnp.arange(n_i * n_t)
        hot_d = (to_d[None, :] == slot[:, None]).astype(bf16)
        hot_e = (to_e[None, :] == slot[:, None]).astype(bf16)
        d_all = nn(hot_d, vecs[:, :nd])
        e_all = nn(hot_e, vecs[:, nd:])
        d_now = jnp.arange(D)
        source = absolute[d_now // BLK] * BLK + d_now % BLK
        perm = (jnp.arange(D)[:, None] == source[None, :]).astype(bf16)
    else:
        main = jnp.concatenate([heads_in, up_weight, down_t], axis=1)
        full = lax.all_gather(lax.all_gather(main, "dp", axis=0, tiled=True), "tensor", axis=0)
        full = full.reshape(n_t, n_i, BLK, -1).transpose(1, 0, 2, 3)
        w_qo, w_up, w_down = full[..., : 4 * hc], full[..., 4 * hc : 4 * hc + fc], full[..., 4 * hc + fc :]
        vecs = lax.all_gather(lax.all_gather(vec, "tensor"), "dp").reshape(n_dp * n_t, -1).astype(f32)
        d_all, e_all = vecs[:, :nd], vecs[:, nd:]
        perm = (jnp.arange(D)[:, None] == jnp.arange(D)[None, :]).astype(bf16)

    vec_d = jnp.concatenate([d_all[:, j * dv : (j + 1) * dv].reshape(1, D) for j in range(6)])
    b_q = e_all[:, :dv].reshape(n_t, 1, hc)
    b_v = e_all[:, dv : 2 * dv].reshape(n_t, 1, hc)
    b_u = e_all[:, 2 * dv :].reshape(n_t, 1, fc)

    x = nn(hidden_in.reshape(T, D), perm).astype(bf16)
    seg_r = segment_ids.reshape(G, L)
    seg_c = segment_ids.reshape(T, 1)
    pg = jnp.einsum("gsd,de->gse", pooled_grad.reshape(G, segs, D), perm.astype(f32), precision=HI)
    n_pairs = G * (hc // HD)
    flop = 2 * T * D

    qkv, prob, o, n1, x1, r1, n1b = call(
        attention_forward, "attention_forward", n_t,
        [(x, whole(x)), (w_qo, weight(w_qo)), (b_q, lead(b_q)), (b_v, lead(b_v)), (seg_c, whole(seg_c)),
         (seg_r, whole(seg_r)), (vec_d, whole(vec_d))],
        [(a, lead(a)) for a in (sds((n_t, T, 3 * hc), bf16), sds((n_t, n_pairs, L, L), f32), sds((n_t, T, hc), bf16))]
        + [(a, whole(a)) for a in (sds((T, D), f32), sds((T, D), f32), sds((T, 1), f32), sds((T, D), bf16))],
        [pltpu.VMEM((T, D), f32)], flop * 4 * D,
    )
    z, dgelu = call(
        up_forward, "up_forward", n_t,
        [(n1b, whole(n1b)), (w_up, weight(w_up)), (b_u, lead(b_u))],
        [(a, lead(a)) for a in (sds((n_t, T, fc), bf16), sds((n_t, T, fc), f32))], [], flop * n_t * fc,
    )
    pooled, db, dbb, sums2 = call(
        down_forward, "down_forward", n_t,
        [(z, lead(z)), (w_down, weight(w_down)), (n1, whole(n1)), (vec_d, whole(vec_d)), (seg_c, whole(seg_c)),
         (seg_r, whole(seg_r)), (pg, whole(pg))],
        [(a, whole(a)) for a in (sds((G, segs, D), f32), sds((T, D), f32), sds((T, D), bf16), sds((3, D), f32))],
        [pltpu.VMEM((T, D), f32)], flop * n_t * fc,
    )
    half = sds((n_i // 2, n_t, BLK, fc), bf16)
    down_keep, down_send = call(
        down_weight, "down_weight", n_t, [(dbb, whole(dbb)), (z, lead(z))],
        [(half, half_spec(half))] * 2, [], flop * n_t * fc,
    )
    up_keep, up_send, g_bu, da, dab, sums1 = call(
        up_backward, "up_backward", n_t,
        [(dbb, whole(dbb)), (w_down, weight(w_down)), (w_up, weight(w_up)), (dgelu, lead(dgelu)), (n1b, whole(n1b)),
         (db, whole(db)), (x1, whole(x1)), (r1, whole(r1)), (vec_d, whole(vec_d))],
        [(half, half_spec(half))] * 2 + [(a, lead(a)) for a in (sds((n_t, 1, fc), f32),)]
        + [(a, whole(a)) for a in (sds((T, D), f32), sds((T, D), bf16), sds((3, D), f32))],
        [pltpu.VMEM((T, D), f32)], 3 * flop * n_t * fc,
    )
    half_qo = sds((n_i // 2, n_t, BLK + 8, 4 * hc), bf16)
    qo_keep, qo_send, g_bqv, dx = call(
        attention_backward, "attention_backward", n_t,
        [(dab, whole(dab)), (x, whole(x)), (w_qo, weight(w_qo)), (qkv, lead(qkv)), (prob, lead(prob)), (o, lead(o)),
         (da, whole(da)), (perm, whole(perm))],
        [(half_qo, half_spec(half_qo))] * 2 + [(a, lead(a)) for a in (sds((n_t, 2, hc), f32),)]
        + [(a, whole(a)) for a in (sds((T, D), f32),)],
        [pltpu.VMEM((T, D), f32)], 2 * flop * 4 * D,
    )
    pooled = jnp.einsum("gse,de->gsd", pooled, perm.astype(f32), precision=HI)

    g_d = jnp.concatenate([v.reshape(n_dp * n_t, dv) for v in (*sums1, *sums2)], axis=1)
    g_e = jnp.concatenate(
        [g_bqv[:, 0].reshape(n_dp * n_t, dv), g_bqv[:, 1].reshape(n_dp * n_t, dv), g_bu.reshape(n_dp * n_t, -1)], axis=1
    )
    if pairwise:
        g_vec = jnp.concatenate([tn(hot_d, g_d.astype(bf16)), tn(hot_e, g_e.astype(bf16))], axis=1).astype(bf16)
        g_vec = g_vec.reshape(2, n_i // 2, n_t, 1, -1)
        qo_keep = lax.dynamic_update_slice(qo_keep, g_vec[0], (0, 0, BLK, 0))
        qo_send = lax.dynamic_update_slice(qo_send, g_vec[1], (0, 0, BLK, 0))

        def flat(a):
            return a.reshape((-1,) + a.shape[2:])

        g_down = scatter_all(flat(down_keep), flat(down_send), "C32ba", tables)
        g_up = scatter_all(flat(up_keep), flat(up_send), "C32ba", tables)
        g_qo = scatter_all(flat(qo_keep), flat(qo_send), "C32ba", tables)
        g_v = g_qo[BLK, : vec.shape[0]]
        g_qo = g_qo[:BLK]
    else:
        def joined(keep, send):
            g = jnp.concatenate([keep, send])[:, :, :BLK]
            return g.transpose(1, 0, 2, 3).reshape(n_t, D, -1)

        g_full = jnp.concatenate([joined(qo_keep, qo_send), joined(up_keep, up_send), joined(down_keep, down_send)], axis=2)
        mine = lax.psum_scatter(g_full, "tensor", scatter_dimension=0)
        mine = lax.psum_scatter(mine, "dp", scatter_dimension=0, tiled=True).astype(f32)
        g_qo, g_up, g_down = mine[:, : 4 * hc], mine[:, 4 * hc : 4 * hc + fc], mine[:, 4 * hc + fc :]
        g_v = lax.psum_scatter(jnp.concatenate([g_d, g_e], axis=1), AXES, scatter_dimension=0)
    vo = [g_v[j * dv : (j + 1) * dv] for j in range(8)]
    return (
        pooled.reshape(micro, seqs, segs, D),
        dx.reshape(micro, tokens, D),
        jnp.stack([g_qo[:, c * hc : (c + 1) * hc] for c in range(3)]),
        jnp.stack([vo[6], vo[7]]),
        g_qo[:, 3 * hc :].T,
        vo[0], vo[1], vo[2],
        g_up,
        g_v[8 * dv :],
        g_down.T,
        vo[3], vo[4], vo[5],
    )


def solution(mesh):
    both = P(AXES)
    row3 = P(None, AXES)
    return jax.shard_map(
        per_device,
        mesh=mesh,
        in_specs=(
            row3, row3, row3, P(None, "dp", "tensor"), row3, P("tensor", "dp"), both, both, both,
            P("dp", "tensor"), both, P("tensor", "dp"), both, both, both,
        ),
        out_specs=(
            row3, row3, P(None, "dp", "tensor"), row3, P("tensor", "dp"), both, both, both,
            P("dp", "tensor"), both, P("tensor", "dp"), both, both, both,
        ),
        check_vma=False,
    )
```

```python
from functools import partial

import jax
import jax.numpy as jnp
from jax import lax
from jax.experimental import pallas as pl
from jax.experimental.pallas import tpu as pltpu
from jax.sharding import PartitionSpec as P

HD = 64
EPS = 1e-12
NEG = -1000000000.0
SCALE = float(HD) ** -0.5
AXES = ("dp", "tensor")
f32 = jnp.float32
bf16 = jnp.bfloat16
HI = lax.Precision.HIGHEST
BLK = 96
VMEM_LIMIT = 24 * 1024 * 1024
COST = 30_000_000


def nn(a, b):
    return lax.dot_general(a, b, (((1,), (0,)), ((), ())), preferred_element_type=f32)


def nt(a, b):
    return lax.dot_general(a, b, (((1,), (1,)), ((), ())), preferred_element_type=f32)


def tn(a, b):
    return lax.dot_general(a, b, (((0,), (0,)), ((), ())), preferred_element_type=f32)


def mean_last(v):
    return jnp.sum(v, axis=-1, keepdims=True) * (1.0 / v.shape[-1])


def normalize(values):
    center = values - mean_last(values)
    inverse = lax.rsqrt(mean_last(center * center) + EPS)
    return center * inverse, inverse


def normalize_back(scaled, normed, inverse):
    return inverse * (scaled - mean_last(scaled) - normed * mean_last(scaled * normed))


def col_sum(v):
    return jnp.sum(v, axis=0, keepdims=True)


def pack(qkv_ref, out_ref, down_ref, ob_ref, g1_ref, s1_ref, db_ref, g2_ref, s2_ref, qv_ref, ub_ref, first_ref, down_t_ref):
    rows, hc = qkv_ref.shape[1:]
    eye = (lax.broadcasted_iota(jnp.int32, (rows, rows), 0) == lax.broadcasted_iota(jnp.int32, (rows, rows), 1)).astype(bf16)
    for c in range(3):
        first_ref[:rows, c * hc : (c + 1) * hc] = qkv_ref[c]
    first_ref[:rows, 3 * hc :] = nt(eye, out_ref[...]).astype(bf16)
    down_t_ref[...] = nt(eye, down_ref[...]).astype(bf16)
    parts = [r[...].astype(f32) for r in (ob_ref, g1_ref, s1_ref, db_ref, g2_ref, s2_ref, qv_ref)]
    short = jnp.concatenate(parts, axis=0).astype(bf16)
    count, size = short.shape
    wide = first_ref.shape[1]

    def spread(values, at):
        lane = lax.broadcasted_iota(jnp.int32, (values.shape[1], wide), 1) - at
        return nn(values, (lax.rem(lane + values.shape[1] * wide, values.shape[1]) == lax.broadcasted_iota(jnp.int32, lane.shape, 0)).astype(bf16))

    lane = lax.broadcasted_iota(jnp.int32, (count, wide), 1)
    start = lax.broadcasted_iota(jnp.int32, (count, wide), 0) * size
    row = col_sum(jnp.where((lane >= start) & (lane < start + size), spread(short, 0), 0.0))
    total, long = count * size, ub_ref.shape[1]
    lane = lax.broadcasted_iota(jnp.int32, (1, wide), 1)
    row = jnp.where((lane >= total) & (lane < total + long), spread(ub_ref[...], total), row)
    extra = first_ref.shape[0] - rows
    here = lax.broadcasted_iota(jnp.int32, (extra, wide), 0)
    first_ref[rows:, :] = jnp.where(here == 0, row, 0.0).astype(bf16)


def stacked(values, hc):
    head = lax.broadcasted_iota(jnp.int32, (1, hc), 1) // HD
    return jnp.concatenate([values * (head == h).astype(f32).astype(bf16) for h in range(hc // HD)], axis=0)


def own_columns(blocks, hc):
    n_heads = hc // HD
    length = blocks.shape[0] // n_heads
    head = lax.broadcasted_iota(jnp.int32, (1, hc), 1) // HD
    out = blocks[:length]
    for h in range(1, n_heads):
        out = jnp.where(head == h, blocks[h * length : (h + 1) * length], out)
    return out


def sections(values, length):
    return [values[:, c : c + length] for c in range(0, values.shape[1], length)]


def attention_forward(x_ref, w0_ref, w1_ref, w2_ref, w3_ref, bq_ref, bv_ref, segc_ref, segr_ref, vec_ref,
                      qkv_ref, p_ref, o_ref, n1_ref, x1_ref, r1_ref, n1b_ref, n1t_ref, acc_ref):
    step = pl.program_id(0)
    hc = bq_ref.shape[-1]
    rows, length = segr_ref.shape
    x = x_ref[...]
    w = rows_of((w0_ref, w1_ref, w2_ref, w3_ref))
    qkv = nn(x, w[:, : 3 * hc])
    q = (qkv[:, :hc] + bq_ref[0]).astype(bf16) * bf16(SCALE)
    k = qkv[:, hc : 2 * hc].astype(bf16)
    v = (qkv[:, 2 * hc :] + bv_ref[0]).astype(bf16)
    qkv_ref[0, :, :hc] = q
    qkv_ref[0, :, hc : 2 * hc] = k
    qkv_ref[0, :, 2 * hc :] = v
    spans = [slice(g * length, (g + 1) * length) for g in range(rows)]
    scores = [nt(q[span], stacked(k[span], hc)) for span in spans]
    probs = []
    for g, span in enumerate(spans):
        same = segc_ref[span, :] == segr_ref[g : g + 1, :]
        parts = []
        for s in sections(scores[g], length):
            s = jnp.where(same, s, NEG)
            e = jnp.exp(s - jnp.max(s, axis=-1, keepdims=True))
            parts.append(e * (1.0 / jnp.sum(e, axis=-1, keepdims=True)))
        probs.append(jnp.concatenate(parts, axis=1))
    for g, span in enumerate(spans):
        p_ref[0, g] = probs[g]
        o_ref[0, span, :] = nn(probs[g].astype(bf16), stacked(v[span], hc)).astype(bf16)
    add = nt(o_ref[0], w[:, 3 * hc :])

    @pl.when(step == 0)
    def _():
        acc_ref[...] = add

    @pl.when(step > 0)
    def _():
        acc_ref[...] += add

    @pl.when(step == pl.num_programs(0) - 1)
    def _():
        a = acc_ref[...] + vec_ref[0:1, :] + x_ref[...].astype(f32)
        normed, inverse = normalize(a)
        n1 = normed * vec_ref[1:2, :] + vec_ref[2:3, :]
        n1_ref[...] = n1
        x1_ref[...] = normed
        r1_ref[...] = inverse
        low = n1.astype(bf16)
        n1b_ref[...] = low
        n1t_ref[...] = low.T


def rows_of(refs):
    return jnp.concatenate([r[...].reshape(r.shape[0] * r.shape[2], r.shape[3]) for r in refs], axis=0)


def up_forward(n_ref, w0_ref, w1_ref, w2_ref, w3_ref, b_ref, z_ref, d_ref):
    u = nn(n_ref[...], rows_of((w0_ref, w1_ref, w2_ref, w3_ref))) + b_ref[0]
    phi = 0.5 + 0.5 * lax.erf(u * (0.5**0.5))
    z_ref[0] = (u * phi).astype(bf16)
    d_ref[0] = phi + u * (jnp.exp(-0.5 * u * u) * 0.3989422804014327)


def down_forward(z_ref, w0_ref, w1_ref, w2_ref, w3_ref, n1_ref, vec_ref, segc_ref, segr_ref, pg_ref,
                 pooled_ref, db_ref, dbb_ref, dbt_ref, sums_ref, acc_ref):
    step = pl.program_id(0)
    add = nt(z_ref[0], rows_of((w0_ref, w1_ref, w2_ref, w3_ref)))

    @pl.when(step == 0)
    def _():
        acc_ref[...] = add

    @pl.when(step > 0)
    def _():
        acc_ref[...] += add

    @pl.when(step == pl.num_programs(0) - 1)
    def _():
        rows, length = segr_ref.shape
        segs = pg_ref.shape[1]
        b = acc_ref[...] + vec_ref[3:4, :] + n1_ref[...]
        x2, r2 = normalize(b)
        y = x2 * vec_ref[4:5, :] + vec_ref[5:6, :]
        grads = []
        for g in range(rows):
            span = slice(g * length, (g + 1) * length)
            ids = lax.broadcasted_iota(jnp.int32, (segs, length), 0)
            hot_t = (ids == segr_ref[g : g + 1, :]).astype(f32)
            idc = lax.broadcasted_iota(jnp.int32, (length, segs), 1)
            hot = (idc == segc_ref[span, :]).astype(f32)
            count = jnp.sum(hot_t, axis=1, keepdims=True)
            sums = lax.dot_general(hot_t, y[span, :], (((1,), (0,)), ((), ())),
                                   precision=HI, preferred_element_type=f32)
            pooled_ref[g] = sums / count
            grads.append(lax.dot_general(hot, pg_ref[g] / count, (((1,), (0,)), ((), ())),
                                         precision=HI, preferred_element_type=f32))
        dy = jnp.concatenate(grads, axis=0)
        db = normalize_back(dy * vec_ref[4:5, :], x2, r2)
        db_ref[...] = db
        low = db.astype(bf16)
        dbb_ref[...] = low
        dbt_ref[...] = low.T
        sums_ref[0:1, :] = col_sum(db)
        sums_ref[1:2, :] = col_sum(dy * x2)
        sums_ref[2:3, :] = col_sum(dy)


def put(grad, ref):
    ref[:, :, :BLK, :] = grad.astype(bf16).reshape(grad.shape[0] // BLK, 1, BLK, grad.shape[1])


def down_weight(dbt_ref, z_ref, out_ref):
    put(nn(dbt_ref[...], z_ref[0]), out_ref)


def up_backward(dbb_ref, w0_ref, w1_ref, w2_ref, w3_ref, d_ref, n1t_ref, keep_ref, send_ref, du_ref, bu_ref):
    width = dbb_ref.shape[1]
    du = (nn(dbb_ref[...], rows_of((w0_ref, w1_ref, w2_ref, w3_ref))) * d_ref[0]).astype(bf16)
    du_ref[0] = du
    bu_ref[0] = col_sum(du.astype(f32))
    grad = nn(n1t_ref[...], du)
    put(grad[width // 2 :], send_ref)
    put(grad[: width // 2], keep_ref)


def norm_backward(du_ref, w0_ref, w1_ref, w2_ref, w3_ref, db_ref, x1_ref, r1_ref, vec_ref, da_ref, dab_ref, dat_ref, sums_ref, acc_ref):
    step = pl.program_id(0)
    add = nt(du_ref[0], rows_of((w0_ref, w1_ref, w2_ref, w3_ref)))

    @pl.when(step == 0)
    def _():
        acc_ref[...] = add

    @pl.when(step > 0)
    def _():
        acc_ref[...] += add

    @pl.when(step == pl.num_programs(0) - 1)
    def _():
        dn1 = acc_ref[...].astype(bf16).astype(f32) + db_ref[...]
        da = normalize_back(dn1 * vec_ref[1:2, :], x1_ref[...], r1_ref[...])
        da_ref[...] = da
        low = da.astype(bf16)
        dab_ref[...] = low
        dat_ref[...] = low.T
        sums_ref[0:1, :] = col_sum(da)
        sums_ref[1:2, :] = col_sum(dn1 * x1_ref[...])
        sums_ref[2:3, :] = col_sum(dn1)


def attention_backward(dab_ref, w0_ref, w1_ref, w2_ref, w3_ref, qkv_ref, p_ref, dqkv_ref, bqv_ref):
    hc = bqv_ref.shape[-1]
    dab = dab_ref[...]
    w = rows_of([r.at[:, :, :, 3 * hc :] for r in (w0_ref, w1_ref, w2_ref, w3_ref)])
    do = nn(dab, w).astype(bf16)
    qkv = qkv_ref[0]
    rows, length = p_ref.shape[1], p_ref.shape[2]
    spans = [slice(g * length, (g + 1) * length) for g in range(rows)]
    q = [qkv[span, :hc] for span in spans]
    k = [stacked(qkv[span, hc : 2 * hc], hc) for span in spans]
    dps = [nt(do[span], stacked(qkv[span, 2 * hc :], hc)) for span in spans]
    dss = []
    for g in range(rows):
        parts = []
        for p, dp in zip(sections(p_ref[0, g], length), sections(dps[g], length)):
            pd = p * dp
            parts.append((pd - p * jnp.sum(pd, axis=-1, keepdims=True)).astype(bf16))
        dss.append(jnp.concatenate(parts, axis=1))
    for g, span in enumerate(spans):
        dqkv_ref[0, span, :hc] = (nn(dss[g], k[g]) * SCALE).astype(bf16)
        dqkv_ref[0, span, hc : 2 * hc] = own_columns(tn(dss[g], q[g]), hc).astype(bf16)
        dqkv_ref[0, span, 2 * hc :] = own_columns(tn(p_ref[0, g].astype(bf16), do[span]), hc).astype(bf16)
    dqkv = dqkv_ref[0]
    bqv_ref[0, 0:1, :] = col_sum(dqkv[:, :hc].astype(f32))
    bqv_ref[0, 1:2, :] = col_sum(dqkv[:, 2 * hc :].astype(f32))


def attention_weights(xt_ref, dat_ref, dqkv_ref, o_ref, vec_ref, keep_ref, send_ref):
    half = xt_ref.shape[0] // 2
    for n, ref in enumerate((keep_ref, send_ref)):
        count = ref.shape[0]
        ref[:, :, BLK:, :] = vec_ref[n * count : (n + 1) * count]
    grad = jnp.concatenate([nn(xt_ref[...], dqkv_ref[0]), nn(dat_ref[...], o_ref[0])], axis=1)
    put(grad[half:], send_ref)
    put(grad[:half], keep_ref)


def input_backward(dqkv_ref, w0_ref, w1_ref, w2_ref, w3_ref, da_ref, perm_ref, dx_ref, acc_ref):
    step = pl.program_id(0)
    cols = dqkv_ref.shape[-1]
    w = rows_of((w0_ref, w1_ref, w2_ref, w3_ref))
    add = nt(dqkv_ref[0], w[:, :cols])

    @pl.when(step == 0)
    def _():
        acc_ref[...] = add

    @pl.when(step > 0)
    def _():
        acc_ref[...] += add

    @pl.when(step == pl.num_programs(0) - 1)
    def _():
        dx = acc_ref[...] + da_ref[...]
        high = dx.astype(bf16)
        rest = dx - high.astype(f32)
        mid = rest.astype(bf16)
        low = (rest - mid.astype(f32)).astype(bf16)
        perm = perm_ref[...]
        dx_ref[...] = nt(high, perm) + nt(mid, perm) + nt(low, perm)


def whole(a):
    nd = len(a.shape)
    return pl.BlockSpec(a.shape, lambda s: (0,) * nd, pipeline_mode=pl.Buffered(1))


def lead(a):
    nd = len(a.shape)
    return pl.BlockSpec((1,) + a.shape[1:], lambda s: (s,) + (0,) * (nd - 1))


def weight(a):
    return pl.BlockSpec((a.shape[0], 1, BLK, a.shape[3]), lambda s: (0, s, 0, 0))


def half_spec(h):
    return pl.BlockSpec((h.shape[0], 1) + h.shape[2:], lambda s: (0, s, 0, 0))


def sds(shape, dtype):
    return jax.ShapeDtypeStruct(shape, dtype)


def far(shape, dtype):
    return pltpu.HBM(shape, dtype)


def call(body, n_t, micros, ins, outs, scratch=()):
    return pl.pallas_call(
        body,
        name=body.__name__,
        grid=(n_t,),
        in_specs=[s for _, s in ins],
        out_specs=[s for _, s in outs],
        out_shape=[a for a, _ in outs],
        scratch_shapes=list(scratch),
        compiler_params=pltpu.CompilerParams(
            dimension_semantics=("arbitrary",), vmem_limit_bytes=VMEM_LIMIT
        ),
        cost_estimate=pl.CostEstimate(flops=int(micros * COST), transcendentals=0, bytes_accessed=0),
    )(*[a for a, _ in ins])


def flips(n_dp, n_t):
    size = n_dp * n_t
    core = n_t
    x_bit, y_bit = 2 * core, 4 * core

    def table(bit_of):
        return [(i, i ^ bit_of(i)) for i in range(size)]

    return {
        "Z": [table(lambda i, d=d: d) for d in range(1, n_t)],
        "C": [table(lambda i: core)],
        "2": [table(lambda i: x_bit if i & core else y_bit)],
        "3": [table(lambda i: y_bit if i & core else x_bit)],
    }


def after(value, *done):
    return lax.optimization_barrier((value, *done))[0] if done else value


class Gather:
    def __init__(self, value, tables):
        self.held, self.tables = [value[None]], tables

    def stage(self, name, *done):
        got = [lax.ppermute(after(h, *done), AXES, t) for t in self.tables[name] for h in self.held]
        self.held = [jnp.concatenate(self.held + got)] if name in "Z2" else self.held + got
        return got

    def pieces(self, n_t):
        return [h.reshape(h.shape[0] // n_t, n_t, *h.shape[1:]) for h in self.held]


class Scatter:
    def __init__(self, keep, send, tables):
        self.keep, self.send, self.tables = keep, [send], tables

    def stage(self, name, parts, *done):
        got = [lax.ppermute(after(s, *done), AXES, t) for s, t in zip(self.send, self.tables[name], strict=True)]
        size = self.keep.shape[0] // parts

        def share(j):
            cut = slice(j * size, (j + 1) * size)
            return sum((g[cut].astype(f32) for g in got), self.keep[cut].astype(f32))

        self.send = [share(j).astype(bf16) for j in range(1, parts)]
        self.keep = share(0) if size <= 4 else share(0).astype(bf16)
        return got


def per_device(
    hidden_in, segment_ids, pooled_grad, qkv_weight, qv_bias, out_weight, out_bias,
    norm1_gain, norm1_shift, up_weight, up_bias, down_weight_in, down_bias, norm2_gain, norm2_shift,
):
    n_dp, n_t = lax.axis_size("dp"), lax.axis_size("tensor")
    at_dp, at_t = lax.axis_index("dp"), lax.axis_index("tensor")
    hc, fc = qkv_weight.shape[2], up_weight.shape[1]
    rows = qkv_weight.shape[1]
    D = rows * n_dp
    micro, tokens = hidden_in.shape[0], hidden_in.shape[1]
    seqs, L = segment_ids.shape[1], segment_ids.shape[2]
    G, T = micro * seqs, micro * tokens
    segs = pooled_grad.shape[2]
    n_i = D // BLK
    pairwise = (n_dp, n_t) == (8, 4) and 4 * hc == fc

    d_parts = [out_bias, norm1_gain, norm1_shift, down_bias, norm2_gain, norm2_shift]
    e_parts = [qv_bias[0], qv_bias[1], up_bias]
    dv = out_bias.shape[0]
    n_vec = sum(p.shape[0] for p in d_parts + e_parts)
    nd = len(d_parts) * dv

    if pairwise:
        tables = flips(n_dp, n_t)
        packed = (qkv_weight, out_weight, down_weight_in, *[p[None] for p in d_parts], qv_bias, up_bias[None])
        packed, down_t = pl.pallas_call(
            pack, name="pack", out_shape=[sds((BLK + 8, 4 * hc), bf16), sds((BLK, fc), bf16)]
        )(*packed)
        first = Gather(packed, tables)
        middle = Gather(up_weight, tables)
        last = Gather(down_t, tables)
        done = first.stage("Z")

        rel = jnp.arange(n_i)
        core = (at_dp & 1) ^ (rel >> 2)
        s3, s2 = (rel >> 1) & 1, rel & 1
        dy, dx = jnp.where(core == 0, s2, s3), jnp.where(core == 0, s3, s2)
        absolute = ((((at_dp >> 2) & 1) ^ dy) << 2) | ((((at_dp >> 1) & 1) ^ dx) << 1) | core
        i_p = jnp.broadcast_to(absolute[:, None], (n_i, n_t)).reshape(-1)
        t_p = jnp.broadcast_to((at_t ^ jnp.arange(n_t))[None], (n_i, n_t)).reshape(-1)
        to_d = jnp.broadcast_to(rel[:, None], (n_i, n_t)).reshape(-1) * n_t + t_p
        to_e = (((i_p * n_t) // n_i) ^ at_t) * n_i + (i_p * n_t + t_p) % n_i
        slot = jnp.arange(n_i * n_t)
        hot_d = (to_d[None, :] == slot[:, None]).astype(bf16)
        hot_e = (to_e[None, :] == slot[:, None]).astype(bf16)
        lane = jnp.arange(D)
        hot_i = (absolute[:, None] == rel[None, :])
        same_block = jnp.repeat(jnp.repeat(hot_i.T, BLK, axis=0), BLK, axis=1)
        perm = (same_block & ((lane[:, None] % BLK) == (lane[None, :] % BLK))).astype(bf16)
    else:
        perm = (jnp.arange(D)[:, None] == jnp.arange(D)[None, :]).astype(bf16)
    x = nn(hidden_in.reshape(T, D), perm).astype(bf16)
    x_t = lax.dot_general(perm, hidden_in.reshape(T, D), (((0,), (1,)), ((), ())), preferred_element_type=f32).astype(bf16)
    pg = jnp.einsum("gsd,de->gse", pooled_grad.reshape(G, segs, D), perm.astype(f32), precision=HI)
    seg_r = segment_ids.reshape(G, L)
    seg_c = segment_ids.reshape(T, 1)

    if pairwise:
        done = first.stage("2", x, x_t, pg, hot_d, hot_e) + middle.stage("Z", *done)
        done = first.stage("3", *done) + middle.stage("2", *done) + last.stage("Z", *done)
        first.stage("C", *done)
        done = middle.stage("3", *done) + last.stage("2", *done)
        w_qo = first.pieces(n_t)
        vecs = jnp.concatenate([w[:, :, BLK, : n_vec].reshape(-1, n_vec) for w in w_qo])
        d_all = nn(hot_d, vecs[:, :nd])
        e_all = nn(hot_e, vecs[:, nd:])
    else:
        heads_in = [qkv_weight[0], qkv_weight[1], qkv_weight[2], out_weight.T]
        main = jnp.concatenate([*heads_in, up_weight, down_weight_in.T], axis=1)
        vec = jnp.concatenate(d_parts + e_parts)
        full = lax.all_gather(lax.all_gather(main, "dp", axis=0, tiled=True), "tensor", axis=0)
        full = full.reshape(n_t, n_i, BLK, -1).transpose(1, 0, 2, 3)
        quarters = [full[j * n_i // 4 : (j + 1) * n_i // 4] for j in range(4)]
        w_qo = [w[..., : 4 * hc] for w in quarters]
        w_up = [w[..., 4 * hc : 4 * hc + fc] for w in quarters]
        w_down = [w[..., 4 * hc + fc :] for w in quarters]
        vecs = lax.all_gather(lax.all_gather(vec, "tensor"), "dp").reshape(n_dp * n_t, -1).astype(f32)
        d_all, e_all = vecs[:, :nd], vecs[:, nd:]

    vec_d = jnp.concatenate([d_all[:, j * dv : (j + 1) * dv].reshape(1, D) for j in range(6)])
    b_q = e_all[:, :dv].reshape(n_t, 1, hc)
    b_v = e_all[:, dv : 2 * dv].reshape(n_t, 1, hc)
    b_u = e_all[:, 2 * dv :].reshape(n_t, 1, fc)
    hl = hc // HD * L

    def leads(*arrays):
        return [(a, lead(a)) for a in arrays]

    def wholes(*arrays):
        return [(a, whole(a)) for a in arrays]

    def weights(*arrays):
        return [(a, weight(a)) for a in arrays]

    if pairwise:
        last.stage("3", *done)
        middle.stage("C", *done)
    qkv, prob, o, n1, x1, r1, n1b, n1_t = call(
        attention_forward, n_t, 10,
        wholes(x) + weights(*w_qo) + leads(b_q, b_v) + wholes(seg_c, seg_r, vec_d),
        leads(far((n_t, T, 3 * hc), bf16), far((n_t, G, L, hl), f32), far((n_t, T, hc), bf16))
        + wholes(sds((T, D), f32), far((T, D), f32), far((T, 1), f32), sds((T, D), bf16), far((D, T), bf16)),
        [pltpu.VMEM((T, D), f32)],
    )
    if pairwise:
        last.stage("C", n1b)
        w_up, w_down = middle.pieces(n_t), last.pieces(n_t)
    z, dgelu = call(
        up_forward, n_t, 4, wholes(n1b) + weights(*w_up) + leads(b_u),
        leads(sds((n_t, T, fc), bf16), sds((n_t, T, fc), f32)),
    )
    pooled, db, dbb, db_t, sums2 = call(
        down_forward, n_t, 5.5, leads(z) + weights(*w_down) + wholes(n1, vec_d, seg_c, seg_r, pg),
        wholes(sds((G, segs, D), f32), sds((T, D), f32), sds((T, D), bf16), sds((D, T), bf16), sds((3, D), f32)),
        [pltpu.VMEM((T, D), f32)],
    )
    half = sds((n_i // 2, n_t, BLK, fc), bf16)

    def halves(h):
        return [(h, half_spec(h))]

    def side_of(side):
        return [(db_t, pl.BlockSpec((D // 2, T), lambda s: (side, 0), pipeline_mode=pl.Buffered(1)))]

    down_send = call(down_weight, n_t, 2.2, side_of(1) + leads(z), halves(half))[0]
    down_keep = call(down_weight, n_t, 2.2, side_of(0) + leads(z), halves(half))[0]

    def flat(a):
        return a.reshape((-1,) + a.shape[2:])

    if pairwise:
        s_down = Scatter(flat(down_keep), flat(down_send), tables)
        s_down.stage("C", 2)
        dbb = after(dbb, down_keep)
    up_keep, up_send, du, g_bu = call(
        up_backward, n_t, 7, wholes(dbb) + weights(*w_down) + leads(dgelu) + wholes(n1_t),
        halves(half) * 2 + leads(sds((n_t, T, fc), bf16), sds((n_t, 1, fc), f32)),
    )
    if pairwise:
        s_up = Scatter(flat(up_keep), flat(up_send), tables)
        got3 = s_down.stage("3", 2)
        got_uc = s_up.stage("C", 2)
    da, dab, da_t, sums1 = call(
        norm_backward, n_t, 4, leads(du) + weights(*w_up) + wholes(db, x1, r1, vec_d),
        wholes(sds((T, D), f32), sds((T, D), bf16), sds((D, T), bf16), sds((3, D), f32)), [pltpu.VMEM((T, D), f32)],
    )
    if pairwise:
        dab = after(dab, *got_uc)
    dqkv, g_bqv = call(
        attention_backward, n_t, 8, wholes(dab) + weights(*w_qo) + leads(qkv, prob),
        leads(sds((n_t, T, 3 * hc), bf16), sds((n_t, 2, hc), f32)),
    )
    if pairwise:
        got_d2, got_u3 = s_down.stage("2", n_t), s_up.stage("3", 2)
        da_t = after(da_t, *got3, *got_u3)
    g_d = jnp.concatenate([v.reshape(n_dp * n_t, dv) for v in (*sums1, *sums2)], axis=1)
    g_e = jnp.concatenate(
        [g_bqv[:, 0].reshape(n_dp * n_t, dv), g_bqv[:, 1].reshape(n_dp * n_t, dv), g_bu.reshape(n_dp * n_t, -1)], axis=1
    )
    if pairwise:
        g_vec = jnp.concatenate([tn(hot_d, g_d.astype(bf16)), tn(hot_e, g_e.astype(bf16))], axis=1).astype(bf16)
        g_vec = jnp.pad(g_vec.reshape(n_i, n_t, 1, -1), ((0, 0), (0, 0), (0, 7), (0, 4 * hc - n_vec)))
    else:
        g_vec = jnp.zeros((n_i, n_t, 8, 4 * hc), bf16)
    half_qo = sds((n_i // 2, n_t, BLK + 8, 4 * hc), bf16)
    qo_keep, qo_send = call(
        attention_weights, n_t, 5,
        wholes(x_t, da_t) + leads(dqkv, o) + [(g_vec, pl.BlockSpec((n_i, 1, 8, 4 * hc), lambda s: (0, s, 0, 0)))],
        halves(half_qo) * 2,
    )
    if pairwise:
        s_qo = Scatter(flat(qo_keep), flat(qo_send), tables)
        s_qo.stage("C", 2)
        dqkv = after(dqkv, qo_send)
    dx = call(
        input_backward, n_t, 4, leads(dqkv) + weights(*w_qo) + wholes(da, perm), wholes(sds((T, D), f32)),
        [pltpu.VMEM((T, D), f32)],
    )[0]
    pooled = jnp.einsum("gse,de->gsd", pooled, perm.astype(f32), precision=HI)

    if pairwise:
        s_down.stage("Z", 1)
        s_up.stage("2", n_t)
        s_qo.stage("3", 2)
        s_up.stage("Z", 1)
        s_qo.stage("2", n_t, dx)
        s_qo.stage("Z", 1)
        g_down, g_up, g_qo = s_down.keep[0], s_up.keep[0], s_qo.keep[0]
        g_v = g_qo[BLK, : n_vec]
        g_qo = g_qo[:BLK]
    else:
        def joined(keep, send):
            g = jnp.concatenate([keep, send])[:, :, :BLK]
            return g.transpose(1, 0, 2, 3).reshape(n_t, D, -1)

        g_full = jnp.concatenate([joined(qo_keep, qo_send), joined(up_keep, up_send), joined(down_keep, down_send)], axis=2)
        mine = lax.psum_scatter(g_full, "tensor", scatter_dimension=0)
        mine = lax.psum_scatter(mine, "dp", scatter_dimension=0, tiled=True).astype(f32)
        g_qo, g_up, g_down = mine[:, : 4 * hc], mine[:, 4 * hc : 4 * hc + fc], mine[:, 4 * hc + fc :]
        g_v = lax.psum_scatter(jnp.concatenate([g_d, g_e], axis=1), AXES, scatter_dimension=0)
    vo = [g_v[j * dv : (j + 1) * dv] for j in range(8)]
    return (
        pooled.reshape(micro, seqs, segs, D),
        dx.reshape(micro, tokens, D),
        jnp.stack([g_qo[:, c * hc : (c + 1) * hc] for c in range(3)]),
        jnp.stack([vo[6], vo[7]]),
        g_qo[:, 3 * hc :].T,
        vo[0], vo[1], vo[2],
        g_up,
        g_v[8 * dv :],
        g_down.T,
        vo[3], vo[4], vo[5],
    )


def solution(mesh):
    both = P(AXES)
    row3 = P(None, AXES)
    return jax.shard_map(
        per_device,
        mesh=mesh,
        in_specs=(
            row3, row3, row3, P(None, "dp", "tensor"), row3, P("tensor", "dp"), both, both, both,
            P("dp", "tensor"), both, P("tensor", "dp"), both, both, both,
        ),
        out_specs=(
            row3, row3, P(None, "dp", "tensor"), row3, P("tensor", "dp"), both, both, both,
            P("dp", "tensor"), both, P("tensor", "dp"), both, both, both,
        ),
        check_vma=False,
    )
```

```python
from functools import partial

import jax
import jax.numpy as jnp
from jax import lax
from jax.experimental import pallas as pl
from jax.experimental.pallas import tpu as pltpu
from jax.sharding import PartitionSpec as P

HD = 64
EPS = 1e-12
NEG = -1000000000.0
SCALE = float(HD) ** -0.5
AXES = ("dp", "tensor")
f32 = jnp.float32
bf16 = jnp.bfloat16
HI = lax.Precision.HIGHEST
BLK = 96
VMEM_LIMIT = 24 * 1024 * 1024
COST = 30_000_000


def nn(a, b):
    return lax.dot_general(a, b, (((1,), (0,)), ((), ())), preferred_element_type=f32)


def nt(a, b):
    return lax.dot_general(a, b, (((1,), (1,)), ((), ())), preferred_element_type=f32)


def tn(a, b):
    return lax.dot_general(a, b, (((0,), (0,)), ((), ())), preferred_element_type=f32)


def mean_last(v):
    return jnp.sum(v, axis=-1, keepdims=True) * (1.0 / v.shape[-1])


def normalize(values):
    center = values - mean_last(values)
    inverse = lax.rsqrt(mean_last(center * center) + EPS)
    return center * inverse, inverse


def normalize_back(scaled, normed, inverse):
    return inverse * (scaled - mean_last(scaled) - normed * mean_last(scaled * normed))


def col_sum(v):
    return jnp.sum(v, axis=0, keepdims=True)


def pack(qkv_ref, out_ref, down_ref, ob_ref, g1_ref, s1_ref, db_ref, g2_ref, s2_ref, qv_ref, ub_ref, first_ref, down_t_ref):
    rows, hc = qkv_ref.shape[1:]
    eye = (lax.broadcasted_iota(jnp.int32, (rows, rows), 0) == lax.broadcasted_iota(jnp.int32, (rows, rows), 1)).astype(bf16)
    for c in range(3):
        first_ref[:rows, c * hc : (c + 1) * hc] = qkv_ref[c]
    first_ref[:rows, 3 * hc :] = nt(eye, out_ref[...]).astype(bf16)
    down_t_ref[...] = nt(eye, down_ref[...]).astype(bf16)
    parts = [r[...].astype(f32) for r in (ob_ref, g1_ref, s1_ref, db_ref, g2_ref, s2_ref, qv_ref)]
    short = jnp.concatenate(parts, axis=0).astype(bf16)
    count, size = short.shape
    wide = first_ref.shape[1]

    def spread(values, at):
        lane = lax.broadcasted_iota(jnp.int32, (values.shape[1], wide), 1) - at
        return nn(values, (lax.rem(lane + values.shape[1] * wide, values.shape[1]) == lax.broadcasted_iota(jnp.int32, lane.shape, 0)).astype(bf16))

    lane = lax.broadcasted_iota(jnp.int32, (count, wide), 1)
    start = lax.broadcasted_iota(jnp.int32, (count, wide), 0) * size
    row = col_sum(jnp.where((lane >= start) & (lane < start + size), spread(short, 0), 0.0))
    total, long = count * size, ub_ref.shape[1]
    lane = lax.broadcasted_iota(jnp.int32, (1, wide), 1)
    row = jnp.where((lane >= total) & (lane < total + long), spread(ub_ref[...], total), row)
    extra = first_ref.shape[0] - rows
    here = lax.broadcasted_iota(jnp.int32, (extra, wide), 0)
    first_ref[rows:, :] = jnp.where(here == 0, row, 0.0).astype(bf16)


def stacked(values, hc):
    head = lax.broadcasted_iota(jnp.int32, (1, hc), 1) // HD
    return jnp.concatenate([values * (head == h).astype(f32).astype(bf16) for h in range(hc // HD)], axis=0)


def own_columns(blocks, hc):
    n_heads = hc // HD
    length = blocks.shape[0] // n_heads
    head = lax.broadcasted_iota(jnp.int32, (1, hc), 1) // HD
    out = blocks[:length]
    for h in range(1, n_heads):
        out = jnp.where(head == h, blocks[h * length : (h + 1) * length], out)
    return out


def sections(values, length):
    return [values[:, c : c + length] for c in range(0, values.shape[1], length)]


def rows_of(refs):
    return jnp.concatenate([r[...].reshape(-1, r.shape[3]) for r in refs], axis=0)


def accumulate(acc_ref, step, add):
    @pl.when(step == 0)
    def _():
        acc_ref[...] = add

    @pl.when(step > 0)
    def _():
        acc_ref[...] += add


def iota(shape, axis):
    return lax.broadcasted_iota(jnp.int32, shape, axis)


def picks(count, first, wide, size):
    return (iota((count, wide), 0) == first + lax.rem(iota((1, wide), 1), size)).astype(bf16)


def belongs(count, wide, size, period):
    lane, row = iota((1, wide), 1), lax.rem(iota((count, 1), 0), period)
    return (lane >= row * size) & (lane < (row + 1) * size)


def read_vectors(rows, hot_d, hot_e, sizes):
    n_d, dv, bu, width, hc, fc, n_t = sizes
    count = rows.shape[0]
    per = count // n_t
    d_all = nn(hot_d, rows[:, : n_d * dv]).astype(bf16)
    mine = belongs(count, width, dv, count)
    d_rows = [col_sum(jnp.where(mine, nn(d_all, picks(n_d * dv, j * dv, width, dv)), 0.0)) for j in range(n_d)]
    e_all = nn(hot_e, rows[:, n_d * dv : n_d * dv + 2 * dv + bu]).astype(bf16)
    out = []
    for first, size, wide in ((0, dv, hc), (dv, dv, hc), (2 * dv, bu, fc)):
        spread = jnp.where(belongs(count, wide, size, per), nn(e_all, picks(e_all.shape[1], first, wide, size)), 0.0)
        out.append(jnp.sum(spread.reshape(n_t, per, wide), axis=1, keepdims=True))
    return jnp.concatenate(d_rows, axis=0), out


def write_vectors(d_rows, e_rows, hot_d, hot_e, sizes):
    n_d, dv, bu, width, hc, fc, n_t = sizes
    count = hot_d.shape[0]
    per = count // n_t
    mine = belongs(count, width, dv, count)
    d_all = sum(
        nt(jnp.where(mine, d_rows[j : j + 1, :], 0.0).astype(bf16), picks(n_d * dv, j * dv, width, dv)) for j in range(n_d)
    ).astype(bf16)
    e_all = 0.0
    for value, first, size, wide in zip(e_rows, (0, dv, 2 * dv), (dv, dv, bu), (hc, hc, fc), strict=True):
        spread = jnp.broadcast_to(value, (n_t, per, wide)).reshape(count, wide)
        spread = jnp.where(belongs(count, wide, size, per), spread, 0.0).astype(bf16)
        e_all = e_all + nt(spread, picks(2 * dv + bu, first, wide, size))
    return jnp.concatenate([tn(hot_d, d_all), tn(hot_e, e_all.astype(bf16))], axis=1)


def attention_forward(sizes, x_ref, w0_ref, w1_ref, w2_ref, w3_ref, v0_ref, v1_ref, v2_ref, v3_ref, hd_ref, he_ref,
                      segc_ref, segr_ref, qkv_ref, p_ref, o_ref, n1_ref, x1_ref, r1_ref, n1b_ref, n1t_ref, n1s_ref,
                      vec_ref, bu_ref, acc_ref, bq_ref, bv_ref):
    step = pl.program_id(0)
    hc = bq_ref.shape[-1]

    @pl.when(step == 0)
    def _():
        rows = jnp.concatenate([r[:, :, 0, :].reshape(-1, r.shape[3]) for r in (v0_ref, v1_ref, v2_ref, v3_ref)], axis=0)
        d_rows, (b_q, b_v, b_u) = read_vectors(rows, hd_ref[...], he_ref[...], sizes)
        vec_ref[...] = d_rows
        bq_ref[...] = b_q
        bv_ref[...] = b_v
        bu_ref[...] = b_u

    rows, length = segr_ref.shape
    x = x_ref[...]
    w = rows_of((w0_ref, w1_ref, w2_ref, w3_ref))
    qkv = nn(x, w[:, : 3 * hc])
    q = (qkv[:, :hc] + bq_ref[step]).astype(bf16) * bf16(SCALE)
    k = qkv[:, hc : 2 * hc].astype(bf16)
    v = (qkv[:, 2 * hc :] + bv_ref[step]).astype(bf16)
    qkv_ref[0, :, :hc] = q
    qkv_ref[0, :, hc : 2 * hc] = k
    qkv_ref[0, :, 2 * hc :] = v
    spans = [slice(g * length, (g + 1) * length) for g in range(rows)]
    scores = [nt(q[span], stacked(k[span], hc)) for span in spans]
    probs = []
    for g, span in enumerate(spans):
        same = segc_ref[span, :] == segr_ref[g : g + 1, :]
        parts = []
        for s in sections(scores[g], length):
            s = jnp.where(same, s, NEG)
            e = jnp.exp(s - jnp.max(s, axis=-1, keepdims=True))
            parts.append(e * (1.0 / jnp.sum(e, axis=-1, keepdims=True)))
        probs.append(jnp.concatenate(parts, axis=1))
    for g, span in enumerate(spans):
        p_ref[0, g] = probs[g]
        o_ref[0, span, :hc] = nn(probs[g].astype(bf16), stacked(v[span], hc)).astype(bf16)
    o_ref[0, :, hc:] = jnp.zeros((o_ref.shape[1], o_ref.shape[2] - hc), bf16)
    add = nt(o_ref[0, :, :hc], w[:, 3 * hc :])

    accumulate(acc_ref, step, add)

    @pl.when(step == pl.num_programs(0) - 1)
    def _():
        a = acc_ref[...] + vec_ref[0:1, :] + x_ref[...].astype(f32)
        normed, inverse = normalize(a)
        n1 = normed * vec_ref[1:2, :] + vec_ref[2:3, :]
        n1_ref[...] = n1
        x1_ref[...] = normed
        r1_ref[...] = inverse
        low = n1.astype(bf16)
        n1b_ref[...] = low
        turned = low.T
        n1t_ref[...] = turned[: low.shape[1] // 2]
        n1s_ref[...] = turned[low.shape[1] // 2 :]


def up_forward(n_ref, w0_ref, w1_ref, w2_ref, w3_ref, b_ref, z_ref, d_ref):
    u = nn(n_ref[...], rows_of((w0_ref, w1_ref, w2_ref, w3_ref))) + b_ref[0]
    phi = 0.5 + 0.5 * lax.erf(u * (0.5**0.5))
    z_ref[0] = (u * phi).astype(bf16)
    d_ref[0] = phi + u * (jnp.exp(-0.5 * u * u) * 0.3989422804014327)


def down_forward(z_ref, w0_ref, w1_ref, w2_ref, w3_ref, n1_ref, vec_ref, segc_ref, segr_ref, pg_ref,
                 pooled_ref, db_ref, dbb_ref, dbt_ref, dbs_ref, sums_ref, acc_ref):
    step = pl.program_id(0)
    add = nt(z_ref[0], rows_of((w0_ref, w1_ref, w2_ref, w3_ref)))

    accumulate(acc_ref, step, add)

    @pl.when(step == pl.num_programs(0) - 1)
    def _():
        rows, length = segr_ref.shape
        segs = pg_ref.shape[1]
        b = acc_ref[...] + vec_ref[3:4, :] + n1_ref[...]
        x2, r2 = normalize(b)
        y = x2 * vec_ref[4:5, :] + vec_ref[5:6, :]
        grads = []
        for g in range(rows):
            span = slice(g * length, (g + 1) * length)
            ids = lax.broadcasted_iota(jnp.int32, (segs, length), 0)
            hot_t = (ids == segr_ref[g : g + 1, :]).astype(f32)
            idc = lax.broadcasted_iota(jnp.int32, (length, segs), 1)
            hot = (idc == segc_ref[span, :]).astype(f32)
            count = jnp.sum(hot_t, axis=1, keepdims=True)
            sums = lax.dot_general(hot_t, y[span, :], (((1,), (0,)), ((), ())),
                                   precision=HI, preferred_element_type=f32)
            pooled_ref[g] = sums / count
            grads.append(lax.dot_general(hot, pg_ref[g] / count, (((1,), (0,)), ((), ())),
                                         precision=HI, preferred_element_type=f32))
        dy = jnp.concatenate(grads, axis=0)
        db = normalize_back(dy * vec_ref[4:5, :], x2, r2)
        db_ref[...] = db
        low = db.astype(bf16)
        dbb_ref[...] = low
        turned = low.T
        dbt_ref[...] = turned[: low.shape[1] // 2]
        dbs_ref[...] = turned[low.shape[1] // 2 :]
        sums_ref[0:1, :] = col_sum(db)
        sums_ref[1:2, :] = col_sum(dy * x2)
        sums_ref[2:3, :] = col_sum(dy)


def put(grad, ref):
    ref[:, :, :BLK, :] = grad.astype(bf16).reshape(grad.shape[0] // BLK, 1, BLK, grad.shape[1])


def hidden_backward(dbb_ref, w0_ref, w1_ref, w2_ref, w3_ref, d_ref, du_ref, bu_ref):
    du = (nn(dbb_ref[...], rows_of((w0_ref, w1_ref, w2_ref, w3_ref))) * d_ref[0]).astype(bf16)
    du_ref[0] = du
    bu_ref[0] = col_sum(du.astype(f32))


def step_value(refs, width):
    if len(refs) == 1:
        return refs[0][0, :, :width]
    return jnp.where(pl.program_id(0) < pl.num_programs(0) // 2, refs[0][0, :, :width], refs[1][0, :, :width])


def weight_gradient(groups, vectors, *refs):
    refs = list(refs)
    parts = []
    for pairs, split, width in groups:
        total = None
        for _ in range(pairs):
            add = nn(refs.pop(0)[...], step_value([refs.pop(0) for _ in range(split)], width))
            total = add if total is None else total + add
        parts.append(total)
    grad = jnp.concatenate(parts, axis=1)
    extra = sum(refs.pop(0)[0].astype(f32) for _ in range(vectors)) if vectors else None
    half = grad.shape[0] // 2
    for n, ref in enumerate(refs):
        put(grad[n * half : (n + 1) * half], ref)
        if vectors:
            for j in range(ref.shape[0]):
                row = extra[n * ref.shape[0] + j : n * ref.shape[0] + j + 1]
                tail = ref.shape[2] - BLK
                ref[j, 0, BLK:, :] = jnp.where(iota((tail, row.shape[1]), 0) == 0, row, 0.0).astype(bf16)


def norm_backward(du_ref, w0_ref, w1_ref, w2_ref, w3_ref, db_ref, x1_ref, r1_ref, vec_ref,
                  da_ref, dab_ref, dat_ref, das_ref, sums_ref, acc_ref):
    step = pl.program_id(0)
    accumulate(acc_ref, step, nt(du_ref[0], rows_of((w0_ref, w1_ref, w2_ref, w3_ref))))

    @pl.when(step == pl.num_programs(0) - 1)
    def _():
        dn1 = acc_ref[...].astype(bf16).astype(f32) + db_ref[...]
        da = normalize_back(dn1 * vec_ref[1:2, :], x1_ref[...], r1_ref[...])
        da_ref[...] = da
        low = da.astype(bf16)
        dab_ref[...] = low
        turned = low.T
        dat_ref[...] = turned[: low.shape[1] // 2]
        das_ref[...] = turned[low.shape[1] // 2 :]
        sums_ref[0:1, :] = col_sum(da)
        sums_ref[1:2, :] = col_sum(dn1 * x1_ref[...])
        sums_ref[2:3, :] = col_sum(dn1)


def attention_backward(sizes, dab_ref, w0_ref, w1_ref, w2_ref, w3_ref, qkv_ref, p_ref, s1_ref, s2_ref, gu_ref, hd_ref, he_ref,
                       low_ref, high_ref, keep_ref, send_ref, bq_ref, bv_ref, dqkv_ref):
    step = pl.program_id(0)
    hc = bq_ref.shape[-1]
    dab = dab_ref[...]
    w = rows_of([r.at[:, :, :, 3 * hc :] for r in (w0_ref, w1_ref, w2_ref, w3_ref)])
    do = nn(dab, w).astype(bf16)
    qkv = qkv_ref[0]
    rows, length = p_ref.shape[1], p_ref.shape[2]
    spans = [slice(g * length, (g + 1) * length) for g in range(rows)]
    q = [qkv[span, :hc] for span in spans]
    k = [stacked(qkv[span, hc : 2 * hc], hc) for span in spans]
    dps = [nt(do[span], stacked(qkv[span, 2 * hc :], hc)) for span in spans]
    dss = []
    for g in range(rows):
        parts = []
        for p, dp in zip(sections(p_ref[0, g], length), sections(dps[g], length)):
            pd = p * dp
            parts.append((pd - p * jnp.sum(pd, axis=-1, keepdims=True)).astype(bf16))
        dss.append(jnp.concatenate(parts, axis=1))
    for g, span in enumerate(spans):
        dqkv_ref[span, :hc] = (nn(dss[g], k[g]) * SCALE).astype(bf16)
        dqkv_ref[span, hc : 2 * hc] = own_columns(tn(dss[g], q[g]), hc).astype(bf16)
        dqkv_ref[span, 2 * hc : 3 * hc] = own_columns(tn(p_ref[0, g].astype(bf16), do[span]), hc).astype(bf16)
    dqkv_ref[:, 3 * hc :] = jnp.zeros((dqkv_ref.shape[0], dqkv_ref.shape[1] - 3 * hc), bf16)
    dqkv = dqkv_ref[...]
    half_steps = pl.num_programs(0) // 2

    @pl.when(step < half_steps)
    def _():
        low_ref[0] = dqkv

    @pl.when(step >= half_steps)
    def _():
        high_ref[0] = dqkv

    bq_ref[step] = col_sum(dqkv[:, :hc].astype(f32))
    bv_ref[step] = col_sum(dqkv[:, 2 * hc : 3 * hc].astype(f32))

    @pl.when(step == pl.num_programs(0) - 1)
    def _():
        d_rows = jnp.concatenate([s1_ref[...], s2_ref[...]], axis=0)
        rows = write_vectors(d_rows, (bq_ref[...], bv_ref[...], gu_ref[...]), hd_ref[...], he_ref[...], sizes)
        half, n_t = rows.shape[0] // 2, bq_ref.shape[0]
        rows = jnp.concatenate([rows, jnp.zeros((rows.shape[0], keep_ref.shape[-1] - rows.shape[1]), f32)], axis=1)
        for n, ref in enumerate((keep_ref, send_ref)):
            for t in range(n_t):
                for j in range(half // n_t):
                    at = n * half + j * n_t + t
                    ref[t, j : j + 1, :] = rows[at : at + 1]


def input_backward(low_ref, high_ref, w0_ref, w1_ref, w2_ref, w3_ref, da_ref, perm_ref, dx_ref, acc_ref):
    step = pl.program_id(0)
    cols = 3 * w0_ref.shape[-1] // 4
    w = rows_of((w0_ref, w1_ref, w2_ref, w3_ref))
    add = nt(step_value((low_ref, high_ref), cols), w[:, :cols])

    accumulate(acc_ref, step, add)

    @pl.when(step == pl.num_programs(0) - 1)
    def _():
        dx = acc_ref[...] + da_ref[...]
        high = dx.astype(bf16)
        rest = dx - high.astype(f32)
        mid = rest.astype(bf16)
        low = (rest - mid.astype(f32)).astype(bf16)
        perm = perm_ref[...]
        dx_ref[...] = nt(high, perm) + nt(mid, perm) + nt(low, perm)


def whole(a):
    nd = len(a.shape)
    return pl.BlockSpec(a.shape, lambda s: (0,) * nd, pipeline_mode=pl.Buffered(1))


def lead(a):
    nd = len(a.shape)
    return pl.BlockSpec((1,) + a.shape[1:], lambda s: (s,) + (0,) * (nd - 1))


def weight(a):
    return pl.BlockSpec((a.shape[0], 1, BLK, a.shape[3]), lambda s: (0, s, 0, 0))


def half_spec(h):
    return pl.BlockSpec((h.shape[0], 1) + h.shape[2:], lambda s: (0, s, 0, 0))


def sds(shape, dtype):
    return jax.ShapeDtypeStruct(shape, dtype)


def far(shape, dtype):
    return pltpu.HBM(shape, dtype)


def call(body, n_t, micros, ins, outs, scratch=()):
    return pl.pallas_call(
        body,
        grid=(n_t,),
        in_specs=[s for _, s in ins],
        out_specs=[s for _, s in outs],
        out_shape=[a for a, _ in outs],
        scratch_shapes=list(scratch),
        compiler_params=pltpu.CompilerParams(
            dimension_semantics=("arbitrary",), vmem_limit_bytes=VMEM_LIMIT
        ),
        cost_estimate=pl.CostEstimate(flops=int(micros * COST), transcendentals=0, bytes_accessed=0),
    )(*[a for a, _ in ins])


def flips(n_dp, n_t):
    size = n_dp * n_t
    core = n_t
    x_bit, y_bit = 2 * core, 4 * core

    def table(bit_of):
        return [(i, i ^ bit_of(i)) for i in range(size)]

    return {
        "Z": [table(lambda i, d=d: d) for d in range(1, n_t)],
        "C": [table(lambda i: core)],
        "2": [table(lambda i: x_bit if i & core else y_bit)],
        "3": [table(lambda i: y_bit if i & core else x_bit)],
    }


def after(value, *done):
    return lax.optimization_barrier((value, *done))[0] if done else value


def swap(value, tables, *done):
    return lax.ppermute(after(value, *done), AXES, tables["C"][0])


class Gather:
    def __init__(self, value, tables):
        self.held, self.tables = [value[None]], tables

    def send(self, name, *done, parts=None):
        sent = self.held if parts is None else [self.held[j] for j in parts]
        return [lax.ppermute(after(h, *done), AXES, t) for t in self.tables[name] for h in sent]

    def take(self, name, got):
        self.held = [jnp.concatenate(self.held + got)] if name in "Z2" else self.held + got
        return got

    def stage(self, name, *done, parts=None):
        return self.take(name, self.send(name, *done, parts=parts))

    def pieces(self, n_t):
        return [h.reshape(h.shape[0] // n_t, n_t, *h.shape[1:]) for h in self.held]


class Scatter:
    def __init__(self, keep, send, tables):
        self.keep, self.send, self.tables = keep, [send], tables

    def stage(self, name, parts, *done):
        got = [lax.ppermute(after(s, *done), AXES, t) for s, t in zip(self.send, self.tables[name], strict=True)]
        size = self.keep.shape[0] // parts

        def share(j):
            cut = slice(j * size, (j + 1) * size)
            return sum((g[cut].astype(f32) for g in got), self.keep[cut].astype(f32))

        self.send = [share(j).astype(bf16) for j in range(1, parts)]
        self.keep = share(0)
        return got


def per_device(
    hidden_in, segment_ids, pooled_grad, qkv_weight, qv_bias, out_weight, out_bias,
    norm1_gain, norm1_shift, up_weight, up_bias, down_weight_in, down_bias, norm2_gain, norm2_shift,
):
    n_dp, n_t = lax.axis_size("dp"), lax.axis_size("tensor")
    at_dp, at_t = lax.axis_index("dp"), lax.axis_index("tensor")
    hc, fc = qkv_weight.shape[2], up_weight.shape[1]
    rows = qkv_weight.shape[1]
    D = rows * n_dp
    micro, tokens = hidden_in.shape[0], hidden_in.shape[1]
    seqs, L = segment_ids.shape[1], segment_ids.shape[2]
    G, T = micro * seqs, micro * tokens
    segs = pooled_grad.shape[2]
    n_i = D // BLK
    pairwise = (n_dp, n_t) == (8, 4) and 4 * hc == fc

    d_parts = [out_bias, norm1_gain, norm1_shift, down_bias, norm2_gain, norm2_shift]
    e_parts = [qv_bias[0], qv_bias[1], up_bias]
    dv = out_bias.shape[0]
    n_vec = sum(p.shape[0] for p in d_parts + e_parts)
    nd = len(d_parts) * dv

    sizes = (6, dv, up_bias.shape[0], D, hc, fc, n_t) if pairwise else (6, D // (n_i * n_t), n_t * fc // (n_i * n_t), D, hc, fc, n_t)
    slot = jnp.arange(n_i * n_t)
    rel = jnp.arange(n_i)
    if pairwise:
        tables = flips(n_dp, n_t)
        packed = (qkv_weight, out_weight, down_weight_in, *[p[None] for p in d_parts], qv_bias, up_bias[None])
        packed, down_t = pl.pallas_call(
            pack, out_shape=[sds((BLK + 8, 4 * hc), bf16), sds((BLK, fc), bf16)]
        )(*packed)
        first, middle, last = Gather(packed, tables), Gather(up_weight, tables), Gather(down_t, tables)
        done = first.stage("Z")

        core = (at_dp & 1) ^ (rel >> 2)
        s3, s2 = (rel >> 1) & 1, rel & 1
        dy, dx = jnp.where(core == 0, s2, s3), jnp.where(core == 0, s3, s2)
        absolute = ((((at_dp >> 2) & 1) ^ dy) << 2) | ((((at_dp >> 1) & 1) ^ dx) << 1) | core
        i_p = jnp.broadcast_to(absolute[:, None], (n_i, n_t)).reshape(-1)
        t_p = jnp.broadcast_to((at_t ^ jnp.arange(n_t))[None], (n_i, n_t)).reshape(-1)
        to_d = jnp.broadcast_to(rel[:, None], (n_i, n_t)).reshape(-1) * n_t + t_p
        to_e = (((i_p * n_t) // n_i) ^ at_t) * n_i + (i_p * n_t + t_p) % n_i
    else:
        absolute, to_d, to_e = rel, slot, slot
    hot_d = (to_d[None, :] == slot[:, None]).astype(bf16)
    hot_e = (to_e[None, :] == slot[:, None]).astype(bf16)
    lane = jnp.arange(D)
    same_block = jnp.repeat(jnp.repeat((absolute[:, None] == rel[None, :]).T, BLK, axis=0), BLK, axis=1)
    perm = (same_block & ((lane[:, None] % BLK) == (lane[None, :] % BLK))).astype(bf16)
    x = nn(hidden_in.reshape(T, D), perm).astype(bf16)
    x_t = lax.dot_general(perm, hidden_in.reshape(T, D), (((0,), (1,)), ((), ())), preferred_element_type=f32).astype(bf16)
    x_keep, x_send = x_t[: D // 2], x_t[D // 2 :]
    pg = jnp.einsum("gsd,de->gse", pooled_grad.reshape(G, segs, D), perm.astype(f32), precision=HI)
    seg_r = segment_ids.reshape(G, L)
    seg_c = segment_ids.reshape(T, 1)

    if pairwise:
        done = first.stage("2", x, x_keep, x_send, pg, hot_d, hot_e) + middle.stage("Z", *done)
        x_other = swap(x_send, tables, *done)
        done = first.stage("3", *done) + middle.stage("2", *done) + last.stage("Z", *done)
        first.stage("C", *done)
        got_u3, got_d2 = middle.send("3", *done), last.send("2", *done)
        w_qo = first.pieces(n_t)
    else:
        heads_in = [qkv_weight[0], qkv_weight[1], qkv_weight[2], out_weight.T]
        main = jnp.concatenate([*heads_in, up_weight, down_weight_in.T], axis=1)
        vec = jnp.concatenate(d_parts + e_parts)
        full = lax.all_gather(lax.all_gather(main, "dp", axis=0, tiled=True), "tensor", axis=0)
        full = full.reshape(n_t, n_i, BLK, -1).transpose(1, 0, 2, 3)
        vecs = lax.all_gather(lax.all_gather(vec, "tensor"), "dp").reshape(n_dp * n_t, -1)
        cuts = [j * dv for j in range(9)] + [n_vec]
        rows8 = jnp.concatenate([vecs[:, a:b].reshape(n_i * n_t, -1) for a, b in zip(cuts[:-1], cuts[1:])], axis=1)
        rows8 = jnp.pad(rows8.reshape(n_i, n_t, 1, -1), ((0, 0), (0, 0), (0, 7), (0, 4 * hc - rows8.shape[1])))
        quarters = [full[j * n_i // 4 : (j + 1) * n_i // 4] for j in range(4)]
        w_qo = [
            jnp.concatenate([w[..., : 4 * hc], rows8[j * n_i // 4 : (j + 1) * n_i // 4]], axis=2)
            for j, w in enumerate(quarters)
        ]
        w_up = [w[..., 4 * hc : 4 * hc + fc] for w in quarters]
        w_down = [w[..., 4 * hc + fc :] for w in quarters]

    hl = hc // HD * L
    o_wide, q_wide = -(-hc // 128) * 128, -(-3 * hc // 128) * 128

    def leads(*arrays):
        return [(a, lead(a)) for a in arrays]

    def wholes(*arrays):
        return [(a, whole(a)) for a in arrays]

    def weights(*arrays):
        return [(a, weight(a)) for a in arrays]

    tails = [
        (w, pl.BlockSpec((w.shape[0], n_t, 8, w.shape[3]), lambda s: (0, 0, BLK // 8, 0), pipeline_mode=pl.Buffered(1)))
        for w in w_qo
    ]
    turned = (D // 2, T)
    qkv, prob, o, n1, x1, r1, n1b, n1_keep, n1_send, vec_d, b_u = call(
        partial(attention_forward, sizes), n_t, 10,
        wholes(x) + weights(*w_qo) + tails + wholes(hot_d, hot_e, seg_c, seg_r),
        leads(far((n_t, T, 3 * hc), bf16), far((n_t, G, L, hl), f32), far((n_t, T, o_wide), bf16))
        + wholes(sds((T, D), f32), far((T, D), f32), far((T, 1), f32), sds((T, D), bf16), far(turned, bf16), far(turned, bf16))
        + wholes(sds((6, D), f32), sds((n_t, 1, fc), f32)),
        [pltpu.VMEM((T, D), f32), pltpu.VMEM((n_t, 1, hc), f32), pltpu.VMEM((n_t, 1, hc), f32)],
    )
    if pairwise:
        last.take("2", [after(g, n1b) for g in got_d2])
        middle.take("3", got_u3)
        last.stage("3", *got_u3)
        middle.stage("C", n1b)
        last.take("C", last.send("C", n1b, parts=(0,)))
        last.take("C", last.send("C", parts=(1,)))
        w_up, w_down = middle.pieces(n_t), last.pieces(n_t)
        n1_other = swap(n1_send, tables)
        o_other = swap(o, tables)
    z, dgelu = call(
        up_forward, n_t, 4, wholes(n1b) + weights(*w_up) + leads(b_u),
        leads(sds((n_t, T, fc), bf16), sds((n_t, T, fc), f32)),
    )
    if pairwise:
        z_other = swap(z, tables)
    pooled, db, dbb, db_keep, db_send, sums2 = call(
        down_forward, n_t, 5.5, leads(z) + weights(*w_down) + wholes(n1, vec_d, seg_c, seg_r, pg),
        wholes(sds((G, segs, D), f32), sds((T, D), f32), sds((T, D), bf16), sds(turned, bf16), sds(turned, bf16), sds((3, D), f32)),
        [pltpu.VMEM((T, D), f32)],
    )

    def gradient(groups, vectors=()):
        ins, kinds = [], []
        for width, *pairs in groups:
            kinds.append((len(pairs), len(pairs[0][1]), width))
            for lhs, values in pairs:
                ins += wholes(lhs) + (leads(*values) if len(values) == 1 else halved(*values))
        out = sds((n_i // 4, n_t, BLK + (8 if vectors else 0), sum(k[2] for k in kinds)), bf16)
        return call(partial(weight_gradient, kinds, len(vectors)), n_t, 4, ins + leads(*vectors), [(out, half_spec(out))] * 2)

    def halved(low, high):
        block = (1,) + low.shape[1:]
        return [
            (low, pl.BlockSpec(block, lambda s: (jnp.minimum(s, n_t // 2 - 1), 0, 0))),
            (high, pl.BlockSpec(block, lambda s: (jnp.maximum(s - n_t // 2, 0), 0, 0))),
        ]

    def flat(a):
        return a.reshape((-1,) + a.shape[2:])

    du, g_bu = call(
        hidden_backward, n_t, 3.5, wholes(dbb) + weights(*w_down) + leads(dgelu),
        leads(sds((n_t, T, fc), bf16), sds((n_t, 1, fc), f32)),
    )
    if pairwise:
        db_other = swap(db_send, tables)
        du_other = swap(du, tables)
        down_keep, down_send = gradient([[fc, (after(db_keep, g_bu), [z]), (db_other, [z_other])]])
        s_down = Scatter(flat(down_keep), flat(down_send), tables)
        got_d3 = s_down.stage("3", 2)
        du_next = after(du, down_keep)
    else:
        du_next = du
    da, dab, da_keep, da_send, sums1 = call(
        norm_backward, n_t, 5, leads(du_next) + weights(*w_up) + wholes(db, x1, r1, vec_d),
        wholes(sds((T, D), f32), sds((T, D), bf16), sds(turned, bf16), sds(turned, bf16), sds((3, D), f32)),
        [pltpu.VMEM((T, D), f32)],
    )
    if pairwise:
        da_other = swap(da_send, tables)
        up_keep, up_send = gradient([[fc, (after(n1_keep, da_keep), [du]), (n1_other, [du_other])]])
        s_up = Scatter(flat(up_keep), flat(up_send), tables)
        got_u3 = s_up.stage("3", 2)
        dab = after(dab, up_keep)
    rows = sds((n_t, n_i // 2, 4 * hc), f32)
    if pairwise:
        dab = after(dab, *got_d3)
    dq_half = sds((n_t // 2, T, q_wide), bf16)
    *dq, v_keep, v_send = call(
        partial(attention_backward, sizes), n_t, 8,
        wholes(dab) + weights(*w_qo) + leads(qkv, prob) + wholes(sums1, sums2, g_bu, hot_d, hot_e),
        halved(dq_half, dq_half) + wholes(rows, rows),
        [pltpu.VMEM((n_t, 1, hc), f32), pltpu.VMEM((n_t, 1, hc), f32), pltpu.VMEM((T, q_wide), bf16)],
    )
    dq_next = dq
    if pairwise:
        dq_other = [swap(d, tables) for d in dq]
        v_other = swap(v_send, tables)
        got_d2 = s_down.stage("2", n_t)
        x_now = after(x_keep, *got_d2, *got_u3)
        qo_keep, qo_send = gradient(
            [[3 * hc, (x_now, dq), (x_other, dq_other)], [hc, (da_keep, [o]), (da_other, [o_other])]], (v_keep, v_other)
        )
        s_qo = Scatter(flat(qo_keep), flat(qo_send), tables)
        got_z = s_down.stage("Z", 1)
        got_u2 = s_up.stage("2", n_t)
        got_q3 = s_qo.stage("3", 2)
        dq_next = [after(d, qo_keep) for d in dq]
    dx = call(
        input_backward, n_t, 4, halved(*dq_next) + weights(*w_qo) + wholes(da, perm), wholes(sds((T, D), f32)),
        [pltpu.VMEM((T, D), f32)],
    )[0]
    pooled = jnp.einsum("gse,de->gsd", pooled, perm.astype(f32), precision=HI)

    if pairwise:
        got = s_up.stage("Z", 1)
        s_qo.stage("2", n_t, dx, *got_z, *got_u2)
        s_qo.stage("Z", 1, *got)
        g_down, g_up, g_qo = s_down.keep[0], s_up.keep[0], s_qo.keep[0]
        g_v = g_qo[BLK, :n_vec]
        g_qo = g_qo[:BLK]
    else:
        def joined(*halves_of):
            g = jnp.concatenate([part[:, :, :BLK] for half in halves_of for part in half])
            return g.transpose(1, 0, 2, 3).reshape(n_t, D, -1)

        x_h, n1_h, db_h, da_h = (x_keep, x_send), (n1_keep, n1_send), (db_keep, db_send), (da_keep, da_send)
        g_full = jnp.concatenate([
            joined(*[gradient([[3 * hc, (x_h[j], dq)], [hc, (da_h[j], [o])]]) for j in range(2)]),
            joined(*[gradient([[fc, (n1_h[j], [du])]]) for j in range(2)]),
            joined(*[gradient([[fc, (db_h[j], [z])]]) for j in range(2)]),
        ], axis=2)
        mine = lax.psum_scatter(g_full, "tensor", scatter_dimension=0)
        mine = lax.psum_scatter(mine, "dp", scatter_dimension=0, tiled=True).astype(f32)
        g_qo, g_up, g_down = mine[:, : 4 * hc], mine[:, 4 * hc : 4 * hc + fc], mine[:, 4 * hc + fc :]
        g_rows = jnp.stack([v_keep, v_send]).transpose(0, 2, 1, 3).reshape(n_i * n_t, -1)
        dv_c, bu_c = sizes[1], sizes[2]
        cuts = [j * dv_c for j in range(9)] + [8 * dv_c + bu_c]
        g_v = jnp.concatenate(
            [g_rows[:, a:b].reshape(n_dp * n_t, -1) for a, b in zip(cuts[:-1], cuts[1:])], axis=1
        )
        g_v = lax.psum_scatter(g_v, AXES, scatter_dimension=0)
    vo = [g_v[j * dv : (j + 1) * dv] for j in range(8)]
    return (
        pooled.reshape(micro, seqs, segs, D),
        dx.reshape(micro, tokens, D),
        jnp.stack([g_qo[:, c * hc : (c + 1) * hc] for c in range(3)]),
        jnp.stack([vo[6], vo[7]]),
        g_qo[:, 3 * hc :].T,
        vo[0], vo[1], vo[2],
        g_up,
        g_v[8 * dv :],
        g_down.T,
        vo[3], vo[4], vo[5],
    )


def solution(mesh):
    both = P(AXES)
    row3 = P(None, AXES)
    return jax.shard_map(
        per_device,
        mesh=mesh,
        in_specs=(
            row3, row3, row3, P(None, "dp", "tensor"), row3, P("tensor", "dp"), both, both, both,
            P("dp", "tensor"), both, P("tensor", "dp"), both, both, both,
        ),
        out_specs=(
            row3, row3, P(None, "dp", "tensor"), row3, P("tensor", "dp"), both, both, both,
            P("dp", "tensor"), both, P("tensor", "dp"), both, both, both,
        ),
        check_vma=False,
    )
```

```python
from functools import partial

import jax
import jax.numpy as jnp
from jax import lax
from jax.experimental import pallas as pl
from jax.experimental.pallas import tpu as pltpu
from jax.sharding import PartitionSpec as P

HD = 64
EPS = 1e-12
NEG = -1000000000.0
SCALE = float(HD) ** -0.5
AXES = ("dp", "tensor")
f32 = jnp.float32
bf16 = jnp.bfloat16
HI = lax.Precision.HIGHEST
BLK = 96
VMEM_LIMIT = 24 * 1024 * 1024
COST = 30_000_000
NORM = 2000


def nn(a, b):
    return lax.dot_general(a, b, (((1,), (0,)), ((), ())), preferred_element_type=f32)


def nt(a, b):
    return lax.dot_general(a, b, (((1,), (1,)), ((), ())), preferred_element_type=f32)


def tn(a, b):
    return lax.dot_general(a, b, (((0,), (0,)), ((), ())), preferred_element_type=f32)


def mean_last(v):
    return jnp.sum(v, axis=-1, keepdims=True) * (1.0 / v.shape[-1])


def normalize(values):
    center = values - mean_last(values)
    inverse = lax.rsqrt(mean_last(center * center) + EPS)
    return center * inverse, inverse


def normalize_back(scaled, normed, inverse):
    return inverse * (scaled - mean_last(scaled) - normed * mean_last(scaled * normed))


def col_sum(v):
    return jnp.sum(v, axis=0, keepdims=True)


def pack(qkv_ref, out_ref, ob_ref, g1_ref, s1_ref, db_ref, g2_ref, s2_ref, qv_ref, ub_ref, first_ref):
    rows, hc = qkv_ref.shape[1:]
    eye = (lax.broadcasted_iota(jnp.int32, (rows, rows), 0) == lax.broadcasted_iota(jnp.int32, (rows, rows), 1)).astype(bf16)
    for c in range(3):
        first_ref[:rows, c * hc : (c + 1) * hc] = qkv_ref[c]
    first_ref[:rows, 3 * hc :] = nt(eye, out_ref[...]).astype(bf16)
    parts = [r[...].astype(f32) for r in (ob_ref, g1_ref, s1_ref, db_ref, g2_ref, s2_ref, qv_ref)]
    short = jnp.concatenate(parts, axis=0).astype(bf16)
    count, size = short.shape
    wide = first_ref.shape[1]

    def spread(values, at):
        lane = lax.broadcasted_iota(jnp.int32, (values.shape[1], wide), 1) - at
        return nn(values, (lax.rem(lane + values.shape[1] * wide, values.shape[1]) == lax.broadcasted_iota(jnp.int32, lane.shape, 0)).astype(bf16))

    lane = lax.broadcasted_iota(jnp.int32, (count, wide), 1)
    start = lax.broadcasted_iota(jnp.int32, (count, wide), 0) * size
    row = col_sum(jnp.where((lane >= start) & (lane < start + size), spread(short, 0), 0.0))
    total, long = count * size, ub_ref.shape[1]
    lane = lax.broadcasted_iota(jnp.int32, (1, wide), 1)
    row = jnp.where((lane >= total) & (lane < total + long), spread(ub_ref[...], total), row)
    extra = first_ref.shape[0] - rows
    here = lax.broadcasted_iota(jnp.int32, (extra, wide), 0)
    first_ref[rows:, :] = jnp.where(here == 0, row, 0.0).astype(bf16)


def stacked(values, hc):
    head = lax.broadcasted_iota(jnp.int32, (1, hc), 1) // HD
    return jnp.concatenate([values * (head == h).astype(f32).astype(bf16) for h in range(hc // HD)], axis=0)


def own_columns(blocks, hc):
    n_heads = hc // HD
    length = blocks.shape[0] // n_heads
    head = lax.broadcasted_iota(jnp.int32, (1, hc), 1) // HD
    out = blocks[:length]
    for h in range(1, n_heads):
        out = jnp.where(head == h, blocks[h * length : (h + 1) * length], out)
    return out


def sections(values, length):
    return [values[:, c : c + length] for c in range(0, values.shape[1], length)]


def rows_of(refs):
    return jnp.concatenate([r[...].reshape(-1, r.shape[3]) for r in refs], axis=0)


def accumulate(acc_ref, step, add):
    @pl.when(step == 0)
    def _():
        acc_ref[...] = add

    @pl.when(step > 0)
    def _():
        acc_ref[...] += add


def iota(shape, axis):
    return lax.broadcasted_iota(jnp.int32, shape, axis)


def picks(count, first, wide, size):
    return (iota((count, wide), 0) == first + lax.rem(iota((1, wide), 1), size)).astype(bf16)


def belongs(count, wide, size, period):
    lane, row = iota((1, wide), 1), lax.rem(iota((count, 1), 0), period)
    return (lane >= row * size) & (lane < (row + 1) * size)


def read_vectors(rows, hot_d, hot_e, sizes):
    n_d, dv, bu, width, hc, fc, n_t = sizes
    count = rows.shape[0]
    per = count // n_t
    d_all = nn(hot_d, rows[:, : n_d * dv]).astype(bf16)
    mine = belongs(count, width, dv, count)
    d_rows = [col_sum(jnp.where(mine, nn(d_all, picks(n_d * dv, j * dv, width, dv)), 0.0)) for j in range(n_d)]
    e_all = nn(hot_e, rows[:, n_d * dv : n_d * dv + 2 * dv + bu]).astype(bf16)
    out = []
    for first, size, wide in ((0, dv, hc), (dv, dv, hc), (2 * dv, bu, fc)):
        spread = jnp.where(belongs(count, wide, size, per), nn(e_all, picks(e_all.shape[1], first, wide, size)), 0.0)
        out.append(jnp.sum(spread.reshape(n_t, per, wide), axis=1, keepdims=True))
    return jnp.concatenate(d_rows, axis=0), out


def write_vectors(d_rows, e_rows, hot_d, hot_e, sizes):
    n_d, dv, bu, width, hc, fc, n_t = sizes
    count = hot_d.shape[0]
    per = count // n_t
    mine = belongs(count, width, dv, count)
    d_all = sum(
        nt(jnp.where(mine, d_rows[j : j + 1, :], 0.0).astype(bf16), picks(n_d * dv, j * dv, width, dv)) for j in range(n_d)
    ).astype(bf16)
    e_all = 0.0
    for value, first, size, wide in zip(e_rows, (0, dv, 2 * dv), (dv, dv, bu), (hc, hc, fc), strict=True):
        spread = jnp.broadcast_to(value, (n_t, per, wide)).reshape(count, wide)
        spread = jnp.where(belongs(count, wide, size, per), spread, 0.0).astype(bf16)
        e_all = e_all + nt(spread, picks(2 * dv + bu, first, wide, size))
    return jnp.concatenate([tn(hot_d, d_all), tn(hot_e, e_all.astype(bf16))], axis=1)


def attention_forward(sizes, x_ref, w0_ref, w1_ref, w2_ref, w3_ref, v0_ref, v1_ref, v2_ref, v3_ref, hd_ref, he_ref,
                      segc_ref, segr_ref, qkv_ref, p_ref, o_ref, n1_ref, x1_ref, r1_ref, n1b_ref, n1t_ref, n1s_ref,
                      vec_ref, bu_ref, acc_ref, bq_ref, bv_ref):
    step = pl.program_id(0)
    hc = bq_ref.shape[-1]

    @pl.when(step == 0)
    def _():
        rows = jnp.concatenate([r[:, :, 0, :].reshape(-1, r.shape[3]) for r in (v0_ref, v1_ref, v2_ref, v3_ref)], axis=0)
        d_rows, (b_q, b_v, b_u) = read_vectors(rows, hd_ref[...], he_ref[...], sizes)
        vec_ref[...] = d_rows
        bq_ref[...] = b_q
        bv_ref[...] = b_v
        bu_ref[...] = b_u

    rows, length = segr_ref.shape
    x = x_ref[...]
    w = rows_of((w0_ref, w1_ref, w2_ref, w3_ref))
    qkv = nn(x, w[:, : 3 * hc])
    q = (qkv[:, :hc] + bq_ref[step]).astype(bf16) * bf16(SCALE)
    k = qkv[:, hc : 2 * hc].astype(bf16)
    v = (qkv[:, 2 * hc :] + bv_ref[step]).astype(bf16)
    qkv_ref[0, :, :hc] = q
    qkv_ref[0, :, hc : 2 * hc] = k
    qkv_ref[0, :, 2 * hc :] = v
    spans = [slice(g * length, (g + 1) * length) for g in range(rows)]
    scores = [nt(q[span], stacked(k[span], hc)) for span in spans]
    probs = []
    for g, span in enumerate(spans):
        same = segc_ref[span, :] == segr_ref[g : g + 1, :]
        parts = []
        for s in sections(scores[g], length):
            s = jnp.where(same, s, NEG)
            e = jnp.exp(s - jnp.max(s, axis=-1, keepdims=True))
            parts.append(e * (1.0 / jnp.sum(e, axis=-1, keepdims=True)))
        probs.append(jnp.concatenate(parts, axis=1))
    for g, span in enumerate(spans):
        p_ref[0, g] = probs[g]
        o_ref[0, span, :hc] = nn(probs[g].astype(bf16), stacked(v[span], hc)).astype(bf16)
    o_ref[0, :, hc:] = jnp.zeros((o_ref.shape[1], o_ref.shape[2] - hc), bf16)
    add = nt(o_ref[0, :, :hc], w[:, 3 * hc :])

    accumulate(acc_ref, step, add)

    @pl.when(step == pl.num_programs(0) - 1)
    def _():
        a = acc_ref[...] + vec_ref[0:1, :] + x_ref[...].astype(f32)
        normed, inverse = normalize(a)
        n1 = normed * vec_ref[1:2, :] + vec_ref[2:3, :]
        n1_ref[...] = n1
        x1_ref[...] = normed
        r1_ref[...] = inverse
        low = n1.astype(bf16)
        n1b_ref[...] = low
        turned = low.T
        n1t_ref[...] = turned[: low.shape[1] // 2]
        n1s_ref[...] = turned[low.shape[1] // 2 :]


def up_forward(n_ref, w0_ref, w1_ref, w2_ref, w3_ref, b_ref, z_ref, d_ref):
    u = nn(n_ref[...], rows_of((w0_ref, w1_ref, w2_ref, w3_ref))) + b_ref[0]
    phi = 0.5 + 0.5 * lax.erf(u * (0.5**0.5))
    z_ref[0] = (u * phi).astype(bf16)
    d_ref[0] = phi + u * (jnp.exp(-0.5 * u * u) * 0.3989422804014327)


def down_forward(z_ref, w0_ref, w1_ref, w2_ref, w3_ref, n1_ref, vec_ref, segc_ref, segr_ref, pg_ref,
                 pooled_ref, db_ref, dbb_ref, dbt_ref, dbs_ref, sums_ref, acc_ref):
    step = pl.program_id(0)
    add = nt(z_ref[0], rows_of((w0_ref, w1_ref, w2_ref, w3_ref)))

    accumulate(acc_ref, step, add)

    @pl.when(step == pl.num_programs(0) - 1)
    def _():
        rows, length = segr_ref.shape
        segs = pg_ref.shape[1]
        b = acc_ref[...] + vec_ref[3:4, :] + n1_ref[...]
        x2, r2 = normalize(b)
        y = x2 * vec_ref[4:5, :] + vec_ref[5:6, :]
        grads = []
        for g in range(rows):
            span = slice(g * length, (g + 1) * length)
            ids = lax.broadcasted_iota(jnp.int32, (segs, length), 0)
            hot_t = (ids == segr_ref[g : g + 1, :]).astype(f32)
            idc = lax.broadcasted_iota(jnp.int32, (length, segs), 1)
            hot = (idc == segc_ref[span, :]).astype(f32)
            count = jnp.sum(hot_t, axis=1, keepdims=True)
            sums = lax.dot_general(hot_t, y[span, :], (((1,), (0,)), ((), ())),
                                   precision=HI, preferred_element_type=f32)
            pooled_ref[g] = sums / count
            grads.append(lax.dot_general(hot, pg_ref[g] / count, (((1,), (0,)), ((), ())),
                                         precision=HI, preferred_element_type=f32))
        dy = jnp.concatenate(grads, axis=0)
        db = normalize_back(dy * vec_ref[4:5, :], x2, r2)
        db_ref[...] = db
        low = db.astype(bf16)
        dbb_ref[...] = low
        turned = low.T
        dbt_ref[...] = turned[: low.shape[1] // 2]
        dbs_ref[...] = turned[low.shape[1] // 2 :]
        sums_ref[0:1, :] = col_sum(db)
        sums_ref[1:2, :] = col_sum(dy * x2)
        sums_ref[2:3, :] = col_sum(dy)


def put(grad, ref):
    ref[:, :, :BLK, :] = grad.astype(bf16).reshape(grad.shape[0] // BLK, 1, BLK, grad.shape[1])


def hidden_backward(dbb_ref, w0_ref, w1_ref, w2_ref, w3_ref, d_ref, du_ref, bu_ref):
    du = (nn(dbb_ref[...], rows_of((w0_ref, w1_ref, w2_ref, w3_ref))) * d_ref[0]).astype(bf16)
    du_ref[0] = du
    bu_ref[0] = col_sum(du.astype(f32))


def step_value(refs, width):
    if len(refs) == 1:
        return refs[0][0, :, :width]
    return jnp.where(pl.program_id(0) < pl.num_programs(0) // 2, refs[0][0, :, :width], refs[1][0, :, :width])


def weight_gradient(groups, vectors, *refs):
    refs = list(refs)
    parts = []
    for pairs, split, width in groups:
        total = None
        for _ in range(pairs):
            add = nn(refs.pop(0)[...], step_value([refs.pop(0) for _ in range(split)], width))
            total = add if total is None else total + add
        parts.append(total)
    grad = jnp.concatenate(parts, axis=1)
    extra = sum(refs.pop(0)[0].astype(f32) for _ in range(vectors)) if vectors else None
    half = grad.shape[0] // 2
    for n, ref in enumerate(refs):
        put(grad[n * half : (n + 1) * half], ref)
        if vectors:
            for j in range(ref.shape[0]):
                row = extra[n * ref.shape[0] + j : n * ref.shape[0] + j + 1]
                tail = ref.shape[2] - BLK
                ref[j, 0, BLK:, :] = jnp.where(iota((tail, row.shape[1]), 0) == 0, row, 0.0).astype(bf16)


def norm_backward(du_ref, w0_ref, w1_ref, w2_ref, w3_ref, db_ref, x1_ref, r1_ref, vec_ref,
                  da_ref, dab_ref, dat_ref, das_ref, sums_ref, acc_ref):
    step = pl.program_id(0)
    accumulate(acc_ref, step, nt(du_ref[0], rows_of((w0_ref, w1_ref, w2_ref, w3_ref))))

    @pl.when(step == pl.num_programs(0) - 1)
    def _():
        dn1 = acc_ref[...].astype(bf16).astype(f32) + db_ref[...]
        da = normalize_back(dn1 * vec_ref[1:2, :], x1_ref[...], r1_ref[...])
        da_ref[...] = da
        low = da.astype(bf16)
        dab_ref[...] = low
        turned = low.T
        dat_ref[...] = turned[: low.shape[1] // 2]
        das_ref[...] = turned[low.shape[1] // 2 :]
        sums_ref[0:1, :] = col_sum(da)
        sums_ref[1:2, :] = col_sum(dn1 * x1_ref[...])
        sums_ref[2:3, :] = col_sum(dn1)


def attention_backward(sizes, dab_ref, w0_ref, w1_ref, w2_ref, w3_ref, qkv_ref, p_ref, s1_ref, s2_ref, gu_ref, hd_ref, he_ref,
                       low_ref, high_ref, keep_ref, send_ref, bq_ref, bv_ref, dqkv_ref):
    step = pl.program_id(0)
    hc = bq_ref.shape[-1]
    dab = dab_ref[...]
    w = rows_of([r.at[:, :, :, 3 * hc :] for r in (w0_ref, w1_ref, w2_ref, w3_ref)])
    do = nn(dab, w).astype(bf16)
    qkv = qkv_ref[0]
    rows, length = p_ref.shape[1], p_ref.shape[2]
    spans = [slice(g * length, (g + 1) * length) for g in range(rows)]
    q = [qkv[span, :hc] for span in spans]
    k = [stacked(qkv[span, hc : 2 * hc], hc) for span in spans]
    dps = [nt(do[span], stacked(qkv[span, 2 * hc :], hc)) for span in spans]
    dss = []
    for g in range(rows):
        parts = []
        for p, dp in zip(sections(p_ref[0, g], length), sections(dps[g], length)):
            pd = p * dp
            parts.append((pd - p * jnp.sum(pd, axis=-1, keepdims=True)).astype(bf16))
        dss.append(jnp.concatenate(parts, axis=1))
    for g, span in enumerate(spans):
        dqkv_ref[span, :hc] = (nn(dss[g], k[g]) * SCALE).astype(bf16)
        dqkv_ref[span, hc : 2 * hc] = own_columns(tn(dss[g], q[g]), hc).astype(bf16)
        dqkv_ref[span, 2 * hc : 3 * hc] = own_columns(tn(p_ref[0, g].astype(bf16), do[span]), hc).astype(bf16)
    dqkv_ref[:, 3 * hc :] = jnp.zeros((dqkv_ref.shape[0], dqkv_ref.shape[1] - 3 * hc), bf16)
    dqkv = dqkv_ref[...]
    half_steps = pl.num_programs(0) // 2

    @pl.when(step < half_steps)
    def _():
        low_ref[0] = dqkv

    @pl.when(step >= half_steps)
    def _():
        high_ref[0] = dqkv

    bq_ref[step] = col_sum(dqkv[:, :hc].astype(f32))
    bv_ref[step] = col_sum(dqkv[:, 2 * hc : 3 * hc].astype(f32))

    @pl.when(step == pl.num_programs(0) - 1)
    def _():
        d_rows = jnp.concatenate([s1_ref[...], s2_ref[...]], axis=0)
        rows = write_vectors(d_rows, (bq_ref[...], bv_ref[...], gu_ref[...]), hd_ref[...], he_ref[...], sizes)
        half, n_t = rows.shape[0] // 2, bq_ref.shape[0]
        rows = jnp.concatenate([rows, jnp.zeros((rows.shape[0], keep_ref.shape[-1] - rows.shape[1]), f32)], axis=1)
        for n, ref in enumerate((keep_ref, send_ref)):
            for t in range(n_t):
                for j in range(half // n_t):
                    at = n * half + j * n_t + t
                    ref[t, j : j + 1, :] = rows[at : at + 1]


def input_backward(low_ref, high_ref, w0_ref, w1_ref, w2_ref, w3_ref, da_ref, perm_ref, dx_ref, acc_ref):
    step = pl.program_id(0)
    cols = 3 * w0_ref.shape[-1] // 4
    w = rows_of((w0_ref, w1_ref, w2_ref, w3_ref))
    add = nt(step_value((low_ref, high_ref), cols), w[:, :cols])

    accumulate(acc_ref, step, add)

    @pl.when(step == pl.num_programs(0) - 1)
    def _():
        dx = acc_ref[...] + da_ref[...]
        high = dx.astype(bf16)
        rest = dx - high.astype(f32)
        mid = rest.astype(bf16)
        low = (rest - mid.astype(f32)).astype(bf16)
        perm = perm_ref[...]
        dx_ref[...] = nt(high, perm) + nt(mid, perm) + nt(low, perm)


def whole(a):
    nd = len(a.shape)
    return pl.BlockSpec(a.shape, lambda s: (0,) * nd, pipeline_mode=pl.Buffered(1))


def lead(a):
    nd = len(a.shape)
    return pl.BlockSpec((1,) + a.shape[1:], lambda s: (s,) + (0,) * (nd - 1))


def weight(a):
    return pl.BlockSpec((a.shape[0], 1, BLK, a.shape[3]), lambda s: (0, s, 0, 0))


def weight_t(a):
    return pl.BlockSpec((1, a.shape[1], BLK, a.shape[3]), lambda s: (s, 0, 0, 0))


def half_spec(h):
    return pl.BlockSpec((h.shape[0], 1) + h.shape[2:], lambda s: (0, s, 0, 0))


def sds(shape, dtype):
    return jax.ShapeDtypeStruct(shape, dtype)


def far(shape, dtype):
    return pltpu.HBM(shape, dtype)


def call(body, n_t, micros, ins, outs, scratch=()):
    return pl.pallas_call(
        body,
        grid=(n_t,),
        in_specs=[s for _, s in ins],
        out_specs=[s for _, s in outs],
        out_shape=[a for a, _ in outs],
        scratch_shapes=list(scratch),
        compiler_params=pltpu.CompilerParams(
            dimension_semantics=("arbitrary",), vmem_limit_bytes=VMEM_LIMIT
        ),
        cost_estimate=pl.CostEstimate(flops=int(micros * COST), transcendentals=0, bytes_accessed=0),
    )(*[a for a, _ in ins])


def flips(n_dp, n_t):
    size = n_dp * n_t
    core = n_t
    x_bit, y_bit = 2 * core, 4 * core

    def table(bit_of):
        return [(i, i ^ bit_of(i)) for i in range(size)]

    return {
        "Z": [table(lambda i, d=d: d) for d in range(1, n_t)],
        "C": [table(lambda i: core)],
        "2": [table(lambda i: x_bit if i & core else y_bit)],
        "3": [table(lambda i: y_bit if i & core else x_bit)],
    }


def after(value, *done):
    return lax.optimization_barrier((value, *done))[0] if done else value


def swap(value, tables, *done):
    return lax.ppermute(after(value, *done), AXES, tables["C"][0])


class Gather:
    def __init__(self, value, tables):
        self.held, self.tables = [value[None]], tables

    def send(self, name, *done, parts=None, tables=None):
        sent = self.held if parts is None else [self.held[j] for j in parts]
        return [lax.ppermute(after(h, *done), AXES, t) for t in self.tables[name][tables or slice(None)] for h in sent]

    def take(self, name, got):
        self.held = [jnp.concatenate(self.held + got)] if name in "Z2" else self.held + got
        return got

    def stage(self, name, *done, parts=None):
        return self.take(name, self.send(name, *done, parts=parts))

    def pieces(self, *lead):
        return [h.reshape(*lead, *h.shape[1:]) for h in self.held]


class Scatter:
    def __init__(self, keep, send, tables):
        self.keep, self.send, self.tables = keep, [send], tables

    def stage(self, name, parts, *done):
        got = [lax.ppermute(after(s, *done), AXES, t) for s, t in zip(self.send, self.tables[name], strict=True)]
        size = self.keep.shape[0] // parts

        def share(j):
            cut = slice(j * size, (j + 1) * size)
            return sum((g[cut].astype(f32) for g in got), self.keep[cut].astype(f32))

        self.send = [share(j).astype(bf16) for j in range(1, parts)]
        self.keep = share(0)
        return got


def per_device(
    hidden_in, segment_ids, pooled_grad, qkv_weight, qv_bias, out_weight, out_bias,
    norm1_gain, norm1_shift, up_weight, up_bias, down_weight_in, down_bias, norm2_gain, norm2_shift,
):
    n_dp, n_t = lax.axis_size("dp"), lax.axis_size("tensor")
    at_dp, at_t = lax.axis_index("dp"), lax.axis_index("tensor")
    hc, fc = qkv_weight.shape[2], up_weight.shape[1]
    rows = qkv_weight.shape[1]
    D = rows * n_dp
    micro, tokens = hidden_in.shape[0], hidden_in.shape[1]
    seqs, L = segment_ids.shape[1], segment_ids.shape[2]
    G, T = micro * seqs, micro * tokens
    segs = pooled_grad.shape[2]
    n_i = D // BLK
    pairwise = (n_dp, n_t) == (8, 4) and 4 * hc == fc

    d_parts = [out_bias, norm1_gain, norm1_shift, down_bias, norm2_gain, norm2_shift]
    e_parts = [qv_bias[0], qv_bias[1], up_bias]
    dv = out_bias.shape[0]
    n_vec = sum(p.shape[0] for p in d_parts + e_parts)
    nd = len(d_parts) * dv

    sizes = (6, dv, up_bias.shape[0], D, hc, fc, n_t) if pairwise else (6, D // (n_i * n_t), n_t * fc // (n_i * n_t), D, hc, fc, n_t)
    slot = jnp.arange(n_i * n_t)
    rel = jnp.arange(n_i)
    if pairwise:
        tables = flips(n_dp, n_t)
        packed = (qkv_weight, out_weight, *[p[None] for p in d_parts], qv_bias, up_bias[None])
        packed = pl.pallas_call(pack, out_shape=sds((BLK + 8, 4 * hc), bf16))(*packed)
        first, middle, last = Gather(packed, tables), Gather(up_weight, tables), Gather(down_weight_in.T, tables)
        done = first.stage("Z") + last.stage("2")

        core = (at_dp & 1) ^ (rel >> 2)
        s3, s2 = (rel >> 1) & 1, rel & 1
        dy, dx = jnp.where(core == 0, s2, s3), jnp.where(core == 0, s3, s2)
        absolute = ((((at_dp >> 2) & 1) ^ dy) << 2) | ((((at_dp >> 1) & 1) ^ dx) << 1) | core
        i_p = jnp.broadcast_to(absolute[:, None], (n_i, n_t)).reshape(-1)
        t_p = jnp.broadcast_to((at_t ^ jnp.arange(n_t))[None], (n_i, n_t)).reshape(-1)
        to_d = jnp.broadcast_to(rel[:, None], (n_i, n_t)).reshape(-1) * n_t + t_p
        to_e = (((i_p * n_t) // n_i) ^ at_t) * n_i + (i_p * n_t + t_p) % n_i
    else:
        absolute, to_d, to_e = rel, slot, slot
    hot_d = (to_d[None, :] == slot[:, None]).astype(bf16)
    hot_e = (to_e[None, :] == slot[:, None]).astype(bf16)
    lane = jnp.arange(D)
    same_block = jnp.repeat(jnp.repeat((absolute[:, None] == rel[None, :]).T, BLK, axis=0), BLK, axis=1)
    perm = (same_block & ((lane[:, None] % BLK) == (lane[None, :] % BLK))).astype(bf16)
    x = nn(hidden_in.reshape(T, D), perm).astype(bf16)
    x_t = lax.dot_general(perm, hidden_in.reshape(T, D), (((0,), (1,)), ((), ())), preferred_element_type=f32).astype(bf16)
    x_keep, x_send = x_t[: D // 2], x_t[D // 2 :]
    pg = jnp.einsum("gsd,de->gse", pooled_grad.reshape(G, segs, D), perm.astype(f32), precision=HI)
    seg_r = segment_ids.reshape(G, L)
    seg_c = segment_ids.reshape(T, 1)

    if pairwise:
        done = first.stage("2", *done, x, x_keep, x_send, pg, hot_d, hot_e) + middle.stage("Z", *done)
        x_other = swap(x_send, tables, *done)
        near_z = last.send("Z", *done, tables=slice(0, 2))
        done = first.stage("3", *done) + middle.stage("2", *done) + near_z
        first.stage("C", *done)
        got_u3, far_z = middle.send("3", *done), last.send("Z", *done, tables=slice(2, None))
        w_qo = first.pieces(2, n_t)
    else:
        heads_in = [qkv_weight[0], qkv_weight[1], qkv_weight[2], out_weight.T]
        main = jnp.concatenate([*heads_in, up_weight, down_weight_in.T], axis=1)
        vec = jnp.concatenate(d_parts + e_parts)
        full = lax.all_gather(lax.all_gather(main, "dp", axis=0, tiled=True), "tensor", axis=0)
        full = full.reshape(n_t, n_i, BLK, -1).transpose(1, 0, 2, 3)
        vecs = lax.all_gather(lax.all_gather(vec, "tensor"), "dp").reshape(n_dp * n_t, -1)
        cuts = [j * dv for j in range(9)] + [n_vec]
        rows8 = jnp.concatenate([vecs[:, a:b].reshape(n_i * n_t, -1) for a, b in zip(cuts[:-1], cuts[1:])], axis=1)
        rows8 = jnp.pad(rows8.reshape(n_i, n_t, 1, -1), ((0, 0), (0, 0), (0, 7), (0, 4 * hc - rows8.shape[1])))
        quarters = [full[j * n_i // 4 : (j + 1) * n_i // 4] for j in range(4)]
        w_qo = [
            jnp.concatenate([w[..., : 4 * hc], rows8[j * n_i // 4 : (j + 1) * n_i // 4]], axis=2)
            for j, w in enumerate(quarters)
        ]
        w_up = [w[..., 4 * hc : 4 * hc + fc] for w in quarters]
        w_down = [w[..., 4 * hc + fc :].transpose(1, 0, 2, 3) for w in quarters]

    hl = hc // HD * L
    o_wide, q_wide = -(-hc // 128) * 128, -(-3 * hc // 128) * 128

    def leads(*arrays):
        return [(a, lead(a)) for a in arrays]

    def wholes(*arrays):
        return [(a, whole(a)) for a in arrays]

    def weights(*arrays):
        return [(a, weight(a)) for a in arrays]

    def weights_t(*arrays):
        return [(a, weight_t(a)) for a in arrays]

    tails = [
        (w, pl.BlockSpec((w.shape[0], n_t, 8, w.shape[3]), lambda s: (0, 0, BLK // 8, 0), pipeline_mode=pl.Buffered(1)))
        for w in w_qo
    ]
    turned = (D // 2, T)
    qkv, prob, o, n1, x1, r1, n1b, n1_keep, n1_send, vec_d, b_u = call(
        partial(attention_forward, sizes), n_t, 10,
        wholes(x) + weights(*w_qo) + tails + wholes(hot_d, hot_e, seg_c, seg_r),
        leads(far((n_t, T, 3 * hc), bf16), far((n_t, G, L, hl), f32), far((n_t, T, o_wide), bf16))
        + wholes(sds((T, D), f32), far((T, D), f32), far((T, 1), f32), sds((T, D), bf16), far(turned, bf16), far(turned, bf16))
        + wholes(sds((6, D), f32), sds((n_t, 1, fc), f32)),
        [pltpu.VMEM((T, D), f32), pltpu.VMEM((n_t, 1, hc), f32), pltpu.VMEM((n_t, 1, hc), f32)],
    )
    if pairwise:
        last.take("Z", near_z + [after(g, n1b) for g in far_z])
        middle.take("3", [after(g, n1b) for g in got_u3])
        last.stage("3", *got_u3)
        middle.stage("C", n1b, *far_z)
        last.take("C", last.send("C", n1b, parts=(0,)))
        last.take("C", last.send("C", parts=(1,)))
        w_up, w_down = middle.pieces(2, n_t), last.pieces(n_t, 2)
        n1_other = swap(n1_send, tables)
        o_other = swap(o, tables)
        pg = after(pg, x_other, n1_other, o_other)
    z, dgelu = call(
        up_forward, n_t, 4, wholes(n1b) + weights(*w_up) + leads(b_u),
        leads(sds((n_t, T, fc), bf16), sds((n_t, T, fc), f32)),
    )
    if pairwise:
        z_other = swap(z, tables)
    pooled, db, dbb, db_keep, db_send, sums2 = call(
        down_forward, n_t, 5.5, leads(z) + weights_t(*w_down) + wholes(n1, vec_d, seg_c, seg_r, pg),
        wholes(sds((G, segs, D), f32), sds((T, D), f32), sds((T, D), bf16), sds(turned, bf16), sds(turned, bf16), sds((3, D), f32)),
        [pltpu.VMEM((T, D), f32)],
    )

    def gradient(groups, vectors=()):
        ins, kinds = [], []
        for width, *pairs in groups:
            kinds.append((len(pairs), len(pairs[0][1]), width))
            for lhs, values in pairs:
                ins += wholes(lhs) + (leads(*values) if len(values) == 1 else halved(*values))
        out = sds((n_i // 4, n_t, BLK + (8 if vectors else 0), sum(k[2] for k in kinds)), bf16)
        return call(partial(weight_gradient, kinds, len(vectors)), n_t, 4, ins + leads(*vectors), [(out, half_spec(out))] * 2)

    def halved(low, high):
        block = (1,) + low.shape[1:]
        return [
            (low, pl.BlockSpec(block, lambda s: (jnp.minimum(s, n_t // 2 - 1), 0, 0))),
            (high, pl.BlockSpec(block, lambda s: (jnp.maximum(s - n_t // 2, 0), 0, 0))),
        ]

    def flat(a):
        return a.reshape((-1,) + a.shape[2:])

    du, g_bu = call(
        hidden_backward, n_t, 3.5, wholes(dbb) + weights_t(*w_down) + leads(dgelu),
        leads(sds((n_t, T, fc), bf16), sds((n_t, 1, fc), f32)),
    )
    if pairwise:
        db_other = swap(db_send, tables)
        du_other = swap(du, tables)
        down_keep, down_send = gradient([[fc, (after(db_keep, g_bu), [z]), (db_other, [z_other])]])
        s_down = Scatter(flat(down_keep), flat(down_send), tables)
        got_d3 = s_down.stage("3", 2)
        du_next = after(du, down_keep)
    else:
        du_next = du
    da, dab, da_keep, da_send, sums1 = call(
        norm_backward, n_t, NORM, leads(du_next) + weights(*w_up) + wholes(db, x1, r1, vec_d),
        wholes(sds((T, D), f32), sds((T, D), bf16), sds(turned, bf16), sds(turned, bf16), sds((3, D), f32)),
        [pltpu.VMEM((T, D), f32)],
    )
    if pairwise:
        da_other = swap(da_send, tables)
        up_keep, up_send = gradient([[fc, (after(n1_keep, da_keep), [du]), (n1_other, [du_other])]])
        s_up = Scatter(flat(up_keep), flat(up_send), tables)
        got_u3 = s_up.stage("3", 2)
        dab = after(dab, up_keep)
    rows = sds((n_t, n_i // 2, 4 * hc), f32)
    if pairwise:
        dab = after(dab, da_other, *got_d3)
    dq_half = sds((n_t // 2, T, q_wide), bf16)
    *dq, v_keep, v_send = call(
        partial(attention_backward, sizes), n_t, 8,
        wholes(dab) + weights(*w_qo) + leads(qkv, prob) + wholes(sums1, sums2, g_bu, hot_d, hot_e),
        halved(dq_half, dq_half) + wholes(rows, rows),
        [pltpu.VMEM((n_t, 1, hc), f32), pltpu.VMEM((n_t, 1, hc), f32), pltpu.VMEM((T, q_wide), bf16)],
    )
    if pairwise:
        dq_other = [swap(d, tables) for d in dq]
        v_other = swap(v_send, tables)
        got_d2 = s_down.stage("2", n_t)
    dx = call(
        input_backward, n_t, 4, halved(*dq) + weights(*w_qo) + wholes(da, perm), wholes(sds((T, D), f32)),
        [pltpu.VMEM((T, D), f32)],
    )[0]
    if pairwise:
        x_now = after(x_keep, dx, *got_d2, *got_u3)
        qo_keep, qo_send = gradient(
            [[3 * hc, (x_now, dq), (x_other, dq_other)], [hc, (da_keep, [o]), (da_other, [o_other])]], (v_keep, v_other)
        )
        s_qo = Scatter(flat(qo_keep), flat(qo_send), tables)
        got_z = s_down.stage("Z", 1)
        got_u2 = s_up.stage("2", n_t)
        got_q3 = s_qo.stage("3", 2)
    pooled = jnp.einsum("gse,de->gsd", pooled, perm.astype(f32), precision=HI)

    if pairwise:
        got = s_up.stage("Z", 1)
        s_qo.stage("2", n_t, *got_z, *got_u2, pooled, s_down.keep, got[0])
        s_qo.stage("Z", 1, *got)
        g_down, g_up, g_qo = s_down.keep[0], s_up.keep[0], s_qo.keep[0]
        g_v = g_qo[BLK, :n_vec]
        g_qo = g_qo[:BLK]
    else:
        def joined(*halves_of):
            g = jnp.concatenate([part[:, :, :BLK] for half in halves_of for part in half])
            return g.transpose(1, 0, 2, 3).reshape(n_t, D, -1)

        x_h, n1_h, db_h, da_h = (x_keep, x_send), (n1_keep, n1_send), (db_keep, db_send), (da_keep, da_send)
        g_full = jnp.concatenate([
            joined(*[gradient([[3 * hc, (x_h[j], dq)], [hc, (da_h[j], [o])]]) for j in range(2)]),
            joined(*[gradient([[fc, (n1_h[j], [du])]]) for j in range(2)]),
            joined(*[gradient([[fc, (db_h[j], [z])]]) for j in range(2)]),
        ], axis=2)
        mine = lax.psum_scatter(g_full, "tensor", scatter_dimension=0)
        mine = lax.psum_scatter(mine, "dp", scatter_dimension=0, tiled=True).astype(f32)
        g_qo, g_up, g_down = mine[:, : 4 * hc], mine[:, 4 * hc : 4 * hc + fc], mine[:, 4 * hc + fc :]
        g_rows = jnp.stack([v_keep, v_send]).transpose(0, 2, 1, 3).reshape(n_i * n_t, -1)
        dv_c, bu_c = sizes[1], sizes[2]
        cuts = [j * dv_c for j in range(9)] + [8 * dv_c + bu_c]
        g_v = jnp.concatenate(
            [g_rows[:, a:b].reshape(n_dp * n_t, -1) for a, b in zip(cuts[:-1], cuts[1:])], axis=1
        )
        g_v = lax.psum_scatter(g_v, AXES, scatter_dimension=0)
    vo = [g_v[j * dv : (j + 1) * dv] for j in range(8)]
    return (
        pooled.reshape(micro, seqs, segs, D),
        dx.reshape(micro, tokens, D),
        jnp.stack([g_qo[:, c * hc : (c + 1) * hc] for c in range(3)]),
        jnp.stack([vo[6], vo[7]]),
        g_qo[:, 3 * hc :].T,
        vo[0], vo[1], vo[2],
        g_up,
        g_v[8 * dv :],
        g_down.T,
        vo[3], vo[4], vo[5],
    )


def solution(mesh):
    both = P(AXES)
    row3 = P(None, AXES)
    return jax.shard_map(
        per_device,
        mesh=mesh,
        in_specs=(
            row3, row3, row3, P(None, "dp", "tensor"), row3, P("tensor", "dp"), both, both, both,
            P("dp", "tensor"), both, P("tensor", "dp"), both, both, both,
        ),
        out_specs=(
            row3, row3, P(None, "dp", "tensor"), row3, P("tensor", "dp"), both, both, both,
            P("dp", "tensor"), both, P("tensor", "dp"), both, both, both,
        ),
        check_vma=False,
    )
```

```python
from functools import partial

import jax
import jax.numpy as jnp
from jax import lax
from jax.experimental import pallas as pl
from jax.experimental.pallas import tpu as pltpu
from jax.sharding import PartitionSpec as P

HD = 64
EPS = 1e-12
NEG = -1000000000.0
SCALE = float(HD) ** -0.5
AXES = ("dp", "tensor")
f32 = jnp.float32
bf16 = jnp.bfloat16
HI = lax.Precision.HIGHEST
BLK = 96
VMEM_LIMIT = 24 * 1024 * 1024
COST = 30_000_000
NORM = 2000
SMALL = pltpu.CompilerParams(vmem_limit_bytes=8 * 1024 * 1024)


def nn(a, b):
    return lax.dot_general(a, b, (((1,), (0,)), ((), ())), preferred_element_type=f32)


def nt(a, b):
    return lax.dot_general(a, b, (((1,), (1,)), ((), ())), preferred_element_type=f32)


def tn(a, b):
    return lax.dot_general(a, b, (((0,), (0,)), ((), ())), preferred_element_type=f32)


def mean_last(v):
    return jnp.sum(v, axis=-1, keepdims=True) * (1.0 / v.shape[-1])


def normalize(values):
    center = values - mean_last(values)
    inverse = lax.rsqrt(mean_last(center * center) + EPS)
    return center * inverse, inverse


def normalize_back(scaled, normed, inverse):
    return inverse * (scaled - mean_last(scaled) - normed * mean_last(scaled * normed))


def col_sum(v):
    return jnp.sum(v, axis=0, keepdims=True)


def pack(qkv_ref, out_ref, ob_ref, g1_ref, s1_ref, db_ref, g2_ref, s2_ref, qv_ref, ub_ref, first_ref):
    rows, hc = qkv_ref.shape[1:]
    eye = (lax.broadcasted_iota(jnp.int32, (rows, rows), 0) == lax.broadcasted_iota(jnp.int32, (rows, rows), 1)).astype(bf16)
    for c in range(3):
        first_ref[:rows, c * hc : (c + 1) * hc] = qkv_ref[c]
    first_ref[:rows, 3 * hc :] = nt(eye, out_ref[...]).astype(bf16)
    parts = [r[...].astype(f32) for r in (ob_ref, g1_ref, s1_ref, db_ref, g2_ref, s2_ref, qv_ref)]
    short = jnp.concatenate(parts, axis=0).astype(bf16)
    count, size = short.shape
    wide = first_ref.shape[1]

    def spread(values, at):
        lane = lax.broadcasted_iota(jnp.int32, (values.shape[1], wide), 1) - at
        return nn(values, (lax.rem(lane + values.shape[1] * wide, values.shape[1]) == lax.broadcasted_iota(jnp.int32, lane.shape, 0)).astype(bf16))

    lane = lax.broadcasted_iota(jnp.int32, (count, wide), 1)
    start = lax.broadcasted_iota(jnp.int32, (count, wide), 0) * size
    row = col_sum(jnp.where((lane >= start) & (lane < start + size), spread(short, 0), 0.0))
    total, long = count * size, ub_ref.shape[1]
    lane = lax.broadcasted_iota(jnp.int32, (1, wide), 1)
    row = jnp.where((lane >= total) & (lane < total + long), spread(ub_ref[...], total), row)
    extra = first_ref.shape[0] - rows
    here = lax.broadcasted_iota(jnp.int32, (extra, wide), 0)
    first_ref[rows:, :] = jnp.where(here == 0, row, 0.0).astype(bf16)


def reorder(h_ref, perm_ref, x_ref, keep_ref, send_ref):
    x = nn(h_ref[...], perm_ref[...]).astype(bf16)
    x_ref[...] = x
    turned = x.T
    keep_ref[...] = turned[: x.shape[1] // 2]
    send_ref[...] = turned[x.shape[1] // 2 :]


def stacked(values, hc):
    head = lax.broadcasted_iota(jnp.int32, (1, hc), 1) // HD
    return jnp.concatenate([values * (head == h).astype(f32).astype(bf16) for h in range(hc // HD)], axis=0)


def own_columns(blocks, hc):
    n_heads = hc // HD
    length = blocks.shape[0] // n_heads
    head = lax.broadcasted_iota(jnp.int32, (1, hc), 1) // HD
    out = blocks[:length]
    for h in range(1, n_heads):
        out = jnp.where(head == h, blocks[h * length : (h + 1) * length], out)
    return out


def sections(values, length):
    return [values[:, c : c + length] for c in range(0, values.shape[1], length)]


def rows_of(refs):
    return jnp.concatenate([r[...].reshape(-1, r.shape[3]) for r in refs], axis=0)


def accumulate(acc_ref, step, add):
    @pl.when(step == 0)
    def _():
        acc_ref[...] = add

    @pl.when(step > 0)
    def _():
        acc_ref[...] += add


def iota(shape, axis):
    return lax.broadcasted_iota(jnp.int32, shape, axis)


def picks(count, first, wide, size):
    return (iota((count, wide), 0) == first + lax.rem(iota((1, wide), 1), size)).astype(bf16)


def belongs(count, wide, size, period):
    lane, row = iota((1, wide), 1), lax.rem(iota((count, 1), 0), period)
    return (lane >= row * size) & (lane < (row + 1) * size)


def read_vectors(rows, hot_d, hot_e, sizes):
    n_d, dv, bu, width, hc, fc, n_t = sizes
    count = rows.shape[0]
    per = count // n_t
    d_all = nn(hot_d, rows[:, : n_d * dv]).astype(bf16)
    mine = belongs(count, width, dv, count)
    d_rows = [col_sum(jnp.where(mine, nn(d_all, picks(n_d * dv, j * dv, width, dv)), 0.0)) for j in range(n_d)]
    e_all = nn(hot_e, rows[:, n_d * dv : n_d * dv + 2 * dv + bu]).astype(bf16)
    out = []
    for first, size, wide in ((0, dv, hc), (dv, dv, hc), (2 * dv, bu, fc)):
        spread = jnp.where(belongs(count, wide, size, per), nn(e_all, picks(e_all.shape[1], first, wide, size)), 0.0)
        out.append(jnp.sum(spread.reshape(n_t, per, wide), axis=1, keepdims=True))
    return jnp.concatenate(d_rows, axis=0), out


def write_vectors(d_rows, e_rows, hot_d, hot_e, sizes):
    n_d, dv, bu, width, hc, fc, n_t = sizes
    count = hot_d.shape[0]
    per = count // n_t
    mine = belongs(count, width, dv, count)
    d_all = sum(
        nt(jnp.where(mine, d_rows[j : j + 1, :], 0.0).astype(bf16), picks(n_d * dv, j * dv, width, dv)) for j in range(n_d)
    ).astype(bf16)
    e_all = 0.0
    for value, first, size, wide in zip(e_rows, (0, dv, 2 * dv), (dv, dv, bu), (hc, hc, fc), strict=True):
        spread = jnp.broadcast_to(value, (n_t, per, wide)).reshape(count, wide)
        spread = jnp.where(belongs(count, wide, size, per), spread, 0.0).astype(bf16)
        e_all = e_all + nt(spread, picks(2 * dv + bu, first, wide, size))
    return jnp.concatenate([tn(hot_d, d_all), tn(hot_e, e_all.astype(bf16))], axis=1)


def attention_forward(sizes, x_ref, w0_ref, w1_ref, w2_ref, w3_ref, v0_ref, v1_ref, v2_ref, v3_ref, hd_ref, he_ref,
                      segc_ref, segr_ref, qkv_ref, p_ref, o_ref, n1_ref, x1_ref, r1_ref, n1b_ref, n1t_ref, n1s_ref,
                      vec_ref, bu_ref, acc_ref, bq_ref, bv_ref):
    step = pl.program_id(0)
    hc = bq_ref.shape[-1]

    @pl.when(step == 0)
    def _():
        rows = jnp.concatenate([r[:, :, 0, :].reshape(-1, r.shape[3]) for r in (v0_ref, v1_ref, v2_ref, v3_ref)], axis=0)
        d_rows, (b_q, b_v, b_u) = read_vectors(rows, hd_ref[...], he_ref[...], sizes)
        vec_ref[...] = d_rows
        bq_ref[...] = b_q
        bv_ref[...] = b_v
        bu_ref[...] = b_u

    rows, length = segr_ref.shape
    x = x_ref[...]
    w = rows_of((w0_ref, w1_ref, w2_ref, w3_ref))
    qkv = nn(x, w[:, : 3 * hc])
    q = (qkv[:, :hc] + bq_ref[step]).astype(bf16) * bf16(SCALE)
    k = qkv[:, hc : 2 * hc].astype(bf16)
    v = (qkv[:, 2 * hc :] + bv_ref[step]).astype(bf16)
    qkv_ref[0, :, :hc] = q
    qkv_ref[0, :, hc : 2 * hc] = k
    qkv_ref[0, :, 2 * hc :] = v
    spans = [slice(g * length, (g + 1) * length) for g in range(rows)]
    scores = [nt(q[span], stacked(k[span], hc)) for span in spans]
    probs = []
    for g, span in enumerate(spans):
        same = segc_ref[span, :] == segr_ref[g : g + 1, :]
        parts = []
        for s in sections(scores[g], length):
            s = jnp.where(same, s, NEG)
            e = jnp.exp(s - jnp.max(s, axis=-1, keepdims=True))
            parts.append(e * (1.0 / jnp.sum(e, axis=-1, keepdims=True)))
        probs.append(jnp.concatenate(parts, axis=1))
    for g, span in enumerate(spans):
        p_ref[0, g] = probs[g]
        o_ref[0, span, :hc] = nn(probs[g].astype(bf16), stacked(v[span], hc)).astype(bf16)
    o_ref[0, :, hc:] = jnp.zeros((o_ref.shape[1], o_ref.shape[2] - hc), bf16)
    add = nt(o_ref[0, :, :hc], w[:, 3 * hc :])

    accumulate(acc_ref, step, add)

    @pl.when(step == pl.num_programs(0) - 1)
    def _():
        a = acc_ref[...] + vec_ref[0:1, :] + x_ref[...].astype(f32)
        normed, inverse = normalize(a)
        n1 = normed * vec_ref[1:2, :] + vec_ref[2:3, :]
        n1_ref[...] = n1
        x1_ref[...] = normed
        r1_ref[...] = inverse
        low = n1.astype(bf16)
        n1b_ref[...] = low
        turned = low.T
        n1t_ref[...] = turned[: low.shape[1] // 2]
        n1s_ref[...] = turned[low.shape[1] // 2 :]


def up_forward(n_ref, w0_ref, w1_ref, w2_ref, w3_ref, b_ref, z_ref, d_ref):
    u = nn(n_ref[...], rows_of((w0_ref, w1_ref, w2_ref, w3_ref))) + b_ref[0]
    phi = 0.5 + 0.5 * lax.erf(u * (0.5**0.5))
    z_ref[0] = (u * phi).astype(bf16)
    d_ref[0] = phi + u * (jnp.exp(-0.5 * u * u) * 0.3989422804014327)


def down_forward(z_ref, w0_ref, w1_ref, w2_ref, w3_ref, n1_ref, vec_ref, segc_ref, segr_ref, pg_ref,
                 pooled_ref, db_ref, dbb_ref, dbt_ref, dbs_ref, sums_ref, acc_ref):
    step = pl.program_id(0)
    add = nt(z_ref[0], rows_of((w0_ref, w1_ref, w2_ref, w3_ref)))

    accumulate(acc_ref, step, add)

    @pl.when(step == pl.num_programs(0) - 1)
    def _():
        rows, length = segr_ref.shape
        segs = pg_ref.shape[1]
        b = acc_ref[...] + vec_ref[3:4, :] + n1_ref[...]
        x2, r2 = normalize(b)
        y = x2 * vec_ref[4:5, :] + vec_ref[5:6, :]
        grads = []
        for g in range(rows):
            span = slice(g * length, (g + 1) * length)
            ids = lax.broadcasted_iota(jnp.int32, (segs, length), 0)
            hot_t = (ids == segr_ref[g : g + 1, :]).astype(f32)
            idc = lax.broadcasted_iota(jnp.int32, (length, segs), 1)
            hot = (idc == segc_ref[span, :]).astype(f32)
            count = jnp.sum(hot_t, axis=1, keepdims=True)
            sums = lax.dot_general(hot_t, y[span, :], (((1,), (0,)), ((), ())),
                                   precision=HI, preferred_element_type=f32)
            pooled_ref[g] = sums / count
            grads.append(lax.dot_general(hot, pg_ref[g] / count, (((1,), (0,)), ((), ())),
                                         precision=HI, preferred_element_type=f32))
        dy = jnp.concatenate(grads, axis=0)
        db = normalize_back(dy * vec_ref[4:5, :], x2, r2)
        db_ref[...] = db
        low = db.astype(bf16)
        dbb_ref[...] = low
        turned = low.T
        dbt_ref[...] = turned[: low.shape[1] // 2]
        dbs_ref[...] = turned[low.shape[1] // 2 :]
        sums_ref[0:1, :] = col_sum(db)
        sums_ref[1:2, :] = col_sum(dy * x2)
        sums_ref[2:3, :] = col_sum(dy)


def put(grad, ref):
    ref[:, :, :BLK, :] = grad.astype(bf16).reshape(grad.shape[0] // BLK, 1, BLK, grad.shape[1])


def hidden_backward(dbb_ref, w0_ref, w1_ref, w2_ref, w3_ref, d_ref, du_ref, bu_ref):
    du = (nn(dbb_ref[...], rows_of((w0_ref, w1_ref, w2_ref, w3_ref))) * d_ref[0]).astype(bf16)
    du_ref[0] = du
    bu_ref[0] = col_sum(du.astype(f32))


def step_value(refs, width):
    if len(refs) == 1:
        return refs[0][0, :, :width]
    return jnp.where(pl.program_id(0) < pl.num_programs(0) // 2, refs[0][0, :, :width], refs[1][0, :, :width])


def weight_gradient(groups, vectors, which, *refs):
    refs = list(refs)
    parts = []
    for pairs, split, width in groups:
        total = None
        for _ in range(pairs):
            rows = refs.pop(0)
            half = rows.shape[0] // 2
            rows = rows[...] if which is None else rows[which * half : (which + 1) * half, :]
            add = nn(rows, step_value([refs.pop(0) for _ in range(split)], width))
            total = add if total is None else total + add
        parts.append(total)
    grad = jnp.concatenate(parts, axis=1)
    extra = sum(refs.pop(0)[0].astype(f32) for _ in range(vectors)) if vectors else None
    half = grad.shape[0] // len(refs)
    for n, ref in enumerate(refs):
        put(grad[n * half : (n + 1) * half], ref)
        if vectors:
            for j in range(ref.shape[0]):
                at = (n if which is None else which) * ref.shape[0] + j
                row = extra[at : at + 1]
                tail = ref.shape[2] - BLK
                ref[j, 0, BLK:, :] = jnp.where(iota((tail, row.shape[1]), 0) == 0, row, 0.0).astype(bf16)


def norm_backward(du_ref, w0_ref, w1_ref, w2_ref, w3_ref, db_ref, x1_ref, r1_ref, vec_ref,
                  da_ref, dab_ref, dat_ref, das_ref, sums_ref, acc_ref):
    step = pl.program_id(0)
    accumulate(acc_ref, step, nt(du_ref[0], rows_of((w0_ref, w1_ref, w2_ref, w3_ref))))

    @pl.when(step == pl.num_programs(0) - 1)
    def _():
        dn1 = acc_ref[...].astype(bf16).astype(f32) + db_ref[...]
        da = normalize_back(dn1 * vec_ref[1:2, :], x1_ref[...], r1_ref[...])
        da_ref[...] = da
        low = da.astype(bf16)
        dab_ref[...] = low
        turned = low.T
        dat_ref[...] = turned[: low.shape[1] // 2]
        das_ref[...] = turned[low.shape[1] // 2 :]
        sums_ref[0:1, :] = col_sum(da)
        sums_ref[1:2, :] = col_sum(dn1 * x1_ref[...])
        sums_ref[2:3, :] = col_sum(dn1)


def attention_backward(sizes, dab_ref, w0_ref, w1_ref, w2_ref, w3_ref, qkv_ref, p_ref, s1_ref, s2_ref, gu_ref, hd_ref, he_ref,
                       low_ref, high_ref, keep_ref, send_ref, bq_ref, bv_ref, dqkv_ref):
    step = pl.program_id(0)
    hc = bq_ref.shape[-1]
    dab = dab_ref[...]
    w = rows_of([r.at[:, :, :, 3 * hc :] for r in (w0_ref, w1_ref, w2_ref, w3_ref)])
    do = nn(dab, w).astype(bf16)
    qkv = qkv_ref[0]
    rows, length = p_ref.shape[1], p_ref.shape[2]
    spans = [slice(g * length, (g + 1) * length) for g in range(rows)]
    q = [qkv[span, :hc] for span in spans]
    k = [stacked(qkv[span, hc : 2 * hc], hc) for span in spans]
    dps = [nt(do[span], stacked(qkv[span, 2 * hc :], hc)) for span in spans]
    dss = []
    for g in range(rows):
        parts = []
        for p, dp in zip(sections(p_ref[0, g], length), sections(dps[g], length)):
            pd = p * dp
            parts.append((pd - p * jnp.sum(pd, axis=-1, keepdims=True)).astype(bf16))
        dss.append(jnp.concatenate(parts, axis=1))
    for g, span in enumerate(spans):
        dqkv_ref[span, :hc] = (nn(dss[g], k[g]) * SCALE).astype(bf16)
        dqkv_ref[span, hc : 2 * hc] = own_columns(tn(dss[g], q[g]), hc).astype(bf16)
        dqkv_ref[span, 2 * hc : 3 * hc] = own_columns(tn(p_ref[0, g].astype(bf16), do[span]), hc).astype(bf16)
    dqkv_ref[:, 3 * hc :] = jnp.zeros((dqkv_ref.shape[0], dqkv_ref.shape[1] - 3 * hc), bf16)
    dqkv = dqkv_ref[...]
    half_steps = pl.num_programs(0) // 2

    @pl.when(step < half_steps)
    def _():
        low_ref[0] = dqkv

    @pl.when(step >= half_steps)
    def _():
        high_ref[0] = dqkv

    bq_ref[step] = col_sum(dqkv[:, :hc].astype(f32))
    bv_ref[step] = col_sum(dqkv[:, 2 * hc : 3 * hc].astype(f32))

    @pl.when(step == pl.num_programs(0) - 1)
    def _():
        d_rows = jnp.concatenate([s1_ref[...], s2_ref[...]], axis=0)
        rows = write_vectors(d_rows, (bq_ref[...], bv_ref[...], gu_ref[...]), hd_ref[...], he_ref[...], sizes)
        half, n_t = rows.shape[0] // 2, bq_ref.shape[0]
        rows = jnp.concatenate([rows, jnp.zeros((rows.shape[0], keep_ref.shape[-1] - rows.shape[1]), f32)], axis=1)
        for n, ref in enumerate((keep_ref, send_ref)):
            for t in range(n_t):
                for j in range(half // n_t):
                    at = n * half + j * n_t + t
                    ref[t, j : j + 1, :] = rows[at : at + 1]


def input_backward(low_ref, high_ref, w0_ref, w1_ref, w2_ref, w3_ref, da_ref, perm_ref, dx_ref, acc_ref):
    step = pl.program_id(0)
    cols = 3 * w0_ref.shape[-1] // 4
    w = rows_of((w0_ref, w1_ref, w2_ref, w3_ref))
    add = nt(step_value((low_ref, high_ref), cols), w[:, :cols])

    accumulate(acc_ref, step, add)

    @pl.when(step == pl.num_programs(0) - 1)
    def _():
        dx = acc_ref[...] + da_ref[...]
        high = dx.astype(bf16)
        rest = dx - high.astype(f32)
        mid = rest.astype(bf16)
        low = (rest - mid.astype(f32)).astype(bf16)
        perm = perm_ref[...]
        dx_ref[...] = nt(high, perm) + nt(mid, perm) + nt(low, perm)


def whole(a):
    nd = len(a.shape)
    return pl.BlockSpec(a.shape, lambda s: (0,) * nd, pipeline_mode=pl.Buffered(1))


def lead(a):
    nd = len(a.shape)
    return pl.BlockSpec((1,) + a.shape[1:], lambda s: (s,) + (0,) * (nd - 1))


def weight(a):
    return pl.BlockSpec((a.shape[0], 1, BLK, a.shape[3]), lambda s: (0, s, 0, 0))


def weight_t(a):
    return pl.BlockSpec((1, a.shape[1], BLK, a.shape[3]), lambda s: (s, 0, 0, 0))


def half_spec(h):
    return pl.BlockSpec((h.shape[0], 1) + h.shape[2:], lambda s: (0, s, 0, 0))


def sds(shape, dtype):
    return jax.ShapeDtypeStruct(shape, dtype)


def far(shape, dtype):
    return pltpu.HBM(shape, dtype)


def call(body, n_t, micros, ins, outs, scratch=()):
    return pl.pallas_call(
        body,
        grid=(n_t,),
        in_specs=[s for _, s in ins],
        out_specs=[s for _, s in outs],
        out_shape=[a for a, _ in outs],
        scratch_shapes=list(scratch),
        compiler_params=pltpu.CompilerParams(
            dimension_semantics=("arbitrary",), vmem_limit_bytes=VMEM_LIMIT
        ),
        cost_estimate=pl.CostEstimate(flops=int(micros * COST), transcendentals=0, bytes_accessed=0),
    )(*[a for a, _ in ins])


def flips(n_dp, n_t):
    size = n_dp * n_t
    core = n_t
    x_bit, y_bit = 2 * core, 4 * core

    def table(bit_of):
        return [(i, i ^ bit_of(i)) for i in range(size)]

    return {
        "Z": [table(lambda i, d=d: d) for d in range(1, n_t)],
        "C": [table(lambda i: core)],
        "2": [table(lambda i: x_bit if i & core else y_bit)],
        "3": [table(lambda i: y_bit if i & core else x_bit)],
    }


def after(value, *done):
    return lax.optimization_barrier((value, *done))[0] if done else value


def swap(value, tables, *done):
    return lax.ppermute(after(value, *done), AXES, tables["C"][0])


class Gather:
    def __init__(self, value, tables):
        self.held, self.tables = [value[None]], tables

    def send(self, name, *done, parts=None, tables=None):
        sent = self.held if parts is None else [self.held[j] for j in parts]
        return [lax.ppermute(after(h, *done), AXES, t) for t in self.tables[name][tables or slice(None)] for h in sent]

    def take(self, name, got):
        self.held = [jnp.concatenate(self.held + got)] if name in "Z2" else self.held + got
        return got

    def stage(self, name, *done, parts=None):
        return self.take(name, self.send(name, *done, parts=parts))

    def pieces(self, *lead):
        return [h.reshape(*lead, *h.shape[1:]) for h in self.held]


class Scatter:
    def __init__(self, keep, send, tables):
        self.keep, self.send, self.tables = keep, [send], tables

    def stage(self, name, parts, *done):
        got = [lax.ppermute(after(s, *done), AXES, t) for s, t in zip(self.send, self.tables[name], strict=True)]
        size = self.keep.shape[0] // parts

        def share(j):
            cut = slice(j * size, (j + 1) * size)
            return sum((g[cut].astype(f32) for g in got), self.keep[cut].astype(f32))

        self.send = [share(j).astype(bf16) for j in range(1, parts)]
        self.keep = share(0)
        return got


def per_device(
    hidden_in, segment_ids, pooled_grad, qkv_weight, qv_bias, out_weight, out_bias,
    norm1_gain, norm1_shift, up_weight, up_bias, down_weight_in, down_bias, norm2_gain, norm2_shift,
):
    n_dp, n_t = lax.axis_size("dp"), lax.axis_size("tensor")
    at_dp, at_t = lax.axis_index("dp"), lax.axis_index("tensor")
    hc, fc = qkv_weight.shape[2], up_weight.shape[1]
    rows = qkv_weight.shape[1]
    D = rows * n_dp
    micro, tokens = hidden_in.shape[0], hidden_in.shape[1]
    seqs, L = segment_ids.shape[1], segment_ids.shape[2]
    G, T = micro * seqs, micro * tokens
    segs = pooled_grad.shape[2]
    n_i = D // BLK
    pairwise = (n_dp, n_t) == (8, 4) and 4 * hc == fc

    d_parts = [out_bias, norm1_gain, norm1_shift, down_bias, norm2_gain, norm2_shift]
    e_parts = [qv_bias[0], qv_bias[1], up_bias]
    dv = out_bias.shape[0]
    n_vec = sum(p.shape[0] for p in d_parts + e_parts)
    nd = len(d_parts) * dv

    sizes = (6, dv, up_bias.shape[0], D, hc, fc, n_t) if pairwise else (6, D // (n_i * n_t), n_t * fc // (n_i * n_t), D, hc, fc, n_t)
    slot = jnp.arange(n_i * n_t)
    rel = jnp.arange(n_i)
    if pairwise:
        tables = flips(n_dp, n_t)
        packed = (qkv_weight, out_weight, *[p[None] for p in d_parts], qv_bias, up_bias[None])
        packed = pl.pallas_call(pack, out_shape=sds((BLK + 8, 4 * hc), bf16))(*packed)
        first, middle, last = Gather(packed, tables), Gather(up_weight, tables), Gather(down_weight_in.T, tables)
        done = first.stage("Z") + last.stage("2")

        core = (at_dp & 1) ^ (rel >> 2)
        s3, s2 = (rel >> 1) & 1, rel & 1
        dy, dx = jnp.where(core == 0, s2, s3), jnp.where(core == 0, s3, s2)
        absolute = ((((at_dp >> 2) & 1) ^ dy) << 2) | ((((at_dp >> 1) & 1) ^ dx) << 1) | core
        i_p = jnp.broadcast_to(absolute[:, None], (n_i, n_t)).reshape(-1)
        t_p = jnp.broadcast_to((at_t ^ jnp.arange(n_t))[None], (n_i, n_t)).reshape(-1)
        to_d = jnp.broadcast_to(rel[:, None], (n_i, n_t)).reshape(-1) * n_t + t_p
        to_e = (((i_p * n_t) // n_i) ^ at_t) * n_i + (i_p * n_t + t_p) % n_i
    else:
        absolute, to_d, to_e = rel, slot, slot
    hot_d = (to_d[None, :] == slot[:, None]).astype(bf16)
    hot_e = (to_e[None, :] == slot[:, None]).astype(bf16)
    lane = jnp.arange(D)
    same_block = jnp.repeat(jnp.repeat((absolute[:, None] == rel[None, :]).T, BLK, axis=0), BLK, axis=1)
    perm = (same_block & ((lane[:, None] % BLK) == (lane[None, :] % BLK))).astype(bf16)
    turned = (D // 2, T)
    x, x_keep, x_send = pl.pallas_call(
        reorder, out_shape=[sds((T, D), bf16), sds(turned, bf16), sds(turned, bf16)], compiler_params=SMALL
    )(hidden_in.reshape(T, D), perm)
    pg = jnp.einsum("gsd,de->gse", pooled_grad.reshape(G, segs, D), perm.astype(f32), precision=HI)
    seg_r = segment_ids.reshape(G, L)
    seg_c = segment_ids.reshape(T, 1)

    if pairwise:
        done = first.stage("2", *done, x, x_keep, x_send, pg, hot_d, hot_e) + middle.stage("Z", *done)
        x_other = swap(x_send, tables, *done)
        near_z = last.send("Z", *done, tables=slice(0, 2))
        done = first.stage("3", *done) + middle.stage("2", *done) + near_z
        first.stage("C", *done)
        x = after(x, x_other)
        got_u3, far_z = middle.send("3", *done), last.send("Z", *done, tables=slice(2, None))
        w_qo = first.pieces(2, n_t)
    else:
        heads_in = [qkv_weight[0], qkv_weight[1], qkv_weight[2], out_weight.T]
        main = jnp.concatenate([*heads_in, up_weight, down_weight_in.T], axis=1)
        vec = jnp.concatenate(d_parts + e_parts)
        full = lax.all_gather(lax.all_gather(main, "dp", axis=0, tiled=True), "tensor", axis=0)
        full = full.reshape(n_t, n_i, BLK, -1).transpose(1, 0, 2, 3)
        vecs = lax.all_gather(lax.all_gather(vec, "tensor"), "dp").reshape(n_dp * n_t, -1)
        cuts = [j * dv for j in range(9)] + [n_vec]
        rows8 = jnp.concatenate([vecs[:, a:b].reshape(n_i * n_t, -1) for a, b in zip(cuts[:-1], cuts[1:])], axis=1)
        rows8 = jnp.pad(rows8.reshape(n_i, n_t, 1, -1), ((0, 0), (0, 0), (0, 7), (0, 4 * hc - rows8.shape[1])))
        quarters = [full[j * n_i // 4 : (j + 1) * n_i // 4] for j in range(4)]
        w_qo = [
            jnp.concatenate([w[..., : 4 * hc], rows8[j * n_i // 4 : (j + 1) * n_i // 4]], axis=2)
            for j, w in enumerate(quarters)
        ]
        w_up = [w[..., 4 * hc : 4 * hc + fc] for w in quarters]
        w_down = [w[..., 4 * hc + fc :].transpose(1, 0, 2, 3) for w in quarters]

    hl = hc // HD * L
    o_wide, q_wide = -(-hc // 128) * 128, -(-3 * hc // 128) * 128

    def leads(*arrays):
        return [(a, lead(a)) for a in arrays]

    def wholes(*arrays):
        return [(a, whole(a)) for a in arrays]

    def weights(*arrays):
        return [(a, weight(a)) for a in arrays]

    def weights_t(*arrays):
        return [(a, weight_t(a)) for a in arrays]

    tails = [
        (w, pl.BlockSpec((w.shape[0], n_t, 8, w.shape[3]), lambda s: (0, 0, BLK // 8, 0), pipeline_mode=pl.Buffered(1)))
        for w in w_qo
    ]
    qkv, prob, o, n1, x1, r1, n1b, n1_keep, n1_send, vec_d, b_u = call(
        partial(attention_forward, sizes), n_t, 10,
        wholes(x) + weights(*w_qo) + tails + wholes(hot_d, hot_e, seg_c, seg_r),
        leads(far((n_t, T, 3 * hc), bf16), far((n_t, G, L, hl), f32), far((n_t, T, o_wide), bf16))
        + wholes(sds((T, D), f32), far((T, D), f32), far((T, 1), f32), sds((T, D), bf16), far(turned, bf16), far(turned, bf16))
        + wholes(sds((6, D), f32), sds((n_t, 1, fc), f32)),
        [pltpu.VMEM((T, D), f32), pltpu.VMEM((n_t, 1, hc), f32), pltpu.VMEM((n_t, 1, hc), f32)],
    )
    if pairwise:
        last.take("Z", near_z + [after(g, n1b) for g in far_z])
        middle.take("3", [after(g, n1b) for g in got_u3])
        last.stage("3", *got_u3)
        middle.stage("C", n1b, *far_z)
        last.take("C", last.send("C", n1b, parts=(0,)))
        last.take("C", last.send("C", parts=(1,)))
        w_up, w_down = middle.pieces(2, n_t), last.pieces(n_t, 2)
        n1_other = swap(n1_send, tables)
        o_other = swap(o, tables)
        b_u = after(b_u, n1_other, o_other)
    z, dgelu = call(
        up_forward, n_t, 4, wholes(n1b) + weights(*w_up) + leads(b_u),
        leads(sds((n_t, T, fc), bf16), sds((n_t, T, fc), f32)),
    )
    if pairwise:
        z_other = swap(z, tables)
    pooled, db, dbb, db_keep, db_send, sums2 = call(
        down_forward, n_t, 5.5, leads(z) + weights_t(*w_down) + wholes(n1, vec_d, seg_c, seg_r, pg),
        wholes(sds((G, segs, D), f32), sds((T, D), f32), sds((T, D), bf16), sds(turned, bf16), sds(turned, bf16), sds((3, D), f32)),
        [pltpu.VMEM((T, D), f32)],
    )

    def gradient(groups, vectors=(), at_once=True):
        ins, kinds = [], []
        for width, *pairs in groups:
            kinds.append((len(pairs), len(pairs[0][1]), width))
            for lhs, values in pairs:
                ins += wholes(lhs) + (leads(*values) if len(values) == 1 else halved(*values))
        out = sds((n_i // 4, n_t, BLK + (8 if vectors else 0), sum(k[2] for k in kinds)), bf16)

        def share(which):
            return call(
                partial(weight_gradient, kinds, len(vectors), which), n_t, 2, ins + leads(*vectors),
                [(out, half_spec(out))] * (2 if which is None else 1),
            )

        return share(None) if at_once else (share(0)[0], share(1)[0])

    def halved(low, high):
        block = (1,) + low.shape[1:]
        return [
            (low, pl.BlockSpec(block, lambda s: (jnp.minimum(s, n_t // 2 - 1), 0, 0))),
            (high, pl.BlockSpec(block, lambda s: (jnp.maximum(s - n_t // 2, 0), 0, 0))),
        ]

    def flat(a):
        return a.reshape((-1,) + a.shape[2:])

    du, g_bu = call(
        hidden_backward, n_t, 3.5, wholes(dbb) + weights_t(*w_down) + leads(dgelu),
        leads(sds((n_t, T, fc), bf16), sds((n_t, 1, fc), f32)),
    )
    if pairwise:
        db_other = swap(db_send, tables)
        du_other = swap(du, tables)
        down_keep, down_send = gradient([[fc, (after(db_keep, g_bu), [z]), (db_other, [z_other])]], at_once=False)
        s_down = Scatter(flat(down_keep), flat(down_send), tables)
        got_d3 = s_down.stage("3", 2)
        du_next = after(du, down_send)
        dab_after = down_keep
    else:
        du_next = du
    da, dab, da_keep, da_send, sums1 = call(
        norm_backward, n_t, NORM, leads(du_next) + weights(*w_up) + wholes(db, x1, r1, vec_d),
        wholes(sds((T, D), f32), sds((T, D), bf16), sds(turned, bf16), sds(turned, bf16), sds((3, D), f32)),
        [pltpu.VMEM((T, D), f32)],
    )
    if pairwise:
        da_other = swap(da_send, tables)
        up_keep, up_send = gradient([[fc, (after(n1_keep, da_keep), [du]), (n1_other, [du_other])]])
        s_up = Scatter(flat(up_keep), flat(up_send), tables)
        got_u3 = s_up.stage("3", 2)
        dab = after(dab, up_keep)
    rows = sds((n_t, n_i // 2, 4 * hc), f32)
    if pairwise:
        dab = after(dab, da_other, dab_after, *got_d3)
    dq_half = sds((n_t // 2, T, q_wide), bf16)
    *dq, v_keep, v_send = call(
        partial(attention_backward, sizes), n_t, 8,
        wholes(dab) + weights(*w_qo) + leads(qkv, prob) + wholes(sums1, sums2, g_bu, hot_d, hot_e),
        halved(dq_half, dq_half) + wholes(rows, rows),
        [pltpu.VMEM((n_t, 1, hc), f32), pltpu.VMEM((n_t, 1, hc), f32), pltpu.VMEM((T, q_wide), bf16)],
    )
    if pairwise:
        dq_other = [swap(d, tables) for d in dq]
        v_other = swap(v_send, tables)
        got_d2 = s_down.stage("2", n_t)
    pooled = jnp.einsum("gse,de->gsd", pooled, perm.astype(f32), precision=HI)
    if pairwise:
        x_now = after(x_keep, *got_u3)
        qo_keep, qo_send = gradient(
            [[3 * hc, (x_now, dq), (x_other, dq_other)], [hc, (da_keep, [o]), (da_other, [o_other])]], (v_keep, v_other)
        )
        s_qo = Scatter(flat(qo_keep), flat(qo_send), tables)
        got_u2 = s_up.stage("2", n_t)
        got_q3 = s_qo.stage("3", 2, *got_d2, *got_u2)
        got_z = s_down.stage("Z", 1)
        dq = [after(d, pooled, qo_keep) for d in dq]
    dx = call(
        input_backward, n_t, 4, halved(*dq) + weights(*w_qo) + wholes(da, perm), wholes(sds((T, D), f32)),
        [pltpu.VMEM((T, D), f32)],
    )[0]

    if pairwise:
        got = s_up.stage("Z", 1)
        s_qo.stage("2", n_t, dx, *got_z)
        s_qo.stage("Z", 1, *got)
        g_down, g_up, g_qo = s_down.keep[0], s_up.keep[0], s_qo.keep[0]
        g_v = g_qo[BLK, :n_vec]
        g_qo = g_qo[:BLK]
    else:
        def joined(*halves_of):
            g = jnp.concatenate([part[:, :, :BLK] for half in halves_of for part in half])
            return g.transpose(1, 0, 2, 3).reshape(n_t, D, -1)

        x_h, n1_h, db_h, da_h = (x_keep, x_send), (n1_keep, n1_send), (db_keep, db_send), (da_keep, da_send)
        g_full = jnp.concatenate([
            joined(*[gradient([[3 * hc, (x_h[j], dq)], [hc, (da_h[j], [o])]]) for j in range(2)]),
            joined(*[gradient([[fc, (n1_h[j], [du])]]) for j in range(2)]),
            joined(*[gradient([[fc, (db_h[j], [z])]]) for j in range(2)]),
        ], axis=2)
        mine = lax.psum_scatter(g_full, "tensor", scatter_dimension=0)
        mine = lax.psum_scatter(mine, "dp", scatter_dimension=0, tiled=True).astype(f32)
        g_qo, g_up, g_down = mine[:, : 4 * hc], mine[:, 4 * hc : 4 * hc + fc], mine[:, 4 * hc + fc :]
        g_rows = jnp.stack([v_keep, v_send]).transpose(0, 2, 1, 3).reshape(n_i * n_t, -1)
        dv_c, bu_c = sizes[1], sizes[2]
        cuts = [j * dv_c for j in range(9)] + [8 * dv_c + bu_c]
        g_v = jnp.concatenate(
            [g_rows[:, a:b].reshape(n_dp * n_t, -1) for a, b in zip(cuts[:-1], cuts[1:])], axis=1
        )
        g_v = lax.psum_scatter(g_v, AXES, scatter_dimension=0)
    vo = [g_v[j * dv : (j + 1) * dv] for j in range(8)]
    return (
        pooled.reshape(micro, seqs, segs, D),
        dx.reshape(micro, tokens, D),
        jnp.stack([g_qo[:, c * hc : (c + 1) * hc] for c in range(3)]),
        jnp.stack([vo[6], vo[7]]),
        g_qo[:, 3 * hc :].T,
        vo[0], vo[1], vo[2],
        g_up,
        g_v[8 * dv :],
        g_down.T,
        vo[3], vo[4], vo[5],
    )


def solution(mesh):
    both = P(AXES)
    row3 = P(None, AXES)
    return jax.shard_map(
        per_device,
        mesh=mesh,
        in_specs=(
            row3, row3, row3, P(None, "dp", "tensor"), row3, P("tensor", "dp"), both, both, both,
            P("dp", "tensor"), both, P("tensor", "dp"), both, both, both,
        ),
        out_specs=(
            row3, row3, P(None, "dp", "tensor"), row3, P("tensor", "dp"), both, both, both,
            P("dp", "tensor"), both, P("tensor", "dp"), both, both, both,
        ),
        check_vma=False,
    )
```

```python
from functools import partial

import jax
import jax.numpy as jnp
from jax import lax
from jax.experimental import pallas as pl
from jax.experimental.pallas import tpu as pltpu
from jax.sharding import PartitionSpec as P

HD = 64
EPS = 1e-12
NEG = -1000000000.0
SCALE = float(HD) ** -0.5
AXES = ("dp", "tensor")
f32 = jnp.float32
bf16 = jnp.bfloat16
HI = lax.Precision.HIGHEST
BLK = 96
VMEM_LIMIT = 24 * 1024 * 1024
COST = 30_000_000
NORM = 2000
CUT = 4
SMALL = pltpu.CompilerParams(vmem_limit_bytes=8 * 1024 * 1024)


def nn(a, b):
    return lax.dot_general(a, b, (((1,), (0,)), ((), ())), preferred_element_type=f32)


def nt(a, b):
    return lax.dot_general(a, b, (((1,), (1,)), ((), ())), preferred_element_type=f32)


def tn(a, b):
    return lax.dot_general(a, b, (((0,), (0,)), ((), ())), preferred_element_type=f32)


def mean_last(v):
    return jnp.sum(v, axis=-1, keepdims=True) * (1.0 / v.shape[-1])


def normalize(values):
    center = values - mean_last(values)
    inverse = lax.rsqrt(mean_last(center * center) + EPS)
    return center * inverse, inverse


def normalize_back(scaled, normed, inverse):
    return inverse * (scaled - mean_last(scaled) - normed * mean_last(scaled * normed))


def col_sum(v):
    return jnp.sum(v, axis=0, keepdims=True)


def pack(qkv_ref, out_ref, ob_ref, g1_ref, s1_ref, db_ref, g2_ref, s2_ref, qv_ref, ub_ref, first_ref):
    rows, hc = qkv_ref.shape[1:]
    eye = (lax.broadcasted_iota(jnp.int32, (rows, rows), 0) == lax.broadcasted_iota(jnp.int32, (rows, rows), 1)).astype(bf16)
    for c in range(3):
        first_ref[:rows, c * hc : (c + 1) * hc] = qkv_ref[c]
    first_ref[:rows, 3 * hc :] = nt(eye, out_ref[...]).astype(bf16)
    parts = [r[...].astype(f32) for r in (ob_ref, g1_ref, s1_ref, db_ref, g2_ref, s2_ref, qv_ref)]
    short = jnp.concatenate(parts, axis=0).astype(bf16)
    count, size = short.shape
    wide = first_ref.shape[1]

    def spread(values, at):
        lane = lax.broadcasted_iota(jnp.int32, (values.shape[1], wide), 1) - at
        return nn(values, (lax.rem(lane + values.shape[1] * wide, values.shape[1]) == lax.broadcasted_iota(jnp.int32, lane.shape, 0)).astype(bf16))

    lane = lax.broadcasted_iota(jnp.int32, (count, wide), 1)
    start = lax.broadcasted_iota(jnp.int32, (count, wide), 0) * size
    row = col_sum(jnp.where((lane >= start) & (lane < start + size), spread(short, 0), 0.0))
    total, long = count * size, ub_ref.shape[1]
    lane = lax.broadcasted_iota(jnp.int32, (1, wide), 1)
    row = jnp.where((lane >= total) & (lane < total + long), spread(ub_ref[...], total), row)
    extra = first_ref.shape[0] - rows
    here = lax.broadcasted_iota(jnp.int32, (extra, wide), 0)
    first_ref[rows:, :] = jnp.where(here == 0, row, 0.0).astype(bf16)


def reorder(h_ref, perm_ref, x_ref, keep_ref, send_ref):
    x = nn(h_ref[...], perm_ref[...]).astype(bf16)
    x_ref[...] = x
    turned = x.T
    keep_ref[...] = turned[: x.shape[1] // 2]
    send_ref[...] = turned[x.shape[1] // 2 :]


def stacked(values, hc):
    head = lax.broadcasted_iota(jnp.int32, (1, hc), 1) // HD
    return jnp.concatenate([values * (head == h).astype(f32).astype(bf16) for h in range(hc // HD)], axis=0)


def own_columns(blocks, hc):
    n_heads = hc // HD
    length = blocks.shape[0] // n_heads
    head = lax.broadcasted_iota(jnp.int32, (1, hc), 1) // HD
    out = blocks[:length]
    for h in range(1, n_heads):
        out = jnp.where(head == h, blocks[h * length : (h + 1) * length], out)
    return out


def sections(values, length):
    return [values[:, c : c + length] for c in range(0, values.shape[1], length)]


def rows_of(refs):
    return jnp.concatenate([r[...].reshape(-1, r.shape[3]) for r in refs], axis=0)


def accumulate(acc_ref, step, add):
    @pl.when(step == 0)
    def _():
        acc_ref[...] = add

    @pl.when(step > 0)
    def _():
        acc_ref[...] += add


def iota(shape, axis):
    return lax.broadcasted_iota(jnp.int32, shape, axis)


def picks(count, first, wide, size):
    return (iota((count, wide), 0) == first + lax.rem(iota((1, wide), 1), size)).astype(bf16)


def belongs(count, wide, size, period):
    lane, row = iota((1, wide), 1), lax.rem(iota((count, 1), 0), period)
    return (lane >= row * size) & (lane < (row + 1) * size)


def read_vectors(rows, hot_d, hot_e, sizes):
    n_d, dv, bu, width, hc, fc, n_t = sizes
    count = rows.shape[0]
    per = count // n_t
    d_all = nn(hot_d, rows[:, : n_d * dv]).astype(bf16)
    mine = belongs(count, width, dv, count)
    d_rows = [col_sum(jnp.where(mine, nn(d_all, picks(n_d * dv, j * dv, width, dv)), 0.0)) for j in range(n_d)]
    e_all = nn(hot_e, rows[:, n_d * dv : n_d * dv + 2 * dv + bu]).astype(bf16)
    out = []
    for first, size, wide in ((0, dv, hc), (dv, dv, hc), (2 * dv, bu, fc)):
        spread = jnp.where(belongs(count, wide, size, per), nn(e_all, picks(e_all.shape[1], first, wide, size)), 0.0)
        out.append(jnp.sum(spread.reshape(n_t, per, wide), axis=1, keepdims=True))
    return jnp.concatenate(d_rows, axis=0), out


def write_vectors(d_rows, e_rows, hot_d, hot_e, sizes):
    n_d, dv, bu, width, hc, fc, n_t = sizes
    count = hot_d.shape[0]
    per = count // n_t
    mine = belongs(count, width, dv, count)
    d_all = sum(
        nt(jnp.where(mine, d_rows[j : j + 1, :], 0.0).astype(bf16), picks(n_d * dv, j * dv, width, dv)) for j in range(n_d)
    ).astype(bf16)
    e_all = 0.0
    for value, first, size, wide in zip(e_rows, (0, dv, 2 * dv), (dv, dv, bu), (hc, hc, fc), strict=True):
        spread = jnp.broadcast_to(value, (n_t, per, wide)).reshape(count, wide)
        spread = jnp.where(belongs(count, wide, size, per), spread, 0.0).astype(bf16)
        e_all = e_all + nt(spread, picks(2 * dv + bu, first, wide, size))
    return jnp.concatenate([tn(hot_d, d_all), tn(hot_e, e_all.astype(bf16))], axis=1)


def attention_forward(sizes, x_ref, w0_ref, w1_ref, w2_ref, w3_ref, v0_ref, v1_ref, v2_ref, v3_ref, hd_ref, he_ref,
                      segc_ref, segr_ref, qkv_ref, p_ref, o_ref, n1_ref, x1_ref, r1_ref, n1b_ref, n1t_ref, n1s_ref,
                      vec_ref, bu_ref, acc_ref, bq_ref, bv_ref):
    step = pl.program_id(0)
    hc = bq_ref.shape[-1]

    @pl.when(step == 0)
    def _():
        rows = jnp.concatenate([r[:, :, 0, :].reshape(-1, r.shape[3]) for r in (v0_ref, v1_ref, v2_ref, v3_ref)], axis=0)
        d_rows, (b_q, b_v, b_u) = read_vectors(rows, hd_ref[...], he_ref[...], sizes)
        vec_ref[...] = d_rows
        bq_ref[...] = b_q
        bv_ref[...] = b_v
        bu_ref[...] = b_u

    rows, length = segr_ref.shape
    x = x_ref[...]
    w = rows_of((w0_ref, w1_ref, w2_ref, w3_ref))
    qkv = nn(x, w[:, : 3 * hc])
    q = (qkv[:, :hc] + bq_ref[step]).astype(bf16) * bf16(SCALE)
    k = qkv[:, hc : 2 * hc].astype(bf16)
    v = (qkv[:, 2 * hc :] + bv_ref[step]).astype(bf16)
    qkv_ref[0, :, :hc] = q
    qkv_ref[0, :, hc : 2 * hc] = k
    qkv_ref[0, :, 2 * hc :] = v
    spans = [slice(g * length, (g + 1) * length) for g in range(rows)]
    scores = [nt(q[span], stacked(k[span], hc)) for span in spans]
    probs = []
    for g, span in enumerate(spans):
        same = segc_ref[span, :] == segr_ref[g : g + 1, :]
        parts = []
        for s in sections(scores[g], length):
            s = jnp.where(same, s, NEG)
            e = jnp.exp(s - jnp.max(s, axis=-1, keepdims=True))
            parts.append(e * (1.0 / jnp.sum(e, axis=-1, keepdims=True)))
        probs.append(jnp.concatenate(parts, axis=1))
    for g, span in enumerate(spans):
        p_ref[0, g] = probs[g]
        o_ref[0, span, :hc] = nn(probs[g].astype(bf16), stacked(v[span], hc)).astype(bf16)
    o_ref[0, :, hc:] = jnp.zeros((o_ref.shape[1], o_ref.shape[2] - hc), bf16)
    add = nt(o_ref[0, :, :hc], w[:, 3 * hc :])

    accumulate(acc_ref, step, add)

    @pl.when(step == pl.num_programs(0) - 1)
    def _():
        a = acc_ref[...] + vec_ref[0:1, :] + x_ref[...].astype(f32)
        normed, inverse = normalize(a)
        n1 = normed * vec_ref[1:2, :] + vec_ref[2:3, :]
        n1_ref[...] = n1
        x1_ref[...] = normed
        r1_ref[...] = inverse
        low = n1.astype(bf16)
        n1b_ref[...] = low
        turned = low.T
        n1t_ref[...] = turned[: low.shape[1] // 2]
        n1s_ref[...] = turned[low.shape[1] // 2 :]


def up_forward(n_ref, w0_ref, w1_ref, w2_ref, w3_ref, b_ref, z_ref, d_ref):
    u = nn(n_ref[...], rows_of((w0_ref, w1_ref, w2_ref, w3_ref))) + b_ref[0]
    phi = 0.5 + 0.5 * lax.erf(u * (0.5**0.5))
    z_ref[0] = (u * phi).astype(bf16)
    d_ref[0] = phi + u * (jnp.exp(-0.5 * u * u) * 0.3989422804014327)


def down_forward(z_ref, w0_ref, w1_ref, w2_ref, w3_ref, n1_ref, vec_ref, segc_ref, segr_ref, pg_ref,
                 pooled_ref, db_ref, dbb_ref, dbt_ref, dbs_ref, sums_ref, acc_ref):
    step = pl.program_id(0)
    add = nt(z_ref[0], rows_of((w0_ref, w1_ref, w2_ref, w3_ref)))

    accumulate(acc_ref, step, add)

    @pl.when(step == pl.num_programs(0) - 1)
    def _():
        rows, length = segr_ref.shape
        segs = pg_ref.shape[1]
        b = acc_ref[...] + vec_ref[3:4, :] + n1_ref[...]
        x2, r2 = normalize(b)
        y = x2 * vec_ref[4:5, :] + vec_ref[5:6, :]
        grads = []
        for g in range(rows):
            span = slice(g * length, (g + 1) * length)
            ids = lax.broadcasted_iota(jnp.int32, (segs, length), 0)
            hot_t = (ids == segr_ref[g : g + 1, :]).astype(f32)
            idc = lax.broadcasted_iota(jnp.int32, (length, segs), 1)
            hot = (idc == segc_ref[span, :]).astype(f32)
            count = jnp.sum(hot_t, axis=1, keepdims=True)
            sums = lax.dot_general(hot_t, y[span, :], (((1,), (0,)), ((), ())),
                                   precision=HI, preferred_element_type=f32)
            pooled_ref[g] = sums / count
            grads.append(lax.dot_general(hot, pg_ref[g] / count, (((1,), (0,)), ((), ())),
                                         precision=HI, preferred_element_type=f32))
        dy = jnp.concatenate(grads, axis=0)
        db = normalize_back(dy * vec_ref[4:5, :], x2, r2)
        db_ref[...] = db
        low = db.astype(bf16)
        dbb_ref[...] = low
        turned = low.T
        dbt_ref[...] = turned[: low.shape[1] // 2]
        dbs_ref[...] = turned[low.shape[1] // 2 :]
        sums_ref[0:1, :] = col_sum(db)
        sums_ref[1:2, :] = col_sum(dy * x2)
        sums_ref[2:3, :] = col_sum(dy)


def put(grad, ref):
    ref[:, :, :BLK, :] = grad.astype(bf16).reshape(grad.shape[0] // BLK, 1, BLK, grad.shape[1])


def hidden_backward(dbb_ref, w0_ref, w1_ref, w2_ref, w3_ref, d_ref, du_ref, bu_ref):
    du = (nn(dbb_ref[...], rows_of((w0_ref, w1_ref, w2_ref, w3_ref))) * d_ref[0]).astype(bf16)
    du_ref[0] = du
    bu_ref[0] = col_sum(du.astype(f32))


def step_value(refs, width):
    if len(refs) == 1:
        return refs[0][0, :, :width]
    return jnp.where(pl.program_id(0) < pl.num_programs(0) // 2, refs[0][0, :, :width], refs[1][0, :, :width])


def weight_gradient(groups, vectors, which, *refs):
    refs = list(refs)
    parts = []
    for pairs, split, width in groups:
        total = None
        for _ in range(pairs):
            rows = refs.pop(0)
            half = rows.shape[0] // 2
            rows = rows[...] if which is None else rows[which * half : (which + 1) * half, :]
            add = nn(rows, step_value([refs.pop(0) for _ in range(split)], width))
            total = add if total is None else total + add
        parts.append(total)
    grad = jnp.concatenate(parts, axis=1)
    extra = sum(refs.pop(0)[0].astype(f32) for _ in range(vectors)) if vectors else None
    half = grad.shape[0] // len(refs)
    for n, ref in enumerate(refs):
        put(grad[n * half : (n + 1) * half], ref)
        if vectors:
            for j in range(ref.shape[0]):
                at = (n if which is None else which) * ref.shape[0] + j
                row = extra[at : at + 1]
                tail = ref.shape[2] - BLK
                ref[j, 0, BLK:, :] = jnp.where(iota((tail, row.shape[1]), 0) == 0, row, 0.0).astype(bf16)


def norm_backward(du_ref, w0_ref, w1_ref, w2_ref, w3_ref, db_ref, x1_ref, r1_ref, vec_ref,
                  da_ref, dab_ref, dat_ref, das_ref, sums_ref, acc_ref):
    step = pl.program_id(0)
    accumulate(acc_ref, step, nt(du_ref[0], rows_of((w0_ref, w1_ref, w2_ref, w3_ref))))

    @pl.when(step == pl.num_programs(0) - 1)
    def _():
        dn1 = acc_ref[...].astype(bf16).astype(f32) + db_ref[...]
        da = normalize_back(dn1 * vec_ref[1:2, :], x1_ref[...], r1_ref[...])
        da_ref[...] = da
        low = da.astype(bf16)
        dab_ref[...] = low
        turned = low.T
        dat_ref[...] = turned[: low.shape[1] // 2]
        das_ref[...] = turned[low.shape[1] // 2 :]
        sums_ref[0:1, :] = col_sum(da)
        sums_ref[1:2, :] = col_sum(dn1 * x1_ref[...])
        sums_ref[2:3, :] = col_sum(dn1)


def attention_backward(sizes, dab_ref, w0_ref, w1_ref, w2_ref, w3_ref, qkv_ref, p_ref, s1_ref, s2_ref, gu_ref, hd_ref, he_ref,
                       low_ref, high_ref, keep_ref, send_ref, bq_ref, bv_ref, dqkv_ref):
    step = pl.program_id(0)
    hc = bq_ref.shape[-1]
    dab = dab_ref[...]
    w = rows_of([r.at[:, :, :, 3 * hc :] for r in (w0_ref, w1_ref, w2_ref, w3_ref)])
    do = nn(dab, w).astype(bf16)
    qkv = qkv_ref[0]
    rows, length = p_ref.shape[1], p_ref.shape[2]
    spans = [slice(g * length, (g + 1) * length) for g in range(rows)]
    q = [qkv[span, :hc] for span in spans]
    k = [stacked(qkv[span, hc : 2 * hc], hc) for span in spans]
    dps = [nt(do[span], stacked(qkv[span, 2 * hc :], hc)) for span in spans]
    dss = []
    for g in range(rows):
        parts = []
        for p, dp in zip(sections(p_ref[0, g], length), sections(dps[g], length)):
            pd = p * dp
            parts.append((pd - p * jnp.sum(pd, axis=-1, keepdims=True)).astype(bf16))
        dss.append(jnp.concatenate(parts, axis=1))
    for g, span in enumerate(spans):
        dqkv_ref[span, :hc] = (nn(dss[g], k[g]) * SCALE).astype(bf16)
        dqkv_ref[span, hc : 2 * hc] = own_columns(tn(dss[g], q[g]), hc).astype(bf16)
        dqkv_ref[span, 2 * hc : 3 * hc] = own_columns(tn(p_ref[0, g].astype(bf16), do[span]), hc).astype(bf16)
    dqkv_ref[:, 3 * hc :] = jnp.zeros((dqkv_ref.shape[0], dqkv_ref.shape[1] - 3 * hc), bf16)
    dqkv = dqkv_ref[...]
    half_steps = pl.num_programs(0) // 2

    @pl.when(step < half_steps)
    def _():
        low_ref[0] = dqkv

    @pl.when(step >= half_steps)
    def _():
        high_ref[0] = dqkv

    bq_ref[step] = col_sum(dqkv[:, :hc].astype(f32))
    bv_ref[step] = col_sum(dqkv[:, 2 * hc : 3 * hc].astype(f32))

    @pl.when(step == pl.num_programs(0) - 1)
    def _():
        d_rows = jnp.concatenate([s1_ref[...], s2_ref[...]], axis=0)
        rows = write_vectors(d_rows, (bq_ref[...], bv_ref[...], gu_ref[...]), hd_ref[...], he_ref[...], sizes)
        half, n_t = rows.shape[0] // 2, bq_ref.shape[0]
        rows = jnp.concatenate([rows, jnp.zeros((rows.shape[0], keep_ref.shape[-1] - rows.shape[1]), f32)], axis=1)
        for n, ref in enumerate((keep_ref, send_ref)):
            for t in range(n_t):
                for j in range(half // n_t):
                    at = n * half + j * n_t + t
                    ref[t, j : j + 1, :] = rows[at : at + 1]


def input_backward(low_ref, high_ref, w0_ref, w1_ref, w2_ref, w3_ref, da_ref, perm_ref, dx_ref, acc_ref):
    step = pl.program_id(0)
    cols = 3 * w0_ref.shape[-1] // 4
    w = rows_of((w0_ref, w1_ref, w2_ref, w3_ref))
    add = nt(step_value((low_ref, high_ref), cols), w[:, :cols])

    accumulate(acc_ref, step, add)

    @pl.when(step == pl.num_programs(0) - 1)
    def _():
        dx = acc_ref[...] + da_ref[...]
        high = dx.astype(bf16)
        rest = dx - high.astype(f32)
        mid = rest.astype(bf16)
        low = (rest - mid.astype(f32)).astype(bf16)
        perm = perm_ref[...]
        dx_ref[...] = nt(high, perm) + nt(mid, perm) + nt(low, perm)


def whole(a):
    nd = len(a.shape)
    return pl.BlockSpec(a.shape, lambda s: (0,) * nd, pipeline_mode=pl.Buffered(1))


def lead(a):
    nd = len(a.shape)
    return pl.BlockSpec((1,) + a.shape[1:], lambda s: (s,) + (0,) * (nd - 1))


def weight(a):
    return pl.BlockSpec((a.shape[0], 1, BLK, a.shape[3]), lambda s: (0, s, 0, 0))


def weight_t(a):
    return pl.BlockSpec((1, a.shape[1], BLK, a.shape[3]), lambda s: (s, 0, 0, 0))


def half_spec(h):
    return pl.BlockSpec((h.shape[0], 1) + h.shape[2:], lambda s: (0, s, 0, 0))


def sds(shape, dtype):
    return jax.ShapeDtypeStruct(shape, dtype)


def far(shape, dtype):
    return pltpu.HBM(shape, dtype)


def call(body, n_t, micros, ins, outs, scratch=()):
    return pl.pallas_call(
        body,
        grid=(n_t,),
        in_specs=[s for _, s in ins],
        out_specs=[s for _, s in outs],
        out_shape=[a for a, _ in outs],
        scratch_shapes=list(scratch),
        compiler_params=pltpu.CompilerParams(
            dimension_semantics=("arbitrary",), vmem_limit_bytes=VMEM_LIMIT
        ),
        cost_estimate=pl.CostEstimate(flops=int(micros * COST), transcendentals=0, bytes_accessed=0),
    )(*[a for a, _ in ins])


def flips(n_dp, n_t):
    size = n_dp * n_t
    core = n_t
    x_bit, y_bit = 2 * core, 4 * core

    def table(bit_of):
        return [(i, i ^ bit_of(i)) for i in range(size)]

    return {
        "Z": [table(lambda i, d=d: d) for d in range(1, n_t)],
        "C": [table(lambda i: core)],
        "2": [table(lambda i: x_bit if i & core else y_bit)],
        "3": [table(lambda i: y_bit if i & core else x_bit)],
    }


def after(value, *done):
    return lax.optimization_barrier((value, *done))[0] if done else value


def swap(value, tables, *done):
    return lax.ppermute(after(value, *done), AXES, tables["C"][0])


class Gather:
    def __init__(self, value, tables):
        self.held, self.tables = [value[None]], tables

    def send(self, name, *done, parts=None, tables=None):
        sent = self.held if parts is None else [self.held[j] for j in parts]
        return [lax.ppermute(after(h, *done), AXES, t) for t in self.tables[name][tables or slice(None)] for h in sent]

    def take(self, name, got):
        self.held = [jnp.concatenate(self.held + got)] if name in "Z2" else self.held + got
        return got

    def stage(self, name, *done, parts=None):
        return self.take(name, self.send(name, *done, parts=parts))

    def pieces(self, *lead):
        return [h.reshape(*lead, *h.shape[1:]) for h in self.held]


class Scatter:
    def __init__(self, keep, send, tables):
        self.keep, self.send, self.tables = keep, [send], tables

    def stage(self, name, parts, *done, cut=1):
        tables = self.tables[name]
        pieces = len(self.send) // len(tables)
        got = [lax.ppermute(after(s, *done), AXES, tables[n // pieces]) for n, s in enumerate(self.send)]
        size = self.keep.shape[0] // parts // cut

        def piece(n):
            at = n * size
            total = self.keep[at : at + size].astype(f32)
            for t in range(len(tables)):
                mine = got[t * pieces : (t + 1) * pieces]
                wide = mine[0].shape[0]
                total = total + mine[at // wide][at % wide : at % wide + size].astype(f32)
            return total

        self.send = [piece(n).astype(bf16) for n in range(cut, parts * cut)]
        kept = [piece(n) for n in range(cut)]
        self.keep = kept[0] if cut == 1 else jnp.concatenate(kept)
        return got


def per_device(
    hidden_in, segment_ids, pooled_grad, qkv_weight, qv_bias, out_weight, out_bias,
    norm1_gain, norm1_shift, up_weight, up_bias, down_weight_in, down_bias, norm2_gain, norm2_shift,
):
    n_dp, n_t = lax.axis_size("dp"), lax.axis_size("tensor")
    at_dp, at_t = lax.axis_index("dp"), lax.axis_index("tensor")
    hc, fc = qkv_weight.shape[2], up_weight.shape[1]
    rows = qkv_weight.shape[1]
    D = rows * n_dp
    micro, tokens = hidden_in.shape[0], hidden_in.shape[1]
    seqs, L = segment_ids.shape[1], segment_ids.shape[2]
    G, T = micro * seqs, micro * tokens
    segs = pooled_grad.shape[2]
    n_i = D // BLK
    pairwise = (n_dp, n_t) == (8, 4) and 4 * hc == fc

    d_parts = [out_bias, norm1_gain, norm1_shift, down_bias, norm2_gain, norm2_shift]
    e_parts = [qv_bias[0], qv_bias[1], up_bias]
    dv = out_bias.shape[0]
    n_vec = sum(p.shape[0] for p in d_parts + e_parts)
    nd = len(d_parts) * dv

    sizes = (6, dv, up_bias.shape[0], D, hc, fc, n_t) if pairwise else (6, D // (n_i * n_t), n_t * fc // (n_i * n_t), D, hc, fc, n_t)
    slot = jnp.arange(n_i * n_t)
    rel = jnp.arange(n_i)
    if pairwise:
        tables = flips(n_dp, n_t)
        packed = (qkv_weight, out_weight, *[p[None] for p in d_parts], qv_bias, up_bias[None])
        packed = pl.pallas_call(pack, out_shape=sds((BLK + 8, 4 * hc), bf16))(*packed)
        first, middle, last = Gather(packed, tables), Gather(up_weight, tables), Gather(down_weight_in.T, tables)
        done = first.stage("Z") + last.stage("2")

        core = (at_dp & 1) ^ (rel >> 2)
        s3, s2 = (rel >> 1) & 1, rel & 1
        dy, dx = jnp.where(core == 0, s2, s3), jnp.where(core == 0, s3, s2)
        absolute = ((((at_dp >> 2) & 1) ^ dy) << 2) | ((((at_dp >> 1) & 1) ^ dx) << 1) | core
        i_p = jnp.broadcast_to(absolute[:, None], (n_i, n_t)).reshape(-1)
        t_p = jnp.broadcast_to((at_t ^ jnp.arange(n_t))[None], (n_i, n_t)).reshape(-1)
        to_d = jnp.broadcast_to(rel[:, None], (n_i, n_t)).reshape(-1) * n_t + t_p
        to_e = (((i_p * n_t) // n_i) ^ at_t) * n_i + (i_p * n_t + t_p) % n_i
    else:
        absolute, to_d, to_e = rel, slot, slot
    hot_d = (to_d[None, :] == slot[:, None]).astype(bf16)
    hot_e = (to_e[None, :] == slot[:, None]).astype(bf16)
    lane = jnp.arange(D)
    same_block = jnp.repeat(jnp.repeat((absolute[:, None] == rel[None, :]).T, BLK, axis=0), BLK, axis=1)
    perm = (same_block & ((lane[:, None] % BLK) == (lane[None, :] % BLK))).astype(bf16)
    turned = (D // 2, T)
    x, x_keep, x_send = pl.pallas_call(
        reorder, out_shape=[sds((T, D), bf16), sds(turned, bf16), sds(turned, bf16)], compiler_params=SMALL
    )(hidden_in.reshape(T, D), perm)
    pg = jnp.einsum("gsd,de->gse", pooled_grad.reshape(G, segs, D), perm.astype(f32), precision=HI)
    seg_r = segment_ids.reshape(G, L)
    seg_c = segment_ids.reshape(T, 1)

    if pairwise:
        done = first.stage("2", *done, x, x_keep, x_send, pg, hot_d, hot_e) + middle.stage("Z", *done)
        x_other = swap(x_send, tables, *done)
        near_z = last.send("Z", *done, tables=slice(0, 2))
        done = first.stage("3", *done) + middle.stage("2", *done) + near_z
        first.stage("C", *done)
        x = after(x, x_other)
        got_u3, far_z = middle.send("3", *done), last.send("Z", *done, tables=slice(2, None))
        w_qo = first.pieces(2, n_t)
    else:
        heads_in = [qkv_weight[0], qkv_weight[1], qkv_weight[2], out_weight.T]
        main = jnp.concatenate([*heads_in, up_weight, down_weight_in.T], axis=1)
        vec = jnp.concatenate(d_parts + e_parts)
        full = lax.all_gather(lax.all_gather(main, "dp", axis=0, tiled=True), "tensor", axis=0)
        full = full.reshape(n_t, n_i, BLK, -1).transpose(1, 0, 2, 3)
        vecs = lax.all_gather(lax.all_gather(vec, "tensor"), "dp").reshape(n_dp * n_t, -1)
        cuts = [j * dv for j in range(9)] + [n_vec]
        rows8 = jnp.concatenate([vecs[:, a:b].reshape(n_i * n_t, -1) for a, b in zip(cuts[:-1], cuts[1:])], axis=1)
        rows8 = jnp.pad(rows8.reshape(n_i, n_t, 1, -1), ((0, 0), (0, 0), (0, 7), (0, 4 * hc - rows8.shape[1])))
        quarters = [full[j * n_i // 4 : (j + 1) * n_i // 4] for j in range(4)]
        w_qo = [
            jnp.concatenate([w[..., : 4 * hc], rows8[j * n_i // 4 : (j + 1) * n_i // 4]], axis=2)
            for j, w in enumerate(quarters)
        ]
        w_up = [w[..., 4 * hc : 4 * hc + fc] for w in quarters]
        w_down = [w[..., 4 * hc + fc :].transpose(1, 0, 2, 3) for w in quarters]

    hl = hc // HD * L
    o_wide, q_wide = -(-hc // 128) * 128, -(-3 * hc // 128) * 128

    def leads(*arrays):
        return [(a, lead(a)) for a in arrays]

    def wholes(*arrays):
        return [(a, whole(a)) for a in arrays]

    def weights(*arrays):
        return [(a, weight(a)) for a in arrays]

    def weights_t(*arrays):
        return [(a, weight_t(a)) for a in arrays]

    tails = [
        (w, pl.BlockSpec((w.shape[0], n_t, 8, w.shape[3]), lambda s: (0, 0, BLK // 8, 0), pipeline_mode=pl.Buffered(1)))
        for w in w_qo
    ]
    qkv, prob, o, n1, x1, r1, n1b, n1_keep, n1_send, vec_d, b_u = call(
        partial(attention_forward, sizes), n_t, 10,
        wholes(x) + weights(*w_qo) + tails + wholes(hot_d, hot_e, seg_c, seg_r),
        leads(far((n_t, T, 3 * hc), bf16), far((n_t, G, L, hl), f32), far((n_t, T, o_wide), bf16))
        + wholes(sds((T, D), f32), far((T, D), f32), far((T, 1), f32), sds((T, D), bf16), far(turned, bf16), far(turned, bf16))
        + wholes(sds((6, D), f32), sds((n_t, 1, fc), f32)),
        [pltpu.VMEM((T, D), f32), pltpu.VMEM((n_t, 1, hc), f32), pltpu.VMEM((n_t, 1, hc), f32)],
    )
    if pairwise:
        last.take("Z", near_z + [after(g, n1b) for g in far_z])
        middle.take("3", [after(g, n1b) for g in got_u3])
        last.stage("3", *got_u3)
        middle.stage("C", n1b, *far_z)
        last.take("C", last.send("C", n1b, parts=(0,)))
        last.take("C", last.send("C", parts=(1,)))
        w_up, w_down = middle.pieces(2, n_t), last.pieces(n_t, 2)
        n1_other = swap(n1_send, tables)
        o_other = swap(o, tables)
        b_u = after(b_u, n1_other, o_other)
    z, dgelu = call(
        up_forward, n_t, 4, wholes(n1b) + weights(*w_up) + leads(b_u),
        leads(sds((n_t, T, fc), bf16), sds((n_t, T, fc), f32)),
    )
    if pairwise:
        z_other = swap(z, tables)
    pooled, db, dbb, db_keep, db_send, sums2 = call(
        down_forward, n_t, 5.5, leads(z) + weights_t(*w_down) + wholes(n1, vec_d, seg_c, seg_r, pg),
        wholes(sds((G, segs, D), f32), sds((T, D), f32), sds((T, D), bf16), sds(turned, bf16), sds(turned, bf16), sds((3, D), f32)),
        [pltpu.VMEM((T, D), f32)],
    )

    def gradient(groups, vectors=(), at_once=True):
        ins, kinds = [], []
        for width, *pairs in groups:
            kinds.append((len(pairs), len(pairs[0][1]), width))
            for lhs, values in pairs:
                ins += wholes(lhs) + (leads(*values) if len(values) == 1 else halved(*values))
        out = sds((n_i // 4, n_t, BLK + (8 if vectors else 0), sum(k[2] for k in kinds)), bf16)

        def share(which):
            return call(
                partial(weight_gradient, kinds, len(vectors), which), n_t, 2, ins + leads(*vectors),
                [(out, half_spec(out))] * (2 if which is None else 1),
            )

        return share(None) if at_once else (share(0)[0], share(1)[0])

    def halved(low, high):
        block = (1,) + low.shape[1:]
        return [
            (low, pl.BlockSpec(block, lambda s: (jnp.minimum(s, n_t // 2 - 1), 0, 0))),
            (high, pl.BlockSpec(block, lambda s: (jnp.maximum(s - n_t // 2, 0), 0, 0))),
        ]

    def flat(a):
        return a.reshape((-1,) + a.shape[2:])

    du, g_bu = call(
        hidden_backward, n_t, 3.5, wholes(dbb) + weights_t(*w_down) + leads(dgelu),
        leads(sds((n_t, T, fc), bf16), sds((n_t, 1, fc), f32)),
    )
    if pairwise:
        db_other = swap(db_send, tables)
        du_other = swap(du, tables)
        down_keep, down_send = gradient([[fc, (after(db_keep, g_bu), [z]), (db_other, [z_other])]], at_once=False)
        s_down = Scatter(flat(down_keep), flat(down_send), tables)
        got_d3 = s_down.stage("3", 2)
        du_next = after(du, down_send)
        dab_after = down_keep
    else:
        du_next = du
    da, dab, da_keep, da_send, sums1 = call(
        norm_backward, n_t, NORM, leads(du_next) + weights(*w_up) + wholes(db, x1, r1, vec_d),
        wholes(sds((T, D), f32), sds((T, D), bf16), sds(turned, bf16), sds(turned, bf16), sds((3, D), f32)),
        [pltpu.VMEM((T, D), f32)],
    )
    if pairwise:
        da_other = swap(da_send, tables)
        up_keep, up_send = gradient([[fc, (after(n1_keep, da_keep), [du]), (n1_other, [du_other])]])
        s_up = Scatter(flat(up_keep), flat(up_send), tables)
        got_u3 = s_up.stage("3", 2)
        dab = after(dab, up_keep)
    rows = sds((n_t, n_i // 2, 4 * hc), f32)
    if pairwise:
        dab = after(dab, da_other, dab_after, *got_d3)
    dq_half = sds((n_t // 2, T, q_wide), bf16)
    *dq, v_keep, v_send = call(
        partial(attention_backward, sizes), n_t, 8,
        wholes(dab) + weights(*w_qo) + leads(qkv, prob) + wholes(sums1, sums2, g_bu, hot_d, hot_e),
        halved(dq_half, dq_half) + wholes(rows, rows),
        [pltpu.VMEM((n_t, 1, hc), f32), pltpu.VMEM((n_t, 1, hc), f32), pltpu.VMEM((T, q_wide), bf16)],
    )
    if pairwise:
        dq_other = [swap(d, tables) for d in dq]
        v_other = swap(v_send, tables)
        got_d2 = s_down.stage("2", n_t)
    pooled = jnp.einsum("gse,de->gsd", pooled, perm.astype(f32), precision=HI)
    if pairwise:
        x_now = after(x_keep, *got_u3)
        qo_keep, qo_send = gradient(
            [[3 * hc, (x_now, dq), (x_other, dq_other)], [hc, (da_keep, [o]), (da_other, [o_other])]], (v_keep, v_other)
        )
        s_qo = Scatter(flat(qo_keep), flat(qo_send), tables)
        got_u2 = s_up.stage("2", n_t)
        s_qo.stage("3", 2, *got_d2, *got_u2, pooled, cut=CUT)
        both = Scatter(jnp.concatenate([s_down.keep, s_up.keep]), None, tables)
        both.send = [jnp.concatenate([a, b]) for a, b in zip(s_down.send, s_up.send, strict=True)]
        got_z = both.stage("Z", 1)
        dq = [after(d, qo_keep) for d in dq]
    dx = call(
        input_backward, n_t, 4, halved(*dq) + weights(*w_qo) + wholes(da, perm), wholes(sds((T, D), f32)),
        [pltpu.VMEM((T, D), f32)],
    )[0]

    if pairwise:
        s_qo.stage("2", n_t, dx)
        s_qo.stage("Z", 1, *got_z)
        g_down, g_up, g_qo = both.keep[0], both.keep[1], s_qo.keep[0]
        g_v = g_qo[BLK, :n_vec]
        g_qo = g_qo[:BLK]
    else:
        def joined(*halves_of):
            g = jnp.concatenate([part[:, :, :BLK] for half in halves_of for part in half])
            return g.transpose(1, 0, 2, 3).reshape(n_t, D, -1)

        x_h, n1_h, db_h, da_h = (x_keep, x_send), (n1_keep, n1_send), (db_keep, db_send), (da_keep, da_send)
        g_full = jnp.concatenate([
            joined(*[gradient([[3 * hc, (x_h[j], dq)], [hc, (da_h[j], [o])]]) for j in range(2)]),
            joined(*[gradient([[fc, (n1_h[j], [du])]]) for j in range(2)]),
            joined(*[gradient([[fc, (db_h[j], [z])]]) for j in range(2)]),
        ], axis=2)
        mine = lax.psum_scatter(g_full, "tensor", scatter_dimension=0)
        mine = lax.psum_scatter(mine, "dp", scatter_dimension=0, tiled=True).astype(f32)
        g_qo, g_up, g_down = mine[:, : 4 * hc], mine[:, 4 * hc : 4 * hc + fc], mine[:, 4 * hc + fc :]
        g_rows = jnp.stack([v_keep, v_send]).transpose(0, 2, 1, 3).reshape(n_i * n_t, -1)
        dv_c, bu_c = sizes[1], sizes[2]
        cuts = [j * dv_c for j in range(9)] + [8 * dv_c + bu_c]
        g_v = jnp.concatenate(
            [g_rows[:, a:b].reshape(n_dp * n_t, -1) for a, b in zip(cuts[:-1], cuts[1:])], axis=1
        )
        g_v = lax.psum_scatter(g_v, AXES, scatter_dimension=0)
    vo = [g_v[j * dv : (j + 1) * dv] for j in range(8)]
    return (
        pooled.reshape(micro, seqs, segs, D),
        dx.reshape(micro, tokens, D),
        jnp.stack([g_qo[:, c * hc : (c + 1) * hc] for c in range(3)]),
        jnp.stack([vo[6], vo[7]]),
        g_qo[:, 3 * hc :].T,
        vo[0], vo[1], vo[2],
        g_up,
        g_v[8 * dv :],
        g_down.T,
        vo[3], vo[4], vo[5],
    )


def solution(mesh):
    both = P(AXES)
    row3 = P(None, AXES)
    return jax.shard_map(
        per_device,
        mesh=mesh,
        in_specs=(
            row3, row3, row3, P(None, "dp", "tensor"), row3, P("tensor", "dp"), both, both, both,
            P("dp", "tensor"), both, P("tensor", "dp"), both, both, both,
        ),
        out_specs=(
            row3, row3, P(None, "dp", "tensor"), row3, P("tensor", "dp"), both, both, both,
            P("dp", "tensor"), both, P("tensor", "dp"), both, both, both,
        ),
        check_vma=False,
    )
```

```python
from functools import partial

import jax
import jax.numpy as jnp
from jax import lax
from jax.experimental import pallas as pl
from jax.experimental.pallas import tpu as pltpu
from jax.sharding import PartitionSpec as P

HD = 64
EPS = 1e-12
NEG = -1000000000.0
SCALE = float(HD) ** -0.5
AXES = ("dp", "tensor")
f32 = jnp.float32
bf16 = jnp.bfloat16
HI = lax.Precision.HIGHEST
BLK = 96
VMEM_LIMIT = 24 * 1024 * 1024
COST = 30_000_000
NORM = 2000
CUT = 4
SMALL = pltpu.CompilerParams(vmem_limit_bytes=8 * 1024 * 1024)


def nn(a, b):
    return lax.dot_general(a, b, (((1,), (0,)), ((), ())), preferred_element_type=f32)


def nt(a, b):
    return lax.dot_general(a, b, (((1,), (1,)), ((), ())), preferred_element_type=f32)


def tn(a, b):
    return lax.dot_general(a, b, (((0,), (0,)), ((), ())), preferred_element_type=f32)


def mean_last(v):
    return jnp.sum(v, axis=-1, keepdims=True) * (1.0 / v.shape[-1])


def normalize(values):
    center = values - mean_last(values)
    inverse = lax.rsqrt(mean_last(center * center) + EPS)
    return center * inverse, inverse


def normalize_back(scaled, normed, inverse):
    return inverse * (scaled - mean_last(scaled) - normed * mean_last(scaled * normed))


def col_sum(v):
    return jnp.sum(v, axis=0, keepdims=True)


def pack(qkv_ref, out_ref, ob_ref, g1_ref, s1_ref, db_ref, g2_ref, s2_ref, qv_ref, ub_ref, first_ref):
    rows, hc = qkv_ref.shape[1:]
    eye = (lax.broadcasted_iota(jnp.int32, (rows, rows), 0) == lax.broadcasted_iota(jnp.int32, (rows, rows), 1)).astype(bf16)
    for c in range(3):
        first_ref[:rows, c * hc : (c + 1) * hc] = qkv_ref[c]
    first_ref[:rows, 3 * hc :] = nt(eye, out_ref[...]).astype(bf16)
    parts = [r[...].astype(f32) for r in (ob_ref, g1_ref, s1_ref, db_ref, g2_ref, s2_ref, qv_ref)]
    short = jnp.concatenate(parts, axis=0).astype(bf16)
    count, size = short.shape
    wide = first_ref.shape[1]

    def spread(values, at):
        lane = lax.broadcasted_iota(jnp.int32, (values.shape[1], wide), 1) - at
        return nn(values, (lax.rem(lane + values.shape[1] * wide, values.shape[1]) == lax.broadcasted_iota(jnp.int32, lane.shape, 0)).astype(bf16))

    lane = lax.broadcasted_iota(jnp.int32, (count, wide), 1)
    start = lax.broadcasted_iota(jnp.int32, (count, wide), 0) * size
    row = col_sum(jnp.where((lane >= start) & (lane < start + size), spread(short, 0), 0.0))
    total, long = count * size, ub_ref.shape[1]
    lane = lax.broadcasted_iota(jnp.int32, (1, wide), 1)
    row = jnp.where((lane >= total) & (lane < total + long), spread(ub_ref[...], total), row)
    extra = first_ref.shape[0] - rows
    here = lax.broadcasted_iota(jnp.int32, (extra, wide), 0)
    first_ref[rows:, :] = jnp.where(here == 0, row, 0.0).astype(bf16)


def reorder(h_ref, perm_ref, x_ref, keep_ref, send_ref):
    x = nn(h_ref[...], perm_ref[...]).astype(bf16)
    x_ref[...] = x
    turned = x.T
    keep_ref[...] = turned[: x.shape[1] // 2]
    send_ref[...] = turned[x.shape[1] // 2 :]


def stacked(values, hc):
    head = lax.broadcasted_iota(jnp.int32, (1, hc), 1) // HD
    return jnp.concatenate([values * (head == h).astype(f32).astype(bf16) for h in range(hc // HD)], axis=0)


def own_columns(blocks, hc):
    n_heads = hc // HD
    length = blocks.shape[0] // n_heads
    head = lax.broadcasted_iota(jnp.int32, (1, hc), 1) // HD
    out = blocks[:length]
    for h in range(1, n_heads):
        out = jnp.where(head == h, blocks[h * length : (h + 1) * length], out)
    return out


def sections(values, length):
    return [values[:, c : c + length] for c in range(0, values.shape[1], length)]


def rows_of(refs):
    return jnp.concatenate([r[...].reshape(-1, r.shape[3]) for r in refs], axis=0)


def thirds(values):
    high = values.astype(bf16)
    rest = values - high.astype(f32)
    middle = rest.astype(bf16)
    return high, middle, (rest - middle.astype(f32)).astype(bf16)


def accumulate(acc_ref, step, add):
    @pl.when(step == 0)
    def _():
        acc_ref[...] = add

    @pl.when(step > 0)
    def _():
        acc_ref[...] += add


def iota(shape, axis):
    return lax.broadcasted_iota(jnp.int32, shape, axis)


def picks(count, first, wide, size):
    return (iota((count, wide), 0) == first + lax.rem(iota((1, wide), 1), size)).astype(bf16)


def belongs(count, wide, size, period):
    lane, row = iota((1, wide), 1), lax.rem(iota((count, 1), 0), period)
    return (lane >= row * size) & (lane < (row + 1) * size)


def read_vectors(rows, hot_d, hot_e, sizes):
    n_d, dv, bu, width, hc, fc, n_t = sizes
    count = rows.shape[0]
    per = count // n_t
    d_all = nn(hot_d, rows[:, : n_d * dv]).astype(bf16)
    mine = belongs(count, width, dv, count)
    d_rows = [col_sum(jnp.where(mine, nn(d_all, picks(n_d * dv, j * dv, width, dv)), 0.0)) for j in range(n_d)]
    e_all = nn(hot_e, rows[:, n_d * dv : n_d * dv + 2 * dv + bu]).astype(bf16)
    out = []
    for first, size, wide in ((0, dv, hc), (dv, dv, hc), (2 * dv, bu, fc)):
        spread = jnp.where(belongs(count, wide, size, per), nn(e_all, picks(e_all.shape[1], first, wide, size)), 0.0)
        out.append(jnp.sum(spread.reshape(n_t, per, wide), axis=1, keepdims=True))
    return jnp.concatenate(d_rows, axis=0), out


def write_vectors(d_rows, e_rows, hot_d, hot_e, sizes):
    n_d, dv, bu, width, hc, fc, n_t = sizes
    count = hot_d.shape[0]
    per = count // n_t
    mine = belongs(count, width, dv, count)
    d_all = sum(
        nt(jnp.where(mine, d_rows[j : j + 1, :], 0.0).astype(bf16), picks(n_d * dv, j * dv, width, dv)) for j in range(n_d)
    ).astype(bf16)
    e_all = 0.0
    for value, first, size, wide in zip(e_rows, (0, dv, 2 * dv), (dv, dv, bu), (hc, hc, fc), strict=True):
        spread = jnp.broadcast_to(value, (n_t, per, wide)).reshape(count, wide)
        spread = jnp.where(belongs(count, wide, size, per), spread, 0.0).astype(bf16)
        e_all = e_all + nt(spread, picks(2 * dv + bu, first, wide, size))
    return jnp.concatenate([tn(hot_d, d_all), tn(hot_e, e_all.astype(bf16))], axis=1)


def attention_forward(sizes, x_ref, w0_ref, w1_ref, w2_ref, w3_ref, v0_ref, v1_ref, v2_ref, v3_ref, hd_ref, he_ref,
                      segc_ref, segr_ref, qkv_ref, p_ref, o_ref, n1_ref, x1_ref, r1_ref, n1b_ref, n1t_ref, n1s_ref,
                      vec_ref, bu_ref, acc_ref, bq_ref, bv_ref):
    step = pl.program_id(0)
    hc = bq_ref.shape[-1]

    @pl.when(step == 0)
    def _():
        rows = jnp.concatenate([r[:, :, 0, :].reshape(-1, r.shape[3]) for r in (v0_ref, v1_ref, v2_ref, v3_ref)], axis=0)
        d_rows, (b_q, b_v, b_u) = read_vectors(rows, hd_ref[...], he_ref[...], sizes)
        vec_ref[...] = d_rows
        bq_ref[...] = b_q
        bv_ref[...] = b_v
        bu_ref[...] = b_u

    rows, length = segr_ref.shape
    x = x_ref[...]
    w = rows_of((w0_ref, w1_ref, w2_ref, w3_ref))
    qkv = nn(x, w[:, : 3 * hc])
    q = (qkv[:, :hc] + bq_ref[step]).astype(bf16) * bf16(SCALE)
    k = qkv[:, hc : 2 * hc].astype(bf16)
    v = (qkv[:, 2 * hc :] + bv_ref[step]).astype(bf16)
    qkv_ref[0, :, :hc] = q
    qkv_ref[0, :, hc : 2 * hc] = k
    qkv_ref[0, :, 2 * hc :] = v
    spans = [slice(g * length, (g + 1) * length) for g in range(rows)]
    scores = [nt(q[span], stacked(k[span], hc)) for span in spans]
    probs = []
    for g, span in enumerate(spans):
        same = segc_ref[span, :] == segr_ref[g : g + 1, :]
        parts = []
        for s in sections(scores[g], length):
            s = jnp.where(same, s, NEG)
            e = jnp.exp(s - jnp.max(s, axis=-1, keepdims=True))
            parts.append(e * (1.0 / jnp.sum(e, axis=-1, keepdims=True)))
        probs.append(jnp.concatenate(parts, axis=1))
    for g, span in enumerate(spans):
        p_ref[0, g] = probs[g]
        o_ref[0, span, :hc] = nn(probs[g].astype(bf16), stacked(v[span], hc)).astype(bf16)
    o_ref[0, :, hc:] = jnp.zeros((o_ref.shape[1], o_ref.shape[2] - hc), bf16)
    add = nt(o_ref[0, :, :hc], w[:, 3 * hc :])

    accumulate(acc_ref, step, add)

    @pl.when(step == pl.num_programs(0) - 1)
    def _():
        a = acc_ref[...] + vec_ref[0:1, :] + x_ref[...].astype(f32)
        normed, inverse = normalize(a)
        n1 = normed * vec_ref[1:2, :] + vec_ref[2:3, :]
        n1_ref[...] = n1
        x1_ref[...] = normed
        r1_ref[...] = inverse
        low = n1.astype(bf16)
        n1b_ref[...] = low
        turned = low.T
        n1t_ref[...] = turned[: low.shape[1] // 2]
        n1s_ref[...] = turned[low.shape[1] // 2 :]


def up_forward(n_ref, w0_ref, w1_ref, w2_ref, w3_ref, b_ref, z_ref, d_ref):
    u = nn(n_ref[...], rows_of((w0_ref, w1_ref, w2_ref, w3_ref))) + b_ref[0]
    phi = 0.5 + 0.5 * lax.erf(u * (0.5**0.5))
    z_ref[0] = (u * phi).astype(bf16)
    d_ref[0] = phi + u * (jnp.exp(-0.5 * u * u) * 0.3989422804014327)


def down_forward(z_ref, w0_ref, w1_ref, w2_ref, w3_ref, n1_ref, vec_ref, segc_ref, segr_ref, pg_ref,
                 pooled_ref, db_ref, dbb_ref, dbt_ref, dbs_ref, sums_ref, acc_ref):
    step = pl.program_id(0)
    add = nt(z_ref[0], rows_of((w0_ref, w1_ref, w2_ref, w3_ref)))

    accumulate(acc_ref, step, add)

    @pl.when(step == pl.num_programs(0) - 1)
    def _():
        rows, length = segr_ref.shape
        segs = pg_ref.shape[1]
        b = acc_ref[...] + vec_ref[3:4, :] + n1_ref[...]
        x2, r2 = normalize(b)
        y = x2 * vec_ref[4:5, :] + vec_ref[5:6, :]
        grads = []
        for g in range(rows):
            span = slice(g * length, (g + 1) * length)
            hot_t = (iota((segs, length), 0) == segr_ref[g : g + 1, :]).astype(f32)
            count = jnp.sum(hot_t, axis=1, keepdims=True)
            hot_t = hot_t.astype(bf16)
            hot = (iota((length, segs), 1) == segc_ref[span, :]).astype(f32).astype(bf16)
            pooled_ref[g] = sum(nn(hot_t, part) for part in thirds(y[span, :])) / count
            grads.append(nn(jnp.concatenate([hot] * 3, axis=1), jnp.concatenate(thirds(pg_ref[g] / count), axis=0)))
        dy = jnp.concatenate(grads, axis=0)
        db = normalize_back(dy * vec_ref[4:5, :], x2, r2)
        db_ref[...] = db
        low = db.astype(bf16)
        dbb_ref[...] = low
        turned = low.T
        dbt_ref[...] = turned[: low.shape[1] // 2]
        dbs_ref[...] = turned[low.shape[1] // 2 :]
        sums_ref[0:1, :] = col_sum(db)
        sums_ref[1:2, :] = col_sum(dy * x2)
        sums_ref[2:3, :] = col_sum(dy)


def put(grad, ref):
    ref[:, :, :BLK, :] = grad.astype(bf16).reshape(grad.shape[0] // BLK, 1, BLK, grad.shape[1])


def hidden_backward(dbb_ref, w0_ref, w1_ref, w2_ref, w3_ref, d_ref, du_ref, bu_ref):
    du = (nn(dbb_ref[...], rows_of((w0_ref, w1_ref, w2_ref, w3_ref))) * d_ref[0]).astype(bf16)
    du_ref[0] = du
    bu_ref[0] = col_sum(du.astype(f32))


def step_value(refs, width):
    if len(refs) == 1:
        return refs[0][0, :, :width]
    return jnp.where(pl.program_id(0) < pl.num_programs(0) // 2, refs[0][0, :, :width], refs[1][0, :, :width])


def weight_gradient(groups, vectors, which, *refs):
    refs = list(refs)
    parts = []
    for pairs, split, width in groups:
        total = None
        for _ in range(pairs):
            rows = refs.pop(0)
            half = rows.shape[0] // 2
            rows = rows[...] if which is None else rows[which * half : (which + 1) * half, :]
            add = nn(rows, step_value([refs.pop(0) for _ in range(split)], width))
            total = add if total is None else total + add
        parts.append(total)
    grad = jnp.concatenate(parts, axis=1)
    extra = sum(refs.pop(0)[0].astype(f32) for _ in range(vectors)) if vectors else None
    half = grad.shape[0] // len(refs)
    for n, ref in enumerate(refs):
        put(grad[n * half : (n + 1) * half], ref)
        if vectors:
            for j in range(ref.shape[0]):
                at = (n if which is None else which) * ref.shape[0] + j
                row = extra[at : at + 1]
                tail = ref.shape[2] - BLK
                ref[j, 0, BLK:, :] = jnp.where(iota((tail, row.shape[1]), 0) == 0, row, 0.0).astype(bf16)


def norm_backward(du_ref, w0_ref, w1_ref, w2_ref, w3_ref, db_ref, x1_ref, r1_ref, vec_ref,
                  da_ref, dab_ref, dat_ref, das_ref, sums_ref, acc_ref):
    step = pl.program_id(0)
    accumulate(acc_ref, step, nt(du_ref[0], rows_of((w0_ref, w1_ref, w2_ref, w3_ref))))

    @pl.when(step == pl.num_programs(0) - 1)
    def _():
        dn1 = acc_ref[...].astype(bf16).astype(f32) + db_ref[...]
        da = normalize_back(dn1 * vec_ref[1:2, :], x1_ref[...], r1_ref[...])
        da_ref[...] = da
        low = da.astype(bf16)
        dab_ref[...] = low
        turned = low.T
        dat_ref[...] = turned[: low.shape[1] // 2]
        das_ref[...] = turned[low.shape[1] // 2 :]
        sums_ref[0:1, :] = col_sum(da)
        sums_ref[1:2, :] = col_sum(dn1 * x1_ref[...])
        sums_ref[2:3, :] = col_sum(dn1)


def attention_backward(sizes, dab_ref, w0_ref, w1_ref, w2_ref, w3_ref, qkv_ref, p_ref, s1_ref, s2_ref, gu_ref, hd_ref, he_ref,
                       low_ref, high_ref, keep_ref, send_ref, bq_ref, bv_ref, dqkv_ref):
    step = pl.program_id(0)
    hc = bq_ref.shape[-1]
    dab = dab_ref[...]
    w = rows_of([r.at[:, :, :, 3 * hc :] for r in (w0_ref, w1_ref, w2_ref, w3_ref)])
    do = nn(dab, w).astype(bf16)
    qkv = qkv_ref[0]
    rows, length = p_ref.shape[1], p_ref.shape[2]
    spans = [slice(g * length, (g + 1) * length) for g in range(rows)]
    q = [qkv[span, :hc] for span in spans]
    k = [stacked(qkv[span, hc : 2 * hc], hc) for span in spans]
    dps = [nt(do[span], stacked(qkv[span, 2 * hc :], hc)) for span in spans]
    dss = []
    for g in range(rows):
        parts = []
        for p, dp in zip(sections(p_ref[0, g], length), sections(dps[g], length)):
            pd = p * dp
            parts.append((pd - p * jnp.sum(pd, axis=-1, keepdims=True)).astype(bf16))
        dss.append(jnp.concatenate(parts, axis=1))
    for g, span in enumerate(spans):
        dqkv_ref[span, :hc] = (nn(dss[g], k[g]) * SCALE).astype(bf16)
        dqkv_ref[span, hc : 2 * hc] = own_columns(tn(dss[g], q[g]), hc).astype(bf16)
        dqkv_ref[span, 2 * hc : 3 * hc] = own_columns(tn(p_ref[0, g].astype(bf16), do[span]), hc).astype(bf16)
    dqkv_ref[:, 3 * hc :] = jnp.zeros((dqkv_ref.shape[0], dqkv_ref.shape[1] - 3 * hc), bf16)
    dqkv = dqkv_ref[...]
    half_steps = pl.num_programs(0) // 2

    @pl.when(step < half_steps)
    def _():
        low_ref[0] = dqkv

    @pl.when(step >= half_steps)
    def _():
        high_ref[0] = dqkv

    bq_ref[step] = col_sum(dqkv[:, :hc].astype(f32))
    bv_ref[step] = col_sum(dqkv[:, 2 * hc : 3 * hc].astype(f32))

    @pl.when(step == pl.num_programs(0) - 1)
    def _():
        d_rows = jnp.concatenate([s1_ref[...], s2_ref[...]], axis=0)
        rows = write_vectors(d_rows, (bq_ref[...], bv_ref[...], gu_ref[...]), hd_ref[...], he_ref[...], sizes)
        half, n_t = rows.shape[0] // 2, bq_ref.shape[0]
        rows = jnp.concatenate([rows, jnp.zeros((rows.shape[0], keep_ref.shape[-1] - rows.shape[1]), f32)], axis=1)
        for n, ref in enumerate((keep_ref, send_ref)):
            for t in range(n_t):
                for j in range(half // n_t):
                    at = n * half + j * n_t + t
                    ref[t, j : j + 1, :] = rows[at : at + 1]


def input_backward(low_ref, high_ref, w0_ref, w1_ref, w2_ref, w3_ref, da_ref, perm_ref, dx_ref, acc_ref):
    step = pl.program_id(0)
    cols = 3 * w0_ref.shape[-1] // 4
    w = rows_of((w0_ref, w1_ref, w2_ref, w3_ref))
    add = nt(step_value((low_ref, high_ref), cols), w[:, :cols])

    accumulate(acc_ref, step, add)

    @pl.when(step == pl.num_programs(0) - 1)
    def _():
        dx = acc_ref[...] + da_ref[...]
        perm = perm_ref[...]
        dx_ref[...] = sum(nt(part, perm) for part in thirds(dx))


def whole(a):
    nd = len(a.shape)
    return pl.BlockSpec(a.shape, lambda s: (0,) * nd, pipeline_mode=pl.Buffered(1))


def lead(a):
    nd = len(a.shape)
    return pl.BlockSpec((1,) + a.shape[1:], lambda s: (s,) + (0,) * (nd - 1))


def weight(a):
    return pl.BlockSpec((a.shape[0], 1, BLK, a.shape[3]), lambda s: (0, s, 0, 0))


def weight_t(a):
    return pl.BlockSpec((1, a.shape[1], BLK, a.shape[3]), lambda s: (s, 0, 0, 0))


def half_spec(h):
    return pl.BlockSpec((h.shape[0], 1) + h.shape[2:], lambda s: (0, s, 0, 0))


def sds(shape, dtype):
    return jax.ShapeDtypeStruct(shape, dtype)


def far(shape, dtype):
    return pltpu.HBM(shape, dtype)


def call(body, n_t, micros, ins, outs, scratch=()):
    return pl.pallas_call(
        body,
        grid=(n_t,),
        in_specs=[s for _, s in ins],
        out_specs=[s for _, s in outs],
        out_shape=[a for a, _ in outs],
        scratch_shapes=list(scratch),
        compiler_params=pltpu.CompilerParams(
            dimension_semantics=("arbitrary",), vmem_limit_bytes=VMEM_LIMIT
        ),
        cost_estimate=pl.CostEstimate(flops=int(micros * COST), transcendentals=0, bytes_accessed=0),
    )(*[a for a, _ in ins])


def flips(n_dp, n_t):
    size = n_dp * n_t
    core = n_t
    x_bit, y_bit = 2 * core, 4 * core

    def table(bit_of):
        return [(i, i ^ bit_of(i)) for i in range(size)]

    return {
        "Z": [table(lambda i, d=d: d) for d in range(1, n_t)],
        "C": [table(lambda i: core)],
        "2": [table(lambda i: x_bit if i & core else y_bit)],
        "3": [table(lambda i: y_bit if i & core else x_bit)],
    }


def after(value, *done):
    return lax.optimization_barrier((value, *done))[0] if done else value


def swap(value, tables, *done):
    return lax.ppermute(after(value, *done), AXES, tables["C"][0])


class Gather:
    def __init__(self, value, tables):
        self.held, self.tables = [value[None]], tables

    def send(self, name, *done, parts=None, tables=None):
        sent = self.held if parts is None else [self.held[j] for j in parts]
        return [lax.ppermute(after(h, *done), AXES, t) for t in self.tables[name][tables or slice(None)] for h in sent]

    def take(self, name, got):
        self.held = [jnp.concatenate(self.held + got)] if name in "Z2" else self.held + got
        return got

    def stage(self, name, *done, parts=None):
        return self.take(name, self.send(name, *done, parts=parts))

    def pieces(self, *lead):
        return [h.reshape(*lead, *h.shape[1:]) for h in self.held]


class Scatter:
    def __init__(self, keep, send, tables):
        self.keep, self.send, self.tables = keep, [send], tables

    def stage(self, name, parts, *done, cut=1):
        tables = self.tables[name]
        pieces = len(self.send) // len(tables)
        got = [lax.ppermute(after(s, *done), AXES, tables[n // pieces]) for n, s in enumerate(self.send)]
        size = self.keep.shape[0] // parts // cut

        def piece(n):
            at = n * size
            total = self.keep[at : at + size].astype(f32)
            for t in range(len(tables)):
                mine = got[t * pieces : (t + 1) * pieces]
                wide = mine[0].shape[0]
                total = total + mine[at // wide][at % wide : at % wide + size].astype(f32)
            return total

        self.send = [piece(n).astype(bf16) for n in range(cut, parts * cut)]
        kept = [piece(n) for n in range(cut)]
        self.keep = kept[0] if cut == 1 else jnp.concatenate(kept)
        return got


def per_device(
    hidden_in, segment_ids, pooled_grad, qkv_weight, qv_bias, out_weight, out_bias,
    norm1_gain, norm1_shift, up_weight, up_bias, down_weight_in, down_bias, norm2_gain, norm2_shift,
):
    n_dp, n_t = lax.axis_size("dp"), lax.axis_size("tensor")
    at_dp, at_t = lax.axis_index("dp"), lax.axis_index("tensor")
    hc, fc = qkv_weight.shape[2], up_weight.shape[1]
    rows = qkv_weight.shape[1]
    D = rows * n_dp
    micro, tokens = hidden_in.shape[0], hidden_in.shape[1]
    seqs, L = segment_ids.shape[1], segment_ids.shape[2]
    G, T = micro * seqs, micro * tokens
    segs = pooled_grad.shape[2]
    n_i = D // BLK
    pairwise = (n_dp, n_t) == (8, 4) and 4 * hc == fc

    d_parts = [out_bias, norm1_gain, norm1_shift, down_bias, norm2_gain, norm2_shift]
    e_parts = [qv_bias[0], qv_bias[1], up_bias]
    dv = out_bias.shape[0]
    n_vec = sum(p.shape[0] for p in d_parts + e_parts)
    nd = len(d_parts) * dv

    sizes = (6, dv, up_bias.shape[0], D, hc, fc, n_t) if pairwise else (6, D // (n_i * n_t), n_t * fc // (n_i * n_t), D, hc, fc, n_t)
    slot = jnp.arange(n_i * n_t)
    rel = jnp.arange(n_i)
    if pairwise:
        tables = flips(n_dp, n_t)
        packed = (qkv_weight, out_weight, *[p[None] for p in d_parts], qv_bias, up_bias[None])
        packed = pl.pallas_call(pack, out_shape=sds((BLK + 8, 4 * hc), bf16))(*packed)
        first, middle, last = Gather(packed, tables), Gather(up_weight, tables), Gather(down_weight_in.T, tables)
        done = first.stage("Z") + last.stage("2")

        core = (at_dp & 1) ^ (rel >> 2)
        s3, s2 = (rel >> 1) & 1, rel & 1
        dy, dx = jnp.where(core == 0, s2, s3), jnp.where(core == 0, s3, s2)
        absolute = ((((at_dp >> 2) & 1) ^ dy) << 2) | ((((at_dp >> 1) & 1) ^ dx) << 1) | core
        i_p = jnp.broadcast_to(absolute[:, None], (n_i, n_t)).reshape(-1)
        t_p = jnp.broadcast_to((at_t ^ jnp.arange(n_t))[None], (n_i, n_t)).reshape(-1)
        to_d = jnp.broadcast_to(rel[:, None], (n_i, n_t)).reshape(-1) * n_t + t_p
        to_e = (((i_p * n_t) // n_i) ^ at_t) * n_i + (i_p * n_t + t_p) % n_i
    else:
        absolute, to_d, to_e = rel, slot, slot
    hot_d = (to_d[None, :] == slot[:, None]).astype(bf16)
    hot_e = (to_e[None, :] == slot[:, None]).astype(bf16)
    lane = jnp.arange(D)
    same_block = jnp.repeat(jnp.repeat((absolute[:, None] == rel[None, :]).T, BLK, axis=0), BLK, axis=1)
    perm = (same_block & ((lane[:, None] % BLK) == (lane[None, :] % BLK))).astype(bf16)
    turned = (D // 2, T)
    x, x_keep, x_send = pl.pallas_call(
        reorder, out_shape=[sds((T, D), bf16), sds(turned, bf16), sds(turned, bf16)], compiler_params=SMALL
    )(hidden_in.reshape(T, D), perm)
    pg = jnp.einsum("gsd,de->gse", pooled_grad.reshape(G, segs, D), perm.astype(f32), precision=HI)
    seg_r = segment_ids.reshape(G, L)
    seg_c = segment_ids.reshape(T, 1)

    if pairwise:
        done = first.stage("2", *done, x, x_keep, x_send, pg, hot_d, hot_e) + middle.stage("Z", *done)
        x_other = swap(x_send, tables, *done)
        near_z = last.send("Z", *done, tables=slice(0, 2))
        done = first.stage("3", *done) + middle.stage("2", *done) + near_z
        first.stage("C", *done)
        x = after(x, x_other)
        got_u3, far_z = middle.send("3", *done), last.send("Z", *done, tables=slice(2, None))
        w_qo = first.pieces(2, n_t)
    else:
        heads_in = [qkv_weight[0], qkv_weight[1], qkv_weight[2], out_weight.T]
        main = jnp.concatenate([*heads_in, up_weight, down_weight_in.T], axis=1)
        vec = jnp.concatenate(d_parts + e_parts)
        full = lax.all_gather(lax.all_gather(main, "dp", axis=0, tiled=True), "tensor", axis=0)
        full = full.reshape(n_t, n_i, BLK, -1).transpose(1, 0, 2, 3)
        vecs = lax.all_gather(lax.all_gather(vec, "tensor"), "dp").reshape(n_dp * n_t, -1)
        cuts = [j * dv for j in range(9)] + [n_vec]
        rows8 = jnp.concatenate([vecs[:, a:b].reshape(n_i * n_t, -1) for a, b in zip(cuts[:-1], cuts[1:])], axis=1)
        rows8 = jnp.pad(rows8.reshape(n_i, n_t, 1, -1), ((0, 0), (0, 0), (0, 7), (0, 4 * hc - rows8.shape[1])))
        quarters = [full[j * n_i // 4 : (j + 1) * n_i // 4] for j in range(4)]
        w_qo = [
            jnp.concatenate([w[..., : 4 * hc], rows8[j * n_i // 4 : (j + 1) * n_i // 4]], axis=2)
            for j, w in enumerate(quarters)
        ]
        w_up = [w[..., 4 * hc : 4 * hc + fc] for w in quarters]
        w_down = [w[..., 4 * hc + fc :].transpose(1, 0, 2, 3) for w in quarters]

    hl = hc // HD * L
    o_wide, q_wide = -(-hc // 128) * 128, -(-3 * hc // 128) * 128

    def leads(*arrays):
        return [(a, lead(a)) for a in arrays]

    def wholes(*arrays):
        return [(a, whole(a)) for a in arrays]

    def weights(*arrays):
        return [(a, weight(a)) for a in arrays]

    def weights_t(*arrays):
        return [(a, weight_t(a)) for a in arrays]

    tails = [
        (w, pl.BlockSpec((w.shape[0], n_t, 8, w.shape[3]), lambda s: (0, 0, BLK // 8, 0), pipeline_mode=pl.Buffered(1)))
        for w in w_qo
    ]
    qkv, prob, o, n1, x1, r1, n1b, n1_keep, n1_send, vec_d, b_u = call(
        partial(attention_forward, sizes), n_t, 10,
        wholes(x) + weights(*w_qo) + tails + wholes(hot_d, hot_e, seg_c, seg_r),
        leads(far((n_t, T, 3 * hc), bf16), far((n_t, G, L, hl), f32), far((n_t, T, o_wide), bf16))
        + wholes(sds((T, D), f32), far((T, D), f32), far((T, 1), f32), sds((T, D), bf16), far(turned, bf16), far(turned, bf16))
        + wholes(sds((6, D), f32), sds((n_t, 1, fc), f32)),
        [pltpu.VMEM((T, D), f32), pltpu.VMEM((n_t, 1, hc), f32), pltpu.VMEM((n_t, 1, hc), f32)],
    )
    if pairwise:
        last.take("Z", near_z + [after(g, n1b) for g in far_z])
        middle.take("3", [after(g, n1b) for g in got_u3])
        last.stage("3", *got_u3)
        middle.stage("C", n1b, *far_z)
        last.take("C", last.send("C", n1b, parts=(0,)))
        last.take("C", last.send("C", parts=(1,)))
        w_up, w_down = middle.pieces(2, n_t), last.pieces(n_t, 2)
        n1_other = swap(n1_send, tables)
        o_other = swap(o, tables)
        b_u = after(b_u, n1_other, o_other)
    z, dgelu = call(
        up_forward, n_t, 4, wholes(n1b) + weights(*w_up) + leads(b_u),
        leads(sds((n_t, T, fc), bf16), sds((n_t, T, fc), f32)),
    )
    if pairwise:
        z_other = swap(z, tables)
    pooled, db, dbb, db_keep, db_send, sums2 = call(
        down_forward, n_t, 5.5, leads(z) + weights_t(*w_down) + wholes(n1, vec_d, seg_c, seg_r, pg),
        wholes(sds((G, segs, D), f32), sds((T, D), f32), sds((T, D), bf16), sds(turned, bf16), sds(turned, bf16), sds((3, D), f32)),
        [pltpu.VMEM((T, D), f32)],
    )

    def gradient(groups, vectors=(), at_once=True):
        ins, kinds = [], []
        for width, *pairs in groups:
            kinds.append((len(pairs), len(pairs[0][1]), width))
            for lhs, values in pairs:
                ins += wholes(lhs) + (leads(*values) if len(values) == 1 else halved(*values))
        out = sds((n_i // 4, n_t, BLK + (8 if vectors else 0), sum(k[2] for k in kinds)), bf16)

        def share(which):
            return call(
                partial(weight_gradient, kinds, len(vectors), which), n_t, 2, ins + leads(*vectors),
                [(out, half_spec(out))] * (2 if which is None else 1),
            )

        return share(None) if at_once else (share(0)[0], share(1)[0])

    def halved(low, high):
        block = (1,) + low.shape[1:]
        return [
            (low, pl.BlockSpec(block, lambda s: (jnp.minimum(s, n_t // 2 - 1), 0, 0))),
            (high, pl.BlockSpec(block, lambda s: (jnp.maximum(s - n_t // 2, 0), 0, 0))),
        ]

    def flat(a):
        return a.reshape((-1,) + a.shape[2:])

    du, g_bu = call(
        hidden_backward, n_t, 3.5, wholes(dbb) + weights_t(*w_down) + leads(dgelu),
        leads(sds((n_t, T, fc), bf16), sds((n_t, 1, fc), f32)),
    )
    if pairwise:
        db_other = swap(db_send, tables)
        du_other = swap(du, tables)
        down_keep, down_send = gradient([[fc, (after(db_keep, g_bu), [z]), (db_other, [z_other])]], at_once=False)
        s_down = Scatter(flat(down_keep), flat(down_send), tables)
        got_d3 = s_down.stage("3", 2)
        du_next = after(du, down_send)
        dab_after = down_keep
    else:
        du_next = du
    da, dab, da_keep, da_send, sums1 = call(
        norm_backward, n_t, NORM, leads(du_next) + weights(*w_up) + wholes(db, x1, r1, vec_d),
        wholes(sds((T, D), f32), sds((T, D), bf16), sds(turned, bf16), sds(turned, bf16), sds((3, D), f32)),
        [pltpu.VMEM((T, D), f32)],
    )
    if pairwise:
        da_other = swap(da_send, tables)
        up_keep, up_send = gradient([[fc, (after(n1_keep, da_keep), [du]), (n1_other, [du_other])]])
        s_up = Scatter(flat(up_keep), flat(up_send), tables)
        got_u3 = s_up.stage("3", 2)
        dab = after(dab, up_keep)
    rows = sds((n_t, n_i // 2, 4 * hc), f32)
    if pairwise:
        dab = after(dab, da_other, dab_after, *got_d3)
    dq_half = sds((n_t // 2, T, q_wide), bf16)
    *dq, v_keep, v_send = call(
        partial(attention_backward, sizes), n_t, 8,
        wholes(dab) + weights(*w_qo) + leads(qkv, prob) + wholes(sums1, sums2, g_bu, hot_d, hot_e),
        halved(dq_half, dq_half) + wholes(rows, rows),
        [pltpu.VMEM((n_t, 1, hc), f32), pltpu.VMEM((n_t, 1, hc), f32), pltpu.VMEM((T, q_wide), bf16)],
    )
    if pairwise:
        dq_other = [swap(d, tables) for d in dq]
        v_other = swap(v_send, tables)
        got_d2 = s_down.stage("2", n_t)
    pooled = jnp.einsum("gse,de->gsd", pooled, perm.astype(f32), precision=HI)
    if pairwise:
        x_now = after(x_keep, *got_u3)
        qo_keep, qo_send = gradient(
            [[3 * hc, (x_now, dq), (x_other, dq_other)], [hc, (da_keep, [o]), (da_other, [o_other])]], (v_keep, v_other)
        )
        s_qo = Scatter(flat(qo_keep), flat(qo_send), tables)
        got_u2 = s_up.stage("2", n_t)
        s_qo.stage("3", 2, *got_d2, *got_u2, pooled, cut=CUT)
        both = Scatter(jnp.concatenate([s_down.keep, s_up.keep]), None, tables)
        both.send = [jnp.concatenate([a, b]) for a, b in zip(s_down.send, s_up.send, strict=True)]
        got_z = both.stage("Z", 1)
        dq = [after(d, qo_keep) for d in dq]
    dx = call(
        input_backward, n_t, 4, halved(*dq) + weights(*w_qo) + wholes(da, perm), wholes(sds((T, D), f32)),
        [pltpu.VMEM((T, D), f32)],
    )[0]

    if pairwise:
        s_qo.stage("2", n_t, dx)
        s_qo.stage("Z", 1, *got_z)
        g_down, g_up, g_qo = both.keep[0], both.keep[1], s_qo.keep[0]
        g_v = g_qo[BLK, :n_vec]
        g_qo = g_qo[:BLK]
    else:
        def joined(*halves_of):
            g = jnp.concatenate([part[:, :, :BLK] for half in halves_of for part in half])
            return g.transpose(1, 0, 2, 3).reshape(n_t, D, -1)

        x_h, n1_h, db_h, da_h = (x_keep, x_send), (n1_keep, n1_send), (db_keep, db_send), (da_keep, da_send)
        g_full = jnp.concatenate([
            joined(*[gradient([[3 * hc, (x_h[j], dq)], [hc, (da_h[j], [o])]]) for j in range(2)]),
            joined(*[gradient([[fc, (n1_h[j], [du])]]) for j in range(2)]),
            joined(*[gradient([[fc, (db_h[j], [z])]]) for j in range(2)]),
        ], axis=2)
        mine = lax.psum_scatter(g_full, "tensor", scatter_dimension=0)
        mine = lax.psum_scatter(mine, "dp", scatter_dimension=0, tiled=True).astype(f32)
        g_qo, g_up, g_down = mine[:, : 4 * hc], mine[:, 4 * hc : 4 * hc + fc], mine[:, 4 * hc + fc :]
        g_rows = jnp.stack([v_keep, v_send]).transpose(0, 2, 1, 3).reshape(n_i * n_t, -1)
        dv_c, bu_c = sizes[1], sizes[2]
        cuts = [j * dv_c for j in range(9)] + [8 * dv_c + bu_c]
        g_v = jnp.concatenate(
            [g_rows[:, a:b].reshape(n_dp * n_t, -1) for a, b in zip(cuts[:-1], cuts[1:])], axis=1
        )
        g_v = lax.psum_scatter(g_v, AXES, scatter_dimension=0)
    vo = [g_v[j * dv : (j + 1) * dv] for j in range(8)]
    return (
        pooled.reshape(micro, seqs, segs, D),
        dx.reshape(micro, tokens, D),
        jnp.stack([g_qo[:, c * hc : (c + 1) * hc] for c in range(3)]),
        jnp.stack([vo[6], vo[7]]),
        g_qo[:, 3 * hc :].T,
        vo[0], vo[1], vo[2],
        g_up,
        g_v[8 * dv :],
        g_down.T,
        vo[3], vo[4], vo[5],
    )


def solution(mesh):
    both = P(AXES)
    row3 = P(None, AXES)
    return jax.shard_map(
        per_device,
        mesh=mesh,
        in_specs=(
            row3, row3, row3, P(None, "dp", "tensor"), row3, P("tensor", "dp"), both, both, both,
            P("dp", "tensor"), both, P("tensor", "dp"), both, both, both,
        ),
        out_specs=(
            row3, row3, P(None, "dp", "tensor"), row3, P("tensor", "dp"), both, both, both,
            P("dp", "tensor"), both, P("tensor", "dp"), both, both, both,
        ),
        check_vma=False,
    )
```

```python
from functools import partial

import jax
import jax.numpy as jnp
from jax import lax
from jax.experimental import pallas as pl
from jax.experimental.pallas import tpu as pltpu
from jax.sharding import PartitionSpec as P

HD = 64
EPS = 1e-12
NEG = -1000000000.0
SCALE = float(HD) ** -0.5
AXES = ("dp", "tensor")
f32 = jnp.float32
bf16 = jnp.bfloat16
HI = lax.Precision.HIGHEST
BLK = 96
VMEM_LIMIT = 24 * 1024 * 1024
COST = 30_000_000
NORM = 2000
CUT = 4
SMALL = pltpu.CompilerParams(vmem_limit_bytes=8 * 1024 * 1024)


def nn(a, b):
    return lax.dot_general(a, b, (((1,), (0,)), ((), ())), preferred_element_type=f32)


def nt(a, b):
    return lax.dot_general(a, b, (((1,), (1,)), ((), ())), preferred_element_type=f32)


def tn(a, b):
    return lax.dot_general(a, b, (((0,), (0,)), ((), ())), preferred_element_type=f32)


def mean_last(v):
    return jnp.sum(v, axis=-1, keepdims=True) * (1.0 / v.shape[-1])


def normalize(values):
    center = values - mean_last(values)
    inverse = lax.rsqrt(mean_last(center * center) + EPS)
    return center * inverse, inverse


def normalize_back(scaled, normed, inverse):
    return inverse * (scaled - mean_last(scaled) - normed * mean_last(scaled * normed))


def col_sum(v):
    return jnp.sum(v, axis=0, keepdims=True)


def pack(qkv_ref, out_ref, ob_ref, g1_ref, s1_ref, db_ref, g2_ref, s2_ref, qv_ref, ub_ref, first_ref):
    rows, hc = qkv_ref.shape[1:]
    eye = (lax.broadcasted_iota(jnp.int32, (rows, rows), 0) == lax.broadcasted_iota(jnp.int32, (rows, rows), 1)).astype(bf16)
    for c in range(3):
        first_ref[:rows, c * hc : (c + 1) * hc] = qkv_ref[c]
    first_ref[:rows, 3 * hc :] = nt(eye, out_ref[...]).astype(bf16)
    parts = [r[...].astype(f32) for r in (ob_ref, g1_ref, s1_ref, db_ref, g2_ref, s2_ref, qv_ref)]
    short = jnp.concatenate(parts, axis=0).astype(bf16)
    count, size = short.shape
    wide = first_ref.shape[1]

    def spread(values, at):
        lane = lax.broadcasted_iota(jnp.int32, (values.shape[1], wide), 1) - at
        return nn(values, (lax.rem(lane + values.shape[1] * wide, values.shape[1]) == lax.broadcasted_iota(jnp.int32, lane.shape, 0)).astype(bf16))

    lane = lax.broadcasted_iota(jnp.int32, (count, wide), 1)
    start = lax.broadcasted_iota(jnp.int32, (count, wide), 0) * size
    row = col_sum(jnp.where((lane >= start) & (lane < start + size), spread(short, 0), 0.0))
    total, long = count * size, ub_ref.shape[1]
    lane = lax.broadcasted_iota(jnp.int32, (1, wide), 1)
    row = jnp.where((lane >= total) & (lane < total + long), spread(ub_ref[...], total), row)
    extra = first_ref.shape[0] - rows
    here = lax.broadcasted_iota(jnp.int32, (extra, wide), 0)
    first_ref[rows:, :] = jnp.where(here == 0, row, 0.0).astype(bf16)


def reorder(h_ref, perm_ref, x_ref, keep_ref, send_ref):
    x = nn(h_ref[...], perm_ref[...]).astype(bf16)
    x_ref[...] = x
    turned = x.T
    keep_ref[...] = turned[: x.shape[1] // 2]
    send_ref[...] = turned[x.shape[1] // 2 :]


def stacked(values, hc):
    head = lax.broadcasted_iota(jnp.int32, (1, hc), 1) // HD
    return jnp.concatenate([values * (head == h).astype(f32).astype(bf16) for h in range(hc // HD)], axis=0)


def own_columns(blocks, hc):
    n_heads = hc // HD
    length = blocks.shape[0] // n_heads
    head = lax.broadcasted_iota(jnp.int32, (1, hc), 1) // HD
    out = blocks[:length]
    for h in range(1, n_heads):
        out = jnp.where(head == h, blocks[h * length : (h + 1) * length], out)
    return out


def sections(values, length):
    return [values[:, c : c + length] for c in range(0, values.shape[1], length)]


def rows_of(refs):
    return jnp.concatenate([r[...].reshape(-1, r.shape[3]) for r in refs], axis=0)


def thirds(values):
    high = values.astype(bf16)
    rest = values - high.astype(f32)
    middle = rest.astype(bf16)
    return high, middle, (rest - middle.astype(f32)).astype(bf16)


def accumulate(acc_ref, step, add):
    @pl.when(step == 0)
    def _():
        acc_ref[...] = add

    @pl.when(step > 0)
    def _():
        acc_ref[...] += add


def iota(shape, axis):
    return lax.broadcasted_iota(jnp.int32, shape, axis)


def picks(count, first, wide, size):
    return (iota((count, wide), 0) == first + lax.rem(iota((1, wide), 1), size)).astype(bf16)


def belongs(count, wide, size, period):
    lane, row = iota((1, wide), 1), lax.rem(iota((count, 1), 0), period)
    return (lane >= row * size) & (lane < (row + 1) * size)


def read_vectors(rows, hot_d, hot_e, sizes):
    n_d, dv, bu, width, hc, fc, n_t = sizes
    count = rows.shape[0]
    per = count // n_t
    d_all = nn(hot_d, rows[:, : n_d * dv]).astype(bf16)
    mine = belongs(count, width, dv, count)
    d_rows = [col_sum(jnp.where(mine, nn(d_all, picks(n_d * dv, j * dv, width, dv)), 0.0)) for j in range(n_d)]
    e_all = nn(hot_e, rows[:, n_d * dv : n_d * dv + 2 * dv + bu]).astype(bf16)
    out = []
    for first, size, wide in ((0, dv, hc), (dv, dv, hc), (2 * dv, bu, fc)):
        spread = jnp.where(belongs(count, wide, size, per), nn(e_all, picks(e_all.shape[1], first, wide, size)), 0.0)
        out.append(jnp.sum(spread.reshape(n_t, per, wide), axis=1, keepdims=True))
    return jnp.concatenate(d_rows, axis=0), out


def write_vectors(d_rows, e_rows, hot_d, hot_e, sizes):
    n_d, dv, bu, width, hc, fc, n_t = sizes
    count = hot_d.shape[0]
    per = count // n_t
    mine = belongs(count, width, dv, count)
    d_all = sum(
        nt(jnp.where(mine, d_rows[j : j + 1, :], 0.0).astype(bf16), picks(n_d * dv, j * dv, width, dv)) for j in range(n_d)
    ).astype(bf16)
    e_all = 0.0
    for value, first, size, wide in zip(e_rows, (0, dv, 2 * dv), (dv, dv, bu), (hc, hc, fc), strict=True):
        spread = jnp.broadcast_to(value, (n_t, per, wide)).reshape(count, wide)
        spread = jnp.where(belongs(count, wide, size, per), spread, 0.0).astype(bf16)
        e_all = e_all + nt(spread, picks(2 * dv + bu, first, wide, size))
    return jnp.concatenate([tn(hot_d, d_all), tn(hot_e, e_all.astype(bf16))], axis=1)


def attention_forward(sizes, x_ref, w0_ref, w1_ref, w2_ref, w3_ref, v0_ref, v1_ref, v2_ref, v3_ref, hd_ref, he_ref,
                      segc_ref, segr_ref, qkv_ref, p_ref, o_ref, n1_ref, x1_ref, r1_ref, n1b_ref, n1t_ref, n1s_ref,
                      vec_ref, bu_ref, acc_ref, bq_ref, bv_ref):
    step = pl.program_id(0)
    hc = bq_ref.shape[-1]

    @pl.when(step == 0)
    def _():
        rows = jnp.concatenate([r[:, :, 0, :].reshape(-1, r.shape[3]) for r in (v0_ref, v1_ref, v2_ref, v3_ref)], axis=0)
        d_rows, (b_q, b_v, b_u) = read_vectors(rows, hd_ref[...], he_ref[...], sizes)
        vec_ref[...] = d_rows
        bq_ref[...] = b_q
        bv_ref[...] = b_v
        bu_ref[...] = b_u

    rows, length = segr_ref.shape
    x = x_ref[...]
    w = rows_of((w0_ref, w1_ref, w2_ref, w3_ref))
    qkv = nn(x, w[:, : 3 * hc])
    q = (qkv[:, :hc] + bq_ref[step]).astype(bf16) * bf16(SCALE)
    k = qkv[:, hc : 2 * hc].astype(bf16)
    v = (qkv[:, 2 * hc :] + bv_ref[step]).astype(bf16)
    qkv_ref[0, :, :hc] = q
    qkv_ref[0, :, hc : 2 * hc] = k
    qkv_ref[0, :, 2 * hc :] = v
    spans = [slice(g * length, (g + 1) * length) for g in range(rows)]
    scores = [nt(q[span], stacked(k[span], hc)) for span in spans]
    probs = []
    for g, span in enumerate(spans):
        same = segc_ref[span, :] == segr_ref[g : g + 1, :]
        parts = []
        for s in sections(scores[g], length):
            s = jnp.where(same, s, NEG)
            e = jnp.exp(s - jnp.max(s, axis=-1, keepdims=True))
            parts.append(e * (1.0 / jnp.sum(e, axis=-1, keepdims=True)))
        probs.append(jnp.concatenate(parts, axis=1))
    for g, span in enumerate(spans):
        p_ref[0, g] = probs[g]
        o_ref[0, span, :hc] = nn(probs[g].astype(bf16), stacked(v[span], hc)).astype(bf16)
    o_ref[0, :, hc:] = jnp.zeros((o_ref.shape[1], o_ref.shape[2] - hc), bf16)
    add = nt(o_ref[0, :, :hc], w[:, 3 * hc :])

    accumulate(acc_ref, step, add)

    @pl.when(step == pl.num_programs(0) - 1)
    def _():
        a = acc_ref[...] + vec_ref[0:1, :] + x_ref[...].astype(f32)
        normed, inverse = normalize(a)
        n1 = normed * vec_ref[1:2, :] + vec_ref[2:3, :]
        n1_ref[...] = n1
        x1_ref[...] = normed
        r1_ref[...] = inverse
        low = n1.astype(bf16)
        n1b_ref[...] = low
        turned = low.T
        n1t_ref[...] = turned[: low.shape[1] // 2]
        n1s_ref[...] = turned[low.shape[1] // 2 :]


def up_forward(n_ref, w0_ref, w1_ref, w2_ref, w3_ref, b_ref, z_ref, d_ref):
    u = nn(n_ref[...], rows_of((w0_ref, w1_ref, w2_ref, w3_ref))) + b_ref[0]
    phi = 0.5 + 0.5 * lax.erf(u * (0.5**0.5))
    z_ref[0] = (u * phi).astype(bf16)
    d_ref[0] = phi + u * (jnp.exp(-0.5 * u * u) * 0.3989422804014327)


def down_forward(z_ref, w0_ref, w1_ref, w2_ref, w3_ref, w4_ref, w5_ref, w6_ref, w7_ref, n1_ref, vec_ref, segc_ref, segr_ref, pg_ref,
                 pooled_ref, db_ref, dbb_ref, dbt_ref, dbs_ref, sums_ref, acc_ref):
    step = pl.program_id(0)
    add = nt(z_ref[0, 0], rows_of((w0_ref, w1_ref, w2_ref, w3_ref))) + nt(z_ref[1, 0], rows_of((w4_ref, w5_ref, w6_ref, w7_ref)))

    accumulate(acc_ref, step, add)

    @pl.when(step == pl.num_programs(0) - 1)
    def _():
        rows, length = segr_ref.shape
        segs = pg_ref.shape[1]
        b = acc_ref[...] + vec_ref[3:4, :] + n1_ref[...]
        x2, r2 = normalize(b)
        y = x2 * vec_ref[4:5, :] + vec_ref[5:6, :]
        grads = []
        for g in range(rows):
            span = slice(g * length, (g + 1) * length)
            hot_t = (iota((segs, length), 0) == segr_ref[g : g + 1, :]).astype(f32)
            count = jnp.sum(hot_t, axis=1, keepdims=True)
            hot_t = hot_t.astype(bf16)
            hot = (iota((length, segs), 1) == segc_ref[span, :]).astype(f32).astype(bf16)
            pooled_ref[g] = sum(nn(hot_t, part) for part in thirds(y[span, :])) / count
            grads.append(nn(jnp.concatenate([hot] * 3, axis=1), jnp.concatenate(thirds(pg_ref[g] / count), axis=0)))
        dy = jnp.concatenate(grads, axis=0)
        db = normalize_back(dy * vec_ref[4:5, :], x2, r2)
        db_ref[...] = db
        low = db.astype(bf16)
        dbb_ref[...] = low
        turned = low.T
        dbt_ref[...] = turned[: low.shape[1] // 2]
        dbs_ref[...] = turned[low.shape[1] // 2 :]
        sums_ref[0:1, :] = col_sum(db)
        sums_ref[1:2, :] = col_sum(dy * x2)
        sums_ref[2:3, :] = col_sum(dy)


def put(grad, ref):
    ref[:, :, :BLK, :] = grad.astype(bf16).reshape(grad.shape[0] // BLK, 1, BLK, grad.shape[1])


def hidden_backward(dbb_ref, w0_ref, w1_ref, w2_ref, w3_ref, w4_ref, w5_ref, w6_ref, w7_ref, d_ref, du_ref, bu_ref):
    for n, refs in enumerate(((w0_ref, w1_ref, w2_ref, w3_ref), (w4_ref, w5_ref, w6_ref, w7_ref))):
        du = (nn(dbb_ref[...], rows_of(refs)) * d_ref[n, 0]).astype(bf16)
        du_ref[n, 0] = du
        bu_ref[n, 0] = col_sum(du.astype(f32))


def step_value(refs, width):
    if len(refs) == 1:
        return refs[0][0, :, :width]
    return jnp.where(pl.program_id(0) < pl.num_programs(0) // 2, refs[0][0, :, :width], refs[1][0, :, :width])


def weight_gradient(groups, vectors, which, *refs):
    refs = list(refs)
    parts = []
    for pairs, split, width in groups:
        total = None
        for _ in range(pairs):
            rows = refs.pop(0)
            half = rows.shape[0] // 2
            rows = rows[...] if which is None else rows[which * half : (which + 1) * half, :]
            add = nn(rows, step_value([refs.pop(0) for _ in range(split)], width))
            total = add if total is None else total + add
        parts.append(total)
    grad = jnp.concatenate(parts, axis=1)
    extra = sum(refs.pop(0)[0].astype(f32) for _ in range(vectors)) if vectors else None
    half = grad.shape[0] // len(refs)
    for n, ref in enumerate(refs):
        put(grad[n * half : (n + 1) * half], ref)
        if vectors:
            for j in range(ref.shape[0]):
                at = (n if which is None else which) * ref.shape[0] + j
                row = extra[at : at + 1]
                tail = ref.shape[2] - BLK
                ref[j, 0, BLK:, :] = jnp.where(iota((tail, row.shape[1]), 0) == 0, row, 0.0).astype(bf16)


def norm_backward(du_ref, w0_ref, w1_ref, w2_ref, w3_ref, db_ref, x1_ref, r1_ref, vec_ref,
                  da_ref, dab_ref, dat_ref, das_ref, sums_ref, acc_ref):
    step = pl.program_id(0)
    accumulate(acc_ref, step, nt(du_ref[0], rows_of((w0_ref, w1_ref, w2_ref, w3_ref))))

    @pl.when(step == pl.num_programs(0) - 1)
    def _():
        dn1 = acc_ref[...].astype(bf16).astype(f32) + db_ref[...]
        da = normalize_back(dn1 * vec_ref[1:2, :], x1_ref[...], r1_ref[...])
        da_ref[...] = da
        low = da.astype(bf16)
        dab_ref[...] = low
        turned = low.T
        dat_ref[...] = turned[: low.shape[1] // 2]
        das_ref[...] = turned[low.shape[1] // 2 :]
        sums_ref[0:1, :] = col_sum(da)
        sums_ref[1:2, :] = col_sum(dn1 * x1_ref[...])
        sums_ref[2:3, :] = col_sum(dn1)


def attention_backward(sizes, dab_ref, w0_ref, w1_ref, w2_ref, w3_ref, qkv_ref, p_ref, s1_ref, s2_ref, gu_ref, hd_ref, he_ref,
                       low_ref, high_ref, keep_ref, send_ref, bq_ref, bv_ref, dqkv_ref):
    step = pl.program_id(0)
    hc = bq_ref.shape[-1]
    dab = dab_ref[...]
    w = rows_of([r.at[:, :, :, 3 * hc :] for r in (w0_ref, w1_ref, w2_ref, w3_ref)])
    do = nn(dab, w).astype(bf16)
    qkv = qkv_ref[0]
    rows, length = p_ref.shape[1], p_ref.shape[2]
    spans = [slice(g * length, (g + 1) * length) for g in range(rows)]
    q = [qkv[span, :hc] for span in spans]
    k = [stacked(qkv[span, hc : 2 * hc], hc) for span in spans]
    dps = [nt(do[span], stacked(qkv[span, 2 * hc :], hc)) for span in spans]
    dss = []
    for g in range(rows):
        parts = []
        for p, dp in zip(sections(p_ref[0, g], length), sections(dps[g], length)):
            pd = p * dp
            parts.append((pd - p * jnp.sum(pd, axis=-1, keepdims=True)).astype(bf16))
        dss.append(jnp.concatenate(parts, axis=1))
    for g, span in enumerate(spans):
        dqkv_ref[span, :hc] = (nn(dss[g], k[g]) * SCALE).astype(bf16)
        dqkv_ref[span, hc : 2 * hc] = own_columns(tn(dss[g], q[g]), hc).astype(bf16)
        dqkv_ref[span, 2 * hc : 3 * hc] = own_columns(tn(p_ref[0, g].astype(bf16), do[span]), hc).astype(bf16)
    dqkv_ref[:, 3 * hc :] = jnp.zeros((dqkv_ref.shape[0], dqkv_ref.shape[1] - 3 * hc), bf16)
    dqkv = dqkv_ref[...]
    half_steps = pl.num_programs(0) // 2

    @pl.when(step < half_steps)
    def _():
        low_ref[0] = dqkv

    @pl.when(step >= half_steps)
    def _():
        high_ref[0] = dqkv

    bq_ref[step] = col_sum(dqkv[:, :hc].astype(f32))
    bv_ref[step] = col_sum(dqkv[:, 2 * hc : 3 * hc].astype(f32))

    @pl.when(step == pl.num_programs(0) - 1)
    def _():
        d_rows = jnp.concatenate([s1_ref[...], s2_ref[...]], axis=0)
        rows = write_vectors(d_rows, (bq_ref[...], bv_ref[...], gu_ref[...]), hd_ref[...], he_ref[...], sizes)
        half, n_t = rows.shape[0] // 2, bq_ref.shape[0]
        rows = jnp.concatenate([rows, jnp.zeros((rows.shape[0], keep_ref.shape[-1] - rows.shape[1]), f32)], axis=1)
        for n, ref in enumerate((keep_ref, send_ref)):
            for t in range(n_t):
                for j in range(half // n_t):
                    at = n * half + j * n_t + t
                    ref[t, j : j + 1, :] = rows[at : at + 1]


def input_backward(low_ref, high_ref, w0_ref, w1_ref, w2_ref, w3_ref, da_ref, perm_ref, dx_ref, acc_ref):
    step = pl.program_id(0)
    cols = 3 * w0_ref.shape[-1] // 4
    w = rows_of((w0_ref, w1_ref, w2_ref, w3_ref))
    add = nt(step_value((low_ref, high_ref), cols), w[:, :cols])

    accumulate(acc_ref, step, add)

    @pl.when(step == pl.num_programs(0) - 1)
    def _():
        dx = acc_ref[...] + da_ref[...]
        perm = perm_ref[...]
        dx_ref[...] = sum(nt(part, perm) for part in thirds(dx))


def whole(a):
    nd = len(a.shape)
    return pl.BlockSpec(a.shape, lambda s: (0,) * nd, pipeline_mode=pl.Buffered(1))


def lead(a):
    nd = len(a.shape)
    return pl.BlockSpec((1,) + a.shape[1:], lambda s: (s,) + (0,) * (nd - 1))


def weight(a):
    return pl.BlockSpec((a.shape[0], 1, BLK, a.shape[3]), lambda s: (0, s, 0, 0))


def half_spec(h):
    return pl.BlockSpec((h.shape[0], 1) + h.shape[2:], lambda s: (0, s, 0, 0))


def sds(shape, dtype):
    return jax.ShapeDtypeStruct(shape, dtype)


def far(shape, dtype):
    return pltpu.HBM(shape, dtype)


def call(body, n_t, micros, ins, outs, scratch=()):
    return pl.pallas_call(
        body,
        grid=(n_t,),
        in_specs=[s for _, s in ins],
        out_specs=[s for _, s in outs],
        out_shape=[a for a, _ in outs],
        scratch_shapes=list(scratch),
        compiler_params=pltpu.CompilerParams(
            dimension_semantics=("arbitrary",), vmem_limit_bytes=VMEM_LIMIT
        ),
        cost_estimate=pl.CostEstimate(flops=int(micros * COST), transcendentals=0, bytes_accessed=0),
    )(*[a for a, _ in ins])


def flips(n_dp, n_t):
    size = n_dp * n_t
    core = n_t
    x_bit, y_bit = 2 * core, 4 * core

    def table(bit_of):
        return [(i, i ^ bit_of(i)) for i in range(size)]

    return {
        "Z": [table(lambda i, d=d: d) for d in range(1, n_t)],
        "C": [table(lambda i: core)],
        "2": [table(lambda i: x_bit if i & core else y_bit)],
        "3": [table(lambda i: y_bit if i & core else x_bit)],
    }


def after(value, *done):
    return lax.optimization_barrier((value, *done))[0] if done else value


def swap(value, tables, *done):
    return lax.ppermute(after(value, *done), AXES, tables["C"][0])


class Gather:
    def __init__(self, value, tables):
        self.held, self.tables = [value[None]], tables

    def send(self, name, *done, parts=None, tables=None):
        sent = self.held if parts is None else [self.held[j] for j in parts]
        return [lax.ppermute(after(h, *done), AXES, t) for t in self.tables[name][tables or slice(None)] for h in sent]

    def take(self, name, got):
        self.held = [jnp.concatenate(self.held + got)] if name in "Z2" else self.held + got
        return got

    def stage(self, name, *done, parts=None):
        return self.take(name, self.send(name, *done, parts=parts))

    def pieces(self, *lead):
        return [h.reshape(*lead, *h.shape[1:]) for h in self.held]


class Scatter:
    def __init__(self, keep, send, tables):
        self.keep, self.send, self.tables = keep, [send], tables

    def stage(self, name, parts, *done, cut=1):
        tables = self.tables[name]
        pieces = len(self.send) // len(tables)
        got = [lax.ppermute(after(s, *done), AXES, tables[n // pieces]) for n, s in enumerate(self.send)]
        size = self.keep.shape[0] // parts // cut

        def piece(n):
            at = n * size
            total = self.keep[at : at + size].astype(f32)
            for t in range(len(tables)):
                mine = got[t * pieces : (t + 1) * pieces]
                wide = mine[0].shape[0]
                total = total + mine[at // wide][at % wide : at % wide + size].astype(f32)
            return total

        self.send = [piece(n).astype(bf16) for n in range(cut, parts * cut)]
        kept = [piece(n) for n in range(cut)]
        self.keep = kept[0] if cut == 1 else jnp.concatenate(kept)
        return got


def per_device(
    hidden_in, segment_ids, pooled_grad, qkv_weight, qv_bias, out_weight, out_bias,
    norm1_gain, norm1_shift, up_weight, up_bias, down_weight_in, down_bias, norm2_gain, norm2_shift,
):
    n_dp, n_t = lax.axis_size("dp"), lax.axis_size("tensor")
    at_dp, at_t = lax.axis_index("dp"), lax.axis_index("tensor")
    hc, fc = qkv_weight.shape[2], up_weight.shape[1]
    rows = qkv_weight.shape[1]
    D = rows * n_dp
    micro, tokens = hidden_in.shape[0], hidden_in.shape[1]
    seqs, L = segment_ids.shape[1], segment_ids.shape[2]
    G, T = micro * seqs, micro * tokens
    segs = pooled_grad.shape[2]
    n_i = D // BLK
    pairwise = (n_dp, n_t) == (8, 4) and 4 * hc == fc

    d_parts = [out_bias, norm1_gain, norm1_shift, down_bias, norm2_gain, norm2_shift]
    e_parts = [qv_bias[0], qv_bias[1], up_bias]
    dv = out_bias.shape[0]
    n_vec = sum(p.shape[0] for p in d_parts + e_parts)
    nd = len(d_parts) * dv

    sizes = (6, dv, up_bias.shape[0], D, hc, fc, n_t) if pairwise else (6, D // (n_i * n_t), n_t * fc // (n_i * n_t), D, hc, fc, n_t)
    slot = jnp.arange(n_i * n_t)
    rel = jnp.arange(n_i)
    if pairwise:
        tables = flips(n_dp, n_t)
        packed = (qkv_weight, out_weight, *[p[None] for p in d_parts], qv_bias, up_bias[None])
        packed = pl.pallas_call(pack, out_shape=sds((BLK + 8, 4 * hc), bf16))(*packed)
        first, middle = Gather(packed, tables), Gather(up_weight, tables)
        own = down_weight_in.T[None]

        def move(value, name, *done, way=0):
            return lax.ppermute(after(value, *done), AXES, tables[name][way])

        own2 = move(own, "2")
        done = first.stage("Z") + [own2]
        own2 = jnp.concatenate([own, own2])

        core = (at_dp & 1) ^ (rel >> 2)
        s3, s2 = (rel >> 1) & 1, rel & 1
        dy, dx = jnp.where(core == 0, s2, s3), jnp.where(core == 0, s3, s2)
        absolute = ((((at_dp >> 2) & 1) ^ dy) << 2) | ((((at_dp >> 1) & 1) ^ dx) << 1) | core
        i_p = jnp.broadcast_to(absolute[:, None], (n_i, n_t)).reshape(-1)
        t_p = jnp.broadcast_to((at_t ^ jnp.arange(n_t))[None], (n_i, n_t)).reshape(-1)
        to_d = jnp.broadcast_to(rel[:, None], (n_i, n_t)).reshape(-1) * n_t + t_p
        to_e = (((i_p * n_t) // n_i) ^ at_t) * n_i + (i_p * n_t + t_p) % n_i
    else:
        absolute, to_d, to_e = rel, slot, slot
    hot_d = (to_d[None, :] == slot[:, None]).astype(bf16)
    hot_e = (to_e[None, :] == slot[:, None]).astype(bf16)
    lane = jnp.arange(D)
    same_block = jnp.repeat(jnp.repeat((absolute[:, None] == rel[None, :]).T, BLK, axis=0), BLK, axis=1)
    perm = (same_block & ((lane[:, None] % BLK) == (lane[None, :] % BLK))).astype(bf16)
    turned = (D // 2, T)
    x, x_keep, x_send = pl.pallas_call(
        reorder, out_shape=[sds((T, D), bf16), sds(turned, bf16), sds(turned, bf16)], compiler_params=SMALL
    )(hidden_in.reshape(T, D), perm)
    pg = jnp.einsum("gsd,de->gse", pooled_grad.reshape(G, segs, D), perm.astype(f32), precision=HI)
    seg_r = segment_ids.reshape(G, L)
    seg_c = segment_ids.reshape(T, 1)

    if pairwise:
        done = first.stage("2", *done, x, x_keep, x_send, pg, hot_d, hot_e) + middle.stage("Z", *done)
        x_other = swap(x_send, tables, *done)
        z_one, z_two = move(own2, "Z", *done, way=0), move(own2, "Z", *done, way=1)
        got_q3, got_u2 = first.stage("3", *done), middle.stage("2", *done)
        first.stage("C", *got_u2, z_one, z_two)
        got_u3 = middle.send("3")
        z_three = move(own2, "Z", *got_q3, z_one, z_two, way=2)
        low = jnp.concatenate([own2, z_one])
        low_far = move(low, "3", *got_q3)
        w_qo = first.pieces(2, n_t)
    else:
        heads_in = [qkv_weight[0], qkv_weight[1], qkv_weight[2], out_weight.T]
        main = jnp.concatenate([*heads_in, up_weight, down_weight_in.T], axis=1)
        vec = jnp.concatenate(d_parts + e_parts)
        full = lax.all_gather(lax.all_gather(main, "dp", axis=0, tiled=True), "tensor", axis=0)
        full = full.reshape(n_t, n_i, BLK, -1).transpose(1, 0, 2, 3)
        vecs = lax.all_gather(lax.all_gather(vec, "tensor"), "dp").reshape(n_dp * n_t, -1)
        cuts = [j * dv for j in range(9)] + [n_vec]
        rows8 = jnp.concatenate([vecs[:, a:b].reshape(n_i * n_t, -1) for a, b in zip(cuts[:-1], cuts[1:])], axis=1)
        rows8 = jnp.pad(rows8.reshape(n_i, n_t, 1, -1), ((0, 0), (0, 0), (0, 7), (0, 4 * hc - rows8.shape[1])))
        quarters = [full[j * n_i // 4 : (j + 1) * n_i // 4] for j in range(4)]
        w_qo = [
            jnp.concatenate([w[..., : 4 * hc], rows8[j * n_i // 4 : (j + 1) * n_i // 4]], axis=2)
            for j, w in enumerate(quarters)
        ]
        w_up = [w[..., 4 * hc : 4 * hc + fc] for w in quarters]
        w_down = [w[..., 4 * hc + fc :].transpose(1, 0, 2, 3) for w in quarters]
        w_down = [w[: n_t // 2] for w in w_down] + [w[n_t // 2 :] for w in w_down]

    hl = hc // HD * L
    o_wide, q_wide = -(-hc // 128) * 128, -(-3 * hc // 128) * 128

    def leads(*arrays):
        return [(a, lead(a)) for a in arrays]

    def wholes(*arrays):
        return [(a, whole(a)) for a in arrays]

    def weights(*arrays):
        return [(a, weight(a)) for a in arrays]

    def weights_t(*arrays):
        return [(a, pl.BlockSpec((1, a.shape[1], BLK, a.shape[3]), lambda s: (s, 0, 0, 0))) for a in arrays]

    def paired(*arrays):
        return [(a, pl.BlockSpec((2, 1) + a.shape[2:], lambda s: (0, s, 0, 0))) for a in arrays]

    def folded(a):
        return a.reshape(2, n_t // 2, *a.shape[1:])

    tails = [
        (w, pl.BlockSpec((w.shape[0], n_t, 8, w.shape[3]), lambda s: (0, 0, BLK // 8, 0), pipeline_mode=pl.Buffered(1)))
        for w in w_qo
    ]
    qkv, prob, o, n1, x1, r1, n1b, n1_keep, n1_send, vec_d, b_u = call(
        partial(attention_forward, sizes), n_t, 10,
        wholes(x) + weights(*w_qo) + tails + wholes(hot_d, hot_e, seg_c, seg_r),
        leads(far((n_t, T, 3 * hc), bf16), far((n_t, G, L, hl), f32), far((n_t, T, o_wide), bf16))
        + wholes(sds((T, D), f32), far((T, D), f32), far((T, 1), f32), sds((T, D), bf16), far(turned, bf16), far(turned, bf16))
        + wholes(sds((6, D), f32), sds((n_t, 1, fc), f32)),
        [pltpu.VMEM((T, D), f32), pltpu.VMEM((n_t, 1, hc), f32), pltpu.VMEM((n_t, 1, hc), f32)],
    )
    if pairwise:
        middle.take("3", [after(g, n1b) for g in got_u3])
        middle.stage("C", n1b, z_three)
        high = jnp.concatenate([z_two, after(z_three, n1b)])
        high_far = move(high, "3")
        w_up = middle.pieces(2, n_t)
        low_other = [swap(low, tables, n1b), swap(after(low_far, n1b), tables)]
        n1_other = swap(n1_send, tables)
        o_other = swap(o, tables)
        b_u = after(b_u, *low_other)
    z, dgelu = call(
        up_forward, n_t, 4, wholes(n1b) + weights(*w_up) + leads(b_u),
        leads(sds((n_t, T, fc), bf16), sds((n_t, T, fc), f32)),
    )
    if pairwise:
        high_other = [swap(high, tables), swap(after(high_far, z), tables)]
        w_down = [low, low_far, *low_other, high, high_far, *high_other]
        w_down = [w.reshape(n_t // 2, 2, BLK, fc) for w in w_down]
        z_other = swap(z, tables, *high_other)
        dgelu = after(dgelu, x_other, n1_other, o_other)
    pooled, db, dbb, db_keep, db_send, sums2 = call(
        down_forward, n_t // 2, 5.5, paired(folded(z)) + weights_t(*w_down) + wholes(n1, vec_d, seg_c, seg_r, pg),
        wholes(sds((G, segs, D), f32), sds((T, D), f32), sds((T, D), bf16), sds(turned, bf16), sds(turned, bf16), sds((3, D), f32)),
        [pltpu.VMEM((T, D), f32)],
    )

    def gradient(groups, vectors=(), at_once=True):
        ins, kinds = [], []
        for width, *pairs in groups:
            kinds.append((len(pairs), len(pairs[0][1]), width))
            for lhs, values in pairs:
                ins += wholes(lhs) + (leads(*values) if len(values) == 1 else halved(*values))
        out = sds((n_i // 4, n_t, BLK + (8 if vectors else 0), sum(k[2] for k in kinds)), bf16)

        def share(which):
            return call(
                partial(weight_gradient, kinds, len(vectors), which), n_t, 2, ins + leads(*vectors),
                [(out, half_spec(out))] * (2 if which is None else 1),
            )

        return share(None) if at_once else (share(0)[0], share(1)[0])

    def halved(low, high):
        block = (1,) + low.shape[1:]
        return [
            (low, pl.BlockSpec(block, lambda s: (jnp.minimum(s, n_t // 2 - 1), 0, 0))),
            (high, pl.BlockSpec(block, lambda s: (jnp.maximum(s - n_t // 2, 0), 0, 0))),
        ]

    def flat(a):
        return a.reshape((-1,) + a.shape[2:])

    du, g_bu = call(
        hidden_backward, n_t // 2, 3.5, wholes(dbb) + weights_t(*w_down) + paired(folded(dgelu)),
        paired(sds((2, n_t // 2, T, fc), bf16), sds((2, n_t // 2, 1, fc), f32)),
    )
    du, g_bu = du.reshape(n_t, T, fc), g_bu.reshape(n_t, 1, fc)
    if pairwise:
        db_other = swap(db_send, tables)
        du_other = swap(du, tables)
        down_keep, down_send = gradient([[fc, (after(db_keep, g_bu), [z]), (db_other, [z_other])]], at_once=False)
        s_down = Scatter(flat(down_keep), flat(down_send), tables)
        got_d3 = s_down.stage("3", 2)
        du_next = after(du, down_send)
        dab_after = down_keep
    else:
        du_next = du
    da, dab, da_keep, da_send, sums1 = call(
        norm_backward, n_t, NORM, leads(du_next) + weights(*w_up) + wholes(db, x1, r1, vec_d),
        wholes(sds((T, D), f32), sds((T, D), bf16), sds(turned, bf16), sds(turned, bf16), sds((3, D), f32)),
        [pltpu.VMEM((T, D), f32)],
    )
    if pairwise:
        da_other = swap(da_send, tables)
        up_keep, up_send = gradient([[fc, (after(n1_keep, da_keep), [du]), (n1_other, [du_other])]])
        s_up = Scatter(flat(up_keep), flat(up_send), tables)
        got_u3 = s_up.stage("3", 2)
        dab = after(dab, up_keep)
    rows = sds((n_t, n_i // 2, 4 * hc), f32)
    if pairwise:
        dab = after(dab, da_other, dab_after, *got_d3)
    dq_half = sds((n_t // 2, T, q_wide), bf16)
    *dq, v_keep, v_send = call(
        partial(attention_backward, sizes), n_t, 8,
        wholes(dab) + weights(*w_qo) + leads(qkv, prob) + wholes(sums1, sums2, g_bu, hot_d, hot_e),
        halved(dq_half, dq_half) + wholes(rows, rows),
        [pltpu.VMEM((n_t, 1, hc), f32), pltpu.VMEM((n_t, 1, hc), f32), pltpu.VMEM((T, q_wide), bf16)],
    )
    if pairwise:
        dq_other = [swap(d, tables) for d in dq]
        v_other = swap(v_send, tables)
        got_d2 = s_down.stage("2", n_t)
    pooled = jnp.einsum("gse,de->gsd", pooled, perm.astype(f32), precision=HI)
    if pairwise:
        x_now = after(x_keep, *got_u3)
        qo_keep, qo_send = gradient(
            [[3 * hc, (x_now, dq), (x_other, dq_other)], [hc, (da_keep, [o]), (da_other, [o_other])]], (v_keep, v_other)
        )
        s_qo = Scatter(flat(qo_keep), flat(qo_send), tables)
        got_u2 = s_up.stage("2", n_t)
        s_qo.stage("3", 2, *got_d2, *got_u2, pooled, cut=CUT)
        both = Scatter(jnp.concatenate([s_down.keep, s_up.keep]), None, tables)
        both.send = [jnp.concatenate([a, b]) for a, b in zip(s_down.send, s_up.send, strict=True)]
        got_z = both.stage("Z", 1)
        dq = [after(d, qo_keep) for d in dq]
    dx = call(
        input_backward, n_t, 4, halved(*dq) + weights(*w_qo) + wholes(da, perm), wholes(sds((T, D), f32)),
        [pltpu.VMEM((T, D), f32)],
    )[0]

    if pairwise:
        s_qo.stage("2", n_t, dx)
        s_qo.stage("Z", 1, *got_z)
        g_down, g_up, g_qo = both.keep[0], both.keep[1], s_qo.keep[0]
        g_v = g_qo[BLK, :n_vec]
        g_qo = g_qo[:BLK]
    else:
        def joined(*halves_of):
            g = jnp.concatenate([part[:, :, :BLK] for half in halves_of for part in half])
            return g.transpose(1, 0, 2, 3).reshape(n_t, D, -1)

        x_h, n1_h, db_h, da_h = (x_keep, x_send), (n1_keep, n1_send), (db_keep, db_send), (da_keep, da_send)
        g_full = jnp.concatenate([
            joined(*[gradient([[3 * hc, (x_h[j], dq)], [hc, (da_h[j], [o])]]) for j in range(2)]),
            joined(*[gradient([[fc, (n1_h[j], [du])]]) for j in range(2)]),
            joined(*[gradient([[fc, (db_h[j], [z])]]) for j in range(2)]),
        ], axis=2)
        mine = lax.psum_scatter(g_full, "tensor", scatter_dimension=0)
        mine = lax.psum_scatter(mine, "dp", scatter_dimension=0, tiled=True).astype(f32)
        g_qo, g_up, g_down = mine[:, : 4 * hc], mine[:, 4 * hc : 4 * hc + fc], mine[:, 4 * hc + fc :]
        g_rows = jnp.stack([v_keep, v_send]).transpose(0, 2, 1, 3).reshape(n_i * n_t, -1)
        dv_c, bu_c = sizes[1], sizes[2]
        cuts = [j * dv_c for j in range(9)] + [8 * dv_c + bu_c]
        g_v = jnp.concatenate(
            [g_rows[:, a:b].reshape(n_dp * n_t, -1) for a, b in zip(cuts[:-1], cuts[1:])], axis=1
        )
        g_v = lax.psum_scatter(g_v, AXES, scatter_dimension=0)
    vo = [g_v[j * dv : (j + 1) * dv] for j in range(8)]
    return (
        pooled.reshape(micro, seqs, segs, D),
        dx.reshape(micro, tokens, D),
        jnp.stack([g_qo[:, c * hc : (c + 1) * hc] for c in range(3)]),
        jnp.stack([vo[6], vo[7]]),
        g_qo[:, 3 * hc :].T,
        vo[0], vo[1], vo[2],
        g_up,
        g_v[8 * dv :],
        g_down.T,
        vo[3], vo[4], vo[5],
    )


def solution(mesh):
    both = P(AXES)
    row3 = P(None, AXES)
    return jax.shard_map(
        per_device,
        mesh=mesh,
        in_specs=(
            row3, row3, row3, P(None, "dp", "tensor"), row3, P("tensor", "dp"), both, both, both,
            P("dp", "tensor"), both, P("tensor", "dp"), both, both, both,
        ),
        out_specs=(
            row3, row3, P(None, "dp", "tensor"), row3, P("tensor", "dp"), both, both, both,
            P("dp", "tensor"), both, P("tensor", "dp"), both, both, both,
        ),
        check_vma=False,
    )
```

```python
from functools import partial

import jax
import jax.numpy as jnp
from jax import lax
from jax.experimental import pallas as pl
from jax.experimental.pallas import tpu as pltpu
from jax.sharding import PartitionSpec as P

HD = 64
EPS = 1e-12
NEG = -1000000000.0
SCALE = float(HD) ** -0.5
AXES = ("dp", "tensor")
f32 = jnp.float32
bf16 = jnp.bfloat16
HI = lax.Precision.HIGHEST
BLK = 96
VMEM_LIMIT = 24 * 1024 * 1024
COST = 30_000_000
NORM = 2000
CUT = 4
SMALL = pltpu.CompilerParams(vmem_limit_bytes=8 * 1024 * 1024)


def nn(a, b):
    return lax.dot_general(a, b, (((1,), (0,)), ((), ())), preferred_element_type=f32)


def nt(a, b):
    return lax.dot_general(a, b, (((1,), (1,)), ((), ())), preferred_element_type=f32)


def tn(a, b):
    return lax.dot_general(a, b, (((0,), (0,)), ((), ())), preferred_element_type=f32)


def mean_last(v):
    return jnp.sum(v, axis=-1, keepdims=True) * (1.0 / v.shape[-1])


def normalize(values):
    center = values - mean_last(values)
    inverse = lax.rsqrt(mean_last(center * center) + EPS)
    return center * inverse, inverse


def normalize_back(scaled, normed, inverse):
    return inverse * (scaled - mean_last(scaled) - normed * mean_last(scaled * normed))


def col_sum(v):
    return jnp.sum(v, axis=0, keepdims=True)


def pack(qkv_ref, out_ref, ob_ref, g1_ref, s1_ref, db_ref, g2_ref, s2_ref, qv_ref, ub_ref, first_ref):
    rows, hc = qkv_ref.shape[1:]
    eye = (lax.broadcasted_iota(jnp.int32, (rows, rows), 0) == lax.broadcasted_iota(jnp.int32, (rows, rows), 1)).astype(bf16)
    for c in range(3):
        first_ref[:rows, c * hc : (c + 1) * hc] = qkv_ref[c]
    first_ref[:rows, 3 * hc :] = nt(eye, out_ref[...]).astype(bf16)
    parts = [r[...].astype(f32) for r in (ob_ref, g1_ref, s1_ref, db_ref, g2_ref, s2_ref, qv_ref)]
    short = jnp.concatenate(parts, axis=0).astype(bf16)
    count, size = short.shape
    wide = first_ref.shape[1]

    def spread(values, at):
        lane = lax.broadcasted_iota(jnp.int32, (values.shape[1], wide), 1) - at
        return nn(values, (lax.rem(lane + values.shape[1] * wide, values.shape[1]) == lax.broadcasted_iota(jnp.int32, lane.shape, 0)).astype(bf16))

    lane = lax.broadcasted_iota(jnp.int32, (count, wide), 1)
    start = lax.broadcasted_iota(jnp.int32, (count, wide), 0) * size
    row = col_sum(jnp.where((lane >= start) & (lane < start + size), spread(short, 0), 0.0))
    total, long = count * size, ub_ref.shape[1]
    lane = lax.broadcasted_iota(jnp.int32, (1, wide), 1)
    row = jnp.where((lane >= total) & (lane < total + long), spread(ub_ref[...], total), row)
    extra = first_ref.shape[0] - rows
    here = lax.broadcasted_iota(jnp.int32, (extra, wide), 0)
    first_ref[rows:, :] = jnp.where(here == 0, row, 0.0).astype(bf16)


def reorder(h_ref, perm_ref, x_ref, keep_ref, send_ref):
    x = nn(h_ref[...], perm_ref[...]).astype(bf16)
    x_ref[...] = x
    turned = x.T
    keep_ref[...] = turned[: x.shape[1] // 2]
    send_ref[...] = turned[x.shape[1] // 2 :]


def stacked(values, hc):
    head = lax.broadcasted_iota(jnp.int32, (1, hc), 1) // HD
    return jnp.concatenate([values * (head == h).astype(f32).astype(bf16) for h in range(hc // HD)], axis=0)


def own_columns(blocks, hc):
    n_heads = hc // HD
    length = blocks.shape[0] // n_heads
    head = lax.broadcasted_iota(jnp.int32, (1, hc), 1) // HD
    out = blocks[:length]
    for h in range(1, n_heads):
        out = jnp.where(head == h, blocks[h * length : (h + 1) * length], out)
    return out


def sections(values, length):
    return [values[:, c : c + length] for c in range(0, values.shape[1], length)]


def rows_of(refs):
    return jnp.concatenate([r[...].reshape(-1, r.shape[3]) for r in refs], axis=0)


def thirds(values):
    high = values.astype(bf16)
    rest = values - high.astype(f32)
    middle = rest.astype(bf16)
    return high, middle, (rest - middle.astype(f32)).astype(bf16)


def accumulate(acc_ref, step, add):
    @pl.when(step == 0)
    def _():
        acc_ref[...] = add

    @pl.when(step > 0)
    def _():
        acc_ref[...] += add


def iota(shape, axis):
    return lax.broadcasted_iota(jnp.int32, shape, axis)


def picks(count, first, wide, size):
    return (iota((count, wide), 0) == first + lax.rem(iota((1, wide), 1), size)).astype(bf16)


def belongs(count, wide, size, period):
    lane, row = iota((1, wide), 1), lax.rem(iota((count, 1), 0), period)
    return (lane >= row * size) & (lane < (row + 1) * size)


def read_vectors(rows, hot_d, hot_e, sizes):
    n_d, dv, bu, width, hc, fc, n_t = sizes
    count = rows.shape[0]
    per = count // n_t
    d_all = nn(hot_d, rows[:, : n_d * dv]).astype(bf16)
    mine = belongs(count, width, dv, count)
    d_rows = [col_sum(jnp.where(mine, nn(d_all, picks(n_d * dv, j * dv, width, dv)), 0.0)) for j in range(n_d)]
    e_all = nn(hot_e, rows[:, n_d * dv : n_d * dv + 2 * dv + bu]).astype(bf16)
    out = []
    for first, size, wide in ((0, dv, hc), (dv, dv, hc), (2 * dv, bu, fc)):
        spread = jnp.where(belongs(count, wide, size, per), nn(e_all, picks(e_all.shape[1], first, wide, size)), 0.0)
        out.append(jnp.sum(spread.reshape(n_t, per, wide), axis=1, keepdims=True))
    return jnp.concatenate(d_rows, axis=0), out


def write_vectors(d_rows, e_rows, hot_d, hot_e, sizes):
    n_d, dv, bu, width, hc, fc, n_t = sizes
    count = hot_d.shape[0]
    per = count // n_t
    mine = belongs(count, width, dv, count)
    d_all = sum(
        nt(jnp.where(mine, d_rows[j : j + 1, :], 0.0).astype(bf16), picks(n_d * dv, j * dv, width, dv)) for j in range(n_d)
    ).astype(bf16)
    e_all = 0.0
    for value, first, size, wide in zip(e_rows, (0, dv, 2 * dv), (dv, dv, bu), (hc, hc, fc), strict=True):
        spread = jnp.broadcast_to(value, (n_t, per, wide)).reshape(count, wide)
        spread = jnp.where(belongs(count, wide, size, per), spread, 0.0).astype(bf16)
        e_all = e_all + nt(spread, picks(2 * dv + bu, first, wide, size))
    return jnp.concatenate([tn(hot_d, d_all), tn(hot_e, e_all.astype(bf16))], axis=1)


def attention_forward(sizes, x_ref, w0_ref, w1_ref, w2_ref, w3_ref, v0_ref, v1_ref, v2_ref, v3_ref, hd_ref, he_ref,
                      segc_ref, segr_ref, qkv_ref, p_ref, o_ref, n1_ref, x1_ref, r1_ref, n1b_ref, n1t_ref, n1s_ref,
                      vec_ref, bu_ref, acc_ref, bq_ref, bv_ref):
    step = pl.program_id(0)
    hc = bq_ref.shape[-1]

    @pl.when(step == 0)
    def _():
        rows = jnp.concatenate([r[:, :, 0, :].reshape(-1, r.shape[3]) for r in (v0_ref, v1_ref, v2_ref, v3_ref)], axis=0)
        d_rows, (b_q, b_v, b_u) = read_vectors(rows, hd_ref[...], he_ref[...], sizes)
        vec_ref[...] = d_rows
        bq_ref[...] = b_q
        bv_ref[...] = b_v
        bu_ref[...] = b_u

    rows, length = segr_ref.shape
    x = x_ref[...]
    w = rows_of((w0_ref, w1_ref, w2_ref, w3_ref))
    qkv = nn(x, w[:, : 3 * hc])
    q = (qkv[:, :hc] + bq_ref[step]).astype(bf16) * bf16(SCALE)
    k = qkv[:, hc : 2 * hc].astype(bf16)
    v = (qkv[:, 2 * hc :] + bv_ref[step]).astype(bf16)
    qkv_ref[0, :, :hc] = q
    qkv_ref[0, :, hc : 2 * hc] = k
    qkv_ref[0, :, 2 * hc :] = v
    spans = [slice(g * length, (g + 1) * length) for g in range(rows)]
    scores = [nt(q[span], stacked(k[span], hc)) for span in spans]
    probs = []
    for g, span in enumerate(spans):
        same = segc_ref[span, :] == segr_ref[g : g + 1, :]
        parts = []
        for s in sections(scores[g], length):
            s = jnp.where(same, s, NEG)
            e = jnp.exp(s - jnp.max(s, axis=-1, keepdims=True))
            parts.append(e * (1.0 / jnp.sum(e, axis=-1, keepdims=True)))
        probs.append(jnp.concatenate(parts, axis=1))
    for g, span in enumerate(spans):
        p_ref[0, g] = probs[g]
        o_ref[0, span, :hc] = nn(probs[g].astype(bf16), stacked(v[span], hc)).astype(bf16)
    o_ref[0, :, hc:] = jnp.zeros((o_ref.shape[1], o_ref.shape[2] - hc), bf16)
    add = nt(o_ref[0, :, :hc], w[:, 3 * hc :])

    accumulate(acc_ref, step, add)

    @pl.when(step == pl.num_programs(0) - 1)
    def _():
        a = acc_ref[...] + vec_ref[0:1, :] + x_ref[...].astype(f32)
        normed, inverse = normalize(a)
        n1 = normed * vec_ref[1:2, :] + vec_ref[2:3, :]
        n1_ref[...] = n1
        x1_ref[...] = normed
        r1_ref[...] = inverse
        low = n1.astype(bf16)
        n1b_ref[...] = low
        turned = low.T
        n1t_ref[...] = turned[: low.shape[1] // 2]
        n1s_ref[...] = turned[low.shape[1] // 2 :]


def up_forward(n_ref, w0_ref, w1_ref, w2_ref, w3_ref, b_ref, z_ref, d_ref):
    u = nn(n_ref[...], rows_of((w0_ref, w1_ref, w2_ref, w3_ref))) + b_ref[0]
    phi = 0.5 + 0.5 * lax.erf(u * (0.5**0.5))
    z_ref[0] = (u * phi).astype(bf16)
    d_ref[0] = phi + u * (jnp.exp(-0.5 * u * u) * 0.3989422804014327)


def down_forward(z_ref, w0_ref, w1_ref, w2_ref, w3_ref, w4_ref, w5_ref, w6_ref, w7_ref, n1_ref, vec_ref, segc_ref, segr_ref, pg_ref,
                 pooled_ref, db_ref, dbb_ref, dbt_ref, dbs_ref, sums_ref, acc_ref):
    step = pl.program_id(0)
    add = nt(z_ref[0, 0], rows_of((w0_ref, w1_ref, w2_ref, w3_ref))) + nt(z_ref[1, 0], rows_of((w4_ref, w5_ref, w6_ref, w7_ref)))

    accumulate(acc_ref, step, add)

    @pl.when(step == pl.num_programs(0) - 1)
    def _():
        rows, length = segr_ref.shape
        segs = pg_ref.shape[1]
        b = acc_ref[...] + vec_ref[3:4, :] + n1_ref[...]
        x2, r2 = normalize(b)
        y = x2 * vec_ref[4:5, :] + vec_ref[5:6, :]
        grads = []
        for g in range(rows):
            span = slice(g * length, (g + 1) * length)
            hot_t = (iota((segs, length), 0) == segr_ref[g : g + 1, :]).astype(f32)
            count = jnp.sum(hot_t, axis=1, keepdims=True)
            hot_t = hot_t.astype(bf16)
            hot = (iota((length, segs), 1) == segc_ref[span, :]).astype(f32).astype(bf16)
            pooled_ref[g] = sum(nn(hot_t, part) for part in thirds(y[span, :])) / count
            grads.append(nn(jnp.concatenate([hot] * 3, axis=1), jnp.concatenate(thirds(pg_ref[g] / count), axis=0)))
        dy = jnp.concatenate(grads, axis=0)
        db = normalize_back(dy * vec_ref[4:5, :], x2, r2)
        db_ref[...] = db
        low = db.astype(bf16)
        dbb_ref[...] = low
        turned = low.T
        dbt_ref[...] = turned[: low.shape[1] // 2]
        dbs_ref[...] = turned[low.shape[1] // 2 :]
        sums_ref[0:1, :] = col_sum(db)
        sums_ref[1:2, :] = col_sum(dy * x2)
        sums_ref[2:3, :] = col_sum(dy)


def put(grad, ref):
    ref[:, :, :BLK, :] = grad.astype(bf16).reshape(grad.shape[0] // BLK, 1, BLK, grad.shape[1])


def hidden_backward(dbb_ref, w0_ref, w1_ref, w2_ref, w3_ref, w4_ref, w5_ref, w6_ref, w7_ref, d_ref, du_ref, bu_ref):
    for n, refs in enumerate(((w0_ref, w1_ref, w2_ref, w3_ref), (w4_ref, w5_ref, w6_ref, w7_ref))):
        du = (nn(dbb_ref[...], rows_of(refs)) * d_ref[n, 0]).astype(bf16)
        du_ref[n, 0] = du
        bu_ref[n, 0] = col_sum(du.astype(f32))


def step_value(refs, width):
    if len(refs) == 1:
        return refs[0][0, :, :width]
    return jnp.where(pl.program_id(0) < pl.num_programs(0) // 2, refs[0][0, :, :width], refs[1][0, :, :width])


def weight_gradient(groups, vectors, which, *refs):
    refs = list(refs)
    parts = []
    for pairs, split, width in groups:
        total = None
        for _ in range(pairs):
            rows = refs.pop(0)
            half = rows.shape[0] // 2
            rows = rows[...] if which is None else rows[which * half : (which + 1) * half, :]
            add = nn(rows, step_value([refs.pop(0) for _ in range(split)], width))
            total = add if total is None else total + add
        parts.append(total)
    grad = jnp.concatenate(parts, axis=1)
    extra = sum(refs.pop(0)[0].astype(f32) for _ in range(vectors)) if vectors else None
    half = grad.shape[0] // len(refs)
    for n, ref in enumerate(refs):
        put(grad[n * half : (n + 1) * half], ref)
        if vectors:
            for j in range(ref.shape[0]):
                at = (n if which is None else which) * ref.shape[0] + j
                row = extra[at : at + 1]
                tail = ref.shape[2] - BLK
                ref[j, 0, BLK:, :] = jnp.where(iota((tail, row.shape[1]), 0) == 0, row, 0.0).astype(bf16)


def norm_backward(du_ref, w0_ref, w1_ref, w2_ref, w3_ref, db_ref, x1_ref, r1_ref, vec_ref,
                  da_ref, dab_ref, dat_ref, das_ref, sums_ref, acc_ref):
    step = pl.program_id(0)
    accumulate(acc_ref, step, nt(du_ref[0], rows_of((w0_ref, w1_ref, w2_ref, w3_ref))))

    @pl.when(step == pl.num_programs(0) - 1)
    def _():
        dn1 = acc_ref[...].astype(bf16).astype(f32) + db_ref[...]
        da = normalize_back(dn1 * vec_ref[1:2, :], x1_ref[...], r1_ref[...])
        da_ref[...] = da
        low = da.astype(bf16)
        dab_ref[...] = low
        turned = low.T
        dat_ref[...] = turned[: low.shape[1] // 2]
        das_ref[...] = turned[low.shape[1] // 2 :]
        sums_ref[0:1, :] = col_sum(da)
        sums_ref[1:2, :] = col_sum(dn1 * x1_ref[...])
        sums_ref[2:3, :] = col_sum(dn1)


def attention_backward(sizes, dab_ref, w0_ref, w1_ref, w2_ref, w3_ref, qkv_ref, p_ref, s1_ref, s2_ref, gu_ref, hd_ref, he_ref,
                       low_ref, high_ref, keep_ref, send_ref, bq_ref, bv_ref, dqkv_ref):
    step = pl.program_id(0)
    hc = bq_ref.shape[-1]
    dab = dab_ref[...]
    w = rows_of([r.at[:, :, :, 3 * hc :] for r in (w0_ref, w1_ref, w2_ref, w3_ref)])
    do = nn(dab, w).astype(bf16)
    qkv = qkv_ref[0]
    rows, length = p_ref.shape[1], p_ref.shape[2]
    spans = [slice(g * length, (g + 1) * length) for g in range(rows)]
    q = [qkv[span, :hc] for span in spans]
    k = [stacked(qkv[span, hc : 2 * hc], hc) for span in spans]
    dps = [nt(do[span], stacked(qkv[span, 2 * hc :], hc)) for span in spans]
    dss = []
    for g in range(rows):
        parts = []
        for p, dp in zip(sections(p_ref[0, g], length), sections(dps[g], length)):
            pd = p * dp
            parts.append((pd - p * jnp.sum(pd, axis=-1, keepdims=True)).astype(bf16))
        dss.append(jnp.concatenate(parts, axis=1))
    for g, span in enumerate(spans):
        dqkv_ref[span, :hc] = (nn(dss[g], k[g]) * SCALE).astype(bf16)
        dqkv_ref[span, hc : 2 * hc] = own_columns(tn(dss[g], q[g]), hc).astype(bf16)
        dqkv_ref[span, 2 * hc : 3 * hc] = own_columns(tn(p_ref[0, g].astype(bf16), do[span]), hc).astype(bf16)
    dqkv_ref[:, 3 * hc :] = jnp.zeros((dqkv_ref.shape[0], dqkv_ref.shape[1] - 3 * hc), bf16)
    dqkv = dqkv_ref[...]
    half_steps = pl.num_programs(0) // 2

    @pl.when(step < half_steps)
    def _():
        low_ref[0] = dqkv

    @pl.when(step >= half_steps)
    def _():
        high_ref[0] = dqkv

    bq_ref[step] = col_sum(dqkv[:, :hc].astype(f32))
    bv_ref[step] = col_sum(dqkv[:, 2 * hc : 3 * hc].astype(f32))

    @pl.when(step == pl.num_programs(0) - 1)
    def _():
        d_rows = jnp.concatenate([s1_ref[...], s2_ref[...]], axis=0)
        rows = write_vectors(d_rows, (bq_ref[...], bv_ref[...], gu_ref[...]), hd_ref[...], he_ref[...], sizes)
        half, n_t = rows.shape[0] // 2, bq_ref.shape[0]
        rows = jnp.concatenate([rows, jnp.zeros((rows.shape[0], keep_ref.shape[-1] - rows.shape[1]), f32)], axis=1)
        for n, ref in enumerate((keep_ref, send_ref)):
            for t in range(n_t):
                for j in range(half // n_t):
                    at = n * half + j * n_t + t
                    ref[t, j : j + 1, :] = rows[at : at + 1]


def input_backward(low_ref, high_ref, w0_ref, w1_ref, w2_ref, w3_ref, da_ref, perm_ref, dx_ref, acc_ref):
    step = pl.program_id(0)
    cols = 3 * w0_ref.shape[-1] // 4
    w = rows_of((w0_ref, w1_ref, w2_ref, w3_ref))
    add = nt(step_value((low_ref, high_ref), cols), w[:, :cols])

    accumulate(acc_ref, step, add)

    @pl.when(step == pl.num_programs(0) - 1)
    def _():
        dx = acc_ref[...] + da_ref[...]
        perm = perm_ref[...]
        dx_ref[...] = sum(nt(part, perm) for part in thirds(dx))


def finish(total_ref, qkv_ref, out_ref, qv_ref, *vector_refs):
    total = total_ref[...]
    rows, hc = qkv_ref.shape[1:]
    for c in range(3):
        qkv_ref[c] = total[:rows, c * hc : (c + 1) * hc]
    out_ref[...] = total[:rows, 3 * hc :].T
    row = total[rows : rows + 1]
    at = 0
    for n, ref in enumerate(vector_refs):
        if n == 6:
            size = qv_ref.shape[1]
            qv_ref[...] = jnp.concatenate([row[:, at : at + size], row[:, at + size : at + 2 * size]], axis=0)
            at += 2 * size
        ref[...] = row[:, at : at + ref.shape[1]]
        at += ref.shape[1]


def whole(a):
    nd = len(a.shape)
    return pl.BlockSpec(a.shape, lambda s: (0,) * nd, pipeline_mode=pl.Buffered(1))


def lead(a):
    nd = len(a.shape)
    return pl.BlockSpec((1,) + a.shape[1:], lambda s: (s,) + (0,) * (nd - 1))


def weight(a):
    return pl.BlockSpec((a.shape[0], 1, BLK, a.shape[3]), lambda s: (0, s, 0, 0))


def half_spec(h):
    return pl.BlockSpec((h.shape[0], 1) + h.shape[2:], lambda s: (0, s, 0, 0))


def sds(shape, dtype):
    return jax.ShapeDtypeStruct(shape, dtype)


def far(shape, dtype):
    return pltpu.HBM(shape, dtype)


def call(body, n_t, micros, ins, outs, scratch=()):
    return pl.pallas_call(
        body,
        grid=(n_t,),
        in_specs=[s for _, s in ins],
        out_specs=[s for _, s in outs],
        out_shape=[a for a, _ in outs],
        scratch_shapes=list(scratch),
        compiler_params=pltpu.CompilerParams(
            dimension_semantics=("arbitrary",), vmem_limit_bytes=VMEM_LIMIT
        ),
        cost_estimate=pl.CostEstimate(flops=int(micros * COST), transcendentals=0, bytes_accessed=0),
    )(*[a for a, _ in ins])


def flips(n_dp, n_t):
    size = n_dp * n_t
    core = n_t
    x_bit, y_bit = 2 * core, 4 * core

    def table(bit_of):
        return [(i, i ^ bit_of(i)) for i in range(size)]

    return {
        "Z": [table(lambda i, d=d: d) for d in range(1, n_t)],
        "C": [table(lambda i: core)],
        "2": [table(lambda i: x_bit if i & core else y_bit)],
        "3": [table(lambda i: y_bit if i & core else x_bit)],
    }


def after(value, *done):
    return lax.optimization_barrier((value, *done))[0] if done else value


def swap(value, tables, *done):
    return lax.ppermute(after(value, *done), AXES, tables["C"][0])


class Gather:
    def __init__(self, value, tables):
        self.held, self.tables = [value[None]], tables

    def send(self, name, *done, parts=None, tables=None):
        sent = self.held if parts is None else [self.held[j] for j in parts]
        return [lax.ppermute(after(h, *done), AXES, t) for t in self.tables[name][tables or slice(None)] for h in sent]

    def take(self, name, got):
        self.held = [jnp.concatenate(self.held + got)] if name in "Z2" else self.held + got
        return got

    def stage(self, name, *done, parts=None):
        return self.take(name, self.send(name, *done, parts=parts))

    def pieces(self, *lead):
        return [h.reshape(*lead, *h.shape[1:]) for h in self.held]


class Scatter:
    def __init__(self, keep, send, tables):
        self.keep, self.send, self.tables = keep, [send], tables

    def stage(self, name, parts, *done, cut=1):
        tables = self.tables[name]
        pieces = len(self.send) // len(tables)
        got = [lax.ppermute(after(s, *done), AXES, tables[n // pieces]) for n, s in enumerate(self.send)]
        size = self.keep.shape[0] // parts // cut

        def piece(n):
            at = n * size
            total = self.keep[at : at + size].astype(f32)
            for t in range(len(tables)):
                mine = got[t * pieces : (t + 1) * pieces]
                wide = mine[0].shape[0]
                total = total + mine[at // wide][at % wide : at % wide + size].astype(f32)
            return total

        self.send = [piece(n).astype(bf16) for n in range(cut, parts * cut)]
        kept = [piece(n) for n in range(cut)]
        self.keep = kept[0] if cut == 1 else jnp.concatenate(kept)
        return got


def per_device(
    hidden_in, segment_ids, pooled_grad, qkv_weight, qv_bias, out_weight, out_bias,
    norm1_gain, norm1_shift, up_weight, up_bias, down_weight_in, down_bias, norm2_gain, norm2_shift,
):
    n_dp, n_t = lax.axis_size("dp"), lax.axis_size("tensor")
    at_dp, at_t = lax.axis_index("dp"), lax.axis_index("tensor")
    hc, fc = qkv_weight.shape[2], up_weight.shape[1]
    rows = qkv_weight.shape[1]
    D = rows * n_dp
    micro, tokens = hidden_in.shape[0], hidden_in.shape[1]
    seqs, L = segment_ids.shape[1], segment_ids.shape[2]
    G, T = micro * seqs, micro * tokens
    segs = pooled_grad.shape[2]
    n_i = D // BLK
    pairwise = (n_dp, n_t) == (8, 4) and 4 * hc == fc

    d_parts = [out_bias, norm1_gain, norm1_shift, down_bias, norm2_gain, norm2_shift]
    e_parts = [qv_bias[0], qv_bias[1], up_bias]
    dv = out_bias.shape[0]
    n_vec = sum(p.shape[0] for p in d_parts + e_parts)
    nd = len(d_parts) * dv

    sizes = (6, dv, up_bias.shape[0], D, hc, fc, n_t) if pairwise else (6, D // (n_i * n_t), n_t * fc // (n_i * n_t), D, hc, fc, n_t)
    slot = jnp.arange(n_i * n_t)
    rel = jnp.arange(n_i)
    if pairwise:
        tables = flips(n_dp, n_t)
        packed = (qkv_weight, out_weight, *[p[None] for p in d_parts], qv_bias, up_bias[None])
        packed = pl.pallas_call(pack, out_shape=sds((BLK + 8, 4 * hc), bf16))(*packed)
        first, middle = Gather(packed, tables), Gather(up_weight, tables)
        own = down_weight_in.T[None]

        def move(value, name, *done, way=0):
            return lax.ppermute(after(value, *done), AXES, tables[name][way])

        own2 = move(own, "2")
        done = first.stage("Z") + [own2]
        own2 = jnp.concatenate([own, own2])

        core = (at_dp & 1) ^ (rel >> 2)
        s3, s2 = (rel >> 1) & 1, rel & 1
        dy, dx = jnp.where(core == 0, s2, s3), jnp.where(core == 0, s3, s2)
        absolute = ((((at_dp >> 2) & 1) ^ dy) << 2) | ((((at_dp >> 1) & 1) ^ dx) << 1) | core
        i_p = jnp.broadcast_to(absolute[:, None], (n_i, n_t)).reshape(-1)
        t_p = jnp.broadcast_to((at_t ^ jnp.arange(n_t))[None], (n_i, n_t)).reshape(-1)
        to_d = jnp.broadcast_to(rel[:, None], (n_i, n_t)).reshape(-1) * n_t + t_p
        to_e = (((i_p * n_t) // n_i) ^ at_t) * n_i + (i_p * n_t + t_p) % n_i
    else:
        absolute, to_d, to_e = rel, slot, slot
    hot_d = (to_d[None, :] == slot[:, None]).astype(bf16)
    hot_e = (to_e[None, :] == slot[:, None]).astype(bf16)
    lane = jnp.arange(D)
    same_block = jnp.repeat(jnp.repeat((absolute[:, None] == rel[None, :]).T, BLK, axis=0), BLK, axis=1)
    perm = (same_block & ((lane[:, None] % BLK) == (lane[None, :] % BLK))).astype(bf16)
    turned = (D // 2, T)
    x, x_keep, x_send = pl.pallas_call(
        reorder, out_shape=[sds((T, D), bf16), sds(turned, bf16), sds(turned, bf16)], compiler_params=SMALL
    )(hidden_in.reshape(T, D), perm)
    pg = jnp.einsum("gsd,de->gse", pooled_grad.reshape(G, segs, D), perm.astype(f32), precision=HI)
    seg_r = segment_ids.reshape(G, L)
    seg_c = segment_ids.reshape(T, 1)

    if pairwise:
        done = first.stage("2", *done, x, x_keep, x_send, pg, hot_d, hot_e) + middle.stage("Z", *done)
        x_other = swap(x_send, tables, *done)
        z_one, z_two = move(own2, "Z", *done, way=0), move(own2, "Z", *done, way=1)
        got_q3, got_u2 = first.stage("3", *done), middle.stage("2", *done)
        first.stage("C", *got_u2, z_one, z_two)
        got_u3 = middle.send("3")
        z_three = move(own2, "Z", *got_q3, z_one, z_two, way=2)
        low = jnp.concatenate([own2, z_one])
        low_far = move(low, "3", *got_q3)
        w_qo = first.pieces(2, n_t)
    else:
        heads_in = [qkv_weight[0], qkv_weight[1], qkv_weight[2], out_weight.T]
        main = jnp.concatenate([*heads_in, up_weight, down_weight_in.T], axis=1)
        vec = jnp.concatenate(d_parts + e_parts)
        full = lax.all_gather(lax.all_gather(main, "dp", axis=0, tiled=True), "tensor", axis=0)
        full = full.reshape(n_t, n_i, BLK, -1).transpose(1, 0, 2, 3)
        vecs = lax.all_gather(lax.all_gather(vec, "tensor"), "dp").reshape(n_dp * n_t, -1)
        cuts = [j * dv for j in range(9)] + [n_vec]
        rows8 = jnp.concatenate([vecs[:, a:b].reshape(n_i * n_t, -1) for a, b in zip(cuts[:-1], cuts[1:])], axis=1)
        rows8 = jnp.pad(rows8.reshape(n_i, n_t, 1, -1), ((0, 0), (0, 0), (0, 7), (0, 4 * hc - rows8.shape[1])))
        quarters = [full[j * n_i // 4 : (j + 1) * n_i // 4] for j in range(4)]
        w_qo = [
            jnp.concatenate([w[..., : 4 * hc], rows8[j * n_i // 4 : (j + 1) * n_i // 4]], axis=2)
            for j, w in enumerate(quarters)
        ]
        w_up = [w[..., 4 * hc : 4 * hc + fc] for w in quarters]
        w_down = [w[..., 4 * hc + fc :].transpose(1, 0, 2, 3) for w in quarters]
        w_down = [w[: n_t // 2] for w in w_down] + [w[n_t // 2 :] for w in w_down]

    hl = hc // HD * L
    o_wide, q_wide = -(-hc // 128) * 128, -(-3 * hc // 128) * 128

    def leads(*arrays):
        return [(a, lead(a)) for a in arrays]

    def wholes(*arrays):
        return [(a, whole(a)) for a in arrays]

    def weights(*arrays):
        return [(a, weight(a)) for a in arrays]

    def weights_t(*arrays):
        return [(a, pl.BlockSpec((1, a.shape[1], BLK, a.shape[3]), lambda s: (s, 0, 0, 0))) for a in arrays]

    def paired(*arrays):
        return [(a, pl.BlockSpec((2, 1) + a.shape[2:], lambda s: (0, s, 0, 0))) for a in arrays]

    def folded(a):
        return a.reshape(2, n_t // 2, *a.shape[1:])

    tails = [
        (w, pl.BlockSpec((w.shape[0], n_t, 8, w.shape[3]), lambda s: (0, 0, BLK // 8, 0), pipeline_mode=pl.Buffered(1)))
        for w in w_qo
    ]
    qkv, prob, o, n1, x1, r1, n1b, n1_keep, n1_send, vec_d, b_u = call(
        partial(attention_forward, sizes), n_t, 10,
        wholes(x) + weights(*w_qo) + tails + wholes(hot_d, hot_e, seg_c, seg_r),
        leads(far((n_t, T, 3 * hc), bf16), far((n_t, G, L, hl), f32), far((n_t, T, o_wide), bf16))
        + wholes(sds((T, D), f32), far((T, D), f32), far((T, 1), f32), sds((T, D), bf16), far(turned, bf16), far(turned, bf16))
        + wholes(sds((6, D), f32), sds((n_t, 1, fc), f32)),
        [pltpu.VMEM((T, D), f32), pltpu.VMEM((n_t, 1, hc), f32), pltpu.VMEM((n_t, 1, hc), f32)],
    )
    if pairwise:
        middle.take("3", [after(g, n1b) for g in got_u3])
        middle.stage("C", n1b, z_three)
        high = jnp.concatenate([z_two, after(z_three, n1b)])
        high_far = move(high, "3")
        w_up = middle.pieces(2, n_t)
        low_other = [swap(low, tables, n1b), swap(after(low_far, n1b), tables)]
        n1_other = swap(n1_send, tables)
        o_other = swap(o, tables)
        b_u = after(b_u, *low_other)
    z, dgelu = call(
        up_forward, n_t, 4, wholes(n1b) + weights(*w_up) + leads(b_u),
        leads(sds((n_t, T, fc), bf16), sds((n_t, T, fc), f32)),
    )
    if pairwise:
        high_other = [swap(high, tables), swap(after(high_far, z), tables)]
        w_down = [low, low_far, *low_other, high, high_far, *high_other]
        w_down = [w.reshape(n_t // 2, 2, BLK, fc) for w in w_down]
        z_other = swap(z, tables, *high_other)
        dgelu = after(dgelu, x_other, n1_other, o_other)
    pooled, db, dbb, db_keep, db_send, sums2 = call(
        down_forward, n_t // 2, 5.5, paired(folded(z)) + weights_t(*w_down) + wholes(n1, vec_d, seg_c, seg_r, pg),
        wholes(sds((G, segs, D), f32), sds((T, D), f32), sds((T, D), bf16), sds(turned, bf16), sds(turned, bf16), sds((3, D), f32)),
        [pltpu.VMEM((T, D), f32)],
    )

    def gradient(groups, vectors=(), at_once=True):
        ins, kinds = [], []
        for width, *pairs in groups:
            kinds.append((len(pairs), len(pairs[0][1]), width))
            for lhs, values in pairs:
                ins += wholes(lhs) + (leads(*values) if len(values) == 1 else halved(*values))
        out = sds((n_i // 4, n_t, BLK + (8 if vectors else 0), sum(k[2] for k in kinds)), bf16)

        def share(which):
            return call(
                partial(weight_gradient, kinds, len(vectors), which), n_t, 2, ins + leads(*vectors),
                [(out, half_spec(out))] * (2 if which is None else 1),
            )

        return share(None) if at_once else (share(0)[0], share(1)[0])

    def halved(low, high):
        block = (1,) + low.shape[1:]
        return [
            (low, pl.BlockSpec(block, lambda s: (jnp.minimum(s, n_t // 2 - 1), 0, 0))),
            (high, pl.BlockSpec(block, lambda s: (jnp.maximum(s - n_t // 2, 0), 0, 0))),
        ]

    def flat(a):
        return a.reshape((-1,) + a.shape[2:])

    du, g_bu = call(
        hidden_backward, n_t // 2, 3.5, wholes(dbb) + weights_t(*w_down) + paired(folded(dgelu)),
        paired(sds((2, n_t // 2, T, fc), bf16), sds((2, n_t // 2, 1, fc), f32)),
    )
    du, g_bu = du.reshape(n_t, T, fc), g_bu.reshape(n_t, 1, fc)
    if pairwise:
        db_other = swap(db_send, tables)
        du_other = swap(du, tables)
        down_keep, down_send = gradient([[fc, (after(db_keep, g_bu), [z]), (db_other, [z_other])]], at_once=False)
        s_down = Scatter(flat(down_keep), flat(down_send), tables)
        got_d3 = s_down.stage("3", 2)
        du_next = after(du, down_send)
        dab_after = down_keep
    else:
        du_next = du
    da, dab, da_keep, da_send, sums1 = call(
        norm_backward, n_t, NORM, leads(du_next) + weights(*w_up) + wholes(db, x1, r1, vec_d),
        wholes(sds((T, D), f32), sds((T, D), bf16), sds(turned, bf16), sds(turned, bf16), sds((3, D), f32)),
        [pltpu.VMEM((T, D), f32)],
    )
    if pairwise:
        da_other = swap(da_send, tables)
        up_keep, up_send = gradient([[fc, (after(n1_keep, da_keep), [du]), (n1_other, [du_other])]])
        s_up = Scatter(flat(up_keep), flat(up_send), tables)
        got_u3 = s_up.stage("3", 2)
        dab = after(dab, up_keep)
    rows = sds((n_t, n_i // 2, 4 * hc), f32)
    if pairwise:
        dab = after(dab, da_other, dab_after, *got_d3)
    dq_half = sds((n_t // 2, T, q_wide), bf16)
    *dq, v_keep, v_send = call(
        partial(attention_backward, sizes), n_t, 8,
        wholes(dab) + weights(*w_qo) + leads(qkv, prob) + wholes(sums1, sums2, g_bu, hot_d, hot_e),
        halved(dq_half, dq_half) + wholes(rows, rows),
        [pltpu.VMEM((n_t, 1, hc), f32), pltpu.VMEM((n_t, 1, hc), f32), pltpu.VMEM((T, q_wide), bf16)],
    )
    if pairwise:
        dq_other = [swap(d, tables) for d in dq]
        v_other = swap(v_send, tables)
        got_d2 = s_down.stage("2", n_t)
    pooled = jnp.einsum("gse,de->gsd", pooled, perm.astype(f32), precision=HI)
    if pairwise:
        x_now = after(x_keep, *got_u3)
        qo_keep, qo_send = gradient(
            [[3 * hc, (x_now, dq), (x_other, dq_other)], [hc, (da_keep, [o]), (da_other, [o_other])]], (v_keep, v_other)
        )
        s_qo = Scatter(flat(qo_keep), flat(qo_send), tables)
        got_u2 = s_up.stage("2", n_t)
        s_qo.stage("3", 2, *got_d2, *got_u2, pooled, cut=CUT)
        both = Scatter(jnp.concatenate([s_down.keep, s_up.keep]), None, tables)
        both.send = [jnp.concatenate([a, b]) for a, b in zip(s_down.send, s_up.send, strict=True)]
        got_z = both.stage("Z", 1)
        dq = [after(d, qo_keep) for d in dq]
    dx = call(
        input_backward, n_t, 4, halved(*dq) + weights(*w_qo) + wholes(da, perm), wholes(sds((T, D), f32)),
        [pltpu.VMEM((T, D), f32)],
    )[0]

    if pairwise:
        s_qo.stage("2", n_t, dx)
        s_qo.stage("Z", 1, *got_z)
        g_qkv, g_out, g_qv, *vo = pl.pallas_call(
            finish,
            out_shape=[sds(qkv_weight.shape, f32), sds(out_weight.shape, f32), sds(qv_bias.shape, f32)]
            + [sds((1, dv), f32)] * 6 + [sds((1, up_bias.shape[0]), f32)],
            compiler_params=SMALL,
        )(s_qo.keep[0])
        vo = [v[0] for v in vo]
        g_down, g_up = both.keep[0], both.keep[1]
    else:
        def joined(*halves_of):
            g = jnp.concatenate([part[:, :, :BLK] for half in halves_of for part in half])
            return g.transpose(1, 0, 2, 3).reshape(n_t, D, -1)

        x_h, n1_h, db_h, da_h = (x_keep, x_send), (n1_keep, n1_send), (db_keep, db_send), (da_keep, da_send)
        g_full = jnp.concatenate([
            joined(*[gradient([[3 * hc, (x_h[j], dq)], [hc, (da_h[j], [o])]]) for j in range(2)]),
            joined(*[gradient([[fc, (n1_h[j], [du])]]) for j in range(2)]),
            joined(*[gradient([[fc, (db_h[j], [z])]]) for j in range(2)]),
        ], axis=2)
        mine = lax.psum_scatter(g_full, "tensor", scatter_dimension=0)
        mine = lax.psum_scatter(mine, "dp", scatter_dimension=0, tiled=True).astype(f32)
        g_qo, g_up, g_down = mine[:, : 4 * hc], mine[:, 4 * hc : 4 * hc + fc], mine[:, 4 * hc + fc :]
        g_rows = jnp.stack([v_keep, v_send]).transpose(0, 2, 1, 3).reshape(n_i * n_t, -1)
        dv_c, bu_c = sizes[1], sizes[2]
        cuts = [j * dv_c for j in range(9)] + [8 * dv_c + bu_c]
        g_v = jnp.concatenate(
            [g_rows[:, a:b].reshape(n_dp * n_t, -1) for a, b in zip(cuts[:-1], cuts[1:])], axis=1
        )
        g_v = lax.psum_scatter(g_v, AXES, scatter_dimension=0)
        g_qkv = jnp.stack([g_qo[:, c * hc : (c + 1) * hc] for c in range(3)])
        g_out = g_qo[:, 3 * hc :].T
        vo = [g_v[j * dv : (j + 1) * dv] for j in range(6)] + [g_v[8 * dv :]]
        g_qv = jnp.stack([g_v[6 * dv : 7 * dv], g_v[7 * dv : 8 * dv]])
    return (
        pooled.reshape(micro, seqs, segs, D),
        dx.reshape(micro, tokens, D),
        g_qkv, g_qv, g_out, vo[0], vo[1], vo[2], g_up, vo[6], g_down.T, vo[3], vo[4], vo[5],
    )


def solution(mesh):
    both = P(AXES)
    row3 = P(None, AXES)
    return jax.shard_map(
        per_device,
        mesh=mesh,
        in_specs=(
            row3, row3, row3, P(None, "dp", "tensor"), row3, P("tensor", "dp"), both, both, both,
            P("dp", "tensor"), both, P("tensor", "dp"), both, both, both,
        ),
        out_specs=(
            row3, row3, P(None, "dp", "tensor"), row3, P("tensor", "dp"), both, both, both,
            P("dp", "tensor"), both, P("tensor", "dp"), both, both, both,
        ),
        check_vma=False,
    )
```

```python
from functools import partial

import jax
import jax.numpy as jnp
from jax import lax
from jax.experimental import pallas as pl
from jax.experimental.pallas import tpu as pltpu
from jax.sharding import PartitionSpec as P

HD = 64
EPS = 1e-12
NEG = -1000000000.0
SCALE = float(HD) ** -0.5
AXES = ("dp", "tensor")
f32 = jnp.float32
bf16 = jnp.bfloat16
HI = lax.Precision.HIGHEST
BLK = 96
VMEM_LIMIT = 24 * 1024 * 1024
COST = 30_000_000
NORM = 2000
CUT = 4
SMALL = pltpu.CompilerParams(vmem_limit_bytes=8 * 1024 * 1024)


def nn(a, b):
    return lax.dot_general(a, b, (((1,), (0,)), ((), ())), preferred_element_type=f32)


def nt(a, b):
    return lax.dot_general(a, b, (((1,), (1,)), ((), ())), preferred_element_type=f32)


def tn(a, b):
    return lax.dot_general(a, b, (((0,), (0,)), ((), ())), preferred_element_type=f32)


def mean_last(v):
    return jnp.sum(v, axis=-1, keepdims=True) * (1.0 / v.shape[-1])


def normalize(values):
    center = values - mean_last(values)
    inverse = lax.rsqrt(mean_last(center * center) + EPS)
    return center * inverse, inverse


def normalize_back(scaled, normed, inverse):
    return inverse * (scaled - mean_last(scaled) - normed * mean_last(scaled * normed))


def col_sum(v):
    return jnp.sum(v, axis=0, keepdims=True)


def pack(qkv_ref, out_ref, ob_ref, g1_ref, s1_ref, db_ref, g2_ref, s2_ref, qv_ref, ub_ref, first_ref):
    rows, hc = qkv_ref.shape[1:]
    eye = (lax.broadcasted_iota(jnp.int32, (rows, rows), 0) == lax.broadcasted_iota(jnp.int32, (rows, rows), 1)).astype(bf16)
    for c in range(3):
        first_ref[:rows, c * hc : (c + 1) * hc] = qkv_ref[c]
    first_ref[:rows, 3 * hc :] = nt(eye, out_ref[...]).astype(bf16)
    parts = [r[...].astype(f32) for r in (ob_ref, g1_ref, s1_ref, db_ref, g2_ref, s2_ref, qv_ref)]
    short = jnp.concatenate(parts, axis=0).astype(bf16)
    count, size = short.shape
    wide = first_ref.shape[1]

    def spread(values, at):
        lane = lax.broadcasted_iota(jnp.int32, (values.shape[1], wide), 1) - at
        return nn(values, (lax.rem(lane + values.shape[1] * wide, values.shape[1]) == lax.broadcasted_iota(jnp.int32, lane.shape, 0)).astype(bf16))

    lane = lax.broadcasted_iota(jnp.int32, (count, wide), 1)
    start = lax.broadcasted_iota(jnp.int32, (count, wide), 0) * size
    row = col_sum(jnp.where((lane >= start) & (lane < start + size), spread(short, 0), 0.0))
    total, long = count * size, ub_ref.shape[1]
    lane = lax.broadcasted_iota(jnp.int32, (1, wide), 1)
    row = jnp.where((lane >= total) & (lane < total + long), spread(ub_ref[...], total), row)
    extra = first_ref.shape[0] - rows
    here = lax.broadcasted_iota(jnp.int32, (extra, wide), 0)
    first_ref[rows:, :] = jnp.where(here == 0, row, 0.0).astype(bf16)


def reorder(h_ref, perm_ref, x_ref, keep_ref, send_ref):
    x = nn(h_ref[...], perm_ref[...]).astype(bf16)
    x_ref[...] = x
    turned = x.T
    keep_ref[...] = turned[: x.shape[1] // 2]
    send_ref[...] = turned[x.shape[1] // 2 :]


def stacked(values, hc):
    head = lax.broadcasted_iota(jnp.int32, (1, hc), 1) // HD
    return jnp.concatenate([values * (head == h).astype(f32).astype(bf16) for h in range(hc // HD)], axis=0)


def own_columns(blocks, hc):
    n_heads = hc // HD
    length = blocks.shape[0] // n_heads
    head = lax.broadcasted_iota(jnp.int32, (1, hc), 1) // HD
    out = blocks[:length]
    for h in range(1, n_heads):
        out = jnp.where(head == h, blocks[h * length : (h + 1) * length], out)
    return out


def sections(values, length):
    return [values[:, c : c + length] for c in range(0, values.shape[1], length)]


def rows_of(refs):
    return jnp.concatenate([r[...].reshape(-1, r.shape[3]) for r in refs], axis=0)


def thirds(values):
    high = values.astype(bf16)
    rest = values - high.astype(f32)
    middle = rest.astype(bf16)
    return high, middle, (rest - middle.astype(f32)).astype(bf16)


def accumulate(acc_ref, step, add):
    @pl.when(step == 0)
    def _():
        acc_ref[...] = add

    @pl.when(step > 0)
    def _():
        acc_ref[...] += add


def iota(shape, axis):
    return lax.broadcasted_iota(jnp.int32, shape, axis)


def picks(count, first, wide, size):
    return (iota((count, wide), 0) == first + lax.rem(iota((1, wide), 1), size)).astype(bf16)


def belongs(count, wide, size, period):
    lane, row = iota((1, wide), 1), lax.rem(iota((count, 1), 0), period)
    return (lane >= row * size) & (lane < (row + 1) * size)


def read_vectors(rows, hot_d, hot_e, sizes):
    n_d, dv, bu, width, hc, fc, n_t = sizes
    count = rows.shape[0]
    per = count // n_t
    d_all = nn(hot_d, rows[:, : n_d * dv]).astype(bf16)
    mine = belongs(count, width, dv, count)
    d_rows = [col_sum(jnp.where(mine, nn(d_all, picks(n_d * dv, j * dv, width, dv)), 0.0)) for j in range(n_d)]
    e_all = nn(hot_e, rows[:, n_d * dv : n_d * dv + 2 * dv + bu]).astype(bf16)
    out = []
    for first, size, wide in ((0, dv, hc), (dv, dv, hc), (2 * dv, bu, fc)):
        spread = jnp.where(belongs(count, wide, size, per), nn(e_all, picks(e_all.shape[1], first, wide, size)), 0.0)
        out.append(jnp.sum(spread.reshape(n_t, per, wide), axis=1, keepdims=True))
    return jnp.concatenate(d_rows, axis=0), out


def write_vectors(d_rows, e_rows, hot_d, hot_e, sizes):
    n_d, dv, bu, width, hc, fc, n_t = sizes
    count = hot_d.shape[0]
    per = count // n_t
    mine = belongs(count, width, dv, count)
    d_all = sum(
        nt(jnp.where(mine, d_rows[j : j + 1, :], 0.0).astype(bf16), picks(n_d * dv, j * dv, width, dv)) for j in range(n_d)
    ).astype(bf16)
    e_all = 0.0
    for value, first, size, wide in zip(e_rows, (0, dv, 2 * dv), (dv, dv, bu), (hc, hc, fc), strict=True):
        spread = jnp.broadcast_to(value, (n_t, per, wide)).reshape(count, wide)
        spread = jnp.where(belongs(count, wide, size, per), spread, 0.0).astype(bf16)
        e_all = e_all + nt(spread, picks(2 * dv + bu, first, wide, size))
    return jnp.concatenate([tn(hot_d, d_all), tn(hot_e, e_all.astype(bf16))], axis=1)


def attention_forward(sizes, x_ref, w0_ref, w1_ref, w2_ref, w3_ref, v0_ref, v1_ref, v2_ref, v3_ref, hd_ref, he_ref,
                      segc_ref, segr_ref, qkv_ref, p_ref, o_ref, n1_ref, x1_ref, r1_ref, n1b_ref, n1t_ref, n1s_ref,
                      vec_ref, bu_ref, acc_ref, bq_ref, bv_ref):
    step = pl.program_id(0)
    hc = bq_ref.shape[-1]

    @pl.when(step == 0)
    def _():
        rows = jnp.concatenate([r[:, :, 0, :].reshape(-1, r.shape[3]) for r in (v0_ref, v1_ref, v2_ref, v3_ref)], axis=0)
        d_rows, (b_q, b_v, b_u) = read_vectors(rows, hd_ref[...], he_ref[...], sizes)
        vec_ref[...] = d_rows
        bq_ref[...] = b_q
        bv_ref[...] = b_v
        bu_ref[...] = b_u

    rows, length = segr_ref.shape
    x = x_ref[...]
    w = rows_of((w0_ref, w1_ref, w2_ref, w3_ref))
    qkv = nn(x, w[:, : 3 * hc])
    q = (qkv[:, :hc] + bq_ref[step]).astype(bf16) * bf16(SCALE)
    k = qkv[:, hc : 2 * hc].astype(bf16)
    v = (qkv[:, 2 * hc :] + bv_ref[step]).astype(bf16)
    qkv_ref[0, :, :hc] = q
    qkv_ref[0, :, hc : 2 * hc] = k
    qkv_ref[0, :, 2 * hc :] = v
    spans = [slice(g * length, (g + 1) * length) for g in range(rows)]
    scores = [nt(q[span], stacked(k[span], hc)) for span in spans]
    probs = []
    for g, span in enumerate(spans):
        same = segc_ref[span, :] == segr_ref[g : g + 1, :]
        parts = []
        for s in sections(scores[g], length):
            s = jnp.where(same, s, NEG)
            e = jnp.exp(s - jnp.max(s, axis=-1, keepdims=True))
            parts.append(e * (1.0 / jnp.sum(e, axis=-1, keepdims=True)))
        probs.append(jnp.concatenate(parts, axis=1))
    for g, span in enumerate(spans):
        p_ref[0, g] = probs[g]
        o_ref[0, span, :hc] = nn(probs[g].astype(bf16), stacked(v[span], hc)).astype(bf16)
    o_ref[0, :, hc:] = jnp.zeros((o_ref.shape[1], o_ref.shape[2] - hc), bf16)
    add = nt(o_ref[0, :, :hc], w[:, 3 * hc :])

    accumulate(acc_ref, step, add)

    @pl.when(step == pl.num_programs(0) - 1)
    def _():
        a = acc_ref[...] + vec_ref[0:1, :] + x_ref[...].astype(f32)
        normed, inverse = normalize(a)
        n1 = normed * vec_ref[1:2, :] + vec_ref[2:3, :]
        n1_ref[...] = n1
        x1_ref[...] = normed
        r1_ref[...] = inverse
        low = n1.astype(bf16)
        n1b_ref[...] = low
        turned = low.T
        n1t_ref[...] = turned[: low.shape[1] // 2]
        n1s_ref[...] = turned[low.shape[1] // 2 :]


def up_forward(n_ref, w0_ref, w1_ref, w2_ref, w3_ref, b_ref, z_ref, d_ref):
    u = nn(n_ref[...], rows_of((w0_ref, w1_ref, w2_ref, w3_ref))) + b_ref[0]
    phi = 0.5 + 0.5 * lax.erf(u * (0.5**0.5))
    z_ref[0] = (u * phi).astype(bf16)
    d_ref[0] = phi + u * (jnp.exp(-0.5 * u * u) * 0.3989422804014327)


def down_forward(z_ref, w0_ref, w1_ref, w2_ref, w3_ref, w4_ref, w5_ref, w6_ref, w7_ref, n1_ref, vec_ref, segc_ref, segr_ref, pg_ref,
                 pooled_ref, db_ref, dbb_ref, dbt_ref, dbs_ref, sums_ref, acc_ref):
    step = pl.program_id(0)
    add = nt(z_ref[0, 0], rows_of((w0_ref, w1_ref, w2_ref, w3_ref))) + nt(z_ref[1, 0], rows_of((w4_ref, w5_ref, w6_ref, w7_ref)))

    accumulate(acc_ref, step, add)

    @pl.when(step == pl.num_programs(0) - 1)
    def _():
        rows, length = segr_ref.shape
        segs = pg_ref.shape[1]
        b = acc_ref[...] + vec_ref[3:4, :] + n1_ref[...]
        x2, r2 = normalize(b)
        y = x2 * vec_ref[4:5, :] + vec_ref[5:6, :]
        grads = []
        for g in range(rows):
            span = slice(g * length, (g + 1) * length)
            hot_t = (iota((segs, length), 0) == segr_ref[g : g + 1, :]).astype(f32)
            count = jnp.sum(hot_t, axis=1, keepdims=True)
            hot_t = hot_t.astype(bf16)
            hot = (iota((length, segs), 1) == segc_ref[span, :]).astype(f32).astype(bf16)
            pooled_ref[g] = sum(nn(hot_t, part) for part in thirds(y[span, :])) / count
            grads.append(nn(jnp.concatenate([hot] * 3, axis=1), jnp.concatenate(thirds(pg_ref[g] / count), axis=0)))
        dy = jnp.concatenate(grads, axis=0)
        db = normalize_back(dy * vec_ref[4:5, :], x2, r2)
        db_ref[...] = db
        low = db.astype(bf16)
        dbb_ref[...] = low
        turned = low.T
        dbt_ref[...] = turned[: low.shape[1] // 2]
        dbs_ref[...] = turned[low.shape[1] // 2 :]
        sums_ref[0:1, :] = col_sum(db)
        sums_ref[1:2, :] = col_sum(dy * x2)
        sums_ref[2:3, :] = col_sum(dy)


def put(grad, ref):
    ref[:, :, :BLK, :] = grad.astype(bf16).reshape(grad.shape[0] // BLK, 1, BLK, grad.shape[1])


def hidden_backward(dbb_ref, w0_ref, w1_ref, w2_ref, w3_ref, w4_ref, w5_ref, w6_ref, w7_ref, d_ref, du_ref, bu_ref):
    for n, refs in enumerate(((w0_ref, w1_ref, w2_ref, w3_ref), (w4_ref, w5_ref, w6_ref, w7_ref))):
        du = (nn(dbb_ref[...], rows_of(refs)) * d_ref[n, 0]).astype(bf16)
        du_ref[n, 0] = du
        bu_ref[n, 0] = col_sum(du.astype(f32))


def step_value(refs, width):
    if len(refs) == 1:
        return refs[0][0, :, :width]
    return jnp.where(pl.program_id(0) < pl.num_programs(0) // 2, refs[0][0, :, :width], refs[1][0, :, :width])


def weight_gradient(groups, vectors, which, *refs):
    refs = list(refs)
    parts = []
    for pairs, split, width in groups:
        total = None
        for _ in range(pairs):
            rows = refs.pop(0)
            half = rows.shape[0] // 2
            rows = rows[...] if which is None else rows[which * half : (which + 1) * half, :]
            add = nn(rows, step_value([refs.pop(0) for _ in range(split)], width))
            total = add if total is None else total + add
        parts.append(total)
    grad = jnp.concatenate(parts, axis=1)
    extra = sum(refs.pop(0)[0].astype(f32) for _ in range(vectors)) if vectors else None
    half = grad.shape[0] // len(refs)
    for n, ref in enumerate(refs):
        put(grad[n * half : (n + 1) * half], ref)
        if vectors:
            for j in range(ref.shape[0]):
                at = (n if which is None else which) * ref.shape[0] + j
                row = extra[at : at + 1]
                tail = ref.shape[2] - BLK
                ref[j, 0, BLK:, :] = jnp.where(iota((tail, row.shape[1]), 0) == 0, row, 0.0).astype(bf16)


def norm_backward(du_ref, w0_ref, w1_ref, w2_ref, w3_ref, db_ref, x1_ref, r1_ref, vec_ref,
                  da_ref, dab_ref, dat_ref, das_ref, sums_ref, acc_ref):
    step = pl.program_id(0)
    accumulate(acc_ref, step, nt(du_ref[0], rows_of((w0_ref, w1_ref, w2_ref, w3_ref))))

    @pl.when(step == pl.num_programs(0) - 1)
    def _():
        dn1 = acc_ref[...].astype(bf16).astype(f32) + db_ref[...]
        da = normalize_back(dn1 * vec_ref[1:2, :], x1_ref[...], r1_ref[...])
        da_ref[...] = da
        low = da.astype(bf16)
        dab_ref[...] = low
        turned = low.T
        dat_ref[...] = turned[: low.shape[1] // 2]
        das_ref[...] = turned[low.shape[1] // 2 :]
        sums_ref[0:1, :] = col_sum(da)
        sums_ref[1:2, :] = col_sum(dn1 * x1_ref[...])
        sums_ref[2:3, :] = col_sum(dn1)


def attention_backward(sizes, dab_ref, w0_ref, w1_ref, w2_ref, w3_ref, qkv_ref, p_ref, s1_ref, s2_ref, gu_ref, hd_ref, he_ref,
                       low_ref, high_ref, keep_ref, send_ref, bq_ref, bv_ref, dqkv_ref):
    step = pl.program_id(0)
    hc = bq_ref.shape[-1]
    dab = dab_ref[...]
    w = rows_of([r.at[:, :, :, 3 * hc :] for r in (w0_ref, w1_ref, w2_ref, w3_ref)])
    do = nn(dab, w).astype(bf16)
    qkv = qkv_ref[0]
    rows, length = p_ref.shape[1], p_ref.shape[2]
    spans = [slice(g * length, (g + 1) * length) for g in range(rows)]
    q = [qkv[span, :hc] for span in spans]
    k = [stacked(qkv[span, hc : 2 * hc], hc) for span in spans]
    dps = [nt(do[span], stacked(qkv[span, 2 * hc :], hc)) for span in spans]
    dss = []
    for g in range(rows):
        parts = []
        for p, dp in zip(sections(p_ref[0, g], length), sections(dps[g], length)):
            pd = p * dp
            parts.append((pd - p * jnp.sum(pd, axis=-1, keepdims=True)).astype(bf16))
        dss.append(jnp.concatenate(parts, axis=1))
    for g, span in enumerate(spans):
        dqkv_ref[span, :hc] = (nn(dss[g], k[g]) * SCALE).astype(bf16)
        dqkv_ref[span, hc : 2 * hc] = own_columns(tn(dss[g], q[g]), hc).astype(bf16)
        dqkv_ref[span, 2 * hc : 3 * hc] = own_columns(tn(p_ref[0, g].astype(bf16), do[span]), hc).astype(bf16)
    dqkv_ref[:, 3 * hc :] = jnp.zeros((dqkv_ref.shape[0], dqkv_ref.shape[1] - 3 * hc), bf16)
    dqkv = dqkv_ref[...]
    half_steps = pl.num_programs(0) // 2

    @pl.when(step < half_steps)
    def _():
        low_ref[0] = dqkv

    @pl.when(step >= half_steps)
    def _():
        high_ref[0] = dqkv

    bq_ref[step] = col_sum(dqkv[:, :hc].astype(f32))
    bv_ref[step] = col_sum(dqkv[:, 2 * hc : 3 * hc].astype(f32))

    @pl.when(step == pl.num_programs(0) - 1)
    def _():
        d_rows = jnp.concatenate([s1_ref[...], s2_ref[...]], axis=0)
        rows = write_vectors(d_rows, (bq_ref[...], bv_ref[...], gu_ref[...]), hd_ref[...], he_ref[...], sizes)
        half, n_t = rows.shape[0] // 2, bq_ref.shape[0]
        rows = jnp.concatenate([rows, jnp.zeros((rows.shape[0], keep_ref.shape[-1] - rows.shape[1]), f32)], axis=1)
        for n, ref in enumerate((keep_ref, send_ref)):
            for t in range(n_t):
                for j in range(half // n_t):
                    at = n * half + j * n_t + t
                    ref[t, j : j + 1, :] = rows[at : at + 1]


def input_backward(low_ref, high_ref, w0_ref, w1_ref, w2_ref, w3_ref, da_ref, perm_ref, dx_ref, acc_ref):
    step = pl.program_id(0)
    cols = 3 * w0_ref.shape[-1] // 4
    w = rows_of((w0_ref, w1_ref, w2_ref, w3_ref))
    add = nt(step_value((low_ref, high_ref), cols), w[:, :cols])

    accumulate(acc_ref, step, add)

    @pl.when(step == pl.num_programs(0) - 1)
    def _():
        dx = acc_ref[...] + da_ref[...]
        perm = perm_ref[...]
        dx_ref[...] = sum(nt(part, perm) for part in thirds(dx))


def finish(total_ref, qkv_ref, out_ref, qv_ref, *vector_refs):
    total = total_ref[...]
    rows, hc = qkv_ref.shape[1:]
    for c in range(3):
        qkv_ref[c] = total[:rows, c * hc : (c + 1) * hc]
    out_ref[...] = total[:rows, 3 * hc :].T
    row = total[rows : rows + 1]
    at = 0
    for n, ref in enumerate(vector_refs):
        if n == 6:
            size = qv_ref.shape[1]
            qv_ref[...] = jnp.concatenate([row[:, at : at + size], row[:, at + size : at + 2 * size]], axis=0)
            at += 2 * size
        ref[...] = row[:, at : at + ref.shape[1]]
        at += ref.shape[1]


def whole(a):
    nd = len(a.shape)
    return pl.BlockSpec(a.shape, lambda s: (0,) * nd, pipeline_mode=pl.Buffered(1))


def lead(a):
    nd = len(a.shape)
    return pl.BlockSpec((1,) + a.shape[1:], lambda s: (s,) + (0,) * (nd - 1))


def weight(a):
    return pl.BlockSpec((a.shape[0], 1, BLK, a.shape[3]), lambda s: (0, s, 0, 0))


def half_spec(h):
    return pl.BlockSpec((h.shape[0], 1) + h.shape[2:], lambda s: (0, s, 0, 0))


def sds(shape, dtype):
    return jax.ShapeDtypeStruct(shape, dtype)


def far(shape, dtype):
    return pltpu.HBM(shape, dtype)


def call(body, n_t, micros, ins, outs, scratch=()):
    return pl.pallas_call(
        body,
        grid=(n_t,),
        in_specs=[s for _, s in ins],
        out_specs=[s for _, s in outs],
        out_shape=[a for a, _ in outs],
        scratch_shapes=list(scratch),
        compiler_params=pltpu.CompilerParams(
            dimension_semantics=("arbitrary",), vmem_limit_bytes=VMEM_LIMIT
        ),
        cost_estimate=pl.CostEstimate(flops=int(micros * COST), transcendentals=0, bytes_accessed=0),
    )(*[a for a, _ in ins])


def flips(n_dp, n_t):
    size = n_dp * n_t
    core = n_t
    x_bit, y_bit = 2 * core, 4 * core

    def table(bit_of):
        return [(i, i ^ bit_of(i)) for i in range(size)]

    return {
        "Z": [table(lambda i, d=d: d) for d in range(1, n_t)],
        "C": [table(lambda i: core)],
        "2": [table(lambda i: x_bit if i & core else y_bit)],
        "3": [table(lambda i: y_bit if i & core else x_bit)],
    }


def after(value, *done):
    return lax.optimization_barrier((value, *done))[0] if done else value


def swap(value, tables, *done):
    return lax.ppermute(after(value, *done), AXES, tables["C"][0])


class Gather:
    def __init__(self, value, tables):
        self.held, self.tables = [value[None]], tables

    def send(self, name, *done, parts=None, tables=None):
        sent = self.held if parts is None else [self.held[j] for j in parts]
        return [lax.ppermute(after(h, *done), AXES, t) for t in self.tables[name][tables or slice(None)] for h in sent]

    def take(self, name, got):
        self.held = [jnp.concatenate(self.held + got)] if name in "Z2" else self.held + got
        return got

    def stage(self, name, *done, parts=None):
        return self.take(name, self.send(name, *done, parts=parts))

    def pieces(self, *lead):
        return [h.reshape(*lead, *h.shape[1:]) for h in self.held]


class Scatter:
    def __init__(self, keep, send, tables):
        self.keep, self.send, self.tables = keep, [send], tables

    def stage(self, name, parts, *done, cut=1):
        tables = self.tables[name]
        pieces = len(self.send) // len(tables)
        got = [lax.ppermute(after(s, *done), AXES, tables[n // pieces]) for n, s in enumerate(self.send)]
        size = self.keep.shape[0] // parts // cut

        def piece(n):
            at = n * size
            total = self.keep[at : at + size].astype(f32)
            for t in range(len(tables)):
                mine = got[t * pieces : (t + 1) * pieces]
                wide = mine[0].shape[0]
                total = total + mine[at // wide][at % wide : at % wide + size].astype(f32)
            return total

        self.send = [piece(n).astype(bf16) for n in range(cut, parts * cut)]
        kept = [piece(n) for n in range(cut)]
        self.keep = kept[0] if cut == 1 else jnp.concatenate(kept)
        return got


def per_device(
    hidden_in, segment_ids, pooled_grad, qkv_weight, qv_bias, out_weight, out_bias,
    norm1_gain, norm1_shift, up_weight, up_bias, down_weight_in, down_bias, norm2_gain, norm2_shift,
):
    n_dp, n_t = lax.axis_size("dp"), lax.axis_size("tensor")
    at_dp, at_t = lax.axis_index("dp"), lax.axis_index("tensor")
    hc, fc = qkv_weight.shape[2], up_weight.shape[1]
    rows = qkv_weight.shape[1]
    D = rows * n_dp
    micro, tokens = hidden_in.shape[0], hidden_in.shape[1]
    seqs, L = segment_ids.shape[1], segment_ids.shape[2]
    G, T = micro * seqs, micro * tokens
    segs = pooled_grad.shape[2]
    n_i = D // BLK
    pairwise = (n_dp, n_t) == (8, 4) and 4 * hc == fc

    d_parts = [out_bias, norm1_gain, norm1_shift, down_bias, norm2_gain, norm2_shift]
    e_parts = [qv_bias[0], qv_bias[1], up_bias]
    dv = out_bias.shape[0]
    n_vec = sum(p.shape[0] for p in d_parts + e_parts)
    nd = len(d_parts) * dv

    sizes = (6, dv, up_bias.shape[0], D, hc, fc, n_t) if pairwise else (6, D // (n_i * n_t), n_t * fc // (n_i * n_t), D, hc, fc, n_t)
    slot = jnp.arange(n_i * n_t)
    rel = jnp.arange(n_i)
    if pairwise:
        tables = flips(n_dp, n_t)
        packed = (qkv_weight, out_weight, *[p[None] for p in d_parts], qv_bias, up_bias[None])
        packed = pl.pallas_call(pack, out_shape=sds((BLK + 8, 4 * hc), bf16))(*packed)
        first, middle = Gather(packed, tables), Gather(up_weight, tables)
        own = down_weight_in.T[None]

        def move(value, name, *done, way=0):
            return lax.ppermute(after(value, *done), AXES, tables[name][way])

        own2 = move(own, "2")
        done = first.stage("Z") + [own2]
        own2 = jnp.concatenate([own, own2])

        core = (at_dp & 1) ^ (rel >> 2)
        s3, s2 = (rel >> 1) & 1, rel & 1
        dy, dx = jnp.where(core == 0, s2, s3), jnp.where(core == 0, s3, s2)
        absolute = ((((at_dp >> 2) & 1) ^ dy) << 2) | ((((at_dp >> 1) & 1) ^ dx) << 1) | core
        i_p = jnp.broadcast_to(absolute[:, None], (n_i, n_t)).reshape(-1)
        t_p = jnp.broadcast_to((at_t ^ jnp.arange(n_t))[None], (n_i, n_t)).reshape(-1)
        to_d = jnp.broadcast_to(rel[:, None], (n_i, n_t)).reshape(-1) * n_t + t_p
        to_e = (((i_p * n_t) // n_i) ^ at_t) * n_i + (i_p * n_t + t_p) % n_i
    else:
        absolute, to_d, to_e = rel, slot, slot
    hot_d = (to_d[None, :] == slot[:, None]).astype(bf16)
    hot_e = (to_e[None, :] == slot[:, None]).astype(bf16)
    lane = jnp.arange(D)
    same_block = jnp.repeat(jnp.repeat((absolute[:, None] == rel[None, :]).T, BLK, axis=0), BLK, axis=1)
    perm = (same_block & ((lane[:, None] % BLK) == (lane[None, :] % BLK))).astype(bf16)
    turned = (D // 2, T)
    x, x_keep, x_send = pl.pallas_call(
        reorder, out_shape=[sds((T, D), bf16), sds(turned, bf16), sds(turned, bf16)], compiler_params=SMALL
    )(hidden_in.reshape(T, D), perm)
    pg = jnp.einsum("gsd,de->gse", pooled_grad.reshape(G, segs, D), perm.astype(f32), precision=HI)
    seg_r = segment_ids.reshape(G, L)
    seg_c = segment_ids.reshape(T, 1)

    if pairwise:
        done = first.stage("2", *done, x, x_keep, x_send, pg, hot_d, hot_e) + middle.stage("Z", *done)
        x_other = swap(x_send, tables, *done)
        z_one, z_two = move(own2, "Z", *done, way=0), move(own2, "Z", *done, way=1)
        got_q3, got_u2 = first.stage("3", *done), middle.stage("2", *done)
        first.stage("C", *got_u2, z_one, z_two)
        got_u3 = middle.send("3")
        z_three = move(own2, "Z", *got_q3, z_one, z_two, way=2)
        low = jnp.concatenate([own2, z_one])
        low_far = move(low, "3", *got_q3)
        w_qo = first.pieces(2, n_t)
    else:
        heads_in = [qkv_weight[0], qkv_weight[1], qkv_weight[2], out_weight.T]
        main = jnp.concatenate([*heads_in, up_weight, down_weight_in.T], axis=1)
        vec = jnp.concatenate(d_parts + e_parts)
        full = lax.all_gather(lax.all_gather(main, "dp", axis=0, tiled=True), "tensor", axis=0)
        full = full.reshape(n_t, n_i, BLK, -1).transpose(1, 0, 2, 3)
        vecs = lax.all_gather(lax.all_gather(vec, "tensor"), "dp").reshape(n_dp * n_t, -1)
        cuts = [j * dv for j in range(9)] + [n_vec]
        rows8 = jnp.concatenate([vecs[:, a:b].reshape(n_i * n_t, -1) for a, b in zip(cuts[:-1], cuts[1:])], axis=1)
        rows8 = jnp.pad(rows8.reshape(n_i, n_t, 1, -1), ((0, 0), (0, 0), (0, 7), (0, 4 * hc - rows8.shape[1])))
        quarters = [full[j * n_i // 4 : (j + 1) * n_i // 4] for j in range(4)]
        w_qo = [
            jnp.concatenate([w[..., : 4 * hc], rows8[j * n_i // 4 : (j + 1) * n_i // 4]], axis=2)
            for j, w in enumerate(quarters)
        ]
        w_up = [w[..., 4 * hc : 4 * hc + fc] for w in quarters]
        w_down = [w[..., 4 * hc + fc :].transpose(1, 0, 2, 3) for w in quarters]
        w_down = [w[: n_t // 2] for w in w_down] + [w[n_t // 2 :] for w in w_down]

    hl = hc // HD * L
    o_wide, q_wide = -(-hc // 128) * 128, -(-3 * hc // 128) * 128

    def leads(*arrays):
        return [(a, lead(a)) for a in arrays]

    def wholes(*arrays):
        return [(a, whole(a)) for a in arrays]

    def weights(*arrays):
        return [(a, weight(a)) for a in arrays]

    def weights_t(*arrays):
        return [(a, pl.BlockSpec((1, a.shape[1], BLK, a.shape[3]), lambda s: (s, 0, 0, 0))) for a in arrays]

    def paired(*arrays):
        return [(a, pl.BlockSpec((2, 1) + a.shape[2:], lambda s: (0, s, 0, 0))) for a in arrays]

    def folded(a):
        return a.reshape(2, n_t // 2, *a.shape[1:])

    tails = [
        (w, pl.BlockSpec((w.shape[0], n_t, 8, w.shape[3]), lambda s: (0, 0, BLK // 8, 0), pipeline_mode=pl.Buffered(1)))
        for w in w_qo
    ]
    qkv, prob, o, n1, x1, r1, n1b, n1_keep, n1_send, vec_d, b_u = call(
        partial(attention_forward, sizes), n_t, 10,
        wholes(x) + weights(*w_qo) + tails + wholes(hot_d, hot_e, seg_c, seg_r),
        leads(far((n_t, T, 3 * hc), bf16), far((n_t, G, L, hl), f32), far((n_t, T, o_wide), bf16))
        + wholes(sds((T, D), f32), far((T, D), f32), far((T, 1), f32), sds((T, D), bf16), far(turned, bf16), far(turned, bf16))
        + wholes(sds((6, D), f32), sds((n_t, 1, fc), f32)),
        [pltpu.VMEM((T, D), f32), pltpu.VMEM((n_t, 1, hc), f32), pltpu.VMEM((n_t, 1, hc), f32)],
    )
    if pairwise:
        middle.take("3", [after(g, n1b) for g in got_u3])
        middle.stage("C", n1b, z_three)
        high = jnp.concatenate([z_two, after(z_three, n1b)])
        high_far = move(high, "3")
        w_up = middle.pieces(2, n_t)
        low_other = [swap(low, tables, n1b), swap(after(low_far, n1b), tables)]
        n1_other = swap(n1_send, tables)
        o_other = swap(o, tables)
        b_u = after(b_u, *low_other)
    z, dgelu = call(
        up_forward, n_t, 4, wholes(n1b) + weights(*w_up) + leads(b_u),
        leads(sds((n_t, T, fc), bf16), sds((n_t, T, fc), f32)),
    )
    if pairwise:
        high_other = [swap(high, tables), swap(after(high_far, z), tables)]
        w_down = [low, low_far, *low_other, high, high_far, *high_other]
        w_down = [w.reshape(n_t // 2, 2, BLK, fc) for w in w_down]
        z_other = swap(z, tables, *high_other)
    pooled, db, dbb, db_keep, db_send, sums2 = call(
        down_forward, n_t // 2, 5.5, paired(folded(z)) + weights_t(*w_down) + wholes(n1, vec_d, seg_c, seg_r, pg),
        wholes(sds((G, segs, D), f32), sds((T, D), f32), sds((T, D), bf16), sds(turned, bf16), sds(turned, bf16), sds((3, D), f32)),
        [pltpu.VMEM((T, D), f32)],
    )

    def gradient(groups, vectors=(), at_once=True):
        ins, kinds = [], []
        for width, *pairs in groups:
            kinds.append((len(pairs), len(pairs[0][1]), width))
            for lhs, values in pairs:
                ins += wholes(lhs) + (leads(*values) if len(values) == 1 else halved(*values))
        out = sds((n_i // 4, n_t, BLK + (8 if vectors else 0), sum(k[2] for k in kinds)), bf16)

        def share(which):
            return call(
                partial(weight_gradient, kinds, len(vectors), which), n_t, 2, ins + leads(*vectors),
                [(out, half_spec(out))] * (2 if which is None else 1),
            )

        return share(None) if at_once else (share(0)[0], share(1)[0])

    def halved(low, high):
        block = (1,) + low.shape[1:]
        return [
            (low, pl.BlockSpec(block, lambda s: (jnp.minimum(s, n_t // 2 - 1), 0, 0))),
            (high, pl.BlockSpec(block, lambda s: (jnp.maximum(s - n_t // 2, 0), 0, 0))),
        ]

    def flat(a):
        return a.reshape((-1,) + a.shape[2:])

    du, g_bu = call(
        hidden_backward, n_t // 2, 3.5, wholes(dbb) + weights_t(*w_down) + paired(folded(dgelu)),
        paired(sds((2, n_t // 2, T, fc), bf16), sds((2, n_t // 2, 1, fc), f32)),
    )
    du, g_bu = du.reshape(n_t, T, fc), g_bu.reshape(n_t, 1, fc)
    if pairwise:
        db_other = swap(db_send, tables)
        du_other = swap(du, tables)
        down_keep, down_send = gradient([[fc, (after(db_keep, g_bu), [z]), (db_other, [z_other])]], at_once=False)
        s_down = Scatter(flat(down_keep), flat(down_send), tables)
        got_d3 = s_down.stage("3", 2)
        du_next = after(du, down_send)
        dab_after = down_keep
    else:
        du_next = du
    da, dab, da_keep, da_send, sums1 = call(
        norm_backward, n_t, NORM, leads(du_next) + weights(*w_up) + wholes(db, x1, r1, vec_d),
        wholes(sds((T, D), f32), sds((T, D), bf16), sds(turned, bf16), sds(turned, bf16), sds((3, D), f32)),
        [pltpu.VMEM((T, D), f32)],
    )
    if pairwise:
        da_other = swap(da_send, tables)
        up_keep, up_send = gradient([[fc, (after(n1_keep, da_keep), [du]), (n1_other, [du_other])]])
        s_up = Scatter(flat(up_keep), flat(up_send), tables)
        got_u3 = s_up.stage("3", 2)
        dab = after(dab, up_keep)
    rows = sds((n_t, n_i // 2, 4 * hc), f32)
    if pairwise:
        dab = after(dab, da_other, dab_after, x_other, o_other, *got_d3)
    dq_half = sds((n_t // 2, T, q_wide), bf16)
    *dq, v_keep, v_send = call(
        partial(attention_backward, sizes), n_t, 8,
        wholes(dab) + weights(*w_qo) + leads(qkv, prob) + wholes(sums1, sums2, g_bu, hot_d, hot_e),
        halved(dq_half, dq_half) + wholes(rows, rows),
        [pltpu.VMEM((n_t, 1, hc), f32), pltpu.VMEM((n_t, 1, hc), f32), pltpu.VMEM((T, q_wide), bf16)],
    )
    if pairwise:
        dq_other = [swap(d, tables) for d in dq]
        v_other = swap(v_send, tables)
        got_d2 = s_down.stage("2", n_t)
    pooled = jnp.einsum("gse,de->gsd", pooled, perm.astype(f32), precision=HI)
    if pairwise:
        x_now = after(x_keep, *got_u3)
        qo_keep, qo_send = gradient(
            [[3 * hc, (x_now, dq), (x_other, dq_other)], [hc, (da_keep, [o]), (da_other, [o_other])]], (v_keep, v_other)
        )
        s_qo = Scatter(flat(qo_keep), flat(qo_send), tables)
        got_u2 = s_up.stage("2", n_t)
        s_qo.stage("3", 2, *got_d2, *got_u2, pooled, cut=CUT)
        both = Scatter(jnp.concatenate([s_down.keep, s_up.keep]), None, tables)
        both.send = [jnp.concatenate([a, b]) for a, b in zip(s_down.send, s_up.send, strict=True)]
        got_z = both.stage("Z", 1)
        dq = [after(d, qo_keep) for d in dq]
    dx = call(
        input_backward, n_t, 4, halved(*dq) + weights(*w_qo) + wholes(da, perm), wholes(sds((T, D), f32)),
        [pltpu.VMEM((T, D), f32)],
    )[0]

    if pairwise:
        s_qo.stage("2", n_t, dx)
        s_qo.stage("Z", 1, *got_z)
        g_qkv, g_out, g_qv, *vo = pl.pallas_call(
            finish,
            out_shape=[sds(qkv_weight.shape, f32), sds(out_weight.shape, f32), sds(qv_bias.shape, f32)]
            + [sds((1, dv), f32)] * 6 + [sds((1, up_bias.shape[0]), f32)],
            compiler_params=SMALL,
        )(s_qo.keep[0])
        vo = [v[0] for v in vo]
        g_down, g_up = both.keep[0], both.keep[1]
    else:
        def joined(*halves_of):
            g = jnp.concatenate([part[:, :, :BLK] for half in halves_of for part in half])
            return g.transpose(1, 0, 2, 3).reshape(n_t, D, -1)

        x_h, n1_h, db_h, da_h = (x_keep, x_send), (n1_keep, n1_send), (db_keep, db_send), (da_keep, da_send)
        g_full = jnp.concatenate([
            joined(*[gradient([[3 * hc, (x_h[j], dq)], [hc, (da_h[j], [o])]]) for j in range(2)]),
            joined(*[gradient([[fc, (n1_h[j], [du])]]) for j in range(2)]),
            joined(*[gradient([[fc, (db_h[j], [z])]]) for j in range(2)]),
        ], axis=2)
        mine = lax.psum_scatter(g_full, "tensor", scatter_dimension=0)
        mine = lax.psum_scatter(mine, "dp", scatter_dimension=0, tiled=True).astype(f32)
        g_qo, g_up, g_down = mine[:, : 4 * hc], mine[:, 4 * hc : 4 * hc + fc], mine[:, 4 * hc + fc :]
        g_rows = jnp.stack([v_keep, v_send]).transpose(0, 2, 1, 3).reshape(n_i * n_t, -1)
        dv_c, bu_c = sizes[1], sizes[2]
        cuts = [j * dv_c for j in range(9)] + [8 * dv_c + bu_c]
        g_v = jnp.concatenate(
            [g_rows[:, a:b].reshape(n_dp * n_t, -1) for a, b in zip(cuts[:-1], cuts[1:])], axis=1
        )
        g_v = lax.psum_scatter(g_v, AXES, scatter_dimension=0)
        g_qkv = jnp.stack([g_qo[:, c * hc : (c + 1) * hc] for c in range(3)])
        g_out = g_qo[:, 3 * hc :].T
        vo = [g_v[j * dv : (j + 1) * dv] for j in range(6)] + [g_v[8 * dv :]]
        g_qv = jnp.stack([g_v[6 * dv : 7 * dv], g_v[7 * dv : 8 * dv]])
    return (
        pooled.reshape(micro, seqs, segs, D),
        dx.reshape(micro, tokens, D),
        g_qkv, g_qv, g_out, vo[0], vo[1], vo[2], g_up, vo[6], g_down.T, vo[3], vo[4], vo[5],
    )


def solution(mesh):
    both = P(AXES)
    row3 = P(None, AXES)
    return jax.shard_map(
        per_device,
        mesh=mesh,
        in_specs=(
            row3, row3, row3, P(None, "dp", "tensor"), row3, P("tensor", "dp"), both, both, both,
            P("dp", "tensor"), both, P("tensor", "dp"), both, both, both,
        ),
        out_specs=(
            row3, row3, P(None, "dp", "tensor"), row3, P("tensor", "dp"), both, both, both,
            P("dp", "tensor"), both, P("tensor", "dp"), both, both, both,
        ),
        check_vma=False,
    )
```

```python
from functools import partial

import jax
import jax.numpy as jnp
from jax import lax
from jax.experimental import pallas as pl
from jax.experimental.pallas import tpu as pltpu
from jax.sharding import PartitionSpec as P

HD = 64
EPS = 1e-12
NEG = -1000000000.0
SCALE = float(HD) ** -0.5
AXES = ("dp", "tensor")
f32 = jnp.float32
bf16 = jnp.bfloat16
HI = lax.Precision.HIGHEST
BLK = 96
VMEM_LIMIT = 24 * 1024 * 1024
COST = 30_000_000
NORM = 2000
CUT = 4
SMALL = pltpu.CompilerParams(vmem_limit_bytes=8 * 1024 * 1024)


def nn(a, b):
    return lax.dot_general(a, b, (((1,), (0,)), ((), ())), preferred_element_type=f32)


def nt(a, b):
    return lax.dot_general(a, b, (((1,), (1,)), ((), ())), preferred_element_type=f32)


def tn(a, b):
    return lax.dot_general(a, b, (((0,), (0,)), ((), ())), preferred_element_type=f32)


def mean_last(v):
    return jnp.sum(v, axis=-1, keepdims=True) * (1.0 / v.shape[-1])


def normalize(values):
    center = values - mean_last(values)
    inverse = lax.rsqrt(mean_last(center * center) + EPS)
    return center * inverse, inverse


def normalize_back(scaled, normed, inverse):
    return inverse * (scaled - mean_last(scaled) - normed * mean_last(scaled * normed))


def col_sum(v):
    return jnp.sum(v, axis=0, keepdims=True)


def pack(qkv_ref, out_ref, ob_ref, g1_ref, s1_ref, db_ref, g2_ref, s2_ref, qv_ref, ub_ref, first_ref):
    rows, hc = qkv_ref.shape[1:]
    eye = (lax.broadcasted_iota(jnp.int32, (rows, rows), 0) == lax.broadcasted_iota(jnp.int32, (rows, rows), 1)).astype(bf16)
    for c in range(3):
        first_ref[:rows, c * hc : (c + 1) * hc] = qkv_ref[c]
    first_ref[:rows, 3 * hc :] = nt(eye, out_ref[...]).astype(bf16)
    parts = [r[...].astype(f32) for r in (ob_ref, g1_ref, s1_ref, db_ref, g2_ref, s2_ref, qv_ref)]
    short = jnp.concatenate(parts, axis=0).astype(bf16)
    count, size = short.shape
    wide = first_ref.shape[1]

    def spread(values, at):
        lane = lax.broadcasted_iota(jnp.int32, (values.shape[1], wide), 1) - at
        return nn(values, (lax.rem(lane + values.shape[1] * wide, values.shape[1]) == lax.broadcasted_iota(jnp.int32, lane.shape, 0)).astype(bf16))

    lane = lax.broadcasted_iota(jnp.int32, (count, wide), 1)
    start = lax.broadcasted_iota(jnp.int32, (count, wide), 0) * size
    row = col_sum(jnp.where((lane >= start) & (lane < start + size), spread(short, 0), 0.0))
    total, long = count * size, ub_ref.shape[1]
    lane = lax.broadcasted_iota(jnp.int32, (1, wide), 1)
    row = jnp.where((lane >= total) & (lane < total + long), spread(ub_ref[...], total), row)
    extra = first_ref.shape[0] - rows
    here = lax.broadcasted_iota(jnp.int32, (extra, wide), 0)
    first_ref[rows:, :] = jnp.where(here == 0, row, 0.0).astype(bf16)


def reorder(h_ref, perm_ref, x_ref, keep_ref, send_ref):
    x = nn(h_ref[...], perm_ref[...]).astype(bf16)
    x_ref[...] = x
    turned = x.T
    keep_ref[...] = turned[: x.shape[1] // 2]
    send_ref[...] = turned[x.shape[1] // 2 :]


def stacked(values, hc):
    head = lax.broadcasted_iota(jnp.int32, (1, hc), 1) // HD
    return jnp.concatenate([values * (head == h).astype(f32).astype(bf16) for h in range(hc // HD)], axis=0)


def own_columns(blocks, hc):
    n_heads = hc // HD
    length = blocks.shape[0] // n_heads
    head = lax.broadcasted_iota(jnp.int32, (1, hc), 1) // HD
    out = blocks[:length]
    for h in range(1, n_heads):
        out = jnp.where(head == h, blocks[h * length : (h + 1) * length], out)
    return out


def sections(values, length):
    return [values[:, c : c + length] for c in range(0, values.shape[1], length)]


def rows_of(refs):
    return jnp.concatenate([r[...].reshape(-1, r.shape[3]) for r in refs], axis=0)


def thirds(values):
    high = values.astype(bf16)
    rest = values - high.astype(f32)
    middle = rest.astype(bf16)
    return high, middle, (rest - middle.astype(f32)).astype(bf16)


def accumulate(acc_ref, step, add):
    @pl.when(step == 0)
    def _():
        acc_ref[...] = add

    @pl.when(step > 0)
    def _():
        acc_ref[...] += add


def iota(shape, axis):
    return lax.broadcasted_iota(jnp.int32, shape, axis)


def picks(count, first, wide, size):
    return (iota((count, wide), 0) == first + lax.rem(iota((1, wide), 1), size)).astype(bf16)


def belongs(count, wide, size, period):
    lane, row = iota((1, wide), 1), lax.rem(iota((count, 1), 0), period)
    return (lane >= row * size) & (lane < (row + 1) * size)


def read_vectors(rows, hot_d, hot_e, sizes):
    n_d, dv, bu, width, hc, fc, n_t = sizes
    count = rows.shape[0]
    per = count // n_t
    d_all = nn(hot_d, rows[:, : n_d * dv]).astype(bf16)
    mine = belongs(count, width, dv, count)
    d_rows = [col_sum(jnp.where(mine, nn(d_all, picks(n_d * dv, j * dv, width, dv)), 0.0)) for j in range(n_d)]
    e_all = nn(hot_e, rows[:, n_d * dv : n_d * dv + 2 * dv + bu]).astype(bf16)
    out = []
    for first, size, wide in ((0, dv, hc), (dv, dv, hc), (2 * dv, bu, fc)):
        spread = jnp.where(belongs(count, wide, size, per), nn(e_all, picks(e_all.shape[1], first, wide, size)), 0.0)
        out.append(jnp.sum(spread.reshape(n_t, per, wide), axis=1, keepdims=True))
    return jnp.concatenate(d_rows, axis=0), out


def write_vectors(d_rows, e_rows, hot_d, hot_e, sizes):
    n_d, dv, bu, width, hc, fc, n_t = sizes
    count = hot_d.shape[0]
    per = count // n_t
    mine = belongs(count, width, dv, count)
    d_all = sum(
        nt(jnp.where(mine, d_rows[j : j + 1, :], 0.0).astype(bf16), picks(n_d * dv, j * dv, width, dv)) for j in range(n_d)
    ).astype(bf16)
    e_all = 0.0
    for value, first, size, wide in zip(e_rows, (0, dv, 2 * dv), (dv, dv, bu), (hc, hc, fc), strict=True):
        spread = jnp.broadcast_to(value, (n_t, per, wide)).reshape(count, wide)
        spread = jnp.where(belongs(count, wide, size, per), spread, 0.0).astype(bf16)
        e_all = e_all + nt(spread, picks(2 * dv + bu, first, wide, size))
    return jnp.concatenate([tn(hot_d, d_all), tn(hot_e, e_all.astype(bf16))], axis=1)


def attention_forward(sizes, x_ref, w0_ref, w1_ref, w2_ref, w3_ref, v0_ref, v1_ref, v2_ref, v3_ref, hd_ref, he_ref,
                      segc_ref, segr_ref, qkv_ref, p_ref, o_ref, n1_ref, x1_ref, r1_ref, n1b_ref, n1t_ref, n1s_ref,
                      vec_ref, bu_ref, acc_ref, bq_ref, bv_ref):
    step = pl.program_id(0)
    hc = bq_ref.shape[-1]

    @pl.when(step == 0)
    def _():
        rows = jnp.concatenate([r[:, :, 0, :].reshape(-1, r.shape[3]) for r in (v0_ref, v1_ref, v2_ref, v3_ref)], axis=0)
        d_rows, (b_q, b_v, b_u) = read_vectors(rows, hd_ref[...], he_ref[...], sizes)
        vec_ref[...] = d_rows
        bq_ref[...] = b_q
        bv_ref[...] = b_v
        bu_ref[...] = b_u

    rows, length = segr_ref.shape
    x = x_ref[...]
    w = rows_of((w0_ref, w1_ref, w2_ref, w3_ref))
    qkv = nn(x, w[:, : 3 * hc])
    q = (qkv[:, :hc] + bq_ref[step]).astype(bf16) * bf16(SCALE)
    k = qkv[:, hc : 2 * hc].astype(bf16)
    v = (qkv[:, 2 * hc :] + bv_ref[step]).astype(bf16)
    qkv_ref[0, :, :hc] = q
    qkv_ref[0, :, hc : 2 * hc] = k
    qkv_ref[0, :, 2 * hc :] = v
    spans = [slice(g * length, (g + 1) * length) for g in range(rows)]
    scores = [nt(q[span], stacked(k[span], hc)) for span in spans]
    probs = []
    for g, span in enumerate(spans):
        same = segc_ref[span, :] == segr_ref[g : g + 1, :]
        parts = []
        for s in sections(scores[g], length):
            s = jnp.where(same, s, NEG)
            e = jnp.exp(s - jnp.max(s, axis=-1, keepdims=True))
            parts.append(e * (1.0 / jnp.sum(e, axis=-1, keepdims=True)))
        probs.append(jnp.concatenate(parts, axis=1))
    for g, span in enumerate(spans):
        p_ref[0, g] = probs[g]
        o_ref[0, span, :hc] = nn(probs[g].astype(bf16), stacked(v[span], hc)).astype(bf16)
    o_ref[0, :, hc:] = jnp.zeros((o_ref.shape[1], o_ref.shape[2] - hc), bf16)
    add = nt(o_ref[0, :, :hc], w[:, 3 * hc :])

    accumulate(acc_ref, step, add)

    @pl.when(step == pl.num_programs(0) - 1)
    def _():
        a = acc_ref[...] + vec_ref[0:1, :] + x_ref[...].astype(f32)
        normed, inverse = normalize(a)
        n1 = normed * vec_ref[1:2, :] + vec_ref[2:3, :]
        n1_ref[...] = n1
        x1_ref[...] = normed
        r1_ref[...] = inverse
        low = n1.astype(bf16)
        n1b_ref[...] = low
        turned = low.T
        n1t_ref[...] = turned[: low.shape[1] // 2]
        n1s_ref[...] = turned[low.shape[1] // 2 :]


def up_forward(n_ref, w0_ref, w1_ref, w2_ref, w3_ref, b_ref, z_ref, d_ref):
    u = nn(n_ref[...], rows_of((w0_ref, w1_ref, w2_ref, w3_ref))) + b_ref[0]
    phi = 0.5 + 0.5 * lax.erf(u * (0.5**0.5))
    z_ref[0] = (u * phi).astype(bf16)
    d_ref[0] = phi + u * (jnp.exp(-0.5 * u * u) * 0.3989422804014327)


def down_forward(z_ref, w0_ref, w1_ref, w2_ref, w3_ref, w4_ref, w5_ref, w6_ref, w7_ref, n1_ref, vec_ref, segc_ref, segr_ref, pg_ref,
                 pooled_ref, db_ref, dbb_ref, dbt_ref, dbs_ref, sums_ref, acc_ref):
    step = pl.program_id(0)
    add = nt(z_ref[0, 0], rows_of((w0_ref, w1_ref, w2_ref, w3_ref))) + nt(z_ref[1, 0], rows_of((w4_ref, w5_ref, w6_ref, w7_ref)))

    accumulate(acc_ref, step, add)

    @pl.when(step == pl.num_programs(0) - 1)
    def _():
        rows, length = segr_ref.shape
        segs = pg_ref.shape[1]
        b = acc_ref[...] + vec_ref[3:4, :] + n1_ref[...]
        x2, r2 = normalize(b)
        y = x2 * vec_ref[4:5, :] + vec_ref[5:6, :]
        grads = []
        for g in range(rows):
            span = slice(g * length, (g + 1) * length)
            hot_t = (iota((segs, length), 0) == segr_ref[g : g + 1, :]).astype(f32)
            count = jnp.sum(hot_t, axis=1, keepdims=True)
            hot_t = hot_t.astype(bf16)
            hot = (iota((length, segs), 1) == segc_ref[span, :]).astype(f32).astype(bf16)
            pooled_ref[g] = sum(nn(hot_t, part) for part in thirds(y[span, :])) / count
            grads.append(nn(jnp.concatenate([hot] * 3, axis=1), jnp.concatenate(thirds(pg_ref[g] / count), axis=0)))
        dy = jnp.concatenate(grads, axis=0)
        db = normalize_back(dy * vec_ref[4:5, :], x2, r2)
        db_ref[...] = db
        low = db.astype(bf16)
        dbb_ref[...] = low
        turned = low.T
        dbt_ref[...] = turned[: low.shape[1] // 2]
        dbs_ref[...] = turned[low.shape[1] // 2 :]
        sums_ref[0:1, :] = col_sum(db)
        sums_ref[1:2, :] = col_sum(dy * x2)
        sums_ref[2:3, :] = col_sum(dy)


def put(grad, ref):
    ref[:, :, :BLK, :] = grad.astype(bf16).reshape(grad.shape[0] // BLK, 1, BLK, grad.shape[1])


def hidden_backward(dbb_ref, w0_ref, w1_ref, w2_ref, w3_ref, w4_ref, w5_ref, w6_ref, w7_ref, d_ref, du_ref, bu_ref):
    for n, refs in enumerate(((w0_ref, w1_ref, w2_ref, w3_ref), (w4_ref, w5_ref, w6_ref, w7_ref))):
        du = (nn(dbb_ref[...], rows_of(refs)) * d_ref[n, 0]).astype(bf16)
        du_ref[n, 0] = du
        bu_ref[n, 0] = col_sum(du.astype(f32))


def step_value(refs, width):
    if len(refs) == 1:
        return refs[0][0, :, :width]
    return jnp.where(pl.program_id(0) < pl.num_programs(0) // 2, refs[0][0, :, :width], refs[1][0, :, :width])


def weight_gradient(groups, vectors, which, *refs):
    refs = list(refs)
    parts = []
    for pairs, split, width in groups:
        total = None
        for _ in range(pairs):
            rows = refs.pop(0)
            half = rows.shape[0] // 2
            rows = rows[...] if which is None else rows[which * half : (which + 1) * half, :]
            add = nn(rows, step_value([refs.pop(0) for _ in range(split)], width))
            total = add if total is None else total + add
        parts.append(total)
    grad = jnp.concatenate(parts, axis=1)
    extra = sum(refs.pop(0)[0].astype(f32) for _ in range(vectors)) if vectors else None
    half = grad.shape[0] // len(refs)
    for n, ref in enumerate(refs):
        put(grad[n * half : (n + 1) * half], ref)
        if vectors:
            for j in range(ref.shape[0]):
                at = (n if which is None else which) * ref.shape[0] + j
                row = extra[at : at + 1]
                tail = ref.shape[2] - BLK
                ref[j, 0, BLK:, :] = jnp.where(iota((tail, row.shape[1]), 0) == 0, row, 0.0).astype(bf16)


def norm_backward(du_ref, w0_ref, w1_ref, w2_ref, w3_ref, db_ref, x1_ref, r1_ref, vec_ref,
                  da_ref, dab_ref, dat_ref, das_ref, sums_ref, acc_ref):
    step = pl.program_id(0)
    accumulate(acc_ref, step, nt(du_ref[0], rows_of((w0_ref, w1_ref, w2_ref, w3_ref))))

    @pl.when(step == pl.num_programs(0) - 1)
    def _():
        dn1 = acc_ref[...].astype(bf16).astype(f32) + db_ref[...]
        da = normalize_back(dn1 * vec_ref[1:2, :], x1_ref[...], r1_ref[...])
        da_ref[...] = da
        low = da.astype(bf16)
        dab_ref[...] = low
        turned = low.T
        dat_ref[...] = turned[: low.shape[1] // 2]
        das_ref[...] = turned[low.shape[1] // 2 :]
        sums_ref[0:1, :] = col_sum(da)
        sums_ref[1:2, :] = col_sum(dn1 * x1_ref[...])
        sums_ref[2:3, :] = col_sum(dn1)


def attention_backward(sizes, dab_ref, w0_ref, w1_ref, w2_ref, w3_ref, qkv_ref, p_ref, s1_ref, s2_ref, gu_ref, hd_ref, he_ref,
                       low_ref, high_ref, keep_ref, send_ref, bq_ref, bv_ref, dqkv_ref):
    step = pl.program_id(0)
    hc = bq_ref.shape[-1]
    dab = dab_ref[...]
    w = rows_of([r.at[:, :, :, 3 * hc :] for r in (w0_ref, w1_ref, w2_ref, w3_ref)])
    do = nn(dab, w).astype(bf16)
    qkv = qkv_ref[0]
    rows, length = p_ref.shape[1], p_ref.shape[2]
    spans = [slice(g * length, (g + 1) * length) for g in range(rows)]
    q = [qkv[span, :hc] for span in spans]
    k = [stacked(qkv[span, hc : 2 * hc], hc) for span in spans]
    dps = [nt(do[span], stacked(qkv[span, 2 * hc :], hc)) for span in spans]
    dss = []
    for g in range(rows):
        parts = []
        for p, dp in zip(sections(p_ref[0, g], length), sections(dps[g], length)):
            pd = p * dp
            parts.append((pd - p * jnp.sum(pd, axis=-1, keepdims=True)).astype(bf16))
        dss.append(jnp.concatenate(parts, axis=1))
    for g, span in enumerate(spans):
        dqkv_ref[span, :hc] = (nn(dss[g], k[g]) * SCALE).astype(bf16)
        dqkv_ref[span, hc : 2 * hc] = own_columns(tn(dss[g], q[g]), hc).astype(bf16)
        dqkv_ref[span, 2 * hc : 3 * hc] = own_columns(tn(p_ref[0, g].astype(bf16), do[span]), hc).astype(bf16)
    dqkv_ref[:, 3 * hc :] = jnp.zeros((dqkv_ref.shape[0], dqkv_ref.shape[1] - 3 * hc), bf16)
    dqkv = dqkv_ref[...]
    half_steps = pl.num_programs(0) // 2

    @pl.when(step < half_steps)
    def _():
        low_ref[0] = dqkv

    @pl.when(step >= half_steps)
    def _():
        high_ref[0] = dqkv

    bq_ref[step] = col_sum(dqkv[:, :hc].astype(f32))
    bv_ref[step] = col_sum(dqkv[:, 2 * hc : 3 * hc].astype(f32))

    @pl.when(step == pl.num_programs(0) - 1)
    def _():
        d_rows = jnp.concatenate([s1_ref[...], s2_ref[...]], axis=0)
        rows = write_vectors(d_rows, (bq_ref[...], bv_ref[...], gu_ref[...]), hd_ref[...], he_ref[...], sizes)
        half, n_t = rows.shape[0] // 2, bq_ref.shape[0]
        rows = jnp.concatenate([rows, jnp.zeros((rows.shape[0], keep_ref.shape[-1] - rows.shape[1]), f32)], axis=1)
        for n, ref in enumerate((keep_ref, send_ref)):
            for t in range(n_t):
                for j in range(half // n_t):
                    at = n * half + j * n_t + t
                    ref[t, j : j + 1, :] = rows[at : at + 1]


def input_backward(low_ref, high_ref, w0_ref, w1_ref, w2_ref, w3_ref, da_ref, perm_ref, dx_ref, acc_ref):
    step = pl.program_id(0)
    cols = 3 * w0_ref.shape[-1] // 4
    w = rows_of((w0_ref, w1_ref, w2_ref, w3_ref))
    add = nt(step_value((low_ref, high_ref), cols), w[:, :cols])

    accumulate(acc_ref, step, add)

    @pl.when(step == pl.num_programs(0) - 1)
    def _():
        dx = acc_ref[...] + da_ref[...]
        perm = perm_ref[...]
        dx_ref[...] = sum(nt(part, perm) for part in thirds(dx))


def finish(total_ref, qkv_ref, out_ref, qv_ref, *vector_refs):
    total = total_ref[...]
    rows, hc = qkv_ref.shape[1:]
    for c in range(3):
        qkv_ref[c] = total[:rows, c * hc : (c + 1) * hc]
    out_ref[...] = total[:rows, 3 * hc :].T
    row = total[rows : rows + 1]
    at = 0
    for n, ref in enumerate(vector_refs):
        if n == 6:
            size = qv_ref.shape[1]
            qv_ref[...] = jnp.concatenate([row[:, at : at + size], row[:, at + size : at + 2 * size]], axis=0)
            at += 2 * size
        ref[...] = row[:, at : at + ref.shape[1]]
        at += ref.shape[1]


def whole(a):
    nd = len(a.shape)
    return pl.BlockSpec(a.shape, lambda s: (0,) * nd, pipeline_mode=pl.Buffered(1))


def lead(a):
    nd = len(a.shape)
    return pl.BlockSpec((1,) + a.shape[1:], lambda s: (s,) + (0,) * (nd - 1))


def weight(a):
    return pl.BlockSpec((a.shape[0], 1, BLK, a.shape[3]), lambda s: (0, s, 0, 0))


def half_spec(h):
    return pl.BlockSpec((h.shape[0], 1) + h.shape[2:], lambda s: (0, s, 0, 0))


def sds(shape, dtype):
    return jax.ShapeDtypeStruct(shape, dtype)


def far(shape, dtype):
    return pltpu.HBM(shape, dtype)


def call(body, n_t, micros, ins, outs, scratch=()):
    return pl.pallas_call(
        body,
        grid=(n_t,),
        in_specs=[s for _, s in ins],
        out_specs=[s for _, s in outs],
        out_shape=[a for a, _ in outs],
        scratch_shapes=list(scratch),
        compiler_params=pltpu.CompilerParams(
            dimension_semantics=("arbitrary",), vmem_limit_bytes=VMEM_LIMIT
        ),
        cost_estimate=pl.CostEstimate(flops=int(micros * COST), transcendentals=0, bytes_accessed=0),
    )(*[a for a, _ in ins])


def flips(n_dp, n_t):
    size = n_dp * n_t
    core = n_t
    x_bit, y_bit = 2 * core, 4 * core

    def table(bit_of):
        return [(i, i ^ bit_of(i)) for i in range(size)]

    return {
        "Z": [table(lambda i, d=d: d) for d in range(1, n_t)],
        "C": [table(lambda i: core)],
        "2": [table(lambda i: x_bit if i & core else y_bit)],
        "3": [table(lambda i: y_bit if i & core else x_bit)],
    }


def after(value, *done):
    return lax.optimization_barrier((value, *done))[0] if done else value


def swap(value, tables, *done):
    return lax.ppermute(after(value, *done), AXES, tables["C"][0])


class Gather:
    def __init__(self, value, tables):
        self.held, self.tables = [value[None]], tables

    def send(self, name, *done, parts=None, tables=None):
        sent = self.held if parts is None else [self.held[j] for j in parts]
        return [lax.ppermute(after(h, *done), AXES, t) for t in self.tables[name][tables or slice(None)] for h in sent]

    def take(self, name, got):
        self.held = [jnp.concatenate(self.held + got)] if name in "Z2" else self.held + got
        return got

    def stage(self, name, *done, parts=None):
        return self.take(name, self.send(name, *done, parts=parts))

    def pieces(self, *lead):
        return [h.reshape(*lead, *h.shape[1:]) for h in self.held]


class Scatter:
    def __init__(self, keep, send, tables):
        self.keep, self.send, self.tables = keep, [send], tables

    def stage(self, name, parts, *done, cut=1):
        tables = self.tables[name]
        pieces = len(self.send) // len(tables)
        got = [lax.ppermute(after(s, *done), AXES, tables[n // pieces]) for n, s in enumerate(self.send)]
        size = self.keep.shape[0] // parts // cut

        def piece(n):
            at = n * size
            total = self.keep[at : at + size].astype(f32)
            for t in range(len(tables)):
                mine = got[t * pieces : (t + 1) * pieces]
                wide = mine[0].shape[0]
                total = total + mine[at // wide][at % wide : at % wide + size].astype(f32)
            return total

        self.send = [piece(n).astype(bf16) for n in range(cut, parts * cut)]
        kept = [piece(n) for n in range(cut)]
        self.keep = kept[0] if cut == 1 else jnp.concatenate(kept)
        return got


def per_device(
    hidden_in, segment_ids, pooled_grad, qkv_weight, qv_bias, out_weight, out_bias,
    norm1_gain, norm1_shift, up_weight, up_bias, down_weight_in, down_bias, norm2_gain, norm2_shift,
):
    n_dp, n_t = lax.axis_size("dp"), lax.axis_size("tensor")
    at_dp, at_t = lax.axis_index("dp"), lax.axis_index("tensor")
    hc, fc = qkv_weight.shape[2], up_weight.shape[1]
    rows = qkv_weight.shape[1]
    D = rows * n_dp
    micro, tokens = hidden_in.shape[0], hidden_in.shape[1]
    seqs, L = segment_ids.shape[1], segment_ids.shape[2]
    G, T = micro * seqs, micro * tokens
    segs = pooled_grad.shape[2]
    n_i = D // BLK
    pairwise = (n_dp, n_t) == (8, 4) and 4 * hc == fc

    d_parts = [out_bias, norm1_gain, norm1_shift, down_bias, norm2_gain, norm2_shift]
    e_parts = [qv_bias[0], qv_bias[1], up_bias]
    dv = out_bias.shape[0]
    n_vec = sum(p.shape[0] for p in d_parts + e_parts)
    nd = len(d_parts) * dv

    sizes = (6, dv, up_bias.shape[0], D, hc, fc, n_t) if pairwise else (6, D // (n_i * n_t), n_t * fc // (n_i * n_t), D, hc, fc, n_t)
    slot = jnp.arange(n_i * n_t)
    rel = jnp.arange(n_i)
    if pairwise:
        tables = flips(n_dp, n_t)
        packed = (qkv_weight, out_weight, *[p[None] for p in d_parts], qv_bias, up_bias[None])
        packed = pl.pallas_call(pack, out_shape=sds((BLK + 8, 4 * hc), bf16))(*packed)
        first, middle = Gather(packed, tables), Gather(up_weight, tables)
        own = down_weight_in.T[None]

        def move(value, name, *done, way=0):
            return lax.ppermute(after(value, *done), AXES, tables[name][way])

        own2 = move(own, "2")
        done = first.stage("Z") + [own2]
        own2 = jnp.concatenate([own, own2])

        core = (at_dp & 1) ^ (rel >> 2)
        s3, s2 = (rel >> 1) & 1, rel & 1
        dy, dx = jnp.where(core == 0, s2, s3), jnp.where(core == 0, s3, s2)
        absolute = ((((at_dp >> 2) & 1) ^ dy) << 2) | ((((at_dp >> 1) & 1) ^ dx) << 1) | core
        i_p = jnp.broadcast_to(absolute[:, None], (n_i, n_t)).reshape(-1)
        t_p = jnp.broadcast_to((at_t ^ jnp.arange(n_t))[None], (n_i, n_t)).reshape(-1)
        to_d = jnp.broadcast_to(rel[:, None], (n_i, n_t)).reshape(-1) * n_t + t_p
        to_e = (((i_p * n_t) // n_i) ^ at_t) * n_i + (i_p * n_t + t_p) % n_i
    else:
        absolute, to_d, to_e = rel, slot, slot
    hot_d = (to_d[None, :] == slot[:, None]).astype(bf16)
    hot_e = (to_e[None, :] == slot[:, None]).astype(bf16)
    lane = jnp.arange(D)
    same_block = jnp.repeat(jnp.repeat((absolute[:, None] == rel[None, :]).T, BLK, axis=0), BLK, axis=1)
    perm = (same_block & ((lane[:, None] % BLK) == (lane[None, :] % BLK))).astype(bf16)
    turned = (D // 2, T)
    x, x_keep, x_send = pl.pallas_call(
        reorder, out_shape=[sds((T, D), bf16), sds(turned, bf16), sds(turned, bf16)], compiler_params=SMALL
    )(hidden_in.reshape(T, D), perm)
    pg = jnp.einsum("gsd,de->gse", pooled_grad.reshape(G, segs, D), perm.astype(f32), precision=HI)
    seg_r = segment_ids.reshape(G, L)
    seg_c = segment_ids.reshape(T, 1)

    if pairwise:
        done = first.stage("2", *done, x, x_keep, x_send, pg, hot_d, hot_e) + middle.stage("Z", *done)
        x_other = swap(x_send, tables, *done)
        z_one, z_two = move(own2, "Z", *done, way=0), move(own2, "Z", *done, way=1)
        got_q3, got_u2 = first.stage("3", *done), middle.stage("2", *done)
        first.stage("C", *got_u2, z_one, z_two)
        got_u3 = middle.send("3")
        z_three = move(own2, "Z", *got_q3, z_one, z_two, way=2)
        low = jnp.concatenate([own2, z_one])
        low_far = move(low, "3", *got_q3)
        w_qo = first.pieces(2, n_t)
    else:
        heads_in = [qkv_weight[0], qkv_weight[1], qkv_weight[2], out_weight.T]
        main = jnp.concatenate([*heads_in, up_weight, down_weight_in.T], axis=1)
        vec = jnp.concatenate(d_parts + e_parts)
        full = lax.all_gather(lax.all_gather(main, "dp", axis=0, tiled=True), "tensor", axis=0)
        full = full.reshape(n_t, n_i, BLK, -1).transpose(1, 0, 2, 3)
        vecs = lax.all_gather(lax.all_gather(vec, "tensor"), "dp").reshape(n_dp * n_t, -1)
        cuts = [j * dv for j in range(9)] + [n_vec]
        rows8 = jnp.concatenate([vecs[:, a:b].reshape(n_i * n_t, -1) for a, b in zip(cuts[:-1], cuts[1:])], axis=1)
        rows8 = jnp.pad(rows8.reshape(n_i, n_t, 1, -1), ((0, 0), (0, 0), (0, 7), (0, 4 * hc - rows8.shape[1])))
        quarters = [full[j * n_i // 4 : (j + 1) * n_i // 4] for j in range(4)]
        w_qo = [
            jnp.concatenate([w[..., : 4 * hc], rows8[j * n_i // 4 : (j + 1) * n_i // 4]], axis=2)
            for j, w in enumerate(quarters)
        ]
        w_up = [w[..., 4 * hc : 4 * hc + fc] for w in quarters]
        w_down = [w[..., 4 * hc + fc :].transpose(1, 0, 2, 3) for w in quarters]
        w_down = [w[: n_t // 2] for w in w_down] + [w[n_t // 2 :] for w in w_down]

    hl = hc // HD * L
    o_wide, q_wide = -(-hc // 128) * 128, -(-3 * hc // 128) * 128

    def leads(*arrays):
        return [(a, lead(a)) for a in arrays]

    def wholes(*arrays):
        return [(a, whole(a)) for a in arrays]

    def weights(*arrays):
        return [(a, weight(a)) for a in arrays]

    def weights_t(*arrays):
        return [(a, pl.BlockSpec((1, a.shape[1], BLK, a.shape[3]), lambda s: (s, 0, 0, 0))) for a in arrays]

    def paired(*arrays):
        return [(a, pl.BlockSpec((2, 1) + a.shape[2:], lambda s: (0, s, 0, 0))) for a in arrays]

    def folded(a):
        return a.reshape(2, n_t // 2, *a.shape[1:])

    tails = [
        (w, pl.BlockSpec((w.shape[0], n_t, 8, w.shape[3]), lambda s: (0, 0, BLK // 8, 0), pipeline_mode=pl.Buffered(1)))
        for w in w_qo
    ]
    qkv, prob, o, n1, x1, r1, n1b, n1_keep, n1_send, vec_d, b_u = call(
        partial(attention_forward, sizes), n_t, 10,
        wholes(x) + weights(*w_qo) + tails + wholes(hot_d, hot_e, seg_c, seg_r),
        leads(far((n_t, T, 3 * hc), bf16), far((n_t, G, L, hl), f32), far((n_t, T, o_wide), bf16))
        + wholes(sds((T, D), f32), far((T, D), f32), far((T, 1), f32), sds((T, D), bf16), far(turned, bf16), far(turned, bf16))
        + wholes(sds((6, D), f32), sds((n_t, 1, fc), f32)),
        [pltpu.VMEM((T, D), f32), pltpu.VMEM((n_t, 1, hc), f32), pltpu.VMEM((n_t, 1, hc), f32)],
    )
    if pairwise:
        middle.take("3", [after(g, n1b) for g in got_u3])
        middle.stage("C", n1b, z_three)
        high = jnp.concatenate([z_two, after(z_three, n1b)])
        high_far = move(high, "3")
        w_up = middle.pieces(2, n_t)
        low_other = [swap(low, tables, n1b), swap(after(low_far, n1b), tables)]
        o_other = swap(o, tables)
        b_u = after(b_u, *low_other)
    z, dgelu = call(
        up_forward, n_t, 4, wholes(n1b) + weights(*w_up) + leads(b_u),
        leads(sds((n_t, T, fc), bf16), sds((n_t, T, fc), f32)),
    )
    if pairwise:
        high_other = [swap(high, tables), swap(after(high_far, z), tables)]
        w_down = [low, low_far, *low_other, high, high_far, *high_other]
        w_down = [w.reshape(n_t // 2, 2, BLK, fc) for w in w_down]
        z_other = swap(z, tables, *high_other)
    pooled, db, dbb, db_keep, db_send, sums2 = call(
        down_forward, n_t // 2, 5.5, paired(folded(z)) + weights_t(*w_down) + wholes(n1, vec_d, seg_c, seg_r, pg),
        wholes(sds((G, segs, D), f32), sds((T, D), f32), sds((T, D), bf16), sds(turned, bf16), sds(turned, bf16), sds((3, D), f32)),
        [pltpu.VMEM((T, D), f32)],
    )

    def gradient(groups, vectors=(), at_once=True):
        ins, kinds = [], []
        for width, *pairs in groups:
            kinds.append((len(pairs), len(pairs[0][1]), width))
            for lhs, values in pairs:
                ins += wholes(lhs) + (leads(*values) if len(values) == 1 else halved(*values))
        out = sds((n_i // 4, n_t, BLK + (8 if vectors else 0), sum(k[2] for k in kinds)), bf16)

        def share(which):
            return call(
                partial(weight_gradient, kinds, len(vectors), which), n_t, 2, ins + leads(*vectors),
                [(out, half_spec(out))] * (2 if which is None else 1),
            )

        return share(None) if at_once else (share(0)[0], share(1)[0])

    def halved(low, high):
        block = (1,) + low.shape[1:]
        return [
            (low, pl.BlockSpec(block, lambda s: (jnp.minimum(s, n_t // 2 - 1), 0, 0))),
            (high, pl.BlockSpec(block, lambda s: (jnp.maximum(s - n_t // 2, 0), 0, 0))),
        ]

    def flat(a):
        return a.reshape((-1,) + a.shape[2:])

    du, g_bu = call(
        hidden_backward, n_t // 2, 3.5, wholes(dbb) + weights_t(*w_down) + paired(folded(dgelu)),
        paired(sds((2, n_t // 2, T, fc), bf16), sds((2, n_t // 2, 1, fc), f32)),
    )
    du, g_bu = du.reshape(n_t, T, fc), g_bu.reshape(n_t, 1, fc)
    if pairwise:
        db_other = swap(db_send, tables)
        du_other = swap(du, tables)
        down_keep, down_send = gradient([[fc, (after(db_keep, g_bu), [z]), (db_other, [z_other])]], at_once=False)
        n1_other = swap(n1_send, tables, down_send)
        s_down = Scatter(flat(down_keep), flat(down_send), tables)
        got_d3 = s_down.stage("3", 2)
        du_next = after(du, down_send)
        dab_after = down_keep
    else:
        du_next = du
    da, dab, da_keep, da_send, sums1 = call(
        norm_backward, n_t, NORM, leads(du_next) + weights(*w_up) + wholes(db, x1, r1, vec_d),
        wholes(sds((T, D), f32), sds((T, D), bf16), sds(turned, bf16), sds(turned, bf16), sds((3, D), f32)),
        [pltpu.VMEM((T, D), f32)],
    )
    if pairwise:
        da_other = swap(da_send, tables)
        up_keep, up_send = gradient([[fc, (after(n1_keep, da_keep), [du]), (n1_other, [du_other])]])
        s_up = Scatter(flat(up_keep), flat(up_send), tables)
        got_u3 = s_up.stage("3", 2)
        dab = after(dab, up_keep)
    rows = sds((n_t, n_i // 2, 4 * hc), f32)
    if pairwise:
        dab = after(dab, da_other, dab_after, x_other, o_other, *got_d3)
    dq_half = sds((n_t // 2, T, q_wide), bf16)
    *dq, v_keep, v_send = call(
        partial(attention_backward, sizes), n_t, 8,
        wholes(dab) + weights(*w_qo) + leads(qkv, prob) + wholes(sums1, sums2, g_bu, hot_d, hot_e),
        halved(dq_half, dq_half) + wholes(rows, rows),
        [pltpu.VMEM((n_t, 1, hc), f32), pltpu.VMEM((n_t, 1, hc), f32), pltpu.VMEM((T, q_wide), bf16)],
    )
    if pairwise:
        dq_other = [swap(d, tables) for d in dq]
        v_other = swap(v_send, tables)
        got_d2 = s_down.stage("2", n_t)
    pooled = jnp.einsum("gse,de->gsd", pooled, perm.astype(f32), precision=HI)
    if pairwise:
        x_now = after(x_keep, *got_u3)
        qo_keep, qo_send = gradient(
            [[3 * hc, (x_now, dq), (x_other, dq_other)], [hc, (da_keep, [o]), (da_other, [o_other])]], (v_keep, v_other)
        )
        s_qo = Scatter(flat(qo_keep), flat(qo_send), tables)
        got_u2 = s_up.stage("2", n_t)
        s_qo.stage("3", 2, *got_d2, *got_u2, pooled, cut=CUT)
        both = Scatter(jnp.concatenate([s_down.keep, s_up.keep]), None, tables)
        both.send = [jnp.concatenate([a, b]) for a, b in zip(s_down.send, s_up.send, strict=True)]
        got_z = both.stage("Z", 1)
        dq = [after(d, qo_keep) for d in dq]
    dx = call(
        input_backward, n_t, 4, halved(*dq) + weights(*w_qo) + wholes(da, perm), wholes(sds((T, D), f32)),
        [pltpu.VMEM((T, D), f32)],
    )[0]

    if pairwise:
        s_qo.stage("2", n_t, dx)
        s_qo.stage("Z", 1, *got_z)
        g_qkv, g_out, g_qv, *vo = pl.pallas_call(
            finish,
            out_shape=[sds(qkv_weight.shape, f32), sds(out_weight.shape, f32), sds(qv_bias.shape, f32)]
            + [sds((1, dv), f32)] * 6 + [sds((1, up_bias.shape[0]), f32)],
            compiler_params=SMALL,
        )(s_qo.keep[0])
        vo = [v[0] for v in vo]
        g_down, g_up = both.keep[0], both.keep[1]
    else:
        def joined(*halves_of):
            g = jnp.concatenate([part[:, :, :BLK] for half in halves_of for part in half])
            return g.transpose(1, 0, 2, 3).reshape(n_t, D, -1)

        x_h, n1_h, db_h, da_h = (x_keep, x_send), (n1_keep, n1_send), (db_keep, db_send), (da_keep, da_send)
        g_full = jnp.concatenate([
            joined(*[gradient([[3 * hc, (x_h[j], dq)], [hc, (da_h[j], [o])]]) for j in range(2)]),
            joined(*[gradient([[fc, (n1_h[j], [du])]]) for j in range(2)]),
            joined(*[gradient([[fc, (db_h[j], [z])]]) for j in range(2)]),
        ], axis=2)
        mine = lax.psum_scatter(g_full, "tensor", scatter_dimension=0)
        mine = lax.psum_scatter(mine, "dp", scatter_dimension=0, tiled=True).astype(f32)
        g_qo, g_up, g_down = mine[:, : 4 * hc], mine[:, 4 * hc : 4 * hc + fc], mine[:, 4 * hc + fc :]
        g_rows = jnp.stack([v_keep, v_send]).transpose(0, 2, 1, 3).reshape(n_i * n_t, -1)
        dv_c, bu_c = sizes[1], sizes[2]
        cuts = [j * dv_c for j in range(9)] + [8 * dv_c + bu_c]
        g_v = jnp.concatenate(
            [g_rows[:, a:b].reshape(n_dp * n_t, -1) for a, b in zip(cuts[:-1], cuts[1:])], axis=1
        )
        g_v = lax.psum_scatter(g_v, AXES, scatter_dimension=0)
        g_qkv = jnp.stack([g_qo[:, c * hc : (c + 1) * hc] for c in range(3)])
        g_out = g_qo[:, 3 * hc :].T
        vo = [g_v[j * dv : (j + 1) * dv] for j in range(6)] + [g_v[8 * dv :]]
        g_qv = jnp.stack([g_v[6 * dv : 7 * dv], g_v[7 * dv : 8 * dv]])
    return (
        pooled.reshape(micro, seqs, segs, D),
        dx.reshape(micro, tokens, D),
        g_qkv, g_qv, g_out, vo[0], vo[1], vo[2], g_up, vo[6], g_down.T, vo[3], vo[4], vo[5],
    )


def solution(mesh):
    both = P(AXES)
    row3 = P(None, AXES)
    return jax.shard_map(
        per_device,
        mesh=mesh,
        in_specs=(
            row3, row3, row3, P(None, "dp", "tensor"), row3, P("tensor", "dp"), both, both, both,
            P("dp", "tensor"), both, P("tensor", "dp"), both, both, both,
        ),
        out_specs=(
            row3, row3, P(None, "dp", "tensor"), row3, P("tensor", "dp"), both, both, both,
            P("dp", "tensor"), both, P("tensor", "dp"), both, both, both,
        ),
        check_vma=False,
    )
```
